128 devices in a mesh: xi: 4 (over x_hi, core), eta: 4 (over y), zeta: 8 (over z, x_lo).
Axes of the slice: x: 4 (x_hi: 2, x_lo: 2; x = x_hi * 2 + x_lo), y: 4, z: 4, core: 2. Of those that a mesh axis runs over, the one named last changes fastest.
Arguments:
- conserved_solution: float32 [5, 64, 64, 1024], P(None, 'xi', 'eta', 'zeta'), may hold values from -1.2 to 6, as said below
- metrics: float32 [3, 3, 64, 64, 1024], P(None, None, 'xi', 'eta', 'zeta'), may hold values from -0.4 to 1.4, as said below
- jacobian: float32 [64, 64, 1024], P('xi', 'eta', 'zeta'), may hold values from 0.7 to 1.4
Outputs:
- filtered: float32 [5, 64, 64, 1024], P(None, 'xi', 'eta', 'zeta')
The draws below stay inside these ranges and needn't reach their ends.
Inputs may be any that keep to these rules, and one draw needn't show every extreme that they name: conserved_solution[0] (density) lies between 0.5 and 2, and the pressure 0.4 (conserved_solution[4] - (conserved_solution[1]^2 + conserved_solution[2]^2 + conserved_solution[3]^2) / (2 conserved_solution[0])) lies between 0.5 and 1.5. The entries metrics[k, k] lie between 0.7 and 1.4, the others between -0.4 and 0.4.
All inputs are finite; a program needn't handle non-finite values.
Results may differ from the reference program's by a relative error of at most 0.00005.
Values sent between devices are 32-bit elements; how exact they have to be, the bound alone decides.
A program may use at most 64 MiB of HBM per device.

```python
import math
import jax
import jax.numpy as jnp
import numpy as np
from jax import lax

CX = 16
CY = 16
CZ = 128
WIDTH = 5
NX = 64
NY = 64
NZ = 1024
N_XI = 4
N_ETA = 4
N_ZETA = 8


def draw_conserved_solution(key, part):
    subkeys = jax.random.split(key, 3)
    density = jnp.exp(jax.random.uniform(subkeys[0], (NX, NY, NZ), jnp.float32, math.log(0.5), math.log(2.0)))
    fluid_speed_vector = jax.random.uniform(subkeys[1], (3, NX, NY, NZ), jnp.float32, -0.6, 0.6)
    thermodynamic_stress_scalar = jax.random.uniform(subkeys[2], (NX, NY, NZ), jnp.float32, 0.5, 1.5)
    momentum_density = density * fluid_speed_vector
    energy = thermodynamic_stress_scalar / 0.4 + 0.5 * jnp.sum(momentum_density * fluid_speed_vector, axis=0)
    return jnp.concatenate([density[None], momentum_density, energy[None]], axis=0)


def draw_metrics(key, part):
    subkeys = jax.random.split(key, 2)
    spread = 0.3
    diagonal = jnp.exp(jax.random.uniform(subkeys[0], (3, 3, NX, NY, NZ), jnp.float32, math.log(0.7), math.log(1.4)))
    offside = jax.random.uniform(subkeys[1], (3, 3, NX, NY, NZ), jnp.float32, -spread, spread)
    identity = jnp.eye(3, dtype=jnp.float32)[:, :, None, None, None] > 0.5
    return jnp.where(identity, diagonal, offside)


def block_levels(key, dims, cuts, least, high):
    factor_of, own = 1.0, jax.random.fold_in(key, 6)
    for dim, shards_of in cuts:
        heights = jnp.exp(jax.random.uniform(jax.random.fold_in(own, dim), (shards_of,), jnp.float32, least / len(cuts), high / len(cuts)))
        factor_of = factor_of * jnp.repeat(heights, dims[dim] // shards_of).reshape([-1 if axis == dim else 1 for axis in range(len(dims))])
    return factor_of


def setup_inputs(seed: int = 0) -> dict:
    arg_keys = jax.random.split(jax.random.key(seed), 4)
    return {
        "conserved_solution": draw_conserved_solution(jax.random.fold_in(arg_keys[3], 71), 0),
        "metrics": draw_metrics(jax.random.fold_in(arg_keys[3], 71), 0),
        "jacobian": jnp.clip(jnp.exp(math.log(1.4) - 0.6931472 * jax.random.uniform(arg_keys[2], (NX, NY, NZ), jnp.float32) ** block_levels(arg_keys[2], (NX, NY, NZ), ((0, 4), (1, 4), (2, 8)), -0.2, 0.2)), 0.7, 1.4),
    }


viscosity = 0.15
conduction = 0.15 * 1.4 / (0.4 * 0.72)
step_duration = 0.08


def banded_solve(system, source):
    extent = system.shape[0]
    lower = np.zeros(extent)
    upper = np.zeros(extent)
    middle = np.array([float(system[index, index]) for index in range(extent)])
    for index in range(1, extent):
        lower[index] = system[index, index - 1]
        upper[index - 1] = system[index - 1, index]
    rights = np.array(source)
    for index in range(1, extent):
        factor = lower[index] / middle[index - 1]
        middle[index] = middle[index] - factor * upper[index - 1]
        rights[index] = rights[index] - factor * rights[index - 1]
    answer = np.zeros(rights.shape)
    answer[extent - 1] = rights[extent - 1] / middle[extent - 1]
    for index in range(extent - 2, -1, -1):
        answer[index] = (rights[index] - upper[index] * answer[index + 1]) / middle[index]
    return answer


def derivative_table(length):
    extent = length + 2 * WIDTH
    system = np.eye(extent)
    source = np.zeros((extent, extent))
    for position in range(2, extent - 2):
        system[position, position - 1] = 1.0 / 3.0
        system[position, position + 1] = 1.0 / 3.0
        source[position, position + 1] = 7.0 / 9.0
        source[position, position - 1] = -7.0 / 9.0
        source[position, position + 2] = 1.0 / 36.0
        source[position, position - 2] = -1.0 / 36.0
    source[1, 2] = 0.5
    source[1, 0] = -0.5
    source[extent - 2, extent - 1] = 0.5
    source[extent - 2, extent - 3] = -0.5
    source[0, 1] = 1.0
    source[0, 0] = -1.0
    source[extent - 1, extent - 1] = 1.0
    source[extent - 1, extent - 2] = -1.0
    return banded_solve(system, source)[WIDTH:WIDTH + length]


def filter_table(length):
    strength = 0.4
    coeffs = [(193.0 + 126.0 * strength) / 256.0, (105.0 + 302.0 * strength) / 256.0,
              15.0 * (2.0 * strength - 1.0) / 64.0, 45.0 * (1.0 - 2.0 * strength) / 512.0,
              5.0 * (2.0 * strength - 1.0) / 256.0, (1.0 - 2.0 * strength) / 512.0]
    extent = length + 2 * WIDTH
    system = np.eye(extent)
    source = np.eye(extent)
    for position in range(5, extent - 5):
        system[position, position - 1] = strength
        system[position, position + 1] = strength
        source[position, position] = coeffs[0]
        for offset in range(1, 6):
            source[position, position + offset] = coeffs[offset] / 2.0
            source[position, position - offset] = coeffs[offset] / 2.0
    return banded_solve(system, source)[WIDTH:WIDTH + length]


def apply_lines(values, matrix, sweep_direction, blocks):
    moved = jnp.moveaxis(values, sweep_direction, -1)
    padded = jnp.concatenate([moved[..., -WIDTH:], moved, moved[..., :WIDTH]], axis=-1)
    length = matrix.shape[0]
    window = np.arange(blocks)[:, None] * length + np.arange(length + 2 * WIDTH)[None, :]
    subdomain_parts = padded[..., window]
    mapped = jnp.einsum('...bl,al->...ba', subdomain_parts, matrix, precision=lax.Precision.HIGHEST)
    return jnp.moveaxis(mapped.reshape(moved.shape), -1, sweep_direction)


def basic_quantities(conserved_solution):
    density = conserved_solution[0]
    fluid_speed_vector = conserved_solution[1:4] / density
    thermodynamic_stress_scalar = 0.4 * (conserved_solution[4] - 0.5 * jnp.sum(conserved_solution[1:4] * fluid_speed_vector, axis=0))
    return fluid_speed_vector, thermodynamic_stress_scalar, thermodynamic_stress_scalar / density


def fluxes(conserved_solution, fluid_speed_vector, thermodynamic_stress_scalar, slopes, metrics, jacobian):
    physical = [[jacobian * (metrics[0, column] * slopes[0][member] + metrics[1, column] * slopes[1][member]
                             + metrics[2, column] * slopes[2][member]) for column in range(3)] for member in range(4)]
    spread = physical[0][0] + physical[1][1] + physical[2][2]
    totals = []
    for column in range(3):
        stress = [viscosity * (physical[member][column] + physical[column][member]) for member in range(3)]
        stress[column] = stress[column] - (2.0 / 3.0) * viscosity * spread
        subdomain_parts = [conserved_solution[1 + column]]
        for member in range(3):
            carried = conserved_solution[1 + member] * fluid_speed_vector[column] - stress[member]
            if member == column:
                carried = carried + thermodynamic_stress_scalar
            subdomain_parts.append(carried)
        worked = fluid_speed_vector[0] * stress[0] + fluid_speed_vector[1] * stress[1] + fluid_speed_vector[2] * stress[2]
        subdomain_parts.append((conserved_solution[4] + thermodynamic_stress_scalar) * fluid_speed_vector[column] - worked - conduction * physical[3][column])
        totals.append(jnp.stack(subdomain_parts))
    return [metrics[direction, 0] * totals[0] + metrics[direction, 1] * totals[1] + metrics[direction, 2] * totals[2]
            for direction in range(3)]


def reference(conserved_solution, metrics, jacobian):
    blocks = (N_XI, N_ETA, N_ZETA)
    lengths = (CX, CY, CZ)
    derive = [jnp.asarray(derivative_table(length), dtype=jnp.float32) for length in lengths]
    smooth = [jnp.asarray(filter_table(length), dtype=jnp.float32) for length in lengths]
    fluid_speed_vector, thermodynamic_stress_scalar, thermal_level = basic_quantities(conserved_solution)
    basic_quantity = jnp.concatenate([fluid_speed_vector, thermal_level[None]], axis=0)
    slopes = [apply_lines(basic_quantity, derive[direction], direction + 1, blocks[direction]) for direction in range(3)]
    contra = fluxes(conserved_solution, fluid_speed_vector, thermodynamic_stress_scalar, slopes, metrics, jacobian)
    divergence = apply_lines(contra[0], derive[0], 1, blocks[0])
    divergence = divergence + apply_lines(contra[1], derive[1], 2, blocks[1])
    divergence = divergence + apply_lines(contra[2], derive[2], 3, blocks[2])
    sectioned = conserved_solution - step_duration * jacobian * divergence
    result = apply_lines(sectioned, smooth[0], 1, blocks[0])
    result = apply_lines(result, smooth[1], 2, blocks[1])
    return apply_lines(result, smooth[2], 3, blocks[2])
```

```python
import jax
import jax.numpy as jnp
import numpy as np
from jax import lax
from jax.sharding import PartitionSpec as P

WIDTH = 5


viscosity = 0.15
conduction = 0.15 * 1.4 / (0.4 * 0.72)
step_duration = 0.08
line_forms = ("", "al,flyz->fayz", "al,fxlz->fxaz", "al,fxyl->fxya")


def with_halo(value, sides, width):
    for axis, dim in sides:
        count, length = (lax.axis_size(axis), value.shape[dim])
        up = [(i, (i + 1) % count) for i in range(count)]
        down = [(j, i) for i, j in up]
        last = lax.slice_in_dim(value, length - width, length, axis=dim)
        initial = lax.slice_in_dim(value, 0, width, axis=dim)
        before = lax.ppermute(last, axis, up)
        after = lax.ppermute(initial, axis, down)
        value = jnp.concatenate([before, value, after], axis=dim)
    return value


def banded_solve(system, source):
    extent = system.shape[0]
    lower = np.zeros(extent)
    upper = np.zeros(extent)
    middle = np.array([float(system[index, index]) for index in range(extent)])
    for index in range(1, extent):
        lower[index] = system[index, index - 1]
        upper[index - 1] = system[index - 1, index]
    rights = np.array(source)
    for index in range(1, extent):
        factor = lower[index] / middle[index - 1]
        middle[index] = middle[index] - factor * upper[index - 1]
        rights[index] = rights[index] - factor * rights[index - 1]
    answer = np.zeros(rights.shape)
    answer[extent - 1] = rights[extent - 1] / middle[extent - 1]
    for index in range(extent - 2, -1, -1):
        answer[index] = (rights[index] - upper[index] * answer[index + 1]) / middle[index]
    return answer


def derivative_table(length):
    extent = length + 2 * WIDTH
    system = np.eye(extent)
    source = np.zeros((extent, extent))
    for position in range(2, extent - 2):
        system[position, position - 1] = 1.0 / 3.0
        system[position, position + 1] = 1.0 / 3.0
        source[position, position + 1] = 7.0 / 9.0
        source[position, position - 1] = -7.0 / 9.0
        source[position, position + 2] = 1.0 / 36.0
        source[position, position - 2] = -1.0 / 36.0
    source[1, 2] = 0.5
    source[1, 0] = -0.5
    source[extent - 2, extent - 1] = 0.5
    source[extent - 2, extent - 3] = -0.5
    source[0, 1] = 1.0
    source[0, 0] = -1.0
    source[extent - 1, extent - 1] = 1.0
    source[extent - 1, extent - 2] = -1.0
    return banded_solve(system, source)[WIDTH : WIDTH + length]


def filter_table(length):
    strength = 0.4
    coeffs = [
        (193.0 + 126.0 * strength) / 256.0,
        (105.0 + 302.0 * strength) / 256.0,
        15.0 * (2.0 * strength - 1.0) / 64.0,
        45.0 * (1.0 - 2.0 * strength) / 512.0,
        5.0 * (2.0 * strength - 1.0) / 256.0,
        (1.0 - 2.0 * strength) / 512.0,
    ]
    extent = length + 2 * WIDTH
    system = np.eye(extent)
    source = np.eye(extent)
    for position in range(5, extent - 5):
        system[position, position - 1] = strength
        system[position, position + 1] = strength
        source[position, position] = coeffs[0]
        for offset in range(1, 6):
            source[position, position + offset] = coeffs[offset] / 2.0
            source[position, position - offset] = coeffs[offset] / 2.0
    return banded_solve(system, source)[WIDTH : WIDTH + length]


def sweep_lines(padded, matrix, dim):
    return jnp.einsum(line_forms[dim], matrix, padded, precision=lax.Precision.HIGHEST)


def faces_xi(values):
    return with_halo(values, (("xi", 1),), WIDTH)


def faces_eta(values):
    return with_halo(values, (("eta", 2),), WIDTH)


def faces_zeta(values):
    return with_halo(values, (("zeta", 3),), WIDTH)


def basic_quantities(conserved_solution):
    density = conserved_solution[0]
    fluid_speed_vector = conserved_solution[1:4] / density
    thermodynamic_stress_scalar = 0.4 * (
        conserved_solution[4] - 0.5 * jnp.sum(conserved_solution[1:4] * fluid_speed_vector, axis=0)
    )
    return (fluid_speed_vector, thermodynamic_stress_scalar, thermodynamic_stress_scalar / density)


def fluxes(
    conserved_solution, fluid_speed_vector, thermodynamic_stress_scalar, slopes, metrics, jacobian
):
    physical = [
        [
            jacobian
            * (
                metrics[0, column] * slopes[0][member]
                + metrics[1, column] * slopes[1][member]
                + metrics[2, column] * slopes[2][member]
            )
            for column in range(3)
        ]
        for member in range(4)
    ]
    spread = physical[0][0] + physical[1][1] + physical[2][2]
    totals = []
    for column in range(3):
        stress = [
            viscosity * (physical[member][column] + physical[column][member]) for member in range(3)
        ]
        stress[column] = stress[column] - 2.0 / 3.0 * viscosity * spread
        subdomain_parts = [conserved_solution[1 + column]]
        for member in range(3):
            carried = conserved_solution[1 + member] * fluid_speed_vector[column] - stress[member]
            if member == column:
                carried = carried + thermodynamic_stress_scalar
            subdomain_parts.append(carried)
        worked = (
            fluid_speed_vector[0] * stress[0]
            + fluid_speed_vector[1] * stress[1]
            + fluid_speed_vector[2] * stress[2]
        )
        subdomain_parts.append(
            (conserved_solution[4] + thermodynamic_stress_scalar) * fluid_speed_vector[column]
            - worked
            - conduction * physical[3][column]
        )
        totals.append(jnp.stack(subdomain_parts))
    return [
        metrics[direction, 0] * totals[0]
        + metrics[direction, 1] * totals[1]
        + metrics[direction, 2] * totals[2]
        for direction in range(3)
    ]


def local(conserved_solution, metrics, jacobian):
    lengths = conserved_solution.shape[1:]
    derive = [jnp.asarray(derivative_table(length), dtype=jnp.float32) for length in lengths]
    smooth = [jnp.asarray(filter_table(length), dtype=jnp.float32) for length in lengths]
    fluid_speed_vector, thermodynamic_stress_scalar, thermal_level = basic_quantities(
        conserved_solution
    )
    basic_quantity = jnp.concatenate([fluid_speed_vector, thermal_level[None]], axis=0)
    slopes = [
        sweep_lines(faces_xi(basic_quantity), derive[0], 1),
        sweep_lines(faces_eta(basic_quantity), derive[1], 2),
        sweep_lines(faces_zeta(basic_quantity), derive[2], 3),
    ]
    contra = fluxes(
        conserved_solution,
        fluid_speed_vector,
        thermodynamic_stress_scalar,
        slopes,
        metrics,
        jacobian,
    )
    divergence = sweep_lines(faces_xi(contra[0]), derive[0], 1)
    divergence = divergence + sweep_lines(faces_eta(contra[1]), derive[1], 2)
    divergence = divergence + sweep_lines(faces_zeta(contra[2]), derive[2], 3)
    sectioned = conserved_solution - step_duration * jacobian * divergence
    result = sweep_lines(faces_xi(sectioned), smooth[0], 1)
    result = sweep_lines(faces_eta(result), smooth[1], 2)
    result = sweep_lines(faces_zeta(result), smooth[2], 3)
    return result


def solution(mesh):
    in_specs = (
        P(None, "xi", "eta", "zeta"),
        P(None, None, "xi", "eta", "zeta"),
        P("xi", "eta", "zeta"),
    )
    out_specs = P(None, "xi", "eta", "zeta")
    return jax.shard_map(local, mesh=mesh, in_specs=in_specs, out_specs=out_specs, check_vma=False)
```

```python
import functools

import jax
import jax.numpy as jnp
import numpy as np
from jax import lax
from jax.experimental import pallas as pl
from jax.experimental.pallas import tpu as pltpu
from jax.sharding import PartitionSpec as P

WIDTH = 5


viscosity = 0.15
conduction = 0.15 * 1.4 / (0.4 * 0.72)
step_duration = 0.08
line_forms = ("", "al,flyz->fayz", "al,fxlz->fxaz", "al,fxyl->fxya")
MESH = pl.DeviceIdType.MESH
AXES = ("xi", "eta", "zeta")


def exchange_kernel(routes, sizes, *refs):
    count = len(routes)
    sources, targets = refs[:count], refs[count : 2 * count]
    send_sems, recv_sems = refs[2 * count :]
    here = [lax.axis_index(axis) for axis in AXES]

    def device(axis, step):
        place = list(here)
        slot = AXES.index(axis)
        place[slot] = lax.rem(here[slot] + step + sizes[slot], sizes[slot])
        return tuple(place)

    partners = []
    for axis, step in routes:
        for way in (step, -step):
            if (axis, way) not in partners:
                partners.append((axis, way))
    barrier = pltpu.get_barrier_semaphore()
    for axis, step in partners:
        pl.semaphore_signal(barrier, inc=1, device_id=device(axis, step), device_id_type=MESH)
    pl.semaphore_wait(barrier, len(partners))
    copies = []
    for index, (axis, step) in enumerate(routes):
        copy = pltpu.make_async_remote_copy(
            src_ref=sources[index],
            dst_ref=targets[index],
            send_sem=send_sems.at[index],
            recv_sem=recv_sems.at[index],
            device_id=device(axis, step),
            device_id_type=MESH,
        )
        copy.start()
        copies.append(copy)
    for copy in copies:
        copy.wait()


def exchange_faces(items, tag):
    sizes = tuple(lax.axis_size(axis) for axis in AXES)
    sends, routes = [], []
    for value, axis, dim in items:
        length = value.shape[dim]
        sends.append(lax.slice_in_dim(value, length - WIDTH, length, axis=dim))
        routes.append((axis, 1))
        sends.append(lax.slice_in_dim(value, 0, WIDTH, axis=dim))
        routes.append((axis, -1))
    received = pl.pallas_call(
        functools.partial(exchange_kernel, tuple(routes), sizes),
        out_shape=[jax.ShapeDtypeStruct(send.shape, send.dtype) for send in sends],
        in_specs=[pl.BlockSpec(memory_space=pltpu.VMEM)] * len(sends),
        out_specs=[pl.BlockSpec(memory_space=pltpu.VMEM)] * len(sends),
        scratch_shapes=[
            pltpu.SemaphoreType.DMA((len(sends),)),
            pltpu.SemaphoreType.DMA((len(sends),)),
        ],
        compiler_params=pltpu.CompilerParams(collective_id=tag, has_side_effects=True),
    )(*sends)
    return [
        jnp.concatenate([received[2 * index], value, received[2 * index + 1]], axis=dim)
        for index, (value, axis, dim) in enumerate(items)
    ]


def with_halo(value, sides, width):
    for axis, dim in sides:
        count, length = (lax.axis_size(axis), value.shape[dim])
        up = [(i, (i + 1) % count) for i in range(count)]
        down = [(j, i) for i, j in up]
        last = lax.slice_in_dim(value, length - width, length, axis=dim)
        initial = lax.slice_in_dim(value, 0, width, axis=dim)
        before = lax.ppermute(last, axis, up)
        after = lax.ppermute(initial, axis, down)
        value = jnp.concatenate([before, value, after], axis=dim)
    return value


def banded_solve(system, source):
    extent = system.shape[0]
    lower = np.zeros(extent)
    upper = np.zeros(extent)
    middle = np.array([float(system[index, index]) for index in range(extent)])
    for index in range(1, extent):
        lower[index] = system[index, index - 1]
        upper[index - 1] = system[index - 1, index]
    rights = np.array(source)
    for index in range(1, extent):
        factor = lower[index] / middle[index - 1]
        middle[index] = middle[index] - factor * upper[index - 1]
        rights[index] = rights[index] - factor * rights[index - 1]
    answer = np.zeros(rights.shape)
    answer[extent - 1] = rights[extent - 1] / middle[extent - 1]
    for index in range(extent - 2, -1, -1):
        answer[index] = (rights[index] - upper[index] * answer[index + 1]) / middle[index]
    return answer


def derivative_table(length):
    extent = length + 2 * WIDTH
    system = np.eye(extent)
    source = np.zeros((extent, extent))
    for position in range(2, extent - 2):
        system[position, position - 1] = 1.0 / 3.0
        system[position, position + 1] = 1.0 / 3.0
        source[position, position + 1] = 7.0 / 9.0
        source[position, position - 1] = -7.0 / 9.0
        source[position, position + 2] = 1.0 / 36.0
        source[position, position - 2] = -1.0 / 36.0
    source[1, 2] = 0.5
    source[1, 0] = -0.5
    source[extent - 2, extent - 1] = 0.5
    source[extent - 2, extent - 3] = -0.5
    source[0, 1] = 1.0
    source[0, 0] = -1.0
    source[extent - 1, extent - 1] = 1.0
    source[extent - 1, extent - 2] = -1.0
    return banded_solve(system, source)[WIDTH : WIDTH + length]


def filter_table(length):
    strength = 0.4
    coeffs = [
        (193.0 + 126.0 * strength) / 256.0,
        (105.0 + 302.0 * strength) / 256.0,
        15.0 * (2.0 * strength - 1.0) / 64.0,
        45.0 * (1.0 - 2.0 * strength) / 512.0,
        5.0 * (2.0 * strength - 1.0) / 256.0,
        (1.0 - 2.0 * strength) / 512.0,
    ]
    extent = length + 2 * WIDTH
    system = np.eye(extent)
    source = np.eye(extent)
    for position in range(5, extent - 5):
        system[position, position - 1] = strength
        system[position, position + 1] = strength
        source[position, position] = coeffs[0]
        for offset in range(1, 6):
            source[position, position + offset] = coeffs[offset] / 2.0
            source[position, position - offset] = coeffs[offset] / 2.0
    return banded_solve(system, source)[WIDTH : WIDTH + length]


def sweep_lines(padded, matrix, dim):
    return jnp.einsum(line_forms[dim], matrix, padded, precision=lax.Precision.HIGHEST)


def faces_xi(values):
    return with_halo(values, (("xi", 1),), WIDTH)


def faces_eta(values):
    return with_halo(values, (("eta", 2),), WIDTH)


def faces_zeta(values):
    return with_halo(values, (("zeta", 3),), WIDTH)


def basic_quantities(conserved_solution):
    density = conserved_solution[0]
    fluid_speed_vector = conserved_solution[1:4] / density
    thermodynamic_stress_scalar = 0.4 * (
        conserved_solution[4] - 0.5 * jnp.sum(conserved_solution[1:4] * fluid_speed_vector, axis=0)
    )
    return (fluid_speed_vector, thermodynamic_stress_scalar, thermodynamic_stress_scalar / density)


def fluxes(
    conserved_solution, fluid_speed_vector, thermodynamic_stress_scalar, slopes, metrics, jacobian
):
    physical = [
        [
            jacobian
            * (
                metrics[0, column] * slopes[0][member]
                + metrics[1, column] * slopes[1][member]
                + metrics[2, column] * slopes[2][member]
            )
            for column in range(3)
        ]
        for member in range(4)
    ]
    spread = physical[0][0] + physical[1][1] + physical[2][2]
    totals = []
    for column in range(3):
        stress = [
            viscosity * (physical[member][column] + physical[column][member]) for member in range(3)
        ]
        stress[column] = stress[column] - 2.0 / 3.0 * viscosity * spread
        subdomain_parts = [conserved_solution[1 + column]]
        for member in range(3):
            carried = conserved_solution[1 + member] * fluid_speed_vector[column] - stress[member]
            if member == column:
                carried = carried + thermodynamic_stress_scalar
            subdomain_parts.append(carried)
        worked = (
            fluid_speed_vector[0] * stress[0]
            + fluid_speed_vector[1] * stress[1]
            + fluid_speed_vector[2] * stress[2]
        )
        subdomain_parts.append(
            (conserved_solution[4] + thermodynamic_stress_scalar) * fluid_speed_vector[column]
            - worked
            - conduction * physical[3][column]
        )
        totals.append(jnp.stack(subdomain_parts))
    return [
        metrics[direction, 0] * totals[0]
        + metrics[direction, 1] * totals[1]
        + metrics[direction, 2] * totals[2]
        for direction in range(3)
    ]


def local(conserved_solution, metrics, jacobian):
    lengths = conserved_solution.shape[1:]
    derive = [jnp.asarray(derivative_table(length), dtype=jnp.float32) for length in lengths]
    smooth = [jnp.asarray(filter_table(length), dtype=jnp.float32) for length in lengths]
    fluid_speed_vector, thermodynamic_stress_scalar, thermal_level = basic_quantities(
        conserved_solution
    )
    basic_quantity = jnp.concatenate([fluid_speed_vector, thermal_level[None]], axis=0)
    padded = exchange_faces(
        [(basic_quantity, "xi", 1), (basic_quantity, "eta", 2), (basic_quantity, "zeta", 3)], 0
    )
    slopes = [sweep_lines(padded[k], derive[k], k + 1) for k in range(3)]
    contra = fluxes(
        conserved_solution,
        fluid_speed_vector,
        thermodynamic_stress_scalar,
        slopes,
        metrics,
        jacobian,
    )
    padded = exchange_faces([(contra[0], "xi", 1), (contra[1], "eta", 2), (contra[2], "zeta", 3)], 1)
    divergence = sweep_lines(padded[0], derive[0], 1)
    divergence = divergence + sweep_lines(padded[1], derive[1], 2)
    divergence = divergence + sweep_lines(padded[2], derive[2], 3)
    sectioned = conserved_solution - step_duration * jacobian * divergence
    result = sweep_lines(exchange_faces([(sectioned, "xi", 1)], 2)[0], smooth[0], 1)
    result = sweep_lines(exchange_faces([(result, "eta", 2)], 3)[0], smooth[1], 2)
    result = sweep_lines(exchange_faces([(result, "zeta", 3)], 4)[0], smooth[2], 3)
    return result


def solution(mesh):
    in_specs = (
        P(None, "xi", "eta", "zeta"),
        P(None, None, "xi", "eta", "zeta"),
        P("xi", "eta", "zeta"),
    )
    out_specs = P(None, "xi", "eta", "zeta")
    return jax.shard_map(local, mesh=mesh, in_specs=in_specs, out_specs=out_specs, check_vma=False)
```

```python
import functools

import jax
import jax.numpy as jnp
import numpy as np
from jax import lax
from jax.experimental import pallas as pl
from jax.experimental.pallas import tpu as pltpu
from jax.sharding import PartitionSpec as P

WIDTH = 5


viscosity = 0.15
conduction = 0.15 * 1.4 / (0.4 * 0.72)
step_duration = 0.08
line_forms = ("", "al,flyz->fayz", "al,fxlz->fxaz", "al,fxyl->fxya")
MESH = pl.DeviceIdType.MESH
AXES = ("xi", "eta", "zeta")


def exchange_kernel(routes, sizes, *refs):
    count = len(routes)
    sources, targets = refs[:count], refs[count : 2 * count]
    send_sems, recv_sems = refs[2 * count :]
    here = [lax.axis_index(axis) for axis in AXES]

    def device(axis, step):
        place = list(here)
        slot = AXES.index(axis)
        place[slot] = lax.rem(here[slot] + step + sizes[slot], sizes[slot])
        return tuple(place)

    partners = []
    for axis, step in routes:
        for way in (step, -step):
            if (axis, way) not in partners:
                partners.append((axis, way))
    barrier = pltpu.get_barrier_semaphore()
    for axis, step in partners:
        pl.semaphore_signal(barrier, inc=1, device_id=device(axis, step), device_id_type=MESH)
    pl.semaphore_wait(barrier, len(partners))
    copies = []
    for index, (axis, step) in enumerate(routes):
        copy = pltpu.make_async_remote_copy(
            src_ref=sources[index],
            dst_ref=targets[index],
            send_sem=send_sems.at[index],
            recv_sem=recv_sems.at[index],
            device_id=device(axis, step),
            device_id_type=MESH,
        )
        copy.start()
        copies.append(copy)
    for copy in copies:
        copy.wait()


def exchange_faces(items, tag):
    sizes = tuple(lax.axis_size(axis) for axis in AXES)
    sends, routes = [], []
    for value, axis, dim in items:
        length = value.shape[dim]
        for face, step in ((slice(length - WIDTH, length), 1), (slice(0, WIDTH), -1)):
            part = lax.slice_in_dim(value, face.start, face.stop, axis=dim)
            if dim == value.ndim - 1:
                part = jnp.moveaxis(part, dim, 1).reshape(part.shape[0], WIDTH, -1)
            sends.append(part)
            routes.append((axis, step))
    received = pl.pallas_call(
        functools.partial(exchange_kernel, tuple(routes), sizes),
        out_shape=[jax.ShapeDtypeStruct(send.shape, send.dtype) for send in sends],
        in_specs=[pl.BlockSpec(memory_space=pltpu.VMEM)] * len(sends),
        out_specs=[pl.BlockSpec(memory_space=pltpu.VMEM)] * len(sends),
        scratch_shapes=[
            pltpu.SemaphoreType.DMA((len(sends),)),
            pltpu.SemaphoreType.DMA((len(sends),)),
        ],
        compiler_params=pltpu.CompilerParams(collective_id=tag, has_side_effects=True),
    )(*sends)
    padded = []
    for index, (value, axis, dim) in enumerate(items):
        before, after = received[2 * index], received[2 * index + 1]
        if dim == value.ndim - 1:
            shape = (value.shape[0], WIDTH) + value.shape[1:dim]
            before = jnp.moveaxis(before.reshape(shape), 1, dim)
            after = jnp.moveaxis(after.reshape(shape), 1, dim)
        padded.append(jnp.concatenate([before, value, after], axis=dim))
    return padded


def with_halo(value, sides, width):
    for axis, dim in sides:
        count, length = (lax.axis_size(axis), value.shape[dim])
        up = [(i, (i + 1) % count) for i in range(count)]
        down = [(j, i) for i, j in up]
        last = lax.slice_in_dim(value, length - width, length, axis=dim)
        initial = lax.slice_in_dim(value, 0, width, axis=dim)
        before = lax.ppermute(last, axis, up)
        after = lax.ppermute(initial, axis, down)
        value = jnp.concatenate([before, value, after], axis=dim)
    return value


def banded_solve(system, source):
    extent = system.shape[0]
    lower = np.zeros(extent)
    upper = np.zeros(extent)
    middle = np.array([float(system[index, index]) for index in range(extent)])
    for index in range(1, extent):
        lower[index] = system[index, index - 1]
        upper[index - 1] = system[index - 1, index]
    rights = np.array(source)
    for index in range(1, extent):
        factor = lower[index] / middle[index - 1]
        middle[index] = middle[index] - factor * upper[index - 1]
        rights[index] = rights[index] - factor * rights[index - 1]
    answer = np.zeros(rights.shape)
    answer[extent - 1] = rights[extent - 1] / middle[extent - 1]
    for index in range(extent - 2, -1, -1):
        answer[index] = (rights[index] - upper[index] * answer[index + 1]) / middle[index]
    return answer


def derivative_table(length):
    extent = length + 2 * WIDTH
    system = np.eye(extent)
    source = np.zeros((extent, extent))
    for position in range(2, extent - 2):
        system[position, position - 1] = 1.0 / 3.0
        system[position, position + 1] = 1.0 / 3.0
        source[position, position + 1] = 7.0 / 9.0
        source[position, position - 1] = -7.0 / 9.0
        source[position, position + 2] = 1.0 / 36.0
        source[position, position - 2] = -1.0 / 36.0
    source[1, 2] = 0.5
    source[1, 0] = -0.5
    source[extent - 2, extent - 1] = 0.5
    source[extent - 2, extent - 3] = -0.5
    source[0, 1] = 1.0
    source[0, 0] = -1.0
    source[extent - 1, extent - 1] = 1.0
    source[extent - 1, extent - 2] = -1.0
    return banded_solve(system, source)[WIDTH : WIDTH + length]


def filter_table(length):
    strength = 0.4
    coeffs = [
        (193.0 + 126.0 * strength) / 256.0,
        (105.0 + 302.0 * strength) / 256.0,
        15.0 * (2.0 * strength - 1.0) / 64.0,
        45.0 * (1.0 - 2.0 * strength) / 512.0,
        5.0 * (2.0 * strength - 1.0) / 256.0,
        (1.0 - 2.0 * strength) / 512.0,
    ]
    extent = length + 2 * WIDTH
    system = np.eye(extent)
    source = np.eye(extent)
    for position in range(5, extent - 5):
        system[position, position - 1] = strength
        system[position, position + 1] = strength
        source[position, position] = coeffs[0]
        for offset in range(1, 6):
            source[position, position + offset] = coeffs[offset] / 2.0
            source[position, position - offset] = coeffs[offset] / 2.0
    return banded_solve(system, source)[WIDTH : WIDTH + length]


def sweep_lines(padded, matrix, dim):
    return jnp.einsum(line_forms[dim], matrix, padded, precision=lax.Precision.HIGHEST)


def faces_xi(values):
    return with_halo(values, (("xi", 1),), WIDTH)


def faces_eta(values):
    return with_halo(values, (("eta", 2),), WIDTH)


def faces_zeta(values):
    return with_halo(values, (("zeta", 3),), WIDTH)


def basic_quantities(conserved_solution):
    density = conserved_solution[0]
    fluid_speed_vector = conserved_solution[1:4] / density
    thermodynamic_stress_scalar = 0.4 * (
        conserved_solution[4] - 0.5 * jnp.sum(conserved_solution[1:4] * fluid_speed_vector, axis=0)
    )
    return (fluid_speed_vector, thermodynamic_stress_scalar, thermodynamic_stress_scalar / density)


def fluxes(
    conserved_solution, fluid_speed_vector, thermodynamic_stress_scalar, slopes, metrics, jacobian
):
    physical = [
        [
            jacobian
            * (
                metrics[0, column] * slopes[0][member]
                + metrics[1, column] * slopes[1][member]
                + metrics[2, column] * slopes[2][member]
            )
            for column in range(3)
        ]
        for member in range(4)
    ]
    spread = physical[0][0] + physical[1][1] + physical[2][2]
    totals = []
    for column in range(3):
        stress = [
            viscosity * (physical[member][column] + physical[column][member]) for member in range(3)
        ]
        stress[column] = stress[column] - 2.0 / 3.0 * viscosity * spread
        subdomain_parts = [conserved_solution[1 + column]]
        for member in range(3):
            carried = conserved_solution[1 + member] * fluid_speed_vector[column] - stress[member]
            if member == column:
                carried = carried + thermodynamic_stress_scalar
            subdomain_parts.append(carried)
        worked = (
            fluid_speed_vector[0] * stress[0]
            + fluid_speed_vector[1] * stress[1]
            + fluid_speed_vector[2] * stress[2]
        )
        subdomain_parts.append(
            (conserved_solution[4] + thermodynamic_stress_scalar) * fluid_speed_vector[column]
            - worked
            - conduction * physical[3][column]
        )
        totals.append(jnp.stack(subdomain_parts))
    return [
        metrics[direction, 0] * totals[0]
        + metrics[direction, 1] * totals[1]
        + metrics[direction, 2] * totals[2]
        for direction in range(3)
    ]


def local(conserved_solution, metrics, jacobian):
    lengths = conserved_solution.shape[1:]
    derive = [jnp.asarray(derivative_table(length), dtype=jnp.float32) for length in lengths]
    smooth = [jnp.asarray(filter_table(length), dtype=jnp.float32) for length in lengths]
    fluid_speed_vector, thermodynamic_stress_scalar, thermal_level = basic_quantities(
        conserved_solution
    )
    basic_quantity = jnp.concatenate([fluid_speed_vector, thermal_level[None]], axis=0)
    padded = exchange_faces(
        [(basic_quantity, "xi", 1), (basic_quantity, "eta", 2), (basic_quantity, "zeta", 3)], 0
    )
    slopes = [sweep_lines(padded[k], derive[k], k + 1) for k in range(3)]
    contra = fluxes(
        conserved_solution,
        fluid_speed_vector,
        thermodynamic_stress_scalar,
        slopes,
        metrics,
        jacobian,
    )
    padded = exchange_faces([(contra[0], "xi", 1), (contra[1], "eta", 2), (contra[2], "zeta", 3)], 1)
    divergence = sweep_lines(padded[0], derive[0], 1)
    divergence = divergence + sweep_lines(padded[1], derive[1], 2)
    divergence = divergence + sweep_lines(padded[2], derive[2], 3)
    sectioned = conserved_solution - step_duration * jacobian * divergence
    result = sweep_lines(exchange_faces([(sectioned, "xi", 1)], 2)[0], smooth[0], 1)
    result = sweep_lines(exchange_faces([(result, "eta", 2)], 3)[0], smooth[1], 2)
    result = sweep_lines(exchange_faces([(result, "zeta", 3)], 4)[0], smooth[2], 3)
    return result


def solution(mesh):
    in_specs = (
        P(None, "xi", "eta", "zeta"),
        P(None, None, "xi", "eta", "zeta"),
        P("xi", "eta", "zeta"),
    )
    out_specs = P(None, "xi", "eta", "zeta")
    return jax.shard_map(local, mesh=mesh, in_specs=in_specs, out_specs=out_specs, check_vma=False)
```

```python
import functools
import itertools

import jax
import jax.numpy as jnp
import numpy as np
from jax import lax
from jax.experimental import pallas as pl
from jax.experimental.pallas import tpu as pltpu
from jax.sharding import PartitionSpec as P

WIDTH = 5


viscosity = 0.15
conduction = 0.15 * 1.4 / (0.4 * 0.72)
step_duration = 0.08
line_forms = ("", "al,flyz->fayz", "al,fxlz->fxaz", "al,fxyl->fxya")
MESH = pl.DeviceIdType.MESH
AXES = ("xi", "eta", "zeta")


def exchange_kernel(routes, sizes, *refs):
    count = len(routes)
    sources, targets = refs[:count], refs[count : 2 * count]
    send_sems, recv_sems = refs[2 * count :]
    here = [lax.axis_index(axis) for axis in AXES]

    def device(offset):
        return tuple(
            lax.rem(here[slot] + offset[slot] + sizes[slot], sizes[slot]) for slot in range(3)
        )

    partners = []
    for offset in routes:
        for way in (offset, tuple(-step for step in offset)):
            if way not in partners:
                partners.append(way)
    barrier = pltpu.get_barrier_semaphore()
    for offset in partners:
        pl.semaphore_signal(barrier, inc=1, device_id=device(offset), device_id_type=MESH)
    pl.semaphore_wait(barrier, len(partners))
    copies = []
    for index, offset in enumerate(routes):
        copy = pltpu.make_async_remote_copy(
            src_ref=sources[index],
            dst_ref=targets[index],
            send_sem=send_sems.at[index],
            recv_sem=recv_sems.at[index],
            device_id=device(offset),
            device_id_type=MESH,
        )
        copy.start()
        copies.append(copy)
    for copy in copies:
        copy.wait()


def exchange(sends, routes, tag):
    sizes = tuple(lax.axis_size(axis) for axis in AXES)
    return pl.pallas_call(
        functools.partial(exchange_kernel, tuple(routes), sizes),
        out_shape=[jax.ShapeDtypeStruct(send.shape, send.dtype) for send in sends],
        in_specs=[pl.BlockSpec(memory_space=pltpu.VMEM)] * len(sends),
        out_specs=[pl.BlockSpec(memory_space=pltpu.VMEM)] * len(sends),
        scratch_shapes=[
            pltpu.SemaphoreType.DMA((len(sends),)),
            pltpu.SemaphoreType.DMA((len(sends),)),
        ],
        compiler_params=pltpu.CompilerParams(collective_id=tag, has_side_effects=True),
    )(*sends)


def offset_along(axis, step):
    return tuple(step if name == axis else 0 for name in AXES)


def exchange_faces(items, tag):
    sends, routes = [], []
    for value, axis, dim in items:
        length = value.shape[dim]
        for face, step in ((slice(length - WIDTH, length), 1), (slice(0, WIDTH), -1)):
            part = lax.slice_in_dim(value, face.start, face.stop, axis=dim)
            if dim == value.ndim - 1:
                part = jnp.moveaxis(part, dim, 1).reshape(part.shape[0], WIDTH, -1)
            sends.append(part)
            routes.append(offset_along(axis, step))
    received = exchange(sends, routes, tag)
    padded = []
    for index, (value, axis, dim) in enumerate(items):
        before, after = received[2 * index], received[2 * index + 1]
        if dim == value.ndim - 1:
            shape = (value.shape[0], WIDTH) + value.shape[1:dim]
            before = jnp.moveaxis(before.reshape(shape), 1, dim)
            after = jnp.moveaxis(after.reshape(shape), 1, dim)
        padded.append(jnp.concatenate([before, value, after], axis=dim))
    return padded


def exchange_box(value, tag):
    fields = value.shape[0]
    sends, routes, shapes = [], [], []
    for offset in itertools.product((-1, 0, 1), repeat=3):
        if offset == (0, 0, 0):
            continue
        part = value
        for slot, step in enumerate(offset):
            length = value.shape[slot + 1]
            if step == 1:
                part = lax.slice_in_dim(part, length - WIDTH, length, axis=slot + 1)
            elif step == -1:
                part = lax.slice_in_dim(part, 0, WIDTH, axis=slot + 1)
        shapes.append(part.shape)
        if offset[2] != 0:
            part = jnp.moveaxis(part, 3, 1).reshape(fields, WIDTH, -1)
        sends.append(part)
        routes.append(offset)
    received = exchange(sends, routes, tag)
    pieces = {}
    for index, offset in enumerate(routes):
        piece = received[index]
        if offset[2] != 0:
            shape = shapes[index]
            piece = jnp.moveaxis(piece.reshape((fields, WIDTH) + shape[1:3]), 1, 3)
        pieces[tuple(1 - step for step in offset)] = piece
    pieces[(1, 1, 1)] = value
    return jnp.concatenate(
        [
            jnp.concatenate(
                [jnp.concatenate([pieces[(ix, iy, iz)] for iz in range(3)], axis=3) for iy in range(3)],
                axis=2,
            )
            for ix in range(3)
        ],
        axis=1,
    )


def with_halo(value, sides, width):
    for axis, dim in sides:
        count, length = (lax.axis_size(axis), value.shape[dim])
        up = [(i, (i + 1) % count) for i in range(count)]
        down = [(j, i) for i, j in up]
        last = lax.slice_in_dim(value, length - width, length, axis=dim)
        initial = lax.slice_in_dim(value, 0, width, axis=dim)
        before = lax.ppermute(last, axis, up)
        after = lax.ppermute(initial, axis, down)
        value = jnp.concatenate([before, value, after], axis=dim)
    return value


def banded_solve(system, source):
    extent = system.shape[0]
    lower = np.zeros(extent)
    upper = np.zeros(extent)
    middle = np.array([float(system[index, index]) for index in range(extent)])
    for index in range(1, extent):
        lower[index] = system[index, index - 1]
        upper[index - 1] = system[index - 1, index]
    rights = np.array(source)
    for index in range(1, extent):
        factor = lower[index] / middle[index - 1]
        middle[index] = middle[index] - factor * upper[index - 1]
        rights[index] = rights[index] - factor * rights[index - 1]
    answer = np.zeros(rights.shape)
    answer[extent - 1] = rights[extent - 1] / middle[extent - 1]
    for index in range(extent - 2, -1, -1):
        answer[index] = (rights[index] - upper[index] * answer[index + 1]) / middle[index]
    return answer


def derivative_table(length):
    extent = length + 2 * WIDTH
    system = np.eye(extent)
    source = np.zeros((extent, extent))
    for position in range(2, extent - 2):
        system[position, position - 1] = 1.0 / 3.0
        system[position, position + 1] = 1.0 / 3.0
        source[position, position + 1] = 7.0 / 9.0
        source[position, position - 1] = -7.0 / 9.0
        source[position, position + 2] = 1.0 / 36.0
        source[position, position - 2] = -1.0 / 36.0
    source[1, 2] = 0.5
    source[1, 0] = -0.5
    source[extent - 2, extent - 1] = 0.5
    source[extent - 2, extent - 3] = -0.5
    source[0, 1] = 1.0
    source[0, 0] = -1.0
    source[extent - 1, extent - 1] = 1.0
    source[extent - 1, extent - 2] = -1.0
    return banded_solve(system, source)[WIDTH : WIDTH + length]


def filter_table(length):
    strength = 0.4
    coeffs = [
        (193.0 + 126.0 * strength) / 256.0,
        (105.0 + 302.0 * strength) / 256.0,
        15.0 * (2.0 * strength - 1.0) / 64.0,
        45.0 * (1.0 - 2.0 * strength) / 512.0,
        5.0 * (2.0 * strength - 1.0) / 256.0,
        (1.0 - 2.0 * strength) / 512.0,
    ]
    extent = length + 2 * WIDTH
    system = np.eye(extent)
    source = np.eye(extent)
    for position in range(5, extent - 5):
        system[position, position - 1] = strength
        system[position, position + 1] = strength
        source[position, position] = coeffs[0]
        for offset in range(1, 6):
            source[position, position + offset] = coeffs[offset] / 2.0
            source[position, position - offset] = coeffs[offset] / 2.0
    return banded_solve(system, source)[WIDTH : WIDTH + length]


def sweep_lines(padded, matrix, dim):
    return jnp.einsum(line_forms[dim], matrix, padded, precision=lax.Precision.HIGHEST)


def faces_xi(values):
    return with_halo(values, (("xi", 1),), WIDTH)


def faces_eta(values):
    return with_halo(values, (("eta", 2),), WIDTH)


def faces_zeta(values):
    return with_halo(values, (("zeta", 3),), WIDTH)


def basic_quantities(conserved_solution):
    density = conserved_solution[0]
    fluid_speed_vector = conserved_solution[1:4] / density
    thermodynamic_stress_scalar = 0.4 * (
        conserved_solution[4] - 0.5 * jnp.sum(conserved_solution[1:4] * fluid_speed_vector, axis=0)
    )
    return (fluid_speed_vector, thermodynamic_stress_scalar, thermodynamic_stress_scalar / density)


def fluxes(
    conserved_solution, fluid_speed_vector, thermodynamic_stress_scalar, slopes, metrics, jacobian
):
    physical = [
        [
            jacobian
            * (
                metrics[0, column] * slopes[0][member]
                + metrics[1, column] * slopes[1][member]
                + metrics[2, column] * slopes[2][member]
            )
            for column in range(3)
        ]
        for member in range(4)
    ]
    spread = physical[0][0] + physical[1][1] + physical[2][2]
    totals = []
    for column in range(3):
        stress = [
            viscosity * (physical[member][column] + physical[column][member]) for member in range(3)
        ]
        stress[column] = stress[column] - 2.0 / 3.0 * viscosity * spread
        subdomain_parts = [conserved_solution[1 + column]]
        for member in range(3):
            carried = conserved_solution[1 + member] * fluid_speed_vector[column] - stress[member]
            if member == column:
                carried = carried + thermodynamic_stress_scalar
            subdomain_parts.append(carried)
        worked = (
            fluid_speed_vector[0] * stress[0]
            + fluid_speed_vector[1] * stress[1]
            + fluid_speed_vector[2] * stress[2]
        )
        subdomain_parts.append(
            (conserved_solution[4] + thermodynamic_stress_scalar) * fluid_speed_vector[column]
            - worked
            - conduction * physical[3][column]
        )
        totals.append(jnp.stack(subdomain_parts))
    return [
        metrics[direction, 0] * totals[0]
        + metrics[direction, 1] * totals[1]
        + metrics[direction, 2] * totals[2]
        for direction in range(3)
    ]


def local(conserved_solution, metrics, jacobian):
    lengths = conserved_solution.shape[1:]
    derive = [jnp.asarray(derivative_table(length), dtype=jnp.float32) for length in lengths]
    smooth = [jnp.asarray(filter_table(length), dtype=jnp.float32) for length in lengths]
    fluid_speed_vector, thermodynamic_stress_scalar, thermal_level = basic_quantities(
        conserved_solution
    )
    basic_quantity = jnp.concatenate([fluid_speed_vector, thermal_level[None]], axis=0)
    padded = exchange_faces(
        [(basic_quantity, "xi", 1), (basic_quantity, "eta", 2), (basic_quantity, "zeta", 3)], 0
    )
    slopes = [sweep_lines(padded[k], derive[k], k + 1) for k in range(3)]
    contra = fluxes(
        conserved_solution,
        fluid_speed_vector,
        thermodynamic_stress_scalar,
        slopes,
        metrics,
        jacobian,
    )
    padded = exchange_faces([(contra[0], "xi", 1), (contra[1], "eta", 2), (contra[2], "zeta", 3)], 1)
    divergence = sweep_lines(padded[0], derive[0], 1)
    divergence = divergence + sweep_lines(padded[1], derive[1], 2)
    divergence = divergence + sweep_lines(padded[2], derive[2], 3)
    sectioned = conserved_solution - step_duration * jacobian * divergence
    result = sweep_lines(exchange_box(sectioned, 2), smooth[0], 1)
    result = sweep_lines(result, smooth[1], 2)
    result = sweep_lines(result, smooth[2], 3)
    return result


def solution(mesh):
    in_specs = (
        P(None, "xi", "eta", "zeta"),
        P(None, None, "xi", "eta", "zeta"),
        P("xi", "eta", "zeta"),
    )
    out_specs = P(None, "xi", "eta", "zeta")
    return jax.shard_map(local, mesh=mesh, in_specs=in_specs, out_specs=out_specs, check_vma=False)
```

```python
import functools

import jax
import jax.numpy as jnp
import numpy as np
from jax import lax
from jax.experimental import pallas as pl
from jax.experimental.pallas import tpu as pltpu
from jax.sharding import PartitionSpec as P

WIDTH = 5


viscosity = 0.15
conduction = 0.15 * 1.4 / (0.4 * 0.72)
step_duration = 0.08
line_forms = ("", "al,flyz->fayz", "al,fxlz->fxaz", "al,fxyl->fxya")
MESH = pl.DeviceIdType.MESH
AXES = ("xi", "eta", "zeta")


def exchange_kernel(routes, sizes, *refs):
    count = len(routes)
    sources, targets = refs[:count], refs[count : 2 * count]
    send_sems, recv_sems = refs[2 * count :]
    here = [lax.axis_index(axis) for axis in AXES]

    def device(axis, step):
        place = list(here)
        slot = AXES.index(axis)
        place[slot] = lax.rem(here[slot] + step + sizes[slot], sizes[slot])
        return tuple(place)

    partners = []
    for axis, step in routes:
        for way in (step, -step):
            if (axis, way) not in partners:
                partners.append((axis, way))
    barrier = pltpu.get_barrier_semaphore()
    for axis, step in partners:
        pl.semaphore_signal(barrier, inc=1, device_id=device(axis, step), device_id_type=MESH)
    pl.semaphore_wait(barrier, len(partners))
    copies = []
    for index, (axis, step) in enumerate(routes):
        copy = pltpu.make_async_remote_copy(
            src_ref=sources[index],
            dst_ref=targets[index],
            send_sem=send_sems.at[index],
            recv_sem=recv_sems.at[index],
            device_id=device(axis, step),
            device_id_type=MESH,
        )
        copy.start()
        copies.append(copy)
    for copy in copies:
        copy.wait()


def exchange_faces(items, tag):
    sizes = tuple(lax.axis_size(axis) for axis in AXES)
    sends, routes = [], []
    for value, axis, dim in items:
        length = value.shape[dim]
        for face, step in ((slice(length - WIDTH, length), 1), (slice(0, WIDTH), -1)):
            part = lax.slice_in_dim(value, face.start, face.stop, axis=dim)
            if dim == value.ndim - 1:
                part = jnp.moveaxis(part, dim, 1).reshape(part.shape[0], WIDTH, -1)
            sends.append(part)
            routes.append((axis, step))
    received = pl.pallas_call(
        functools.partial(exchange_kernel, tuple(routes), sizes),
        out_shape=[jax.ShapeDtypeStruct(send.shape, send.dtype) for send in sends],
        in_specs=[pl.BlockSpec(memory_space=pl.ANY)] * len(sends),
        out_specs=[pl.BlockSpec(memory_space=pl.ANY)] * len(sends),
        scratch_shapes=[
            pltpu.SemaphoreType.DMA((len(sends),)),
            pltpu.SemaphoreType.DMA((len(sends),)),
        ],
        compiler_params=pltpu.CompilerParams(collective_id=tag, has_side_effects=True),
    )(*sends)
    padded = []
    for index, (value, axis, dim) in enumerate(items):
        before, after = received[2 * index], received[2 * index + 1]
        if dim == value.ndim - 1:
            shape = (value.shape[0], WIDTH) + value.shape[1:dim]
            before = jnp.moveaxis(before.reshape(shape), 1, dim)
            after = jnp.moveaxis(after.reshape(shape), 1, dim)
        padded.append(jnp.concatenate([before, value, after], axis=dim))
    return padded


def with_halo(value, sides, width):
    for axis, dim in sides:
        count, length = (lax.axis_size(axis), value.shape[dim])
        up = [(i, (i + 1) % count) for i in range(count)]
        down = [(j, i) for i, j in up]
        last = lax.slice_in_dim(value, length - width, length, axis=dim)
        initial = lax.slice_in_dim(value, 0, width, axis=dim)
        before = lax.ppermute(last, axis, up)
        after = lax.ppermute(initial, axis, down)
        value = jnp.concatenate([before, value, after], axis=dim)
    return value


def banded_solve(system, source):
    extent = system.shape[0]
    lower = np.zeros(extent)
    upper = np.zeros(extent)
    middle = np.array([float(system[index, index]) for index in range(extent)])
    for index in range(1, extent):
        lower[index] = system[index, index - 1]
        upper[index - 1] = system[index - 1, index]
    rights = np.array(source)
    for index in range(1, extent):
        factor = lower[index] / middle[index - 1]
        middle[index] = middle[index] - factor * upper[index - 1]
        rights[index] = rights[index] - factor * rights[index - 1]
    answer = np.zeros(rights.shape)
    answer[extent - 1] = rights[extent - 1] / middle[extent - 1]
    for index in range(extent - 2, -1, -1):
        answer[index] = (rights[index] - upper[index] * answer[index + 1]) / middle[index]
    return answer


def derivative_table(length):
    extent = length + 2 * WIDTH
    system = np.eye(extent)
    source = np.zeros((extent, extent))
    for position in range(2, extent - 2):
        system[position, position - 1] = 1.0 / 3.0
        system[position, position + 1] = 1.0 / 3.0
        source[position, position + 1] = 7.0 / 9.0
        source[position, position - 1] = -7.0 / 9.0
        source[position, position + 2] = 1.0 / 36.0
        source[position, position - 2] = -1.0 / 36.0
    source[1, 2] = 0.5
    source[1, 0] = -0.5
    source[extent - 2, extent - 1] = 0.5
    source[extent - 2, extent - 3] = -0.5
    source[0, 1] = 1.0
    source[0, 0] = -1.0
    source[extent - 1, extent - 1] = 1.0
    source[extent - 1, extent - 2] = -1.0
    return banded_solve(system, source)[WIDTH : WIDTH + length]


def filter_table(length):
    strength = 0.4
    coeffs = [
        (193.0 + 126.0 * strength) / 256.0,
        (105.0 + 302.0 * strength) / 256.0,
        15.0 * (2.0 * strength - 1.0) / 64.0,
        45.0 * (1.0 - 2.0 * strength) / 512.0,
        5.0 * (2.0 * strength - 1.0) / 256.0,
        (1.0 - 2.0 * strength) / 512.0,
    ]
    extent = length + 2 * WIDTH
    system = np.eye(extent)
    source = np.eye(extent)
    for position in range(5, extent - 5):
        system[position, position - 1] = strength
        system[position, position + 1] = strength
        source[position, position] = coeffs[0]
        for offset in range(1, 6):
            source[position, position + offset] = coeffs[offset] / 2.0
            source[position, position - offset] = coeffs[offset] / 2.0
    return banded_solve(system, source)[WIDTH : WIDTH + length]


def sweep_lines(padded, matrix, dim):
    return jnp.einsum(line_forms[dim], matrix, padded, precision=lax.Precision.HIGHEST)


def faces_xi(values):
    return with_halo(values, (("xi", 1),), WIDTH)


def faces_eta(values):
    return with_halo(values, (("eta", 2),), WIDTH)


def faces_zeta(values):
    return with_halo(values, (("zeta", 3),), WIDTH)


def basic_quantities(conserved_solution):
    density = conserved_solution[0]
    fluid_speed_vector = conserved_solution[1:4] / density
    thermodynamic_stress_scalar = 0.4 * (
        conserved_solution[4] - 0.5 * jnp.sum(conserved_solution[1:4] * fluid_speed_vector, axis=0)
    )
    return (fluid_speed_vector, thermodynamic_stress_scalar, thermodynamic_stress_scalar / density)


def fluxes(
    conserved_solution, fluid_speed_vector, thermodynamic_stress_scalar, slopes, metrics, jacobian
):
    physical = [
        [
            jacobian
            * (
                metrics[0, column] * slopes[0][member]
                + metrics[1, column] * slopes[1][member]
                + metrics[2, column] * slopes[2][member]
            )
            for column in range(3)
        ]
        for member in range(4)
    ]
    spread = physical[0][0] + physical[1][1] + physical[2][2]
    totals = []
    for column in range(3):
        stress = [
            viscosity * (physical[member][column] + physical[column][member]) for member in range(3)
        ]
        stress[column] = stress[column] - 2.0 / 3.0 * viscosity * spread
        subdomain_parts = [conserved_solution[1 + column]]
        for member in range(3):
            carried = conserved_solution[1 + member] * fluid_speed_vector[column] - stress[member]
            if member == column:
                carried = carried + thermodynamic_stress_scalar
            subdomain_parts.append(carried)
        worked = (
            fluid_speed_vector[0] * stress[0]
            + fluid_speed_vector[1] * stress[1]
            + fluid_speed_vector[2] * stress[2]
        )
        subdomain_parts.append(
            (conserved_solution[4] + thermodynamic_stress_scalar) * fluid_speed_vector[column]
            - worked
            - conduction * physical[3][column]
        )
        totals.append(jnp.stack(subdomain_parts))
    return [
        metrics[direction, 0] * totals[0]
        + metrics[direction, 1] * totals[1]
        + metrics[direction, 2] * totals[2]
        for direction in range(3)
    ]


def local(conserved_solution, metrics, jacobian):
    lengths = conserved_solution.shape[1:]
    derive = [jnp.asarray(derivative_table(length), dtype=jnp.float32) for length in lengths]
    smooth = [jnp.asarray(filter_table(length), dtype=jnp.float32) for length in lengths]
    fluid_speed_vector, thermodynamic_stress_scalar, thermal_level = basic_quantities(
        conserved_solution
    )
    basic_quantity = jnp.concatenate([fluid_speed_vector, thermal_level[None]], axis=0)
    padded = exchange_faces(
        [(basic_quantity, "xi", 1), (basic_quantity, "eta", 2), (basic_quantity, "zeta", 3)], 0
    )
    slopes = [sweep_lines(padded[k], derive[k], k + 1) for k in range(3)]
    contra = fluxes(
        conserved_solution,
        fluid_speed_vector,
        thermodynamic_stress_scalar,
        slopes,
        metrics,
        jacobian,
    )
    padded = exchange_faces([(contra[0], "xi", 1), (contra[1], "eta", 2), (contra[2], "zeta", 3)], 1)
    divergence = sweep_lines(padded[0], derive[0], 1)
    divergence = divergence + sweep_lines(padded[1], derive[1], 2)
    divergence = divergence + sweep_lines(padded[2], derive[2], 3)
    sectioned = conserved_solution - step_duration * jacobian * divergence
    result = sweep_lines(exchange_faces([(sectioned, "xi", 1)], 2)[0], smooth[0], 1)
    result = sweep_lines(exchange_faces([(result, "eta", 2)], 3)[0], smooth[1], 2)
    result = sweep_lines(exchange_faces([(result, "zeta", 3)], 4)[0], smooth[2], 3)
    return result


def solution(mesh):
    in_specs = (
        P(None, "xi", "eta", "zeta"),
        P(None, None, "xi", "eta", "zeta"),
        P("xi", "eta", "zeta"),
    )
    out_specs = P(None, "xi", "eta", "zeta")
    return jax.shard_map(local, mesh=mesh, in_specs=in_specs, out_specs=out_specs, check_vma=False)
```

```python
import functools

import jax
import jax.numpy as jnp
import numpy as np
from jax import lax
from jax.experimental import pallas as pl
from jax.experimental.pallas import tpu as pltpu
from jax.sharding import PartitionSpec as P

WIDTH = 5


viscosity = 0.15
conduction = 0.15 * 1.4 / (0.4 * 0.72)
step_duration = 0.08
line_forms = ("", "al,flyz->fayz", "al,fxlz->fxaz", "al,fxyl->fxya")
MESH = pl.DeviceIdType.MESH
AXES = ("xi", "eta", "zeta")


def exchange_kernel(routes, sizes, count, *refs):
    sources, targets = refs[:count], refs[count:-2]
    send_sems, recv_sems = refs[-2:]
    here = [lax.axis_index(axis) for axis in AXES]

    def device(offset):
        return tuple(
            lax.rem(here[slot] + offset[slot] + sizes[slot], sizes[slot]) for slot in range(3)
        )

    partners = []
    for offset, *_ in routes:
        for way in (offset, tuple(-step for step in offset)):
            if way not in partners:
                partners.append(way)
    barrier = pltpu.get_barrier_semaphore()
    for offset in partners:
        pl.semaphore_signal(barrier, inc=1, device_id=device(offset), device_id_type=MESH)
    pl.semaphore_wait(barrier, len(partners))
    copies = []
    for index, (offset, source, source_at, target, target_at) in enumerate(routes):
        copy = pltpu.make_async_remote_copy(
            src_ref=sources[source].at[source_at],
            dst_ref=targets[target].at[target_at],
            send_sem=send_sems.at[index],
            recv_sem=recv_sems.at[index],
            device_id=device(offset),
            device_id_type=MESH,
        )
        copy.start()
        copies.append(copy)
    for copy in copies:
        copy.wait()


def exchange(arrays, routes, out_shapes, tag):
    sizes = tuple(lax.axis_size(axis) for axis in AXES)
    return pl.pallas_call(
        functools.partial(exchange_kernel, tuple(routes), sizes, len(arrays)),
        out_shape=out_shapes,
        in_specs=[pl.BlockSpec(memory_space=pl.ANY)] * len(arrays),
        out_specs=[pl.BlockSpec(memory_space=pl.ANY)] * len(out_shapes),
        scratch_shapes=[
            pltpu.SemaphoreType.DMA((len(routes),)),
            pltpu.SemaphoreType.DMA((len(routes),)),
        ],
        compiler_params=pltpu.CompilerParams(collective_id=tag, has_side_effects=True),
    )(*arrays)


def offset_along(axis, step):
    return tuple(step if name == axis else 0 for name in AXES)


def window(ndim, dim, start, stop):
    return tuple(slice(start, stop) if axis == dim else slice(None) for axis in range(ndim))


def exchange_faces(items, tag):
    arrays, routes, out_shapes = [], [], []
    for value, axis, dim in items:
        ndim, length = value.ndim, value.shape[dim]
        if dim == ndim - 1:
            both = jnp.stack(
                [
                    lax.slice_in_dim(value, length - WIDTH, length, axis=dim),
                    lax.slice_in_dim(value, 0, WIDTH, axis=dim),
                ]
            )
            both = jnp.moveaxis(both, dim + 1, 2).reshape(2, value.shape[0], WIDTH, -1)
            arrays.append(both)
            out_shapes.append(jax.ShapeDtypeStruct(both.shape, both.dtype))
            source, target = len(arrays) - 1, len(out_shapes) - 1
            routes.append((offset_along(axis, 1), source, 0, target, 0))
            routes.append((offset_along(axis, -1), source, 1, target, 1))
        elif dim == ndim - 2:
            face = value.shape[:dim] + (WIDTH,) + value.shape[dim + 1 :]
            arrays.append(lax.slice_in_dim(value, length - WIDTH, length, axis=dim))
            arrays.append(lax.slice_in_dim(value, 0, WIDTH, axis=dim))
            out_shapes += [jax.ShapeDtypeStruct(face, value.dtype)] * 2
            source, target = len(arrays) - 2, len(out_shapes) - 2
            whole = window(ndim, dim, None, None)
            routes.append((offset_along(axis, 1), source, whole, target, whole))
            routes.append((offset_along(axis, -1), source + 1, whole, target + 1, whole))
        else:
            arrays.append(value)
            face = value.shape[:dim] + (WIDTH,) + value.shape[dim + 1 :]
            out_shapes += [jax.ShapeDtypeStruct(face, value.dtype)] * 2
            source, target = len(arrays) - 1, len(out_shapes) - 2
            whole = window(ndim, dim, None, None)
            last, first = window(ndim, dim, length - WIDTH, length), window(ndim, dim, 0, WIDTH)
            routes.append((offset_along(axis, 1), source, last, target, whole))
            routes.append((offset_along(axis, -1), source, first, target + 1, whole))
    received = exchange(arrays, routes, out_shapes, tag)
    padded, place = [], 0
    for value, axis, dim in items:
        if dim == value.ndim - 1:
            both = received[place].reshape((2, value.shape[0], WIDTH) + value.shape[1:dim])
            both = jnp.moveaxis(both, 2, dim + 1)
            before, after = both[0], both[1]
            place += 1
        else:
            before, after = received[place], received[place + 1]
            place += 2
        padded.append(jnp.concatenate([before, value, after], axis=dim))
    return padded


def with_halo(value, sides, width):
    for axis, dim in sides:
        count, length = (lax.axis_size(axis), value.shape[dim])
        up = [(i, (i + 1) % count) for i in range(count)]
        down = [(j, i) for i, j in up]
        last = lax.slice_in_dim(value, length - width, length, axis=dim)
        initial = lax.slice_in_dim(value, 0, width, axis=dim)
        before = lax.ppermute(last, axis, up)
        after = lax.ppermute(initial, axis, down)
        value = jnp.concatenate([before, value, after], axis=dim)
    return value


def banded_solve(system, source):
    extent = system.shape[0]
    lower = np.zeros(extent)
    upper = np.zeros(extent)
    middle = np.array([float(system[index, index]) for index in range(extent)])
    for index in range(1, extent):
        lower[index] = system[index, index - 1]
        upper[index - 1] = system[index - 1, index]
    rights = np.array(source)
    for index in range(1, extent):
        factor = lower[index] / middle[index - 1]
        middle[index] = middle[index] - factor * upper[index - 1]
        rights[index] = rights[index] - factor * rights[index - 1]
    answer = np.zeros(rights.shape)
    answer[extent - 1] = rights[extent - 1] / middle[extent - 1]
    for index in range(extent - 2, -1, -1):
        answer[index] = (rights[index] - upper[index] * answer[index + 1]) / middle[index]
    return answer


def derivative_table(length):
    extent = length + 2 * WIDTH
    system = np.eye(extent)
    source = np.zeros((extent, extent))
    for position in range(2, extent - 2):
        system[position, position - 1] = 1.0 / 3.0
        system[position, position + 1] = 1.0 / 3.0
        source[position, position + 1] = 7.0 / 9.0
        source[position, position - 1] = -7.0 / 9.0
        source[position, position + 2] = 1.0 / 36.0
        source[position, position - 2] = -1.0 / 36.0
    source[1, 2] = 0.5
    source[1, 0] = -0.5
    source[extent - 2, extent - 1] = 0.5
    source[extent - 2, extent - 3] = -0.5
    source[0, 1] = 1.0
    source[0, 0] = -1.0
    source[extent - 1, extent - 1] = 1.0
    source[extent - 1, extent - 2] = -1.0
    return banded_solve(system, source)[WIDTH : WIDTH + length]


def filter_table(length):
    strength = 0.4
    coeffs = [
        (193.0 + 126.0 * strength) / 256.0,
        (105.0 + 302.0 * strength) / 256.0,
        15.0 * (2.0 * strength - 1.0) / 64.0,
        45.0 * (1.0 - 2.0 * strength) / 512.0,
        5.0 * (2.0 * strength - 1.0) / 256.0,
        (1.0 - 2.0 * strength) / 512.0,
    ]
    extent = length + 2 * WIDTH
    system = np.eye(extent)
    source = np.eye(extent)
    for position in range(5, extent - 5):
        system[position, position - 1] = strength
        system[position, position + 1] = strength
        source[position, position] = coeffs[0]
        for offset in range(1, 6):
            source[position, position + offset] = coeffs[offset] / 2.0
            source[position, position - offset] = coeffs[offset] / 2.0
    return banded_solve(system, source)[WIDTH : WIDTH + length]


def sweep_lines(padded, matrix, dim):
    return jnp.einsum(line_forms[dim], matrix, padded, precision=lax.Precision.HIGHEST)


def faces_xi(values):
    return with_halo(values, (("xi", 1),), WIDTH)


def faces_eta(values):
    return with_halo(values, (("eta", 2),), WIDTH)


def faces_zeta(values):
    return with_halo(values, (("zeta", 3),), WIDTH)


def basic_quantities(conserved_solution):
    density = conserved_solution[0]
    fluid_speed_vector = conserved_solution[1:4] / density
    thermodynamic_stress_scalar = 0.4 * (
        conserved_solution[4] - 0.5 * jnp.sum(conserved_solution[1:4] * fluid_speed_vector, axis=0)
    )
    return (fluid_speed_vector, thermodynamic_stress_scalar, thermodynamic_stress_scalar / density)


def fluxes(
    conserved_solution, fluid_speed_vector, thermodynamic_stress_scalar, slopes, metrics, jacobian
):
    physical = [
        [
            jacobian
            * (
                metrics[0, column] * slopes[0][member]
                + metrics[1, column] * slopes[1][member]
                + metrics[2, column] * slopes[2][member]
            )
            for column in range(3)
        ]
        for member in range(4)
    ]
    spread = physical[0][0] + physical[1][1] + physical[2][2]
    totals = []
    for column in range(3):
        stress = [
            viscosity * (physical[member][column] + physical[column][member]) for member in range(3)
        ]
        stress[column] = stress[column] - 2.0 / 3.0 * viscosity * spread
        subdomain_parts = [conserved_solution[1 + column]]
        for member in range(3):
            carried = conserved_solution[1 + member] * fluid_speed_vector[column] - stress[member]
            if member == column:
                carried = carried + thermodynamic_stress_scalar
            subdomain_parts.append(carried)
        worked = (
            fluid_speed_vector[0] * stress[0]
            + fluid_speed_vector[1] * stress[1]
            + fluid_speed_vector[2] * stress[2]
        )
        subdomain_parts.append(
            (conserved_solution[4] + thermodynamic_stress_scalar) * fluid_speed_vector[column]
            - worked
            - conduction * physical[3][column]
        )
        totals.append(jnp.stack(subdomain_parts))
    return [
        metrics[direction, 0] * totals[0]
        + metrics[direction, 1] * totals[1]
        + metrics[direction, 2] * totals[2]
        for direction in range(3)
    ]


def local(conserved_solution, metrics, jacobian):
    lengths = conserved_solution.shape[1:]
    derive = [jnp.asarray(derivative_table(length), dtype=jnp.float32) for length in lengths]
    smooth = [jnp.asarray(filter_table(length), dtype=jnp.float32) for length in lengths]
    fluid_speed_vector, thermodynamic_stress_scalar, thermal_level = basic_quantities(
        conserved_solution
    )
    basic_quantity = jnp.concatenate([fluid_speed_vector, thermal_level[None]], axis=0)
    padded = exchange_faces(
        [(basic_quantity, "xi", 1), (basic_quantity, "eta", 2), (basic_quantity, "zeta", 3)], 0
    )
    slopes = [sweep_lines(padded[k], derive[k], k + 1) for k in range(3)]
    contra = fluxes(
        conserved_solution,
        fluid_speed_vector,
        thermodynamic_stress_scalar,
        slopes,
        metrics,
        jacobian,
    )
    padded = exchange_faces([(contra[0], "xi", 1), (contra[1], "eta", 2), (contra[2], "zeta", 3)], 1)
    divergence = sweep_lines(padded[0], derive[0], 1)
    divergence = divergence + sweep_lines(padded[1], derive[1], 2)
    divergence = divergence + sweep_lines(padded[2], derive[2], 3)
    sectioned = conserved_solution - step_duration * jacobian * divergence
    result = sweep_lines(exchange_faces([(sectioned, "xi", 1)], 2)[0], smooth[0], 1)
    result = sweep_lines(exchange_faces([(result, "eta", 2)], 3)[0], smooth[1], 2)
    result = sweep_lines(exchange_faces([(result, "zeta", 3)], 4)[0], smooth[2], 3)
    return result


def solution(mesh):
    in_specs = (
        P(None, "xi", "eta", "zeta"),
        P(None, None, "xi", "eta", "zeta"),
        P("xi", "eta", "zeta"),
    )
    out_specs = P(None, "xi", "eta", "zeta")
    return jax.shard_map(local, mesh=mesh, in_specs=in_specs, out_specs=out_specs, check_vma=False)
```

```python
import functools

import jax
import jax.numpy as jnp
import numpy as np
from jax import lax
from jax.experimental import pallas as pl
from jax.experimental.pallas import tpu as pltpu
from jax.sharding import PartitionSpec as P

WIDTH = 5


viscosity = 0.15
conduction = 0.15 * 1.4 / (0.4 * 0.72)
step_duration = 0.08
line_forms = ("", "al,flyz->fayz", "al,fxlz->fxaz", "al,fxyl->fxya")
MESH = pl.DeviceIdType.MESH
AXES = ("xi", "eta", "zeta")


def exchange_kernel(routes, sizes, count, *refs):
    sources, targets = refs[:count], refs[count:-2]
    send_sems, recv_sems = refs[-2:]
    here = [lax.axis_index(axis) for axis in AXES]

    def device(offset):
        return tuple(
            lax.rem(here[slot] + offset[slot] + sizes[slot], sizes[slot]) for slot in range(3)
        )

    partners = []
    for offset, *_ in routes:
        for way in (offset, tuple(-step for step in offset)):
            if way not in partners:
                partners.append(way)
    barrier = pltpu.get_barrier_semaphore()
    for offset in partners:
        pl.semaphore_signal(barrier, inc=1, device_id=device(offset), device_id_type=MESH)
    pl.semaphore_wait(barrier, len(partners))
    copies = []
    for index, (offset, source, source_at, target, target_at) in enumerate(routes):
        copy = pltpu.make_async_remote_copy(
            src_ref=sources[source].at[source_at],
            dst_ref=targets[target].at[target_at],
            send_sem=send_sems.at[index],
            recv_sem=recv_sems.at[index],
            device_id=device(offset),
            device_id_type=MESH,
        )
        copy.start()
        copies.append(copy)
    for copy in copies:
        copy.wait()


def exchange(arrays, routes, out_shapes, tag):
    sizes = tuple(lax.axis_size(axis) for axis in AXES)
    return pl.pallas_call(
        functools.partial(exchange_kernel, tuple(routes), sizes, len(arrays)),
        out_shape=out_shapes,
        in_specs=[pl.BlockSpec(memory_space=pl.ANY)] * len(arrays),
        out_specs=[pl.BlockSpec(memory_space=pl.ANY)] * len(out_shapes),
        scratch_shapes=[
            pltpu.SemaphoreType.DMA((len(routes),)),
            pltpu.SemaphoreType.DMA((len(routes),)),
        ],
        compiler_params=pltpu.CompilerParams(collective_id=tag, has_side_effects=True),
    )(*arrays)


def offset_along(axis, step):
    return tuple(step if name == axis else 0 for name in AXES)


def window(ndim, dim, start, stop):
    return tuple(slice(start, stop) if axis == dim else slice(None) for axis in range(ndim))


def exchange_faces(items, tag):
    arrays, routes, out_shapes = [], [], []
    for value, axis, dim in items:
        ndim, length = value.ndim, value.shape[dim]
        if dim == ndim - 1:
            both = jnp.stack(
                [
                    lax.slice_in_dim(value, length - WIDTH, length, axis=dim),
                    lax.slice_in_dim(value, 0, WIDTH, axis=dim),
                ]
            )
            both = jnp.moveaxis(both, dim + 1, 2).reshape(2, value.shape[0], WIDTH, -1)
            arrays.append(both)
            out_shapes.append(jax.ShapeDtypeStruct(both.shape, both.dtype))
            source, target = len(arrays) - 1, len(out_shapes) - 1
            routes.append((offset_along(axis, 1), source, 0, target, 0))
            routes.append((offset_along(axis, -1), source, 1, target, 1))
        elif dim == ndim - 2:
            face = value.shape[:dim] + (WIDTH,) + value.shape[dim + 1 :]
            arrays.append(lax.slice_in_dim(value, length - WIDTH, length, axis=dim))
            arrays.append(lax.slice_in_dim(value, 0, WIDTH, axis=dim))
            out_shapes += [jax.ShapeDtypeStruct(face, value.dtype)] * 2
            source, target = len(arrays) - 2, len(out_shapes) - 2
            whole = window(ndim, dim, None, None)
            routes.append((offset_along(axis, 1), source, whole, target, whole))
            routes.append((offset_along(axis, -1), source + 1, whole, target + 1, whole))
        else:
            arrays.append(value)
            face = value.shape[:dim] + (WIDTH,) + value.shape[dim + 1 :]
            out_shapes += [jax.ShapeDtypeStruct(face, value.dtype)] * 2
            source, target = len(arrays) - 1, len(out_shapes) - 2
            whole = window(ndim, dim, None, None)
            last, first = window(ndim, dim, length - WIDTH, length), window(ndim, dim, 0, WIDTH)
            routes.append((offset_along(axis, 1), source, last, target, whole))
            routes.append((offset_along(axis, -1), source, first, target + 1, whole))
    received = exchange(arrays, routes, out_shapes, tag)
    padded, place = [], 0
    for value, axis, dim in items:
        if dim == value.ndim - 1:
            both = received[place].reshape((2, value.shape[0], WIDTH) + value.shape[1:dim])
            both = jnp.moveaxis(both, 2, dim + 1)
            before, after = both[0], both[1]
            place += 1
        else:
            before, after = received[place], received[place + 1]
            place += 2
        padded.append(jnp.concatenate([before, value, after], axis=dim))
    return padded


def exchange_plane(value, tag):
    length_x, length_y = value.shape[1], value.shape[2]
    faces_y = jnp.stack(
        [
            lax.slice_in_dim(value, length_y - WIDTH, length_y, axis=2),
            lax.slice_in_dim(value, 0, WIDTH, axis=2),
        ]
    )
    last_x, first_x = slice(length_x - WIDTH, length_x), slice(0, WIDTH)
    every = slice(None)
    routes = [
        ((1, 0, 0), 0, (every, last_x), 0, 0),
        ((-1, 0, 0), 0, (every, first_x), 0, 1),
        ((0, 1, 0), 1, 0, 1, 0),
        ((0, -1, 0), 1, 1, 1, 1),
        ((1, 1, 0), 1, (0, every, last_x), 2, (0, 0)),
        ((-1, 1, 0), 1, (0, every, first_x), 2, (0, 1)),
        ((1, -1, 0), 1, (1, every, last_x), 2, (1, 0)),
        ((-1, -1, 0), 1, (1, every, first_x), 2, (1, 1)),
    ]
    fields, depth = value.shape[0], value.shape[3]
    out_shapes = [
        jax.ShapeDtypeStruct((2, fields, WIDTH, length_y, depth), value.dtype),
        jax.ShapeDtypeStruct((2, fields, length_x, WIDTH, depth), value.dtype),
        jax.ShapeDtypeStruct((2, 2, fields, WIDTH, WIDTH, depth), value.dtype),
    ]
    along_x, along_y, edges = exchange([value, faces_y], routes, out_shapes, tag)
    sections = [
        jnp.concatenate([edges[0, 0], along_x[0], edges[1, 0]], axis=2),
        jnp.concatenate([along_y[0], value, along_y[1]], axis=2),
        jnp.concatenate([edges[0, 1], along_x[1], edges[1, 1]], axis=2),
    ]
    return jnp.concatenate(sections, axis=1)


def with_halo(value, sides, width):
    for axis, dim in sides:
        count, length = (lax.axis_size(axis), value.shape[dim])
        up = [(i, (i + 1) % count) for i in range(count)]
        down = [(j, i) for i, j in up]
        last = lax.slice_in_dim(value, length - width, length, axis=dim)
        initial = lax.slice_in_dim(value, 0, width, axis=dim)
        before = lax.ppermute(last, axis, up)
        after = lax.ppermute(initial, axis, down)
        value = jnp.concatenate([before, value, after], axis=dim)
    return value


def banded_solve(system, source):
    extent = system.shape[0]
    lower = np.zeros(extent)
    upper = np.zeros(extent)
    middle = np.array([float(system[index, index]) for index in range(extent)])
    for index in range(1, extent):
        lower[index] = system[index, index - 1]
        upper[index - 1] = system[index - 1, index]
    rights = np.array(source)
    for index in range(1, extent):
        factor = lower[index] / middle[index - 1]
        middle[index] = middle[index] - factor * upper[index - 1]
        rights[index] = rights[index] - factor * rights[index - 1]
    answer = np.zeros(rights.shape)
    answer[extent - 1] = rights[extent - 1] / middle[extent - 1]
    for index in range(extent - 2, -1, -1):
        answer[index] = (rights[index] - upper[index] * answer[index + 1]) / middle[index]
    return answer


def derivative_table(length):
    extent = length + 2 * WIDTH
    system = np.eye(extent)
    source = np.zeros((extent, extent))
    for position in range(2, extent - 2):
        system[position, position - 1] = 1.0 / 3.0
        system[position, position + 1] = 1.0 / 3.0
        source[position, position + 1] = 7.0 / 9.0
        source[position, position - 1] = -7.0 / 9.0
        source[position, position + 2] = 1.0 / 36.0
        source[position, position - 2] = -1.0 / 36.0
    source[1, 2] = 0.5
    source[1, 0] = -0.5
    source[extent - 2, extent - 1] = 0.5
    source[extent - 2, extent - 3] = -0.5
    source[0, 1] = 1.0
    source[0, 0] = -1.0
    source[extent - 1, extent - 1] = 1.0
    source[extent - 1, extent - 2] = -1.0
    return banded_solve(system, source)[WIDTH : WIDTH + length]


def filter_table(length):
    strength = 0.4
    coeffs = [
        (193.0 + 126.0 * strength) / 256.0,
        (105.0 + 302.0 * strength) / 256.0,
        15.0 * (2.0 * strength - 1.0) / 64.0,
        45.0 * (1.0 - 2.0 * strength) / 512.0,
        5.0 * (2.0 * strength - 1.0) / 256.0,
        (1.0 - 2.0 * strength) / 512.0,
    ]
    extent = length + 2 * WIDTH
    system = np.eye(extent)
    source = np.eye(extent)
    for position in range(5, extent - 5):
        system[position, position - 1] = strength
        system[position, position + 1] = strength
        source[position, position] = coeffs[0]
        for offset in range(1, 6):
            source[position, position + offset] = coeffs[offset] / 2.0
            source[position, position - offset] = coeffs[offset] / 2.0
    return banded_solve(system, source)[WIDTH : WIDTH + length]


def sweep_lines(padded, matrix, dim):
    return jnp.einsum(line_forms[dim], matrix, padded, precision=lax.Precision.HIGHEST)


def faces_xi(values):
    return with_halo(values, (("xi", 1),), WIDTH)


def faces_eta(values):
    return with_halo(values, (("eta", 2),), WIDTH)


def faces_zeta(values):
    return with_halo(values, (("zeta", 3),), WIDTH)


def basic_quantities(conserved_solution):
    density = conserved_solution[0]
    fluid_speed_vector = conserved_solution[1:4] / density
    thermodynamic_stress_scalar = 0.4 * (
        conserved_solution[4] - 0.5 * jnp.sum(conserved_solution[1:4] * fluid_speed_vector, axis=0)
    )
    return (fluid_speed_vector, thermodynamic_stress_scalar, thermodynamic_stress_scalar / density)


def fluxes(
    conserved_solution, fluid_speed_vector, thermodynamic_stress_scalar, slopes, metrics, jacobian
):
    physical = [
        [
            jacobian
            * (
                metrics[0, column] * slopes[0][member]
                + metrics[1, column] * slopes[1][member]
                + metrics[2, column] * slopes[2][member]
            )
            for column in range(3)
        ]
        for member in range(4)
    ]
    spread = physical[0][0] + physical[1][1] + physical[2][2]
    totals = []
    for column in range(3):
        stress = [
            viscosity * (physical[member][column] + physical[column][member]) for member in range(3)
        ]
        stress[column] = stress[column] - 2.0 / 3.0 * viscosity * spread
        subdomain_parts = [conserved_solution[1 + column]]
        for member in range(3):
            carried = conserved_solution[1 + member] * fluid_speed_vector[column] - stress[member]
            if member == column:
                carried = carried + thermodynamic_stress_scalar
            subdomain_parts.append(carried)
        worked = (
            fluid_speed_vector[0] * stress[0]
            + fluid_speed_vector[1] * stress[1]
            + fluid_speed_vector[2] * stress[2]
        )
        subdomain_parts.append(
            (conserved_solution[4] + thermodynamic_stress_scalar) * fluid_speed_vector[column]
            - worked
            - conduction * physical[3][column]
        )
        totals.append(jnp.stack(subdomain_parts))
    return [
        metrics[direction, 0] * totals[0]
        + metrics[direction, 1] * totals[1]
        + metrics[direction, 2] * totals[2]
        for direction in range(3)
    ]


def local(conserved_solution, metrics, jacobian):
    lengths = conserved_solution.shape[1:]
    derive = [jnp.asarray(derivative_table(length), dtype=jnp.float32) for length in lengths]
    smooth = [jnp.asarray(filter_table(length), dtype=jnp.float32) for length in lengths]
    fluid_speed_vector, thermodynamic_stress_scalar, thermal_level = basic_quantities(
        conserved_solution
    )
    basic_quantity = jnp.concatenate([fluid_speed_vector, thermal_level[None]], axis=0)
    padded = exchange_faces(
        [(basic_quantity, "xi", 1), (basic_quantity, "eta", 2), (basic_quantity, "zeta", 3)], 0
    )
    slopes = [sweep_lines(padded[k], derive[k], k + 1) for k in range(3)]
    contra = fluxes(
        conserved_solution,
        fluid_speed_vector,
        thermodynamic_stress_scalar,
        slopes,
        metrics,
        jacobian,
    )
    padded = exchange_faces([(contra[0], "xi", 1), (contra[1], "eta", 2), (contra[2], "zeta", 3)], 1)
    divergence = sweep_lines(padded[0], derive[0], 1)
    divergence = divergence + sweep_lines(padded[1], derive[1], 2)
    divergence = divergence + sweep_lines(padded[2], derive[2], 3)
    sectioned = conserved_solution - step_duration * jacobian * divergence
    result = sweep_lines(exchange_plane(sectioned, 2), smooth[0], 1)
    result = sweep_lines(result, smooth[1], 2)
    result = sweep_lines(exchange_faces([(result, "zeta", 3)], 4)[0], smooth[2], 3)
    return result


def solution(mesh):
    in_specs = (
        P(None, "xi", "eta", "zeta"),
        P(None, None, "xi", "eta", "zeta"),
        P("xi", "eta", "zeta"),
    )
    out_specs = P(None, "xi", "eta", "zeta")
    return jax.shard_map(local, mesh=mesh, in_specs=in_specs, out_specs=out_specs, check_vma=False)
```

```python
import functools

import jax
import jax.numpy as jnp
import numpy as np
from jax import lax
from jax.experimental import pallas as pl
from jax.experimental.pallas import tpu as pltpu
from jax.sharding import PartitionSpec as P

WIDTH = 5


viscosity = 0.15
conduction = 0.15 * 1.4 / (0.4 * 0.72)
step_duration = 0.08
line_forms = ("", "al,flyz->fayz", "al,fxlz->fxaz", "al,fxyl->fxya")
MESH = pl.DeviceIdType.MESH
AXES = ("xi", "eta", "zeta")


def exchange_kernel(routes, sizes, count, *refs):
    sources, targets = refs[:count], refs[count:-2]
    send_sems, recv_sems = refs[-2:]
    here = [lax.axis_index(axis) for axis in AXES]

    def device(offset):
        return tuple(
            lax.rem(here[slot] + offset[slot] + sizes[slot], sizes[slot]) for slot in range(3)
        )

    partners = []
    for offset, *_ in routes:
        for way in (offset, tuple(-step for step in offset)):
            if way not in partners:
                partners.append(way)
    barrier = pltpu.get_barrier_semaphore()
    for offset in partners:
        pl.semaphore_signal(barrier, inc=1, device_id=device(offset), device_id_type=MESH)
    pl.semaphore_wait(barrier, len(partners))
    copies = []
    for index, (offset, source, source_at, target, target_at) in enumerate(routes):
        copy = pltpu.make_async_remote_copy(
            src_ref=sources[source].at[source_at],
            dst_ref=targets[target].at[target_at],
            send_sem=send_sems.at[index],
            recv_sem=recv_sems.at[index],
            device_id=device(offset),
            device_id_type=MESH,
        )
        copy.start()
        copies.append(copy)
    for copy in copies:
        copy.wait()


def exchange(arrays, routes, out_shapes, tag):
    sizes = tuple(lax.axis_size(axis) for axis in AXES)
    return pl.pallas_call(
        functools.partial(exchange_kernel, tuple(routes), sizes, len(arrays)),
        out_shape=out_shapes,
        in_specs=[pl.BlockSpec(memory_space=pl.ANY)] * len(arrays),
        out_specs=[pl.BlockSpec(memory_space=pltpu.VMEM)] * len(out_shapes),
        scratch_shapes=[
            pltpu.SemaphoreType.DMA((len(routes),)),
            pltpu.SemaphoreType.DMA((len(routes),)),
        ],
        compiler_params=pltpu.CompilerParams(collective_id=tag, has_side_effects=True),
    )(*arrays)


def offset_along(axis, step):
    return tuple(step if name == axis else 0 for name in AXES)


def window(ndim, dim, start, stop):
    return tuple(slice(start, stop) if axis == dim else slice(None) for axis in range(ndim))


def exchange_faces(items, tag):
    arrays, routes, out_shapes = [], [], []
    for value, axis, dim in items:
        ndim, length = value.ndim, value.shape[dim]
        if dim == ndim - 1:
            both = jnp.stack(
                [
                    lax.slice_in_dim(value, length - WIDTH, length, axis=dim),
                    lax.slice_in_dim(value, 0, WIDTH, axis=dim),
                ]
            )
            both = jnp.moveaxis(both, dim + 1, 2).reshape(2, value.shape[0], WIDTH, -1)
            arrays.append(both)
            out_shapes.append(jax.ShapeDtypeStruct(both.shape, both.dtype))
            source, target = len(arrays) - 1, len(out_shapes) - 1
            routes.append((offset_along(axis, 1), source, 0, target, 0))
            routes.append((offset_along(axis, -1), source, 1, target, 1))
        elif dim == ndim - 2:
            face = value.shape[:dim] + (WIDTH,) + value.shape[dim + 1 :]
            arrays.append(lax.slice_in_dim(value, length - WIDTH, length, axis=dim))
            arrays.append(lax.slice_in_dim(value, 0, WIDTH, axis=dim))
            out_shapes += [jax.ShapeDtypeStruct(face, value.dtype)] * 2
            source, target = len(arrays) - 2, len(out_shapes) - 2
            whole = window(ndim, dim, None, None)
            routes.append((offset_along(axis, 1), source, whole, target, whole))
            routes.append((offset_along(axis, -1), source + 1, whole, target + 1, whole))
        else:
            arrays.append(value)
            face = value.shape[:dim] + (WIDTH,) + value.shape[dim + 1 :]
            out_shapes += [jax.ShapeDtypeStruct(face, value.dtype)] * 2
            source, target = len(arrays) - 1, len(out_shapes) - 2
            whole = window(ndim, dim, None, None)
            last, first = window(ndim, dim, length - WIDTH, length), window(ndim, dim, 0, WIDTH)
            routes.append((offset_along(axis, 1), source, last, target, whole))
            routes.append((offset_along(axis, -1), source, first, target + 1, whole))
    received = exchange(arrays, routes, out_shapes, tag)
    padded, place = [], 0
    for value, axis, dim in items:
        if dim == value.ndim - 1:
            both = received[place].reshape((2, value.shape[0], WIDTH) + value.shape[1:dim])
            both = jnp.moveaxis(both, 2, dim + 1)
            before, after = both[0], both[1]
            place += 1
        else:
            before, after = received[place], received[place + 1]
            place += 2
        padded.append(jnp.concatenate([before, value, after], axis=dim))
    return padded


def exchange_plane(value, tag):
    length_x, length_y = value.shape[1], value.shape[2]
    faces_y = jnp.stack(
        [
            lax.slice_in_dim(value, length_y - WIDTH, length_y, axis=2),
            lax.slice_in_dim(value, 0, WIDTH, axis=2),
        ]
    )
    last_x, first_x = slice(length_x - WIDTH, length_x), slice(0, WIDTH)
    every = slice(None)
    routes = [
        ((1, 0, 0), 0, (every, last_x), 0, 0),
        ((-1, 0, 0), 0, (every, first_x), 0, 1),
        ((0, 1, 0), 1, 0, 1, 0),
        ((0, -1, 0), 1, 1, 1, 1),
        ((1, 1, 0), 1, (0, every, last_x), 2, (0, 0)),
        ((-1, 1, 0), 1, (0, every, first_x), 2, (0, 1)),
        ((1, -1, 0), 1, (1, every, last_x), 2, (1, 0)),
        ((-1, -1, 0), 1, (1, every, first_x), 2, (1, 1)),
    ]
    fields, depth = value.shape[0], value.shape[3]
    out_shapes = [
        jax.ShapeDtypeStruct((2, fields, WIDTH, length_y, depth), value.dtype),
        jax.ShapeDtypeStruct((2, fields, length_x, WIDTH, depth), value.dtype),
        jax.ShapeDtypeStruct((2, 2, fields, WIDTH, WIDTH, depth), value.dtype),
    ]
    along_x, along_y, edges = exchange([value, faces_y], routes, out_shapes, tag)
    sections = [
        jnp.concatenate([edges[0, 0], along_x[0], edges[1, 0]], axis=2),
        jnp.concatenate([along_y[0], value, along_y[1]], axis=2),
        jnp.concatenate([edges[0, 1], along_x[1], edges[1, 1]], axis=2),
    ]
    return jnp.concatenate(sections, axis=1)


def with_halo(value, sides, width):
    for axis, dim in sides:
        count, length = (lax.axis_size(axis), value.shape[dim])
        up = [(i, (i + 1) % count) for i in range(count)]
        down = [(j, i) for i, j in up]
        last = lax.slice_in_dim(value, length - width, length, axis=dim)
        initial = lax.slice_in_dim(value, 0, width, axis=dim)
        before = lax.ppermute(last, axis, up)
        after = lax.ppermute(initial, axis, down)
        value = jnp.concatenate([before, value, after], axis=dim)
    return value


def banded_solve(system, source):
    extent = system.shape[0]
    lower = np.zeros(extent)
    upper = np.zeros(extent)
    middle = np.array([float(system[index, index]) for index in range(extent)])
    for index in range(1, extent):
        lower[index] = system[index, index - 1]
        upper[index - 1] = system[index - 1, index]
    rights = np.array(source)
    for index in range(1, extent):
        factor = lower[index] / middle[index - 1]
        middle[index] = middle[index] - factor * upper[index - 1]
        rights[index] = rights[index] - factor * rights[index - 1]
    answer = np.zeros(rights.shape)
    answer[extent - 1] = rights[extent - 1] / middle[extent - 1]
    for index in range(extent - 2, -1, -1):
        answer[index] = (rights[index] - upper[index] * answer[index + 1]) / middle[index]
    return answer


def derivative_table(length):
    extent = length + 2 * WIDTH
    system = np.eye(extent)
    source = np.zeros((extent, extent))
    for position in range(2, extent - 2):
        system[position, position - 1] = 1.0 / 3.0
        system[position, position + 1] = 1.0 / 3.0
        source[position, position + 1] = 7.0 / 9.0
        source[position, position - 1] = -7.0 / 9.0
        source[position, position + 2] = 1.0 / 36.0
        source[position, position - 2] = -1.0 / 36.0
    source[1, 2] = 0.5
    source[1, 0] = -0.5
    source[extent - 2, extent - 1] = 0.5
    source[extent - 2, extent - 3] = -0.5
    source[0, 1] = 1.0
    source[0, 0] = -1.0
    source[extent - 1, extent - 1] = 1.0
    source[extent - 1, extent - 2] = -1.0
    return banded_solve(system, source)[WIDTH : WIDTH + length]


def filter_table(length):
    strength = 0.4
    coeffs = [
        (193.0 + 126.0 * strength) / 256.0,
        (105.0 + 302.0 * strength) / 256.0,
        15.0 * (2.0 * strength - 1.0) / 64.0,
        45.0 * (1.0 - 2.0 * strength) / 512.0,
        5.0 * (2.0 * strength - 1.0) / 256.0,
        (1.0 - 2.0 * strength) / 512.0,
    ]
    extent = length + 2 * WIDTH
    system = np.eye(extent)
    source = np.eye(extent)
    for position in range(5, extent - 5):
        system[position, position - 1] = strength
        system[position, position + 1] = strength
        source[position, position] = coeffs[0]
        for offset in range(1, 6):
            source[position, position + offset] = coeffs[offset] / 2.0
            source[position, position - offset] = coeffs[offset] / 2.0
    return banded_solve(system, source)[WIDTH : WIDTH + length]


def sweep_lines(padded, matrix, dim):
    return jnp.einsum(line_forms[dim], matrix, padded, precision=lax.Precision.HIGHEST)


def faces_xi(values):
    return with_halo(values, (("xi", 1),), WIDTH)


def faces_eta(values):
    return with_halo(values, (("eta", 2),), WIDTH)


def faces_zeta(values):
    return with_halo(values, (("zeta", 3),), WIDTH)


def basic_quantities(conserved_solution):
    density = conserved_solution[0]
    fluid_speed_vector = conserved_solution[1:4] / density
    thermodynamic_stress_scalar = 0.4 * (
        conserved_solution[4] - 0.5 * jnp.sum(conserved_solution[1:4] * fluid_speed_vector, axis=0)
    )
    return (fluid_speed_vector, thermodynamic_stress_scalar, thermodynamic_stress_scalar / density)


def fluxes(
    conserved_solution, fluid_speed_vector, thermodynamic_stress_scalar, slopes, metrics, jacobian
):
    physical = [
        [
            jacobian
            * (
                metrics[0, column] * slopes[0][member]
                + metrics[1, column] * slopes[1][member]
                + metrics[2, column] * slopes[2][member]
            )
            for column in range(3)
        ]
        for member in range(4)
    ]
    spread = physical[0][0] + physical[1][1] + physical[2][2]
    totals = []
    for column in range(3):
        stress = [
            viscosity * (physical[member][column] + physical[column][member]) for member in range(3)
        ]
        stress[column] = stress[column] - 2.0 / 3.0 * viscosity * spread
        subdomain_parts = [conserved_solution[1 + column]]
        for member in range(3):
            carried = conserved_solution[1 + member] * fluid_speed_vector[column] - stress[member]
            if member == column:
                carried = carried + thermodynamic_stress_scalar
            subdomain_parts.append(carried)
        worked = (
            fluid_speed_vector[0] * stress[0]
            + fluid_speed_vector[1] * stress[1]
            + fluid_speed_vector[2] * stress[2]
        )
        subdomain_parts.append(
            (conserved_solution[4] + thermodynamic_stress_scalar) * fluid_speed_vector[column]
            - worked
            - conduction * physical[3][column]
        )
        totals.append(jnp.stack(subdomain_parts))
    return [
        metrics[direction, 0] * totals[0]
        + metrics[direction, 1] * totals[1]
        + metrics[direction, 2] * totals[2]
        for direction in range(3)
    ]


def local(conserved_solution, metrics, jacobian):
    lengths = conserved_solution.shape[1:]
    derive = [jnp.asarray(derivative_table(length), dtype=jnp.float32) for length in lengths]
    smooth = [jnp.asarray(filter_table(length), dtype=jnp.float32) for length in lengths]
    fluid_speed_vector, thermodynamic_stress_scalar, thermal_level = basic_quantities(
        conserved_solution
    )
    basic_quantity = jnp.concatenate([fluid_speed_vector, thermal_level[None]], axis=0)
    padded = exchange_faces(
        [(basic_quantity, "xi", 1), (basic_quantity, "eta", 2), (basic_quantity, "zeta", 3)], 0
    )
    slopes = [sweep_lines(padded[k], derive[k], k + 1) for k in range(3)]
    contra = fluxes(
        conserved_solution,
        fluid_speed_vector,
        thermodynamic_stress_scalar,
        slopes,
        metrics,
        jacobian,
    )
    padded = exchange_faces([(contra[0], "xi", 1), (contra[1], "eta", 2), (contra[2], "zeta", 3)], 1)
    divergence = sweep_lines(padded[0], derive[0], 1)
    divergence = divergence + sweep_lines(padded[1], derive[1], 2)
    divergence = divergence + sweep_lines(padded[2], derive[2], 3)
    sectioned = conserved_solution - step_duration * jacobian * divergence
    result = sweep_lines(exchange_plane(sectioned, 2), smooth[0], 1)
    result = sweep_lines(result, smooth[1], 2)
    result = sweep_lines(exchange_faces([(result, "zeta", 3)], 4)[0], smooth[2], 3)
    return result


def solution(mesh):
    in_specs = (
        P(None, "xi", "eta", "zeta"),
        P(None, None, "xi", "eta", "zeta"),
        P("xi", "eta", "zeta"),
    )
    out_specs = P(None, "xi", "eta", "zeta")
    return jax.shard_map(local, mesh=mesh, in_specs=in_specs, out_specs=out_specs, check_vma=False)
```

```python
import functools

import jax
import jax.numpy as jnp
import numpy as np
from jax import lax
from jax.experimental import pallas as pl
from jax.experimental.pallas import tpu as pltpu
from jax.sharding import PartitionSpec as P

WIDTH = 5


viscosity = 0.15
conduction = 0.15 * 1.4 / (0.4 * 0.72)
step_duration = 0.08
line_forms = ("", "al,flyz->fayz", "al,fxlz->fxaz", "al,fxyl->fxya")
MESH = pl.DeviceIdType.MESH
AXES = ("xi", "eta", "zeta")


def exchange_kernel(routes, sizes, count, *refs):
    sources, targets = refs[:count], refs[count:-2]
    send_sems, recv_sems = refs[-2:]
    here = [lax.axis_index(axis) for axis in AXES]

    def device(offset):
        return tuple(
            lax.rem(here[slot] + offset[slot] + sizes[slot], sizes[slot]) for slot in range(3)
        )

    partners = []
    for offset, *_ in routes:
        for way in (offset, tuple(-step for step in offset)):
            if way not in partners:
                partners.append(way)
    barrier = pltpu.get_barrier_semaphore()
    for offset in partners:
        pl.semaphore_signal(barrier, inc=1, device_id=device(offset), device_id_type=MESH)
    pl.semaphore_wait(barrier, len(partners))
    copies = []
    for index, (offset, source, source_at, target, target_at) in enumerate(routes):
        copy = pltpu.make_async_remote_copy(
            src_ref=sources[source].at[source_at],
            dst_ref=targets[target].at[target_at],
            send_sem=send_sems.at[index],
            recv_sem=recv_sems.at[index],
            device_id=device(offset),
            device_id_type=MESH,
        )
        copy.start()
        copies.append(copy)
    for copy in copies:
        copy.wait()


def exchange(arrays, routes, out_shapes, tag):
    sizes = tuple(lax.axis_size(axis) for axis in AXES)
    return pl.pallas_call(
        functools.partial(exchange_kernel, tuple(routes), sizes, len(arrays)),
        out_shape=out_shapes,
        in_specs=[pl.BlockSpec(memory_space=pl.ANY)] * len(arrays),
        out_specs=[pl.BlockSpec(memory_space=pl.ANY)] * len(out_shapes),
        scratch_shapes=[
            pltpu.SemaphoreType.DMA((len(routes),)),
            pltpu.SemaphoreType.DMA((len(routes),)),
        ],
        compiler_params=pltpu.CompilerParams(collective_id=tag, has_side_effects=True),
    )(*arrays)


def offset_along(axis, step):
    return tuple(step if name == axis else 0 for name in AXES)


def window(ndim, dim, start, stop):
    return tuple(slice(start, stop) if axis == dim else slice(None) for axis in range(ndim))


def exchange_faces(items, tag):
    arrays, routes, out_shapes = [], [], []
    for value, axis, dim in items:
        ndim, length = value.ndim, value.shape[dim]
        if dim == ndim - 1:
            both = jnp.stack(
                [
                    lax.slice_in_dim(value, length - WIDTH, length, axis=dim),
                    lax.slice_in_dim(value, 0, WIDTH, axis=dim),
                ]
            )
            both = jnp.moveaxis(both, dim + 1, 2).reshape(2, value.shape[0], WIDTH, -1)
            arrays.append(both)
            out_shapes.append(jax.ShapeDtypeStruct(both.shape, both.dtype))
            source, target = len(arrays) - 1, len(out_shapes) - 1
            routes.append((offset_along(axis, 1), source, 0, target, 0))
            routes.append((offset_along(axis, -1), source, 1, target, 1))
        elif dim == ndim - 2:
            face = value.shape[:dim] + (WIDTH,) + value.shape[dim + 1 :]
            arrays.append(lax.slice_in_dim(value, length - WIDTH, length, axis=dim))
            arrays.append(lax.slice_in_dim(value, 0, WIDTH, axis=dim))
            out_shapes += [jax.ShapeDtypeStruct(face, value.dtype)] * 2
            source, target = len(arrays) - 2, len(out_shapes) - 2
            whole = window(ndim, dim, None, None)
            routes.append((offset_along(axis, 1), source, whole, target, whole))
            routes.append((offset_along(axis, -1), source + 1, whole, target + 1, whole))
        else:
            arrays.append(value)
            face = value.shape[:dim] + (WIDTH,) + value.shape[dim + 1 :]
            out_shapes += [jax.ShapeDtypeStruct(face, value.dtype)] * 2
            source, target = len(arrays) - 1, len(out_shapes) - 2
            whole = window(ndim, dim, None, None)
            last, first = window(ndim, dim, length - WIDTH, length), window(ndim, dim, 0, WIDTH)
            routes.append((offset_along(axis, 1), source, last, target, whole))
            routes.append((offset_along(axis, -1), source, first, target + 1, whole))
    received = exchange(arrays, routes, out_shapes, tag)
    padded, place = [], 0
    for value, axis, dim in items:
        if dim == value.ndim - 1:
            both = received[place].reshape((2, value.shape[0], WIDTH) + value.shape[1:dim])
            both = jnp.moveaxis(both, 2, dim + 1)
            before, after = both[0], both[1]
            place += 1
        else:
            before, after = received[place], received[place + 1]
            place += 2
        padded.append(jnp.concatenate([before, value, after], axis=dim))
    return padded


def exchange_plane(value, tag):
    length_x, length_y = value.shape[1], value.shape[2]
    faces_y = jnp.stack(
        [
            lax.slice_in_dim(value, length_y - WIDTH, length_y, axis=2),
            lax.slice_in_dim(value, 0, WIDTH, axis=2),
        ]
    )
    last_x, first_x = slice(length_x - WIDTH, length_x), slice(0, WIDTH)
    every = slice(None)
    routes = [
        ((1, 0, 0), 0, (every, last_x), 0, 0),
        ((-1, 0, 0), 0, (every, first_x), 0, 1),
        ((0, 1, 0), 1, 0, 1, 0),
        ((0, -1, 0), 1, 1, 1, 1),
        ((1, 1, 0), 1, (0, every, last_x), 2, (0, 0)),
        ((-1, 1, 0), 1, (0, every, first_x), 2, (0, 1)),
        ((1, -1, 0), 1, (1, every, last_x), 2, (1, 0)),
        ((-1, -1, 0), 1, (1, every, first_x), 2, (1, 1)),
    ]
    fields, depth = value.shape[0], value.shape[3]
    out_shapes = [
        jax.ShapeDtypeStruct((2, fields, WIDTH, length_y, depth), value.dtype),
        jax.ShapeDtypeStruct((2, fields, length_x, WIDTH, depth), value.dtype),
        jax.ShapeDtypeStruct((2, 2, fields, WIDTH, WIDTH, depth), value.dtype),
    ]
    along_x, along_y, edges = exchange([value, faces_y], routes, out_shapes, tag)
    sections = [
        jnp.concatenate([edges[0, 0], along_x[0], edges[1, 0]], axis=2),
        jnp.concatenate([along_y[0], value, along_y[1]], axis=2),
        jnp.concatenate([edges[0, 1], along_x[1], edges[1, 1]], axis=2),
    ]
    return jnp.concatenate(sections, axis=1)


def sweep_zeta_kernel(sizes, block_ref, middle_ref, lower_ref, upper_ref, out_ref,
                      turned, before, after, send_sems, recv_sems):
    fields, length_x, length_y, depth = block_ref.shape
    rows = fields * length_x * length_y
    here = [lax.axis_index(axis) for axis in AXES]
    up = tuple(here[:2]) + (lax.rem(here[2] + 1, sizes[2]),)
    down = tuple(here[:2]) + (lax.rem(here[2] + sizes[2] - 1, sizes[2]),)
    turned[...] = block_ref[...].reshape(rows, depth).T
    barrier = pltpu.get_barrier_semaphore()
    for partner in (up, down):
        pl.semaphore_signal(barrier, inc=1, device_id=partner, device_id_type=MESH)
    pl.semaphore_wait(barrier, 2)
    copies = [
        pltpu.make_async_remote_copy(
            src_ref=turned.at[pl.ds(depth - 8, 8)], dst_ref=before,
            send_sem=send_sems.at[0], recv_sem=recv_sems.at[0],
            device_id=up, device_id_type=MESH,
        ),
        pltpu.make_async_remote_copy(
            src_ref=turned.at[pl.ds(0, 8)], dst_ref=after,
            send_sem=send_sems.at[1], recv_sem=recv_sems.at[1],
            device_id=down, device_id_type=MESH,
        ),
    ]
    for copy in copies:
        copy.start()
    total = jnp.dot(middle_ref[...], turned[...], precision=lax.Precision.HIGHEST,
                    preferred_element_type=jnp.float32)
    for copy in copies:
        copy.wait()
    total = total + jnp.dot(lower_ref[...], before[...], precision=lax.Precision.HIGHEST,
                            preferred_element_type=jnp.float32)
    total = total + jnp.dot(upper_ref[...], after[...], precision=lax.Precision.HIGHEST,
                            preferred_element_type=jnp.float32)
    out_ref[...] = total.T.reshape(fields, length_x, length_y, depth)


def sweep_zeta(value, matrix, tag):
    sizes = tuple(lax.axis_size(axis) for axis in AXES)
    fields, length_x, length_y, depth = value.shape
    rows = fields * length_x * length_y
    middle = matrix[:, WIDTH : WIDTH + depth]
    lower = jnp.concatenate([jnp.zeros((depth, 8 - WIDTH), matrix.dtype), matrix[:, :WIDTH]], axis=1)
    upper = jnp.concatenate([matrix[:, WIDTH + depth :], jnp.zeros((depth, 8 - WIDTH), matrix.dtype)], axis=1)
    return pl.pallas_call(
        functools.partial(sweep_zeta_kernel, sizes),
        out_shape=jax.ShapeDtypeStruct(value.shape, value.dtype),
        in_specs=[pl.BlockSpec(memory_space=pltpu.VMEM)] * 4,
        out_specs=pl.BlockSpec(memory_space=pltpu.VMEM),
        scratch_shapes=[
            pltpu.VMEM((depth, rows), jnp.float32),
            pltpu.VMEM((8, rows), jnp.float32),
            pltpu.VMEM((8, rows), jnp.float32),
            pltpu.SemaphoreType.DMA((2,)),
            pltpu.SemaphoreType.DMA((2,)),
        ],
        compiler_params=pltpu.CompilerParams(collective_id=tag, has_side_effects=True),
    )(value, middle, lower, upper)


def with_halo(value, sides, width):
    for axis, dim in sides:
        count, length = (lax.axis_size(axis), value.shape[dim])
        up = [(i, (i + 1) % count) for i in range(count)]
        down = [(j, i) for i, j in up]
        last = lax.slice_in_dim(value, length - width, length, axis=dim)
        initial = lax.slice_in_dim(value, 0, width, axis=dim)
        before = lax.ppermute(last, axis, up)
        after = lax.ppermute(initial, axis, down)
        value = jnp.concatenate([before, value, after], axis=dim)
    return value


def banded_solve(system, source):
    extent = system.shape[0]
    lower = np.zeros(extent)
    upper = np.zeros(extent)
    middle = np.array([float(system[index, index]) for index in range(extent)])
    for index in range(1, extent):
        lower[index] = system[index, index - 1]
        upper[index - 1] = system[index - 1, index]
    rights = np.array(source)
    for index in range(1, extent):
        factor = lower[index] / middle[index - 1]
        middle[index] = middle[index] - factor * upper[index - 1]
        rights[index] = rights[index] - factor * rights[index - 1]
    answer = np.zeros(rights.shape)
    answer[extent - 1] = rights[extent - 1] / middle[extent - 1]
    for index in range(extent - 2, -1, -1):
        answer[index] = (rights[index] - upper[index] * answer[index + 1]) / middle[index]
    return answer


def derivative_table(length):
    extent = length + 2 * WIDTH
    system = np.eye(extent)
    source = np.zeros((extent, extent))
    for position in range(2, extent - 2):
        system[position, position - 1] = 1.0 / 3.0
        system[position, position + 1] = 1.0 / 3.0
        source[position, position + 1] = 7.0 / 9.0
        source[position, position - 1] = -7.0 / 9.0
        source[position, position + 2] = 1.0 / 36.0
        source[position, position - 2] = -1.0 / 36.0
    source[1, 2] = 0.5
    source[1, 0] = -0.5
    source[extent - 2, extent - 1] = 0.5
    source[extent - 2, extent - 3] = -0.5
    source[0, 1] = 1.0
    source[0, 0] = -1.0
    source[extent - 1, extent - 1] = 1.0
    source[extent - 1, extent - 2] = -1.0
    return banded_solve(system, source)[WIDTH : WIDTH + length]


def filter_table(length):
    strength = 0.4
    coeffs = [
        (193.0 + 126.0 * strength) / 256.0,
        (105.0 + 302.0 * strength) / 256.0,
        15.0 * (2.0 * strength - 1.0) / 64.0,
        45.0 * (1.0 - 2.0 * strength) / 512.0,
        5.0 * (2.0 * strength - 1.0) / 256.0,
        (1.0 - 2.0 * strength) / 512.0,
    ]
    extent = length + 2 * WIDTH
    system = np.eye(extent)
    source = np.eye(extent)
    for position in range(5, extent - 5):
        system[position, position - 1] = strength
        system[position, position + 1] = strength
        source[position, position] = coeffs[0]
        for offset in range(1, 6):
            source[position, position + offset] = coeffs[offset] / 2.0
            source[position, position - offset] = coeffs[offset] / 2.0
    return banded_solve(system, source)[WIDTH : WIDTH + length]


def sweep_lines(padded, matrix, dim):
    return jnp.einsum(line_forms[dim], matrix, padded, precision=lax.Precision.HIGHEST)


def faces_xi(values):
    return with_halo(values, (("xi", 1),), WIDTH)


def faces_eta(values):
    return with_halo(values, (("eta", 2),), WIDTH)


def faces_zeta(values):
    return with_halo(values, (("zeta", 3),), WIDTH)


def basic_quantities(conserved_solution):
    density = conserved_solution[0]
    fluid_speed_vector = conserved_solution[1:4] / density
    thermodynamic_stress_scalar = 0.4 * (
        conserved_solution[4] - 0.5 * jnp.sum(conserved_solution[1:4] * fluid_speed_vector, axis=0)
    )
    return (fluid_speed_vector, thermodynamic_stress_scalar, thermodynamic_stress_scalar / density)


def fluxes(
    conserved_solution, fluid_speed_vector, thermodynamic_stress_scalar, slopes, metrics, jacobian
):
    physical = [
        [
            jacobian
            * (
                metrics[0, column] * slopes[0][member]
                + metrics[1, column] * slopes[1][member]
                + metrics[2, column] * slopes[2][member]
            )
            for column in range(3)
        ]
        for member in range(4)
    ]
    spread = physical[0][0] + physical[1][1] + physical[2][2]
    totals = []
    for column in range(3):
        stress = [
            viscosity * (physical[member][column] + physical[column][member]) for member in range(3)
        ]
        stress[column] = stress[column] - 2.0 / 3.0 * viscosity * spread
        subdomain_parts = [conserved_solution[1 + column]]
        for member in range(3):
            carried = conserved_solution[1 + member] * fluid_speed_vector[column] - stress[member]
            if member == column:
                carried = carried + thermodynamic_stress_scalar
            subdomain_parts.append(carried)
        worked = (
            fluid_speed_vector[0] * stress[0]
            + fluid_speed_vector[1] * stress[1]
            + fluid_speed_vector[2] * stress[2]
        )
        subdomain_parts.append(
            (conserved_solution[4] + thermodynamic_stress_scalar) * fluid_speed_vector[column]
            - worked
            - conduction * physical[3][column]
        )
        totals.append(jnp.stack(subdomain_parts))
    return [
        metrics[direction, 0] * totals[0]
        + metrics[direction, 1] * totals[1]
        + metrics[direction, 2] * totals[2]
        for direction in range(3)
    ]


def local(conserved_solution, metrics, jacobian):
    lengths = conserved_solution.shape[1:]
    derive = [jnp.asarray(derivative_table(length), dtype=jnp.float32) for length in lengths]
    smooth = [jnp.asarray(filter_table(length), dtype=jnp.float32) for length in lengths]
    fluid_speed_vector, thermodynamic_stress_scalar, thermal_level = basic_quantities(
        conserved_solution
    )
    basic_quantity = jnp.concatenate([fluid_speed_vector, thermal_level[None]], axis=0)
    padded = exchange_faces(
        [(basic_quantity, "xi", 1), (basic_quantity, "eta", 2), (basic_quantity, "zeta", 3)], 0
    )
    slopes = [sweep_lines(padded[k], derive[k], k + 1) for k in range(3)]
    contra = fluxes(
        conserved_solution,
        fluid_speed_vector,
        thermodynamic_stress_scalar,
        slopes,
        metrics,
        jacobian,
    )
    padded = exchange_faces([(contra[0], "xi", 1), (contra[1], "eta", 2), (contra[2], "zeta", 3)], 1)
    divergence = sweep_lines(padded[0], derive[0], 1)
    divergence = divergence + sweep_lines(padded[1], derive[1], 2)
    divergence = divergence + sweep_lines(padded[2], derive[2], 3)
    sectioned = conserved_solution - step_duration * jacobian * divergence
    result = sweep_lines(exchange_plane(sectioned, 2), smooth[0], 1)
    result = sweep_lines(result, smooth[1], 2)
    result = sweep_zeta(result, smooth[2], 4)
    return result


def solution(mesh):
    in_specs = (
        P(None, "xi", "eta", "zeta"),
        P(None, None, "xi", "eta", "zeta"),
        P("xi", "eta", "zeta"),
    )
    out_specs = P(None, "xi", "eta", "zeta")
    return jax.shard_map(local, mesh=mesh, in_specs=in_specs, out_specs=out_specs, check_vma=False)
```

```python
import functools

import jax
import jax.numpy as jnp
import numpy as np
from jax import lax
from jax.experimental import pallas as pl
from jax.experimental.pallas import tpu as pltpu
from jax.sharding import PartitionSpec as P

WIDTH = 5


viscosity = 0.15
conduction = 0.15 * 1.4 / (0.4 * 0.72)
step_duration = 0.08
line_forms = ("", "al,flyz->fayz", "al,fxlz->fxaz", "al,fxyl->fxya")
MESH = pl.DeviceIdType.MESH
AXES = ("xi", "eta", "zeta")


def exchange_kernel(routes, sizes, count, zeta, *refs):
    sources = refs[:count]
    refs = refs[count:]
    if zeta:
        block_ref, middle_ref, lower_ref, upper_ref = refs[:4]
        refs = refs[4:]
    targets = refs[: len(refs) - 2 - (4 if zeta else 0)]
    refs = refs[len(targets) :]
    if zeta:
        out_ref, turned, before, after = refs[:4]
        refs = refs[4:]
    send_sems, recv_sems = refs
    here = [lax.axis_index(axis) for axis in AXES]

    def device(offset):
        return tuple(
            lax.rem(here[slot] + offset[slot] + sizes[slot], sizes[slot]) for slot in range(3)
        )

    if zeta:
        fields, length_x, length_y, depth = block_ref.shape
        rows = fields * length_x * length_y
        turned[...] = block_ref[...].reshape(rows, depth).T
    offsets = [route[0] for route in routes] + ([(0, 0, 1), (0, 0, -1)] if zeta else [])
    partners = []
    for offset in offsets:
        for way in (offset, tuple(-step for step in offset)):
            if way not in partners:
                partners.append(way)
    barrier = pltpu.get_barrier_semaphore()
    for offset in partners:
        pl.semaphore_signal(barrier, inc=1, device_id=device(offset), device_id_type=MESH)
    pl.semaphore_wait(barrier, len(partners))
    copies = []
    for index, (offset, source, source_at, target, target_at) in enumerate(routes):
        copies.append(
            pltpu.make_async_remote_copy(
                src_ref=sources[source].at[source_at],
                dst_ref=targets[target].at[target_at],
                send_sem=send_sems.at[index],
                recv_sem=recv_sems.at[index],
                device_id=device(offset),
                device_id_type=MESH,
            )
        )
    if zeta:
        for index, (rows_at, landing, offset) in enumerate(
            ((pl.ds(depth - 8, 8), before, (0, 0, 1)), (pl.ds(0, 8), after, (0, 0, -1)))
        ):
            copies.append(
                pltpu.make_async_remote_copy(
                    src_ref=turned.at[rows_at],
                    dst_ref=landing,
                    send_sem=send_sems.at[len(routes) + index],
                    recv_sem=recv_sems.at[len(routes) + index],
                    device_id=device(offset),
                    device_id_type=MESH,
                )
            )
    for copy in copies:
        copy.start()
    if zeta:
        total = jnp.dot(middle_ref[...], turned[...], precision=lax.Precision.HIGHEST,
                        preferred_element_type=jnp.float32)
    for copy in copies:
        copy.wait()
    if zeta:
        total = total + jnp.dot(lower_ref[...], before[...], precision=lax.Precision.HIGHEST,
                                preferred_element_type=jnp.float32)
        total = total + jnp.dot(upper_ref[...], after[...], precision=lax.Precision.HIGHEST,
                                preferred_element_type=jnp.float32)
        out_ref[...] = total.T.reshape(fields, length_x, length_y, depth)


def exchange(arrays, routes, out_shapes, tag, zeta=None):
    sizes = tuple(lax.axis_size(axis) for axis in AXES)
    operands = list(arrays)
    in_specs = [pl.BlockSpec(memory_space=pl.ANY)] * len(arrays)
    out_specs = [pl.BlockSpec(memory_space=pl.ANY)] * len(out_shapes)
    out_shapes = list(out_shapes)
    scratch = []
    copies = len(routes)
    if zeta is not None:
        value, matrix = zeta
        fields, length_x, length_y, depth = value.shape
        rows = fields * length_x * length_y
        padding = jnp.zeros((depth, 8 - WIDTH), matrix.dtype)
        operands += [
            value,
            matrix[:, WIDTH : WIDTH + depth],
            jnp.concatenate([padding, matrix[:, :WIDTH]], axis=1),
            jnp.concatenate([matrix[:, WIDTH + depth :], padding], axis=1),
        ]
        in_specs += [pl.BlockSpec(memory_space=pltpu.VMEM)] * 4
        out_shapes.append(jax.ShapeDtypeStruct(value.shape, value.dtype))
        out_specs.append(pl.BlockSpec(memory_space=pltpu.VMEM))
        scratch = [pltpu.VMEM((depth, rows), jnp.float32), pltpu.VMEM((8, rows), jnp.float32),
                   pltpu.VMEM((8, rows), jnp.float32)]
        copies += 2
    return pl.pallas_call(
        functools.partial(exchange_kernel, tuple(routes), sizes, len(arrays), zeta is not None),
        out_shape=out_shapes,
        in_specs=in_specs,
        out_specs=out_specs,
        scratch_shapes=scratch + [
            pltpu.SemaphoreType.DMA((copies,)),
            pltpu.SemaphoreType.DMA((copies,)),
        ],
        compiler_params=pltpu.CompilerParams(collective_id=tag, has_side_effects=True),
    )(*operands)


def offset_along(axis, step):
    return tuple(step if name == axis else 0 for name in AXES)


def window(ndim, dim, start, stop):
    return tuple(slice(start, stop) if axis == dim else slice(None) for axis in range(ndim))


def exchange_faces(items, tag, zeta=None):
    arrays, routes, out_shapes = [], [], []
    for value, axis, dim in items:
        ndim, length = value.ndim, value.shape[dim]
        if dim == ndim - 1:
            both = jnp.stack(
                [
                    lax.slice_in_dim(value, length - WIDTH, length, axis=dim),
                    lax.slice_in_dim(value, 0, WIDTH, axis=dim),
                ]
            )
            both = jnp.moveaxis(both, dim + 1, 2).reshape(2, value.shape[0], WIDTH, -1)
            arrays.append(both)
            out_shapes.append(jax.ShapeDtypeStruct(both.shape, both.dtype))
            source, target = len(arrays) - 1, len(out_shapes) - 1
            routes.append((offset_along(axis, 1), source, 0, target, 0))
            routes.append((offset_along(axis, -1), source, 1, target, 1))
        elif dim == ndim - 2:
            face = value.shape[:dim] + (WIDTH,) + value.shape[dim + 1 :]
            arrays.append(lax.slice_in_dim(value, length - WIDTH, length, axis=dim))
            arrays.append(lax.slice_in_dim(value, 0, WIDTH, axis=dim))
            out_shapes += [jax.ShapeDtypeStruct(face, value.dtype)] * 2
            source, target = len(arrays) - 2, len(out_shapes) - 2
            whole = window(ndim, dim, None, None)
            routes.append((offset_along(axis, 1), source, whole, target, whole))
            routes.append((offset_along(axis, -1), source + 1, whole, target + 1, whole))
        else:
            arrays.append(value)
            face = value.shape[:dim] + (WIDTH,) + value.shape[dim + 1 :]
            out_shapes += [jax.ShapeDtypeStruct(face, value.dtype)] * 2
            source, target = len(arrays) - 1, len(out_shapes) - 2
            whole = window(ndim, dim, None, None)
            last, first = window(ndim, dim, length - WIDTH, length), window(ndim, dim, 0, WIDTH)
            routes.append((offset_along(axis, 1), source, last, target, whole))
            routes.append((offset_along(axis, -1), source, first, target + 1, whole))
    received = exchange(arrays, routes, out_shapes, tag, zeta)
    padded, place = [], 0
    for value, axis, dim in items:
        if dim == value.ndim - 1:
            both = received[place].reshape((2, value.shape[0], WIDTH) + value.shape[1:dim])
            both = jnp.moveaxis(both, 2, dim + 1)
            before, after = both[0], both[1]
            place += 1
        else:
            before, after = received[place], received[place + 1]
            place += 2
        padded.append(jnp.concatenate([before, value, after], axis=dim))
    if zeta is not None:
        padded.append(received[-1])
    return padded


def exchange_plane(value, tag):
    length_x, length_y = value.shape[1], value.shape[2]
    faces_y = jnp.stack(
        [
            lax.slice_in_dim(value, length_y - WIDTH, length_y, axis=2),
            lax.slice_in_dim(value, 0, WIDTH, axis=2),
        ]
    )
    last_x, first_x = slice(length_x - WIDTH, length_x), slice(0, WIDTH)
    every = slice(None)
    routes = [
        ((1, 0, 0), 0, (every, last_x), 0, 0),
        ((-1, 0, 0), 0, (every, first_x), 0, 1),
        ((0, 1, 0), 1, 0, 1, 0),
        ((0, -1, 0), 1, 1, 1, 1),
        ((1, 1, 0), 1, (0, every, last_x), 2, (0, 0)),
        ((-1, 1, 0), 1, (0, every, first_x), 2, (0, 1)),
        ((1, -1, 0), 1, (1, every, last_x), 2, (1, 0)),
        ((-1, -1, 0), 1, (1, every, first_x), 2, (1, 1)),
    ]
    fields, depth = value.shape[0], value.shape[3]
    out_shapes = [
        jax.ShapeDtypeStruct((2, fields, WIDTH, length_y, depth), value.dtype),
        jax.ShapeDtypeStruct((2, fields, length_x, WIDTH, depth), value.dtype),
        jax.ShapeDtypeStruct((2, 2, fields, WIDTH, WIDTH, depth), value.dtype),
    ]
    along_x, along_y, edges = exchange([value, faces_y], routes, out_shapes, tag)
    sections = [
        jnp.concatenate([edges[0, 0], along_x[0], edges[1, 0]], axis=2),
        jnp.concatenate([along_y[0], value, along_y[1]], axis=2),
        jnp.concatenate([edges[0, 1], along_x[1], edges[1, 1]], axis=2),
    ]
    return jnp.concatenate(sections, axis=1)


def sweep_zeta(value, matrix, tag):
    return exchange([], [], [], tag, (value, matrix))[-1]


def with_halo(value, sides, width):
    for axis, dim in sides:
        count, length = (lax.axis_size(axis), value.shape[dim])
        up = [(i, (i + 1) % count) for i in range(count)]
        down = [(j, i) for i, j in up]
        last = lax.slice_in_dim(value, length - width, length, axis=dim)
        initial = lax.slice_in_dim(value, 0, width, axis=dim)
        before = lax.ppermute(last, axis, up)
        after = lax.ppermute(initial, axis, down)
        value = jnp.concatenate([before, value, after], axis=dim)
    return value


def banded_solve(system, source):
    extent = system.shape[0]
    lower = np.zeros(extent)
    upper = np.zeros(extent)
    middle = np.array([float(system[index, index]) for index in range(extent)])
    for index in range(1, extent):
        lower[index] = system[index, index - 1]
        upper[index - 1] = system[index - 1, index]
    rights = np.array(source)
    for index in range(1, extent):
        factor = lower[index] / middle[index - 1]
        middle[index] = middle[index] - factor * upper[index - 1]
        rights[index] = rights[index] - factor * rights[index - 1]
    answer = np.zeros(rights.shape)
    answer[extent - 1] = rights[extent - 1] / middle[extent - 1]
    for index in range(extent - 2, -1, -1):
        answer[index] = (rights[index] - upper[index] * answer[index + 1]) / middle[index]
    return answer


def derivative_table(length):
    extent = length + 2 * WIDTH
    system = np.eye(extent)
    source = np.zeros((extent, extent))
    for position in range(2, extent - 2):
        system[position, position - 1] = 1.0 / 3.0
        system[position, position + 1] = 1.0 / 3.0
        source[position, position + 1] = 7.0 / 9.0
        source[position, position - 1] = -7.0 / 9.0
        source[position, position + 2] = 1.0 / 36.0
        source[position, position - 2] = -1.0 / 36.0
    source[1, 2] = 0.5
    source[1, 0] = -0.5
    source[extent - 2, extent - 1] = 0.5
    source[extent - 2, extent - 3] = -0.5
    source[0, 1] = 1.0
    source[0, 0] = -1.0
    source[extent - 1, extent - 1] = 1.0
    source[extent - 1, extent - 2] = -1.0
    return banded_solve(system, source)[WIDTH : WIDTH + length]


def filter_table(length):
    strength = 0.4
    coeffs = [
        (193.0 + 126.0 * strength) / 256.0,
        (105.0 + 302.0 * strength) / 256.0,
        15.0 * (2.0 * strength - 1.0) / 64.0,
        45.0 * (1.0 - 2.0 * strength) / 512.0,
        5.0 * (2.0 * strength - 1.0) / 256.0,
        (1.0 - 2.0 * strength) / 512.0,
    ]
    extent = length + 2 * WIDTH
    system = np.eye(extent)
    source = np.eye(extent)
    for position in range(5, extent - 5):
        system[position, position - 1] = strength
        system[position, position + 1] = strength
        source[position, position] = coeffs[0]
        for offset in range(1, 6):
            source[position, position + offset] = coeffs[offset] / 2.0
            source[position, position - offset] = coeffs[offset] / 2.0
    return banded_solve(system, source)[WIDTH : WIDTH + length]


def sweep_lines(padded, matrix, dim):
    return jnp.einsum(line_forms[dim], matrix, padded, precision=lax.Precision.HIGHEST)


def faces_xi(values):
    return with_halo(values, (("xi", 1),), WIDTH)


def faces_eta(values):
    return with_halo(values, (("eta", 2),), WIDTH)


def faces_zeta(values):
    return with_halo(values, (("zeta", 3),), WIDTH)


def basic_quantities(conserved_solution):
    density = conserved_solution[0]
    fluid_speed_vector = conserved_solution[1:4] / density
    thermodynamic_stress_scalar = 0.4 * (
        conserved_solution[4] - 0.5 * jnp.sum(conserved_solution[1:4] * fluid_speed_vector, axis=0)
    )
    return (fluid_speed_vector, thermodynamic_stress_scalar, thermodynamic_stress_scalar / density)


def fluxes(
    conserved_solution, fluid_speed_vector, thermodynamic_stress_scalar, slopes, metrics, jacobian
):
    physical = [
        [
            jacobian
            * (
                metrics[0, column] * slopes[0][member]
                + metrics[1, column] * slopes[1][member]
                + metrics[2, column] * slopes[2][member]
            )
            for column in range(3)
        ]
        for member in range(4)
    ]
    spread = physical[0][0] + physical[1][1] + physical[2][2]
    totals = []
    for column in range(3):
        stress = [
            viscosity * (physical[member][column] + physical[column][member]) for member in range(3)
        ]
        stress[column] = stress[column] - 2.0 / 3.0 * viscosity * spread
        subdomain_parts = [conserved_solution[1 + column]]
        for member in range(3):
            carried = conserved_solution[1 + member] * fluid_speed_vector[column] - stress[member]
            if member == column:
                carried = carried + thermodynamic_stress_scalar
            subdomain_parts.append(carried)
        worked = (
            fluid_speed_vector[0] * stress[0]
            + fluid_speed_vector[1] * stress[1]
            + fluid_speed_vector[2] * stress[2]
        )
        subdomain_parts.append(
            (conserved_solution[4] + thermodynamic_stress_scalar) * fluid_speed_vector[column]
            - worked
            - conduction * physical[3][column]
        )
        totals.append(jnp.stack(subdomain_parts))
    return [
        metrics[direction, 0] * totals[0]
        + metrics[direction, 1] * totals[1]
        + metrics[direction, 2] * totals[2]
        for direction in range(3)
    ]


def local(conserved_solution, metrics, jacobian):
    lengths = conserved_solution.shape[1:]
    derive = [jnp.asarray(derivative_table(length), dtype=jnp.float32) for length in lengths]
    smooth = [jnp.asarray(filter_table(length), dtype=jnp.float32) for length in lengths]
    fluid_speed_vector, thermodynamic_stress_scalar, thermal_level = basic_quantities(
        conserved_solution
    )
    basic_quantity = jnp.concatenate([fluid_speed_vector, thermal_level[None]], axis=0)
    padded = exchange_faces(
        [(basic_quantity, "xi", 1), (basic_quantity, "eta", 2)], 0, (basic_quantity, derive[2])
    )
    slopes = [sweep_lines(padded[k], derive[k], k + 1) for k in range(2)] + [padded[2]]
    contra = fluxes(
        conserved_solution,
        fluid_speed_vector,
        thermodynamic_stress_scalar,
        slopes,
        metrics,
        jacobian,
    )
    padded = exchange_faces([(contra[0], "xi", 1), (contra[1], "eta", 2)], 1, (contra[2], derive[2]))
    divergence = sweep_lines(padded[0], derive[0], 1)
    divergence = divergence + sweep_lines(padded[1], derive[1], 2)
    divergence = divergence + padded[2]
    sectioned = conserved_solution - step_duration * jacobian * divergence
    result = sweep_lines(exchange_plane(sectioned, 2), smooth[0], 1)
    result = sweep_lines(result, smooth[1], 2)
    result = sweep_zeta(result, smooth[2], 4)
    return result


def solution(mesh):
    in_specs = (
        P(None, "xi", "eta", "zeta"),
        P(None, None, "xi", "eta", "zeta"),
        P("xi", "eta", "zeta"),
    )
    out_specs = P(None, "xi", "eta", "zeta")
    return jax.shard_map(local, mesh=mesh, in_specs=in_specs, out_specs=out_specs, check_vma=False)
```

```python
import functools

import jax
import jax.numpy as jnp
import numpy as np
from jax import lax
from jax.experimental import pallas as pl
from jax.experimental.pallas import tpu as pltpu
from jax.sharding import PartitionSpec as P

WIDTH = 5


viscosity = 0.15
conduction = 0.15 * 1.4 / (0.4 * 0.72)
step_duration = 0.08
line_forms = ("", "al,flyz->fayz", "al,fxlz->fxaz", "al,fxyl->fxya")
MESH = pl.DeviceIdType.MESH
AXES = ("xi", "eta", "zeta")


def exchange_kernel(routes, sizes, count, zeta, *refs):
    sources = refs[:count]
    refs = refs[count:]
    if zeta:
        block_ref, middle_ref, lower_ref, upper_ref = refs[:4]
        refs = refs[4:]
    targets = refs[: len(refs) - 2 - (4 if zeta else 0)]
    refs = refs[len(targets) :]
    if zeta:
        out_ref, turned, before, after = refs[:4]
        refs = refs[4:]
    send_sems, recv_sems = refs
    here = [lax.axis_index(axis) for axis in AXES]

    def device(offset):
        return tuple(
            lax.rem(here[slot] + offset[slot] + sizes[slot], sizes[slot]) for slot in range(3)
        )

    offsets = [route[0] for route in routes] + ([(0, 0, 1), (0, 0, -1)] if zeta else [])
    partners = []
    for offset in offsets:
        for way in (offset, tuple(-step for step in offset)):
            if way not in partners:
                partners.append(way)
    barrier = pltpu.get_barrier_semaphore()
    for offset in partners:
        pl.semaphore_signal(barrier, inc=1, device_id=device(offset), device_id_type=MESH)
    if zeta:
        fields, length_x, length_y, depth = block_ref.shape
        rows = fields * length_x * length_y
        turned[...] = block_ref[...].reshape(rows, depth).T
    pl.semaphore_wait(barrier, len(partners))
    copies = []
    for index, (offset, source, source_at, target, target_at) in enumerate(routes):
        copies.append(
            pltpu.make_async_remote_copy(
                src_ref=sources[source].at[source_at],
                dst_ref=targets[target].at[target_at],
                send_sem=send_sems.at[index],
                recv_sem=recv_sems.at[index],
                device_id=device(offset),
                device_id_type=MESH,
            )
        )
    if zeta:
        for index, (rows_at, landing, offset) in enumerate(
            ((pl.ds(depth - 8, 8), before, (0, 0, 1)), (pl.ds(0, 8), after, (0, 0, -1)))
        ):
            copies.append(
                pltpu.make_async_remote_copy(
                    src_ref=turned.at[rows_at],
                    dst_ref=landing,
                    send_sem=send_sems.at[len(routes) + index],
                    recv_sem=recv_sems.at[len(routes) + index],
                    device_id=device(offset),
                    device_id_type=MESH,
                )
            )
    for copy in copies:
        copy.start()
    if zeta:
        total = jnp.dot(middle_ref[...], turned[...], precision=lax.Precision.HIGHEST,
                        preferred_element_type=jnp.float32)
    for copy in copies:
        copy.wait()
    if zeta:
        total = total + jnp.dot(lower_ref[...], before[...], precision=lax.Precision.HIGHEST,
                                preferred_element_type=jnp.float32)
        total = total + jnp.dot(upper_ref[...], after[...], precision=lax.Precision.HIGHEST,
                                preferred_element_type=jnp.float32)
        out_ref[...] = total.T.reshape(fields, length_x, length_y, depth)


def exchange(arrays, routes, out_shapes, tag, zeta=None):
    sizes = tuple(lax.axis_size(axis) for axis in AXES)
    operands = list(arrays)
    in_specs = [pl.BlockSpec(memory_space=pl.ANY)] * len(arrays)
    out_specs = [pl.BlockSpec(memory_space=pl.ANY)] * len(out_shapes)
    out_shapes = list(out_shapes)
    scratch = []
    copies = len(routes)
    if zeta is not None:
        value, matrix = zeta
        fields, length_x, length_y, depth = value.shape
        rows = fields * length_x * length_y
        padding = jnp.zeros((depth, 8 - WIDTH), matrix.dtype)
        operands += [
            value,
            matrix[:, WIDTH : WIDTH + depth],
            jnp.concatenate([padding, matrix[:, :WIDTH]], axis=1),
            jnp.concatenate([matrix[:, WIDTH + depth :], padding], axis=1),
        ]
        in_specs += [pl.BlockSpec(memory_space=pltpu.VMEM)] * 4
        out_shapes.append(jax.ShapeDtypeStruct(value.shape, value.dtype))
        out_specs.append(pl.BlockSpec(memory_space=pltpu.VMEM))
        scratch = [pltpu.VMEM((depth, rows), jnp.float32), pltpu.VMEM((8, rows), jnp.float32),
                   pltpu.VMEM((8, rows), jnp.float32)]
        copies += 2
    return pl.pallas_call(
        functools.partial(exchange_kernel, tuple(routes), sizes, len(arrays), zeta is not None),
        out_shape=out_shapes,
        in_specs=in_specs,
        out_specs=out_specs,
        scratch_shapes=scratch + [
            pltpu.SemaphoreType.DMA((copies,)),
            pltpu.SemaphoreType.DMA((copies,)),
        ],
        compiler_params=pltpu.CompilerParams(collective_id=tag, has_side_effects=True),
    )(*operands)


def offset_along(axis, step):
    return tuple(step if name == axis else 0 for name in AXES)


def window(ndim, dim, start, stop):
    return tuple(slice(start, stop) if axis == dim else slice(None) for axis in range(ndim))


def exchange_faces(items, tag, zeta=None):
    arrays, routes, out_shapes = [], [], []
    for value, axis, dim in items:
        ndim, length = value.ndim, value.shape[dim]
        if dim == ndim - 1:
            both = jnp.stack(
                [
                    lax.slice_in_dim(value, length - WIDTH, length, axis=dim),
                    lax.slice_in_dim(value, 0, WIDTH, axis=dim),
                ]
            )
            both = jnp.moveaxis(both, dim + 1, 2).reshape(2, value.shape[0], WIDTH, -1)
            arrays.append(both)
            out_shapes.append(jax.ShapeDtypeStruct(both.shape, both.dtype))
            source, target = len(arrays) - 1, len(out_shapes) - 1
            routes.append((offset_along(axis, 1), source, 0, target, 0))
            routes.append((offset_along(axis, -1), source, 1, target, 1))
        elif dim == ndim - 2:
            face = value.shape[:dim] + (WIDTH,) + value.shape[dim + 1 :]
            arrays.append(lax.slice_in_dim(value, length - WIDTH, length, axis=dim))
            arrays.append(lax.slice_in_dim(value, 0, WIDTH, axis=dim))
            out_shapes += [jax.ShapeDtypeStruct(face, value.dtype)] * 2
            source, target = len(arrays) - 2, len(out_shapes) - 2
            whole = window(ndim, dim, None, None)
            routes.append((offset_along(axis, 1), source, whole, target, whole))
            routes.append((offset_along(axis, -1), source + 1, whole, target + 1, whole))
        else:
            arrays.append(value)
            face = value.shape[:dim] + (WIDTH,) + value.shape[dim + 1 :]
            out_shapes += [jax.ShapeDtypeStruct(face, value.dtype)] * 2
            source, target = len(arrays) - 1, len(out_shapes) - 2
            whole = window(ndim, dim, None, None)
            last, first = window(ndim, dim, length - WIDTH, length), window(ndim, dim, 0, WIDTH)
            routes.append((offset_along(axis, 1), source, last, target, whole))
            routes.append((offset_along(axis, -1), source, first, target + 1, whole))
    received = exchange(arrays, routes, out_shapes, tag, zeta)
    padded, place = [], 0
    for value, axis, dim in items:
        if dim == value.ndim - 1:
            both = received[place].reshape((2, value.shape[0], WIDTH) + value.shape[1:dim])
            both = jnp.moveaxis(both, 2, dim + 1)
            before, after = both[0], both[1]
            place += 1
        else:
            before, after = received[place], received[place + 1]
            place += 2
        padded.append(jnp.concatenate([before, value, after], axis=dim))
    if zeta is not None:
        padded.append(received[-1])
    return padded


def exchange_plane(value, tag):
    length_x, length_y = value.shape[1], value.shape[2]
    faces_y = jnp.stack(
        [
            lax.slice_in_dim(value, length_y - WIDTH, length_y, axis=2),
            lax.slice_in_dim(value, 0, WIDTH, axis=2),
        ]
    )
    last_x, first_x = slice(length_x - WIDTH, length_x), slice(0, WIDTH)
    every = slice(None)
    routes = [
        ((1, 0, 0), 0, (every, last_x), 0, 0),
        ((-1, 0, 0), 0, (every, first_x), 0, 1),
        ((0, 1, 0), 1, 0, 1, 0),
        ((0, -1, 0), 1, 1, 1, 1),
        ((1, 1, 0), 1, (0, every, last_x), 2, (0, 0)),
        ((-1, 1, 0), 1, (0, every, first_x), 2, (0, 1)),
        ((1, -1, 0), 1, (1, every, last_x), 2, (1, 0)),
        ((-1, -1, 0), 1, (1, every, first_x), 2, (1, 1)),
    ]
    fields, depth = value.shape[0], value.shape[3]
    out_shapes = [
        jax.ShapeDtypeStruct((2, fields, WIDTH, length_y, depth), value.dtype),
        jax.ShapeDtypeStruct((2, fields, length_x, WIDTH, depth), value.dtype),
        jax.ShapeDtypeStruct((2, 2, fields, WIDTH, WIDTH, depth), value.dtype),
    ]
    along_x, along_y, edges = exchange([value, faces_y], routes, out_shapes, tag)
    sections = [
        jnp.concatenate([edges[0, 0], along_x[0], edges[1, 0]], axis=2),
        jnp.concatenate([along_y[0], value, along_y[1]], axis=2),
        jnp.concatenate([edges[0, 1], along_x[1], edges[1, 1]], axis=2),
    ]
    return jnp.concatenate(sections, axis=1)


def sweep_zeta(value, matrix, tag):
    return exchange([], [], [], tag, (value, matrix))[-1]


def with_halo(value, sides, width):
    for axis, dim in sides:
        count, length = (lax.axis_size(axis), value.shape[dim])
        up = [(i, (i + 1) % count) for i in range(count)]
        down = [(j, i) for i, j in up]
        last = lax.slice_in_dim(value, length - width, length, axis=dim)
        initial = lax.slice_in_dim(value, 0, width, axis=dim)
        before = lax.ppermute(last, axis, up)
        after = lax.ppermute(initial, axis, down)
        value = jnp.concatenate([before, value, after], axis=dim)
    return value


def banded_solve(system, source):
    extent = system.shape[0]
    lower = np.zeros(extent)
    upper = np.zeros(extent)
    middle = np.array([float(system[index, index]) for index in range(extent)])
    for index in range(1, extent):
        lower[index] = system[index, index - 1]
        upper[index - 1] = system[index - 1, index]
    rights = np.array(source)
    for index in range(1, extent):
        factor = lower[index] / middle[index - 1]
        middle[index] = middle[index] - factor * upper[index - 1]
        rights[index] = rights[index] - factor * rights[index - 1]
    answer = np.zeros(rights.shape)
    answer[extent - 1] = rights[extent - 1] / middle[extent - 1]
    for index in range(extent - 2, -1, -1):
        answer[index] = (rights[index] - upper[index] * answer[index + 1]) / middle[index]
    return answer


def derivative_table(length):
    extent = length + 2 * WIDTH
    system = np.eye(extent)
    source = np.zeros((extent, extent))
    for position in range(2, extent - 2):
        system[position, position - 1] = 1.0 / 3.0
        system[position, position + 1] = 1.0 / 3.0
        source[position, position + 1] = 7.0 / 9.0
        source[position, position - 1] = -7.0 / 9.0
        source[position, position + 2] = 1.0 / 36.0
        source[position, position - 2] = -1.0 / 36.0
    source[1, 2] = 0.5
    source[1, 0] = -0.5
    source[extent - 2, extent - 1] = 0.5
    source[extent - 2, extent - 3] = -0.5
    source[0, 1] = 1.0
    source[0, 0] = -1.0
    source[extent - 1, extent - 1] = 1.0
    source[extent - 1, extent - 2] = -1.0
    return banded_solve(system, source)[WIDTH : WIDTH + length]


def filter_table(length):
    strength = 0.4
    coeffs = [
        (193.0 + 126.0 * strength) / 256.0,
        (105.0 + 302.0 * strength) / 256.0,
        15.0 * (2.0 * strength - 1.0) / 64.0,
        45.0 * (1.0 - 2.0 * strength) / 512.0,
        5.0 * (2.0 * strength - 1.0) / 256.0,
        (1.0 - 2.0 * strength) / 512.0,
    ]
    extent = length + 2 * WIDTH
    system = np.eye(extent)
    source = np.eye(extent)
    for position in range(5, extent - 5):
        system[position, position - 1] = strength
        system[position, position + 1] = strength
        source[position, position] = coeffs[0]
        for offset in range(1, 6):
            source[position, position + offset] = coeffs[offset] / 2.0
            source[position, position - offset] = coeffs[offset] / 2.0
    return banded_solve(system, source)[WIDTH : WIDTH + length]


def sweep_lines(padded, matrix, dim):
    return jnp.einsum(line_forms[dim], matrix, padded, precision=lax.Precision.HIGHEST)


def faces_xi(values):
    return with_halo(values, (("xi", 1),), WIDTH)


def faces_eta(values):
    return with_halo(values, (("eta", 2),), WIDTH)


def faces_zeta(values):
    return with_halo(values, (("zeta", 3),), WIDTH)


def basic_quantities(conserved_solution):
    density = conserved_solution[0]
    fluid_speed_vector = conserved_solution[1:4] / density
    thermodynamic_stress_scalar = 0.4 * (
        conserved_solution[4] - 0.5 * jnp.sum(conserved_solution[1:4] * fluid_speed_vector, axis=0)
    )
    return (fluid_speed_vector, thermodynamic_stress_scalar, thermodynamic_stress_scalar / density)


def fluxes(
    conserved_solution, fluid_speed_vector, thermodynamic_stress_scalar, slopes, metrics, jacobian
):
    physical = [
        [
            jacobian
            * (
                metrics[0, column] * slopes[0][member]
                + metrics[1, column] * slopes[1][member]
                + metrics[2, column] * slopes[2][member]
            )
            for column in range(3)
        ]
        for member in range(4)
    ]
    spread = physical[0][0] + physical[1][1] + physical[2][2]
    totals = []
    for column in range(3):
        stress = [
            viscosity * (physical[member][column] + physical[column][member]) for member in range(3)
        ]
        stress[column] = stress[column] - 2.0 / 3.0 * viscosity * spread
        subdomain_parts = [conserved_solution[1 + column]]
        for member in range(3):
            carried = conserved_solution[1 + member] * fluid_speed_vector[column] - stress[member]
            if member == column:
                carried = carried + thermodynamic_stress_scalar
            subdomain_parts.append(carried)
        worked = (
            fluid_speed_vector[0] * stress[0]
            + fluid_speed_vector[1] * stress[1]
            + fluid_speed_vector[2] * stress[2]
        )
        subdomain_parts.append(
            (conserved_solution[4] + thermodynamic_stress_scalar) * fluid_speed_vector[column]
            - worked
            - conduction * physical[3][column]
        )
        totals.append(jnp.stack(subdomain_parts))
    return [
        metrics[direction, 0] * totals[0]
        + metrics[direction, 1] * totals[1]
        + metrics[direction, 2] * totals[2]
        for direction in range(3)
    ]


def local(conserved_solution, metrics, jacobian):
    lengths = conserved_solution.shape[1:]
    derive = [jnp.asarray(derivative_table(length), dtype=jnp.float32) for length in lengths]
    smooth = [jnp.asarray(filter_table(length), dtype=jnp.float32) for length in lengths]
    fluid_speed_vector, thermodynamic_stress_scalar, thermal_level = basic_quantities(
        conserved_solution
    )
    basic_quantity = jnp.concatenate([fluid_speed_vector, thermal_level[None]], axis=0)
    padded = exchange_faces(
        [(basic_quantity, "xi", 1), (basic_quantity, "eta", 2)], 0, (basic_quantity, derive[2])
    )
    slopes = [sweep_lines(padded[k], derive[k], k + 1) for k in range(2)] + [padded[2]]
    contra = fluxes(
        conserved_solution,
        fluid_speed_vector,
        thermodynamic_stress_scalar,
        slopes,
        metrics,
        jacobian,
    )
    padded = exchange_faces([(contra[0], "xi", 1), (contra[1], "eta", 2)], 1, (contra[2], derive[2]))
    divergence = sweep_lines(padded[0], derive[0], 1)
    divergence = divergence + sweep_lines(padded[1], derive[1], 2)
    divergence = divergence + padded[2]
    sectioned = conserved_solution - step_duration * jacobian * divergence
    result = sweep_lines(exchange_plane(sectioned, 2), smooth[0], 1)
    result = sweep_lines(result, smooth[1], 2)
    result = sweep_zeta(result, smooth[2], 4)
    return result


def solution(mesh):
    in_specs = (
        P(None, "xi", "eta", "zeta"),
        P(None, None, "xi", "eta", "zeta"),
        P("xi", "eta", "zeta"),
    )
    out_specs = P(None, "xi", "eta", "zeta")
    return jax.shard_map(local, mesh=mesh, in_specs=in_specs, out_specs=out_specs, check_vma=False)
```

```python
import functools

import jax
import jax.numpy as jnp
import numpy as np
from jax import lax
from jax.experimental import pallas as pl
from jax.experimental.pallas import tpu as pltpu
from jax.sharding import PartitionSpec as P

WIDTH = 5


viscosity = 0.15
conduction = 0.15 * 1.4 / (0.4 * 0.72)
step_duration = 0.08
line_forms = ("", "al,flyz->fayz", "al,fxlz->fxaz", "al,fxyl->fxya")
MESH = pl.DeviceIdType.MESH
AXES = ("xi", "eta", "zeta")


def exchange_kernel(routes, sizes, count, zeta, *refs):
    sources = refs[:count]
    refs = refs[count:]
    if zeta:
        block_ref, middle_ref, lower_ref, upper_ref = refs[:4]
        refs = refs[4:]
    targets = refs[: len(refs) - 2 - (4 if zeta else 0)]
    refs = refs[len(targets) :]
    if zeta:
        out_ref, turned, before, after = refs[:4]
        refs = refs[4:]
    send_sems, recv_sems = refs
    here = [lax.axis_index(axis) for axis in AXES]

    def device(offset):
        return tuple(
            lax.rem(here[slot] + offset[slot] + sizes[slot], sizes[slot]) for slot in range(3)
        )

    offsets = [route[0] for route in routes] + ([(0, 0, 1), (0, 0, -1)] if zeta else [])
    partners = []
    for offset in offsets:
        for way in (offset, tuple(-step for step in offset)):
            if way not in partners:
                partners.append(way)
    barrier = pltpu.get_barrier_semaphore()
    for offset in partners:
        pl.semaphore_signal(barrier, inc=1, device_id=device(offset), device_id_type=MESH)
    if zeta:
        fields, length_x, length_y, depth = block_ref.shape
        rows = fields * length_x * length_y
        turned[...] = block_ref[...].reshape(rows, depth).T
    pl.semaphore_wait(barrier, len(partners))
    copies = []
    for index, (offset, source, source_at, target, target_at) in enumerate(routes):
        copies.append(
            pltpu.make_async_remote_copy(
                src_ref=sources[source].at[source_at],
                dst_ref=targets[target].at[target_at],
                send_sem=send_sems.at[index],
                recv_sem=recv_sems.at[index],
                device_id=device(offset),
                device_id_type=MESH,
            )
        )
    if zeta:
        for index, (rows_at, landing, offset) in enumerate(
            ((pl.ds(depth - 8, 8), before, (0, 0, 1)), (pl.ds(0, 8), after, (0, 0, -1)))
        ):
            copies.append(
                pltpu.make_async_remote_copy(
                    src_ref=turned.at[rows_at],
                    dst_ref=landing,
                    send_sem=send_sems.at[len(routes) + index],
                    recv_sem=recv_sems.at[len(routes) + index],
                    device_id=device(offset),
                    device_id_type=MESH,
                )
            )
    for copy in copies:
        copy.start()
    if zeta:
        total = jnp.dot(middle_ref[...], turned[...], precision=lax.Precision.HIGHEST,
                        preferred_element_type=jnp.float32)
    for copy in copies:
        copy.wait()
    if zeta:
        total = total + jnp.dot(lower_ref[...], before[...], precision=lax.Precision.HIGHEST,
                                preferred_element_type=jnp.float32)
        total = total + jnp.dot(upper_ref[...], after[...], precision=lax.Precision.HIGHEST,
                                preferred_element_type=jnp.float32)
        out_ref[...] = total.T.reshape(fields, length_x, length_y, depth)


def exchange(arrays, routes, out_shapes, tag, zeta=None):
    sizes = tuple(lax.axis_size(axis) for axis in AXES)
    operands = list(arrays)
    in_specs = [pl.BlockSpec(memory_space=pl.ANY)] * len(arrays)
    out_specs = [pl.BlockSpec(memory_space=pl.ANY)] * len(out_shapes)
    out_shapes = list(out_shapes)
    scratch = []
    copies = len(routes)
    if zeta is not None:
        value, matrix = zeta
        fields, length_x, length_y, depth = value.shape
        rows = fields * length_x * length_y
        padding = jnp.zeros((depth, 8 - WIDTH), matrix.dtype)
        operands += [
            value,
            matrix[:, WIDTH : WIDTH + depth],
            jnp.concatenate([padding, matrix[:, :WIDTH]], axis=1),
            jnp.concatenate([matrix[:, WIDTH + depth :], padding], axis=1),
        ]
        in_specs += [pl.BlockSpec(memory_space=pltpu.VMEM)] * 4
        out_shapes.append(jax.ShapeDtypeStruct(value.shape, value.dtype))
        out_specs.append(pl.BlockSpec(memory_space=pltpu.VMEM))
        scratch = [pltpu.VMEM((depth, rows), jnp.float32), pltpu.VMEM((8, rows), jnp.float32),
                   pltpu.VMEM((8, rows), jnp.float32)]
        copies += 2
    return pl.pallas_call(
        functools.partial(exchange_kernel, tuple(routes), sizes, len(arrays), zeta is not None),
        out_shape=out_shapes,
        in_specs=in_specs,
        out_specs=out_specs,
        scratch_shapes=scratch + [
            pltpu.SemaphoreType.DMA((copies,)),
            pltpu.SemaphoreType.DMA((copies,)),
        ],
        compiler_params=pltpu.CompilerParams(collective_id=tag, has_side_effects=True),
    )(*operands)


def offset_along(axis, step):
    return tuple(step if name == axis else 0 for name in AXES)


def window(ndim, dim, start, stop):
    return tuple(slice(start, stop) if axis == dim else slice(None) for axis in range(ndim))


def exchange_faces(items, tag, zeta=None):
    arrays, routes, out_shapes = [], [], []
    for value, axis, dim in items:
        ndim, length = value.ndim, value.shape[dim]
        if dim == ndim - 1:
            both = jnp.stack(
                [
                    lax.slice_in_dim(value, length - WIDTH, length, axis=dim),
                    lax.slice_in_dim(value, 0, WIDTH, axis=dim),
                ]
            )
            both = jnp.moveaxis(both, dim + 1, 2).reshape(2, value.shape[0], WIDTH, -1)
            arrays.append(both)
            out_shapes.append(jax.ShapeDtypeStruct(both.shape, both.dtype))
            source, target = len(arrays) - 1, len(out_shapes) - 1
            routes.append((offset_along(axis, 1), source, 0, target, 0))
            routes.append((offset_along(axis, -1), source, 1, target, 1))
        elif dim == ndim - 2:
            face = value.shape[:dim] + (WIDTH,) + value.shape[dim + 1 :]
            arrays.append(lax.slice_in_dim(value, length - WIDTH, length, axis=dim))
            arrays.append(lax.slice_in_dim(value, 0, WIDTH, axis=dim))
            out_shapes += [jax.ShapeDtypeStruct(face, value.dtype)] * 2
            source, target = len(arrays) - 2, len(out_shapes) - 2
            whole = window(ndim, dim, None, None)
            routes.append((offset_along(axis, 1), source, whole, target, whole))
            routes.append((offset_along(axis, -1), source + 1, whole, target + 1, whole))
        else:
            arrays.append(value)
            face = value.shape[:dim] + (WIDTH,) + value.shape[dim + 1 :]
            out_shapes += [jax.ShapeDtypeStruct(face, value.dtype)] * 2
            source, target = len(arrays) - 1, len(out_shapes) - 2
            whole = window(ndim, dim, None, None)
            last, first = window(ndim, dim, length - WIDTH, length), window(ndim, dim, 0, WIDTH)
            routes.append((offset_along(axis, 1), source, last, target, whole))
            routes.append((offset_along(axis, -1), source, first, target + 1, whole))
    received = exchange(arrays, routes, out_shapes, tag, zeta)
    padded, place = [], 0
    for value, axis, dim in items:
        if dim == value.ndim - 1:
            both = received[place].reshape((2, value.shape[0], WIDTH) + value.shape[1:dim])
            both = jnp.moveaxis(both, 2, dim + 1)
            before, after = both[0], both[1]
            place += 1
        else:
            before, after = received[place], received[place + 1]
            place += 2
        padded.append(jnp.concatenate([before, value, after], axis=dim))
    if zeta is not None:
        padded.append(received[-1])
    return padded


def exchange_plane(value, tag):
    length_x, length_y = value.shape[1], value.shape[2]
    faces_y = jnp.stack(
        [
            lax.slice_in_dim(value, length_y - WIDTH, length_y, axis=2),
            lax.slice_in_dim(value, 0, WIDTH, axis=2),
        ]
    )
    last_x, first_x = slice(length_x - WIDTH, length_x), slice(0, WIDTH)
    every = slice(None)
    routes = [
        ((1, 0, 0), 0, (every, last_x), 0, 0),
        ((-1, 0, 0), 0, (every, first_x), 0, 1),
        ((0, 1, 0), 1, 0, 1, 0),
        ((0, -1, 0), 1, 1, 1, 1),
        ((1, 1, 0), 1, (0, every, last_x), 2, (0, 0)),
        ((-1, 1, 0), 1, (0, every, first_x), 2, (0, 1)),
        ((1, -1, 0), 1, (1, every, last_x), 2, (1, 0)),
        ((-1, -1, 0), 1, (1, every, first_x), 2, (1, 1)),
    ]
    fields, depth = value.shape[0], value.shape[3]
    out_shapes = [
        jax.ShapeDtypeStruct((2, fields, WIDTH, length_y, depth), value.dtype),
        jax.ShapeDtypeStruct((2, fields, length_x, WIDTH, depth), value.dtype),
        jax.ShapeDtypeStruct((2, 2, fields, WIDTH, WIDTH, depth), value.dtype),
    ]
    along_x, along_y, edges = exchange([value, faces_y], routes, out_shapes, tag)
    sections = [
        jnp.concatenate([edges[0, 0], along_x[0], edges[1, 0]], axis=2),
        jnp.concatenate([along_y[0], value, along_y[1]], axis=2),
        jnp.concatenate([edges[0, 1], along_x[1], edges[1, 1]], axis=2),
    ]
    return jnp.concatenate(sections, axis=1)


def sweep_zeta(value, matrix, tag):
    return exchange([], [], [], tag, (value, matrix))[-1]


def with_halo(value, sides, width):
    for axis, dim in sides:
        count, length = (lax.axis_size(axis), value.shape[dim])
        up = [(i, (i + 1) % count) for i in range(count)]
        down = [(j, i) for i, j in up]
        last = lax.slice_in_dim(value, length - width, length, axis=dim)
        initial = lax.slice_in_dim(value, 0, width, axis=dim)
        before = lax.ppermute(last, axis, up)
        after = lax.ppermute(initial, axis, down)
        value = jnp.concatenate([before, value, after], axis=dim)
    return value


def banded_solve(system, source):
    extent = system.shape[0]
    lower = np.zeros(extent)
    upper = np.zeros(extent)
    middle = np.array([float(system[index, index]) for index in range(extent)])
    for index in range(1, extent):
        lower[index] = system[index, index - 1]
        upper[index - 1] = system[index - 1, index]
    rights = np.array(source)
    for index in range(1, extent):
        factor = lower[index] / middle[index - 1]
        middle[index] = middle[index] - factor * upper[index - 1]
        rights[index] = rights[index] - factor * rights[index - 1]
    answer = np.zeros(rights.shape)
    answer[extent - 1] = rights[extent - 1] / middle[extent - 1]
    for index in range(extent - 2, -1, -1):
        answer[index] = (rights[index] - upper[index] * answer[index + 1]) / middle[index]
    return answer


def derivative_table(length):
    extent = length + 2 * WIDTH
    system = np.eye(extent)
    source = np.zeros((extent, extent))
    for position in range(2, extent - 2):
        system[position, position - 1] = 1.0 / 3.0
        system[position, position + 1] = 1.0 / 3.0
        source[position, position + 1] = 7.0 / 9.0
        source[position, position - 1] = -7.0 / 9.0
        source[position, position + 2] = 1.0 / 36.0
        source[position, position - 2] = -1.0 / 36.0
    source[1, 2] = 0.5
    source[1, 0] = -0.5
    source[extent - 2, extent - 1] = 0.5
    source[extent - 2, extent - 3] = -0.5
    source[0, 1] = 1.0
    source[0, 0] = -1.0
    source[extent - 1, extent - 1] = 1.0
    source[extent - 1, extent - 2] = -1.0
    return banded_solve(system, source)[WIDTH : WIDTH + length]


def filter_table(length):
    strength = 0.4
    coeffs = [
        (193.0 + 126.0 * strength) / 256.0,
        (105.0 + 302.0 * strength) / 256.0,
        15.0 * (2.0 * strength - 1.0) / 64.0,
        45.0 * (1.0 - 2.0 * strength) / 512.0,
        5.0 * (2.0 * strength - 1.0) / 256.0,
        (1.0 - 2.0 * strength) / 512.0,
    ]
    extent = length + 2 * WIDTH
    system = np.eye(extent)
    source = np.eye(extent)
    for position in range(5, extent - 5):
        system[position, position - 1] = strength
        system[position, position + 1] = strength
        source[position, position] = coeffs[0]
        for offset in range(1, 6):
            source[position, position + offset] = coeffs[offset] / 2.0
            source[position, position - offset] = coeffs[offset] / 2.0
    return banded_solve(system, source)[WIDTH : WIDTH + length]


def sweep_lines(padded, matrix, dim):
    return jnp.einsum(line_forms[dim], matrix, padded, precision=lax.Precision.HIGHEST)


def faces_xi(values):
    return with_halo(values, (("xi", 1),), WIDTH)


def faces_eta(values):
    return with_halo(values, (("eta", 2),), WIDTH)


def faces_zeta(values):
    return with_halo(values, (("zeta", 3),), WIDTH)


def basic_quantities(conserved_solution):
    density = conserved_solution[0]
    fluid_speed_vector = conserved_solution[1:4] / density
    thermodynamic_stress_scalar = 0.4 * (
        conserved_solution[4] - 0.5 * jnp.sum(conserved_solution[1:4] * fluid_speed_vector, axis=0)
    )
    return (fluid_speed_vector, thermodynamic_stress_scalar, thermodynamic_stress_scalar / density)


def fluxes(
    conserved_solution, fluid_speed_vector, thermodynamic_stress_scalar, slopes, metrics, jacobian
):
    physical = [
        [
            jacobian
            * (
                metrics[0, column] * slopes[0][member]
                + metrics[1, column] * slopes[1][member]
                + metrics[2, column] * slopes[2][member]
            )
            for column in range(3)
        ]
        for member in range(4)
    ]
    spread = physical[0][0] + physical[1][1] + physical[2][2]
    totals = []
    for column in range(3):
        stress = [
            viscosity * (physical[member][column] + physical[column][member]) for member in range(3)
        ]
        stress[column] = stress[column] - 2.0 / 3.0 * viscosity * spread
        subdomain_parts = [conserved_solution[1 + column]]
        for member in range(3):
            carried = conserved_solution[1 + member] * fluid_speed_vector[column] - stress[member]
            if member == column:
                carried = carried + thermodynamic_stress_scalar
            subdomain_parts.append(carried)
        worked = (
            fluid_speed_vector[0] * stress[0]
            + fluid_speed_vector[1] * stress[1]
            + fluid_speed_vector[2] * stress[2]
        )
        subdomain_parts.append(
            (conserved_solution[4] + thermodynamic_stress_scalar) * fluid_speed_vector[column]
            - worked
            - conduction * physical[3][column]
        )
        totals.append(jnp.stack(subdomain_parts))
    return [
        metrics[direction, 0] * totals[0]
        + metrics[direction, 1] * totals[1]
        + metrics[direction, 2] * totals[2]
        for direction in range(3)
    ]


def local(conserved_solution, metrics, jacobian):
    lengths = conserved_solution.shape[1:]
    derive = [jnp.asarray(derivative_table(length), dtype=jnp.float32) for length in lengths]
    smooth = [jnp.asarray(filter_table(length), dtype=jnp.float32) for length in lengths]
    fluid_speed_vector, thermodynamic_stress_scalar, thermal_level = basic_quantities(
        conserved_solution
    )
    basic_quantity = jnp.concatenate([fluid_speed_vector, thermal_level[None]], axis=0)
    padded = exchange_faces(
        [(basic_quantity, "xi", 1), (basic_quantity, "eta", 2)], 0, (basic_quantity, derive[2])
    )
    slopes = [sweep_lines(padded[k], derive[k], k + 1) for k in range(2)] + [padded[2]]
    contra = fluxes(
        conserved_solution,
        fluid_speed_vector,
        thermodynamic_stress_scalar,
        slopes,
        metrics,
        jacobian,
    )
    padded = exchange_faces([(contra[0], "xi", 1), (contra[1], "eta", 2)], 1, (contra[2], derive[2]))
    divergence = sweep_lines(padded[0], derive[0], 1)
    divergence = divergence + sweep_lines(padded[1], derive[1], 2)
    divergence = divergence + padded[2]
    sectioned = conserved_solution - step_duration * jacobian * divergence
    result = sweep_zeta(sectioned, smooth[2], 4)
    result = sweep_lines(exchange_plane(result, 2), smooth[0], 1)
    result = sweep_lines(result, smooth[1], 2)
    return result


def solution(mesh):
    in_specs = (
        P(None, "xi", "eta", "zeta"),
        P(None, None, "xi", "eta", "zeta"),
        P("xi", "eta", "zeta"),
    )
    out_specs = P(None, "xi", "eta", "zeta")
    return jax.shard_map(local, mesh=mesh, in_specs=in_specs, out_specs=out_specs, check_vma=False)
```

```python
import functools

import jax
import jax.numpy as jnp
import numpy as np
from jax import lax
from jax.experimental import pallas as pl
from jax.experimental.pallas import tpu as pltpu
from jax.sharding import PartitionSpec as P

WIDTH = 5


viscosity = 0.15
conduction = 0.15 * 1.4 / (0.4 * 0.72)
step_duration = 0.08
line_forms = ("", "al,flyz->fayz", "al,fxlz->fxaz", "al,fxyl->fxya")
MESH = pl.DeviceIdType.MESH
AXES = ("xi", "eta", "zeta")


def exchange_kernel(routes, sizes, count, zeta, *refs):
    sources = refs[:count]
    refs = refs[count:]
    if zeta:
        block_ref, middle_ref, lower_ref, upper_ref = refs[:4]
        refs = refs[4:]
    targets = refs[: len(refs) - 2 - (4 if zeta else 0)]
    refs = refs[len(targets) :]
    if zeta:
        out_ref, turned, before, after = refs[:4]
        refs = refs[4:]
    send_sems, recv_sems = refs
    here = [lax.axis_index(axis) for axis in AXES]

    def device(offset):
        return tuple(
            lax.rem(here[slot] + offset[slot] + sizes[slot], sizes[slot]) for slot in range(3)
        )

    offsets = [route[0] for route in routes] + ([(0, 0, 1), (0, 0, -1)] if zeta else [])
    partners = []
    for offset in offsets:
        for way in (offset, tuple(-step for step in offset)):
            if way not in partners:
                partners.append(way)
    barrier = pltpu.get_barrier_semaphore()
    for offset in partners:
        pl.semaphore_signal(barrier, inc=1, device_id=device(offset), device_id_type=MESH)
    if zeta:
        fields, length_x, length_y, depth = block_ref.shape
        rows = fields * length_x * length_y
        turned[...] = block_ref[...].reshape(rows, depth).T
    pl.semaphore_wait(barrier, len(partners))
    copies = []
    for index, (offset, source, source_at, target, target_at) in enumerate(routes):
        copies.append(
            pltpu.make_async_remote_copy(
                src_ref=sources[source].at[source_at],
                dst_ref=targets[target].at[target_at],
                send_sem=send_sems.at[index],
                recv_sem=recv_sems.at[index],
                device_id=device(offset),
                device_id_type=MESH,
            )
        )
    if zeta:
        for index, (rows_at, landing, offset) in enumerate(
            ((pl.ds(depth - 8, 8), before, (0, 0, 1)), (pl.ds(0, 8), after, (0, 0, -1)))
        ):
            copies.append(
                pltpu.make_async_remote_copy(
                    src_ref=turned.at[rows_at],
                    dst_ref=landing,
                    send_sem=send_sems.at[len(routes) + index],
                    recv_sem=recv_sems.at[len(routes) + index],
                    device_id=device(offset),
                    device_id_type=MESH,
                )
            )
    for copy in copies:
        copy.start()
    if zeta:
        total = jnp.dot(middle_ref[...], turned[...], precision=lax.Precision.HIGHEST,
                        preferred_element_type=jnp.float32)
    for copy in copies:
        copy.wait()
    if zeta:
        total = total + jnp.dot(lower_ref[...], before[...], precision=lax.Precision.HIGHEST,
                                preferred_element_type=jnp.float32)
        total = total + jnp.dot(upper_ref[...], after[...], precision=lax.Precision.HIGHEST,
                                preferred_element_type=jnp.float32)
        out_ref[...] = total.T.reshape(fields, length_x, length_y, depth)


def exchange(arrays, routes, out_shapes, tag, zeta=None):
    sizes = tuple(lax.axis_size(axis) for axis in AXES)
    operands = [array for array, _ in arrays]
    in_specs = [pl.BlockSpec(memory_space=space) for _, space in arrays]
    out_specs = [pl.BlockSpec(memory_space=pl.ANY)] * len(out_shapes)
    out_shapes = list(out_shapes)
    scratch = []
    copies = len(routes)
    if zeta is not None:
        value, matrix = zeta
        fields, length_x, length_y, depth = value.shape
        rows = fields * length_x * length_y
        padding = jnp.zeros((depth, 8 - WIDTH), matrix.dtype)
        operands += [
            value,
            matrix[:, WIDTH : WIDTH + depth],
            jnp.concatenate([padding, matrix[:, :WIDTH]], axis=1),
            jnp.concatenate([matrix[:, WIDTH + depth :], padding], axis=1),
        ]
        in_specs += [pl.BlockSpec(memory_space=pltpu.VMEM)] * 4
        out_shapes.append(jax.ShapeDtypeStruct(value.shape, value.dtype))
        out_specs.append(pl.BlockSpec(memory_space=pltpu.VMEM))
        scratch = [pltpu.VMEM((depth, rows), jnp.float32), pltpu.VMEM((8, rows), jnp.float32),
                   pltpu.VMEM((8, rows), jnp.float32)]
        copies += 2
    return pl.pallas_call(
        functools.partial(exchange_kernel, tuple(routes), sizes, len(arrays), zeta is not None),
        out_shape=out_shapes,
        in_specs=in_specs,
        out_specs=out_specs,
        scratch_shapes=scratch + [
            pltpu.SemaphoreType.DMA((copies,)),
            pltpu.SemaphoreType.DMA((copies,)),
        ],
        compiler_params=pltpu.CompilerParams(collective_id=tag, has_side_effects=True),
    )(*operands)


def offset_along(axis, step):
    return tuple(step if name == axis else 0 for name in AXES)


def window(ndim, dim, start, stop):
    return tuple(slice(start, stop) if axis == dim else slice(None) for axis in range(ndim))


def exchange_faces(items, tag, zeta=None):
    arrays, routes, out_shapes = [], [], []
    for value, axis, dim in items:
        ndim, length = value.ndim, value.shape[dim]
        if dim == ndim - 1:
            both = jnp.stack(
                [
                    lax.slice_in_dim(value, length - WIDTH, length, axis=dim),
                    lax.slice_in_dim(value, 0, WIDTH, axis=dim),
                ]
            )
            both = jnp.moveaxis(both, dim + 1, 2).reshape(2, value.shape[0], WIDTH, -1)
            arrays.append((both, pl.ANY))
            out_shapes.append(jax.ShapeDtypeStruct(both.shape, both.dtype))
            source, target = len(arrays) - 1, len(out_shapes) - 1
            routes.append((offset_along(axis, 1), source, 0, target, 0))
            routes.append((offset_along(axis, -1), source, 1, target, 1))
        elif dim == ndim - 2:
            face = value.shape[:dim] + (WIDTH,) + value.shape[dim + 1 :]
            arrays.append((value, pltpu.VMEM))
            out_shapes += [jax.ShapeDtypeStruct(face, value.dtype)] * 2
            source, target = len(arrays) - 1, len(out_shapes) - 2
            whole = window(ndim, dim, None, None)
            last, first = window(ndim, dim, length - WIDTH, length), window(ndim, dim, 0, WIDTH)
            routes.append((offset_along(axis, 1), source, last, target, whole))
            routes.append((offset_along(axis, -1), source, first, target + 1, whole))
        else:
            arrays.append((value, pl.ANY))
            face = value.shape[:dim] + (WIDTH,) + value.shape[dim + 1 :]
            out_shapes += [jax.ShapeDtypeStruct(face, value.dtype)] * 2
            source, target = len(arrays) - 1, len(out_shapes) - 2
            whole = window(ndim, dim, None, None)
            last, first = window(ndim, dim, length - WIDTH, length), window(ndim, dim, 0, WIDTH)
            routes.append((offset_along(axis, 1), source, last, target, whole))
            routes.append((offset_along(axis, -1), source, first, target + 1, whole))
    received = exchange(arrays, routes, out_shapes, tag, zeta)
    padded, place = [], 0
    for value, axis, dim in items:
        if dim == value.ndim - 1:
            both = received[place].reshape((2, value.shape[0], WIDTH) + value.shape[1:dim])
            both = jnp.moveaxis(both, 2, dim + 1)
            before, after = both[0], both[1]
            place += 1
        else:
            before, after = received[place], received[place + 1]
            place += 2
        padded.append(jnp.concatenate([before, value, after], axis=dim))
    if zeta is not None:
        padded.append(received[-1])
    return padded


def exchange_plane(value, tag):
    length_x, length_y = value.shape[1], value.shape[2]
    faces_y = jnp.stack(
        [
            lax.slice_in_dim(value, length_y - WIDTH, length_y, axis=2),
            lax.slice_in_dim(value, 0, WIDTH, axis=2),
        ]
    )
    last_x, first_x = slice(length_x - WIDTH, length_x), slice(0, WIDTH)
    every = slice(None)
    routes = [
        ((1, 0, 0), 0, (every, last_x), 0, 0),
        ((-1, 0, 0), 0, (every, first_x), 0, 1),
        ((0, 1, 0), 1, 0, 1, 0),
        ((0, -1, 0), 1, 1, 1, 1),
        ((1, 1, 0), 1, (0, every, last_x), 2, (0, 0)),
        ((-1, 1, 0), 1, (0, every, first_x), 2, (0, 1)),
        ((1, -1, 0), 1, (1, every, last_x), 2, (1, 0)),
        ((-1, -1, 0), 1, (1, every, first_x), 2, (1, 1)),
    ]
    fields, depth = value.shape[0], value.shape[3]
    out_shapes = [
        jax.ShapeDtypeStruct((2, fields, WIDTH, length_y, depth), value.dtype),
        jax.ShapeDtypeStruct((2, fields, length_x, WIDTH, depth), value.dtype),
        jax.ShapeDtypeStruct((2, 2, fields, WIDTH, WIDTH, depth), value.dtype),
    ]
    along_x, along_y, edges = exchange([(value, pl.ANY), (faces_y, pl.ANY)], routes, out_shapes, tag)
    sections = [
        jnp.concatenate([edges[0, 0], along_x[0], edges[1, 0]], axis=2),
        jnp.concatenate([along_y[0], value, along_y[1]], axis=2),
        jnp.concatenate([edges[0, 1], along_x[1], edges[1, 1]], axis=2),
    ]
    return jnp.concatenate(sections, axis=1)


def sweep_zeta(value, matrix, tag):
    return exchange([], [], [], tag, (value, matrix))[-1]


def with_halo(value, sides, width):
    for axis, dim in sides:
        count, length = (lax.axis_size(axis), value.shape[dim])
        up = [(i, (i + 1) % count) for i in range(count)]
        down = [(j, i) for i, j in up]
        last = lax.slice_in_dim(value, length - width, length, axis=dim)
        initial = lax.slice_in_dim(value, 0, width, axis=dim)
        before = lax.ppermute(last, axis, up)
        after = lax.ppermute(initial, axis, down)
        value = jnp.concatenate([before, value, after], axis=dim)
    return value


def banded_solve(system, source):
    extent = system.shape[0]
    lower = np.zeros(extent)
    upper = np.zeros(extent)
    middle = np.array([float(system[index, index]) for index in range(extent)])
    for index in range(1, extent):
        lower[index] = system[index, index - 1]
        upper[index - 1] = system[index - 1, index]
    rights = np.array(source)
    for index in range(1, extent):
        factor = lower[index] / middle[index - 1]
        middle[index] = middle[index] - factor * upper[index - 1]
        rights[index] = rights[index] - factor * rights[index - 1]
    answer = np.zeros(rights.shape)
    answer[extent - 1] = rights[extent - 1] / middle[extent - 1]
    for index in range(extent - 2, -1, -1):
        answer[index] = (rights[index] - upper[index] * answer[index + 1]) / middle[index]
    return answer


def derivative_table(length):
    extent = length + 2 * WIDTH
    system = np.eye(extent)
    source = np.zeros((extent, extent))
    for position in range(2, extent - 2):
        system[position, position - 1] = 1.0 / 3.0
        system[position, position + 1] = 1.0 / 3.0
        source[position, position + 1] = 7.0 / 9.0
        source[position, position - 1] = -7.0 / 9.0
        source[position, position + 2] = 1.0 / 36.0
        source[position, position - 2] = -1.0 / 36.0
    source[1, 2] = 0.5
    source[1, 0] = -0.5
    source[extent - 2, extent - 1] = 0.5
    source[extent - 2, extent - 3] = -0.5
    source[0, 1] = 1.0
    source[0, 0] = -1.0
    source[extent - 1, extent - 1] = 1.0
    source[extent - 1, extent - 2] = -1.0
    return banded_solve(system, source)[WIDTH : WIDTH + length]


def filter_table(length):
    strength = 0.4
    coeffs = [
        (193.0 + 126.0 * strength) / 256.0,
        (105.0 + 302.0 * strength) / 256.0,
        15.0 * (2.0 * strength - 1.0) / 64.0,
        45.0 * (1.0 - 2.0 * strength) / 512.0,
        5.0 * (2.0 * strength - 1.0) / 256.0,
        (1.0 - 2.0 * strength) / 512.0,
    ]
    extent = length + 2 * WIDTH
    system = np.eye(extent)
    source = np.eye(extent)
    for position in range(5, extent - 5):
        system[position, position - 1] = strength
        system[position, position + 1] = strength
        source[position, position] = coeffs[0]
        for offset in range(1, 6):
            source[position, position + offset] = coeffs[offset] / 2.0
            source[position, position - offset] = coeffs[offset] / 2.0
    return banded_solve(system, source)[WIDTH : WIDTH + length]


def sweep_lines(padded, matrix, dim):
    return jnp.einsum(line_forms[dim], matrix, padded, precision=lax.Precision.HIGHEST)


def faces_xi(values):
    return with_halo(values, (("xi", 1),), WIDTH)


def faces_eta(values):
    return with_halo(values, (("eta", 2),), WIDTH)


def faces_zeta(values):
    return with_halo(values, (("zeta", 3),), WIDTH)


def basic_quantities(conserved_solution):
    density = conserved_solution[0]
    fluid_speed_vector = conserved_solution[1:4] / density
    thermodynamic_stress_scalar = 0.4 * (
        conserved_solution[4] - 0.5 * jnp.sum(conserved_solution[1:4] * fluid_speed_vector, axis=0)
    )
    return (fluid_speed_vector, thermodynamic_stress_scalar, thermodynamic_stress_scalar / density)


def fluxes(
    conserved_solution, fluid_speed_vector, thermodynamic_stress_scalar, slopes, metrics, jacobian
):
    physical = [
        [
            jacobian
            * (
                metrics[0, column] * slopes[0][member]
                + metrics[1, column] * slopes[1][member]
                + metrics[2, column] * slopes[2][member]
            )
            for column in range(3)
        ]
        for member in range(4)
    ]
    spread = physical[0][0] + physical[1][1] + physical[2][2]
    totals = []
    for column in range(3):
        stress = [
            viscosity * (physical[member][column] + physical[column][member]) for member in range(3)
        ]
        stress[column] = stress[column] - 2.0 / 3.0 * viscosity * spread
        subdomain_parts = [conserved_solution[1 + column]]
        for member in range(3):
            carried = conserved_solution[1 + member] * fluid_speed_vector[column] - stress[member]
            if member == column:
                carried = carried + thermodynamic_stress_scalar
            subdomain_parts.append(carried)
        worked = (
            fluid_speed_vector[0] * stress[0]
            + fluid_speed_vector[1] * stress[1]
            + fluid_speed_vector[2] * stress[2]
        )
        subdomain_parts.append(
            (conserved_solution[4] + thermodynamic_stress_scalar) * fluid_speed_vector[column]
            - worked
            - conduction * physical[3][column]
        )
        totals.append(jnp.stack(subdomain_parts))
    return [
        metrics[direction, 0] * totals[0]
        + metrics[direction, 1] * totals[1]
        + metrics[direction, 2] * totals[2]
        for direction in range(3)
    ]


def local(conserved_solution, metrics, jacobian):
    lengths = conserved_solution.shape[1:]
    derive = [jnp.asarray(derivative_table(length), dtype=jnp.float32) for length in lengths]
    smooth = [jnp.asarray(filter_table(length), dtype=jnp.float32) for length in lengths]
    fluid_speed_vector, thermodynamic_stress_scalar, thermal_level = basic_quantities(
        conserved_solution
    )
    basic_quantity = jnp.concatenate([fluid_speed_vector, thermal_level[None]], axis=0)
    padded = exchange_faces(
        [(basic_quantity, "xi", 1), (basic_quantity, "eta", 2)], 0, (basic_quantity, derive[2])
    )
    slopes = [sweep_lines(padded[k], derive[k], k + 1) for k in range(2)] + [padded[2]]
    contra = fluxes(
        conserved_solution,
        fluid_speed_vector,
        thermodynamic_stress_scalar,
        slopes,
        metrics,
        jacobian,
    )
    padded = exchange_faces([(contra[0], "xi", 1), (contra[1], "eta", 2)], 1, (contra[2], derive[2]))
    divergence = sweep_lines(padded[0], derive[0], 1)
    divergence = divergence + sweep_lines(padded[1], derive[1], 2)
    divergence = divergence + padded[2]
    sectioned = conserved_solution - step_duration * jacobian * divergence
    result = sweep_lines(exchange_plane(sectioned, 2), smooth[0], 1)
    result = sweep_lines(result, smooth[1], 2)
    result = sweep_zeta(result, smooth[2], 4)
    return result


def solution(mesh):
    in_specs = (
        P(None, "xi", "eta", "zeta"),
        P(None, None, "xi", "eta", "zeta"),
        P("xi", "eta", "zeta"),
    )
    out_specs = P(None, "xi", "eta", "zeta")
    return jax.shard_map(local, mesh=mesh, in_specs=in_specs, out_specs=out_specs, check_vma=False)
```

```python
import functools

import jax
import jax.numpy as jnp
import numpy as np
from jax import lax
from jax.experimental import pallas as pl
from jax.experimental.pallas import tpu as pltpu
from jax.sharding import PartitionSpec as P

WIDTH = 5


viscosity = 0.15
conduction = 0.15 * 1.4 / (0.4 * 0.72)
step_duration = 0.08
line_forms = ("", "al,flyz->fayz", "al,fxlz->fxaz", "al,fxyl->fxya")
MESH = pl.DeviceIdType.MESH
AXES = ("xi", "eta", "zeta")


def exchange_kernel(routes, sizes, count, zeta, *refs):
    sources = refs[:count]
    refs = refs[count:]
    if zeta:
        block_ref, middle_ref, lower_ref, upper_ref = refs[:4]
        refs = refs[4:]
    targets = refs[: len(refs) - 2 - (4 if zeta else 0)]
    refs = refs[len(targets) :]
    if zeta:
        out_ref, turned, before, after = refs[:4]
        refs = refs[4:]
    send_sems, recv_sems = refs
    here = [lax.axis_index(axis) for axis in AXES]

    def device(offset):
        return tuple(
            lax.rem(here[slot] + offset[slot] + sizes[slot], sizes[slot]) for slot in range(3)
        )

    offsets = [route[0] for route in routes] + ([(0, 0, 1), (0, 0, -1)] if zeta else [])
    partners = []
    for offset in offsets:
        for way in (offset, tuple(-step for step in offset)):
            if way not in partners:
                partners.append(way)
    barrier = pltpu.get_barrier_semaphore()
    for offset in partners:
        pl.semaphore_signal(barrier, inc=1, device_id=device(offset), device_id_type=MESH)
    if zeta:
        fields, length_x, length_y, depth = block_ref.shape
        rows = fields * length_x * length_y
        turned[...] = block_ref[...].reshape(rows, depth).T
    pl.semaphore_wait(barrier, len(partners))
    copies = []
    for index, (offset, source, source_at, target, target_at) in enumerate(routes):
        copies.append(
            pltpu.make_async_remote_copy(
                src_ref=sources[source].at[source_at],
                dst_ref=targets[target].at[target_at],
                send_sem=send_sems.at[index],
                recv_sem=recv_sems.at[index],
                device_id=device(offset),
                device_id_type=MESH,
            )
        )
    if zeta:
        for index, (rows_at, landing, offset) in enumerate(
            ((pl.ds(depth - 8, 8), before, (0, 0, 1)), (pl.ds(0, 8), after, (0, 0, -1)))
        ):
            copies.append(
                pltpu.make_async_remote_copy(
                    src_ref=turned.at[rows_at],
                    dst_ref=landing,
                    send_sem=send_sems.at[len(routes) + index],
                    recv_sem=recv_sems.at[len(routes) + index],
                    device_id=device(offset),
                    device_id_type=MESH,
                )
            )
    for copy in copies:
        copy.start()
    if zeta:
        total = jnp.dot(middle_ref[...], turned[...], precision=lax.Precision.HIGHEST,
                        preferred_element_type=jnp.float32)
    for copy in copies:
        copy.wait()
    if zeta:
        total = total + jnp.dot(lower_ref[...], before[...], precision=lax.Precision.HIGHEST,
                                preferred_element_type=jnp.float32)
        total = total + jnp.dot(upper_ref[...], after[...], precision=lax.Precision.HIGHEST,
                                preferred_element_type=jnp.float32)
        out_ref[...] = total.T.reshape(fields, length_x, length_y, depth)


def exchange(arrays, routes, out_shapes, tag, zeta=None):
    sizes = tuple(lax.axis_size(axis) for axis in AXES)
    operands = [array for array, _ in arrays]
    in_specs = [pl.BlockSpec(memory_space=space) for _, space in arrays]
    out_specs = [pl.BlockSpec(memory_space=pl.ANY)] * len(out_shapes)
    out_shapes = list(out_shapes)
    scratch = []
    copies = len(routes)
    if zeta is not None:
        value, matrix = zeta
        fields, length_x, length_y, depth = value.shape
        rows = fields * length_x * length_y
        padding = jnp.zeros((depth, 8 - WIDTH), matrix.dtype)
        operands += [
            value,
            matrix[:, WIDTH : WIDTH + depth],
            jnp.concatenate([padding, matrix[:, :WIDTH]], axis=1),
            jnp.concatenate([matrix[:, WIDTH + depth :], padding], axis=1),
        ]
        in_specs += [pl.BlockSpec(memory_space=pltpu.VMEM)] * 4
        out_shapes.append(jax.ShapeDtypeStruct(value.shape, value.dtype))
        out_specs.append(pl.BlockSpec(memory_space=pltpu.VMEM))
        scratch = [pltpu.VMEM((depth, rows), jnp.float32), pltpu.VMEM((8, rows), jnp.float32),
                   pltpu.VMEM((8, rows), jnp.float32)]
        copies += 2
    return pl.pallas_call(
        functools.partial(exchange_kernel, tuple(routes), sizes, len(arrays), zeta is not None),
        out_shape=out_shapes,
        in_specs=in_specs,
        out_specs=out_specs,
        scratch_shapes=scratch + [
            pltpu.SemaphoreType.DMA((copies,)),
            pltpu.SemaphoreType.DMA((copies,)),
        ],
        compiler_params=pltpu.CompilerParams(collective_id=tag, has_side_effects=True),
    )(*operands)


def offset_along(axis, step):
    return tuple(step if name == axis else 0 for name in AXES)


def window(ndim, dim, start, stop):
    return tuple(slice(start, stop) if axis == dim else slice(None) for axis in range(ndim))


def exchange_faces(items, tag, zeta=None):
    arrays, routes, out_shapes = [], [], []
    for value, axis, dim in items:
        ndim, length = value.ndim, value.shape[dim]
        if dim == ndim - 1:
            both = jnp.stack(
                [
                    lax.slice_in_dim(value, length - WIDTH, length, axis=dim),
                    lax.slice_in_dim(value, 0, WIDTH, axis=dim),
                ]
            )
            both = jnp.moveaxis(both, dim + 1, 2).reshape(2, value.shape[0], WIDTH, -1)
            arrays.append((both, pl.ANY))
            out_shapes.append(jax.ShapeDtypeStruct(both.shape, both.dtype))
            source, target = len(arrays) - 1, len(out_shapes) - 1
            routes.append((offset_along(axis, 1), source, 0, target, 0))
            routes.append((offset_along(axis, -1), source, 1, target, 1))
        elif dim == ndim - 2:
            face = value.shape[:dim] + (WIDTH,) + value.shape[dim + 1 :]
            arrays.append((value, pltpu.VMEM))
            out_shapes += [jax.ShapeDtypeStruct(face, value.dtype)] * 2
            source, target = len(arrays) - 1, len(out_shapes) - 2
            whole = window(ndim, dim, None, None)
            last, first = window(ndim, dim, length - WIDTH, length), window(ndim, dim, 0, WIDTH)
            routes.append((offset_along(axis, 1), source, last, target, whole))
            routes.append((offset_along(axis, -1), source, first, target + 1, whole))
        else:
            arrays.append((value, pl.ANY))
            face = value.shape[:dim] + (WIDTH,) + value.shape[dim + 1 :]
            out_shapes += [jax.ShapeDtypeStruct(face, value.dtype)] * 2
            source, target = len(arrays) - 1, len(out_shapes) - 2
            whole = window(ndim, dim, None, None)
            last, first = window(ndim, dim, length - WIDTH, length), window(ndim, dim, 0, WIDTH)
            routes.append((offset_along(axis, 1), source, last, target, whole))
            routes.append((offset_along(axis, -1), source, first, target + 1, whole))
    received = exchange(arrays, routes, out_shapes, tag, zeta)
    padded, place = [], 0
    for value, axis, dim in items:
        if dim == value.ndim - 1:
            both = received[place].reshape((2, value.shape[0], WIDTH) + value.shape[1:dim])
            both = jnp.moveaxis(both, 2, dim + 1)
            before, after = both[0], both[1]
            place += 1
        else:
            before, after = received[place], received[place + 1]
            place += 2
        padded.append(jnp.concatenate([before, value, after], axis=dim))
    if zeta is not None:
        padded.append(received[-1])
    return padded


def exchange_plane(value, tag):
    length_x, length_y = value.shape[1], value.shape[2]
    last_x, first_x = slice(length_x - WIDTH, length_x), slice(0, WIDTH)
    last_y, first_y = slice(length_y - WIDTH, length_y), slice(0, WIDTH)
    every = slice(None)
    routes = [
        ((1, 0, 0), 0, (every, last_x), 0, 0),
        ((-1, 0, 0), 0, (every, first_x), 0, 1),
        ((0, 1, 0), 1, (every, every, last_y), 1, 0),
        ((0, -1, 0), 1, (every, every, first_y), 1, 1),
        ((1, 1, 0), 1, (every, last_x, last_y), 2, (0, 0)),
        ((-1, 1, 0), 1, (every, first_x, last_y), 2, (0, 1)),
        ((1, -1, 0), 1, (every, last_x, first_y), 2, (1, 0)),
        ((-1, -1, 0), 1, (every, first_x, first_y), 2, (1, 1)),
    ]
    fields, depth = value.shape[0], value.shape[3]
    out_shapes = [
        jax.ShapeDtypeStruct((2, fields, WIDTH, length_y, depth), value.dtype),
        jax.ShapeDtypeStruct((2, fields, length_x, WIDTH, depth), value.dtype),
        jax.ShapeDtypeStruct((2, 2, fields, WIDTH, WIDTH, depth), value.dtype),
    ]
    along_x, along_y, edges = exchange(
        [(value, pl.ANY), (value, pltpu.VMEM)], routes, out_shapes, tag
    )
    sections = [
        jnp.concatenate([edges[0, 0], along_x[0], edges[1, 0]], axis=2),
        jnp.concatenate([along_y[0], value, along_y[1]], axis=2),
        jnp.concatenate([edges[0, 1], along_x[1], edges[1, 1]], axis=2),
    ]
    return jnp.concatenate(sections, axis=1)


def sweep_zeta(value, matrix, tag):
    return exchange([], [], [], tag, (value, matrix))[-1]


def with_halo(value, sides, width):
    for axis, dim in sides:
        count, length = (lax.axis_size(axis), value.shape[dim])
        up = [(i, (i + 1) % count) for i in range(count)]
        down = [(j, i) for i, j in up]
        last = lax.slice_in_dim(value, length - width, length, axis=dim)
        initial = lax.slice_in_dim(value, 0, width, axis=dim)
        before = lax.ppermute(last, axis, up)
        after = lax.ppermute(initial, axis, down)
        value = jnp.concatenate([before, value, after], axis=dim)
    return value


def banded_solve(system, source):
    extent = system.shape[0]
    lower = np.zeros(extent)
    upper = np.zeros(extent)
    middle = np.array([float(system[index, index]) for index in range(extent)])
    for index in range(1, extent):
        lower[index] = system[index, index - 1]
        upper[index - 1] = system[index - 1, index]
    rights = np.array(source)
    for index in range(1, extent):
        factor = lower[index] / middle[index - 1]
        middle[index] = middle[index] - factor * upper[index - 1]
        rights[index] = rights[index] - factor * rights[index - 1]
    answer = np.zeros(rights.shape)
    answer[extent - 1] = rights[extent - 1] / middle[extent - 1]
    for index in range(extent - 2, -1, -1):
        answer[index] = (rights[index] - upper[index] * answer[index + 1]) / middle[index]
    return answer


def derivative_table(length):
    extent = length + 2 * WIDTH
    system = np.eye(extent)
    source = np.zeros((extent, extent))
    for position in range(2, extent - 2):
        system[position, position - 1] = 1.0 / 3.0
        system[position, position + 1] = 1.0 / 3.0
        source[position, position + 1] = 7.0 / 9.0
        source[position, position - 1] = -7.0 / 9.0
        source[position, position + 2] = 1.0 / 36.0
        source[position, position - 2] = -1.0 / 36.0
    source[1, 2] = 0.5
    source[1, 0] = -0.5
    source[extent - 2, extent - 1] = 0.5
    source[extent - 2, extent - 3] = -0.5
    source[0, 1] = 1.0
    source[0, 0] = -1.0
    source[extent - 1, extent - 1] = 1.0
    source[extent - 1, extent - 2] = -1.0
    return banded_solve(system, source)[WIDTH : WIDTH + length]


def filter_table(length):
    strength = 0.4
    coeffs = [
        (193.0 + 126.0 * strength) / 256.0,
        (105.0 + 302.0 * strength) / 256.0,
        15.0 * (2.0 * strength - 1.0) / 64.0,
        45.0 * (1.0 - 2.0 * strength) / 512.0,
        5.0 * (2.0 * strength - 1.0) / 256.0,
        (1.0 - 2.0 * strength) / 512.0,
    ]
    extent = length + 2 * WIDTH
    system = np.eye(extent)
    source = np.eye(extent)
    for position in range(5, extent - 5):
        system[position, position - 1] = strength
        system[position, position + 1] = strength
        source[position, position] = coeffs[0]
        for offset in range(1, 6):
            source[position, position + offset] = coeffs[offset] / 2.0
            source[position, position - offset] = coeffs[offset] / 2.0
    return banded_solve(system, source)[WIDTH : WIDTH + length]


def sweep_lines(padded, matrix, dim):
    return jnp.einsum(line_forms[dim], matrix, padded, precision=lax.Precision.HIGHEST)


def faces_xi(values):
    return with_halo(values, (("xi", 1),), WIDTH)


def faces_eta(values):
    return with_halo(values, (("eta", 2),), WIDTH)


def faces_zeta(values):
    return with_halo(values, (("zeta", 3),), WIDTH)


def basic_quantities(conserved_solution):
    density = conserved_solution[0]
    fluid_speed_vector = conserved_solution[1:4] / density
    thermodynamic_stress_scalar = 0.4 * (
        conserved_solution[4] - 0.5 * jnp.sum(conserved_solution[1:4] * fluid_speed_vector, axis=0)
    )
    return (fluid_speed_vector, thermodynamic_stress_scalar, thermodynamic_stress_scalar / density)


def fluxes(
    conserved_solution, fluid_speed_vector, thermodynamic_stress_scalar, slopes, metrics, jacobian
):
    physical = [
        [
            jacobian
            * (
                metrics[0, column] * slopes[0][member]
                + metrics[1, column] * slopes[1][member]
                + metrics[2, column] * slopes[2][member]
            )
            for column in range(3)
        ]
        for member in range(4)
    ]
    spread = physical[0][0] + physical[1][1] + physical[2][2]
    totals = []
    for column in range(3):
        stress = [
            viscosity * (physical[member][column] + physical[column][member]) for member in range(3)
        ]
        stress[column] = stress[column] - 2.0 / 3.0 * viscosity * spread
        subdomain_parts = [conserved_solution[1 + column]]
        for member in range(3):
            carried = conserved_solution[1 + member] * fluid_speed_vector[column] - stress[member]
            if member == column:
                carried = carried + thermodynamic_stress_scalar
            subdomain_parts.append(carried)
        worked = (
            fluid_speed_vector[0] * stress[0]
            + fluid_speed_vector[1] * stress[1]
            + fluid_speed_vector[2] * stress[2]
        )
        subdomain_parts.append(
            (conserved_solution[4] + thermodynamic_stress_scalar) * fluid_speed_vector[column]
            - worked
            - conduction * physical[3][column]
        )
        totals.append(jnp.stack(subdomain_parts))
    return [
        metrics[direction, 0] * totals[0]
        + metrics[direction, 1] * totals[1]
        + metrics[direction, 2] * totals[2]
        for direction in range(3)
    ]


def local(conserved_solution, metrics, jacobian):
    lengths = conserved_solution.shape[1:]
    derive = [jnp.asarray(derivative_table(length), dtype=jnp.float32) for length in lengths]
    smooth = [jnp.asarray(filter_table(length), dtype=jnp.float32) for length in lengths]
    fluid_speed_vector, thermodynamic_stress_scalar, thermal_level = basic_quantities(
        conserved_solution
    )
    basic_quantity = jnp.concatenate([fluid_speed_vector, thermal_level[None]], axis=0)
    padded = exchange_faces(
        [(basic_quantity, "xi", 1), (basic_quantity, "eta", 2)], 0, (basic_quantity, derive[2])
    )
    slopes = [sweep_lines(padded[k], derive[k], k + 1) for k in range(2)] + [padded[2]]
    contra = fluxes(
        conserved_solution,
        fluid_speed_vector,
        thermodynamic_stress_scalar,
        slopes,
        metrics,
        jacobian,
    )
    padded = exchange_faces([(contra[0], "xi", 1), (contra[1], "eta", 2)], 1, (contra[2], derive[2]))
    divergence = sweep_lines(padded[0], derive[0], 1)
    divergence = divergence + sweep_lines(padded[1], derive[1], 2)
    divergence = divergence + padded[2]
    sectioned = conserved_solution - step_duration * jacobian * divergence
    result = sweep_lines(exchange_plane(sectioned, 2), smooth[0], 1)
    result = sweep_lines(result, smooth[1], 2)
    result = sweep_zeta(result, smooth[2], 4)
    return result


def solution(mesh):
    in_specs = (
        P(None, "xi", "eta", "zeta"),
        P(None, None, "xi", "eta", "zeta"),
        P("xi", "eta", "zeta"),
    )
    out_specs = P(None, "xi", "eta", "zeta")
    return jax.shard_map(local, mesh=mesh, in_specs=in_specs, out_specs=out_specs, check_vma=False)
```

```python
import functools

import jax
import jax.numpy as jnp
import numpy as np
from jax import lax
from jax.experimental import pallas as pl
from jax.experimental.pallas import tpu as pltpu
from jax.sharding import PartitionSpec as P

WIDTH = 5


viscosity = 0.15
conduction = 0.15 * 1.4 / (0.4 * 0.72)
step_duration = 0.08
line_forms = ("", "al,flyz->fayz", "al,fxlz->fxaz", "al,fxyl->fxya")
MESH = pl.DeviceIdType.MESH
AXES = ("xi", "eta", "zeta")


def primitive_state(conserved):
    density = conserved[0]
    speed = conserved[1:4] / density
    pressure = 0.4 * (conserved[4] - 0.5 * jnp.sum(conserved[1:4] * speed, axis=0))
    return speed, pressure / density


def exchange_kernel(routes, sizes, count, zeta, prepare, *refs):
    sources = list(refs[:count])
    refs = refs[count:]
    if prepare:
        conserved_ref = sources.pop()
    if zeta:
        if not prepare:
            block_ref = refs[0]
            refs = refs[1:]
        middle_ref, lower_ref, upper_ref = refs[:3]
        refs = refs[3:]
    targets = refs[: len(refs) - 2 - (4 if zeta else 0) - (1 if prepare else 0)]
    refs = refs[len(targets) :]
    if zeta:
        out_ref, turned, before, after = refs[:4]
        refs = refs[4:]
    if prepare:
        made = refs[0]
        refs = refs[1:]
        sources.append(made)
        if zeta:
            block_ref = made
    send_sems, recv_sems = refs
    here = [lax.axis_index(axis) for axis in AXES]

    def device(offset):
        return tuple(
            lax.rem(here[slot] + offset[slot] + sizes[slot], sizes[slot]) for slot in range(3)
        )

    offsets = [route[0] for route in routes] + ([(0, 0, 1), (0, 0, -1)] if zeta else [])
    partners = []
    for offset in offsets:
        for way in (offset, tuple(-step for step in offset)):
            if way not in partners:
                partners.append(way)
    barrier = pltpu.get_barrier_semaphore()
    for offset in partners:
        pl.semaphore_signal(barrier, inc=1, device_id=device(offset), device_id_type=MESH)
    if prepare:
        speed, temperature = primitive_state(conserved_ref[...])
        made[0:3] = speed
        made[3] = temperature
    if zeta:
        fields, length_x, length_y, depth = block_ref.shape
        rows = fields * length_x * length_y
        turned[...] = block_ref[...].reshape(rows, depth).T
    pl.semaphore_wait(barrier, len(partners))
    copies = []
    for index, (offset, source, source_at, target, target_at) in enumerate(routes):
        copies.append(
            pltpu.make_async_remote_copy(
                src_ref=sources[source].at[source_at],
                dst_ref=targets[target].at[target_at],
                send_sem=send_sems.at[index],
                recv_sem=recv_sems.at[index],
                device_id=device(offset),
                device_id_type=MESH,
            )
        )
    if zeta:
        for index, (rows_at, landing, offset) in enumerate(
            ((pl.ds(depth - 8, 8), before, (0, 0, 1)), (pl.ds(0, 8), after, (0, 0, -1)))
        ):
            copies.append(
                pltpu.make_async_remote_copy(
                    src_ref=turned.at[rows_at],
                    dst_ref=landing,
                    send_sem=send_sems.at[len(routes) + index],
                    recv_sem=recv_sems.at[len(routes) + index],
                    device_id=device(offset),
                    device_id_type=MESH,
                )
            )
    for copy in copies:
        copy.start()
    if zeta:
        total = jnp.dot(middle_ref[...], turned[...], precision=lax.Precision.HIGHEST,
                        preferred_element_type=jnp.float32)
    for copy in copies:
        copy.wait()
    if zeta:
        total = total + jnp.dot(lower_ref[...], before[...], precision=lax.Precision.HIGHEST,
                                preferred_element_type=jnp.float32)
        total = total + jnp.dot(upper_ref[...], after[...], precision=lax.Precision.HIGHEST,
                                preferred_element_type=jnp.float32)
        out_ref[...] = total.T.reshape(fields, length_x, length_y, depth)


def exchange(arrays, routes, out_shapes, tag, zeta=None, prepare=None):
    sizes = tuple(lax.axis_size(axis) for axis in AXES)
    operands = [array for array, _ in arrays]
    in_specs = [pl.BlockSpec(memory_space=space) for _, space in arrays]
    out_specs = [pl.BlockSpec(memory_space=pl.ANY)] * len(out_shapes)
    out_shapes = list(out_shapes)
    scratch = []
    copies = len(routes)
    if prepare is not None:
        operands.append(prepare)
        in_specs.append(pl.BlockSpec(memory_space=pltpu.VMEM))
    if zeta is not None:
        value, matrix = zeta
        fields, length_x, length_y, depth = value.shape
        rows = fields * length_x * length_y
        padding = jnp.zeros((depth, 8 - WIDTH), matrix.dtype)
        if prepare is None:
            operands.append(value)
            in_specs.append(pl.BlockSpec(memory_space=pltpu.VMEM))
        operands += [
            matrix[:, WIDTH : WIDTH + depth],
            jnp.concatenate([padding, matrix[:, :WIDTH]], axis=1),
            jnp.concatenate([matrix[:, WIDTH + depth :], padding], axis=1),
        ]
        in_specs += [pl.BlockSpec(memory_space=pltpu.VMEM)] * 3
        out_shapes.append(jax.ShapeDtypeStruct(value.shape, value.dtype))
        out_specs.append(pl.BlockSpec(memory_space=pltpu.VMEM))
        scratch = [pltpu.VMEM((depth, rows), jnp.float32), pltpu.VMEM((8, rows), jnp.float32),
                   pltpu.VMEM((8, rows), jnp.float32)]
        copies += 2
    if prepare is not None:
        scratch.append(pltpu.VMEM(zeta[0].shape, jnp.float32))
    return pl.pallas_call(
        functools.partial(
            exchange_kernel, tuple(routes), sizes, len(arrays) + (prepare is not None),
            zeta is not None, prepare is not None,
        ),
        out_shape=out_shapes,
        in_specs=in_specs,
        out_specs=out_specs,
        scratch_shapes=scratch + [
            pltpu.SemaphoreType.DMA((copies,)),
            pltpu.SemaphoreType.DMA((copies,)),
        ],
        compiler_params=pltpu.CompilerParams(collective_id=tag, has_side_effects=True),
    )(*operands)


def offset_along(axis, step):
    return tuple(step if name == axis else 0 for name in AXES)


def window(ndim, dim, start, stop):
    return tuple(slice(start, stop) if axis == dim else slice(None) for axis in range(ndim))


def exchange_faces(items, tag, zeta=None):
    arrays, routes, out_shapes = [], [], []
    for value, axis, dim in items:
        ndim, length = value.ndim, value.shape[dim]
        if dim == ndim - 1:
            both = jnp.stack(
                [
                    lax.slice_in_dim(value, length - WIDTH, length, axis=dim),
                    lax.slice_in_dim(value, 0, WIDTH, axis=dim),
                ]
            )
            both = jnp.moveaxis(both, dim + 1, 2).reshape(2, value.shape[0], WIDTH, -1)
            arrays.append((both, pl.ANY))
            out_shapes.append(jax.ShapeDtypeStruct(both.shape, both.dtype))
            source, target = len(arrays) - 1, len(out_shapes) - 1
            routes.append((offset_along(axis, 1), source, 0, target, 0))
            routes.append((offset_along(axis, -1), source, 1, target, 1))
        elif dim == ndim - 2:
            face = value.shape[:dim] + (WIDTH,) + value.shape[dim + 1 :]
            arrays.append((value, pltpu.VMEM))
            out_shapes += [jax.ShapeDtypeStruct(face, value.dtype)] * 2
            source, target = len(arrays) - 1, len(out_shapes) - 2
            whole = window(ndim, dim, None, None)
            last, first = window(ndim, dim, length - WIDTH, length), window(ndim, dim, 0, WIDTH)
            routes.append((offset_along(axis, 1), source, last, target, whole))
            routes.append((offset_along(axis, -1), source, first, target + 1, whole))
        else:
            arrays.append((value, pl.ANY))
            face = value.shape[:dim] + (WIDTH,) + value.shape[dim + 1 :]
            out_shapes += [jax.ShapeDtypeStruct(face, value.dtype)] * 2
            source, target = len(arrays) - 1, len(out_shapes) - 2
            whole = window(ndim, dim, None, None)
            last, first = window(ndim, dim, length - WIDTH, length), window(ndim, dim, 0, WIDTH)
            routes.append((offset_along(axis, 1), source, last, target, whole))
            routes.append((offset_along(axis, -1), source, first, target + 1, whole))
    received = exchange(arrays, routes, out_shapes, tag, zeta)
    padded, place = [], 0
    for value, axis, dim in items:
        if dim == value.ndim - 1:
            both = received[place].reshape((2, value.shape[0], WIDTH) + value.shape[1:dim])
            both = jnp.moveaxis(both, 2, dim + 1)
            before, after = both[0], both[1]
            place += 1
        else:
            before, after = received[place], received[place + 1]
            place += 2
        padded.append(jnp.concatenate([before, value, after], axis=dim))
    if zeta is not None:
        padded.append(received[-1])
    return padded


def exchange_primitive(conserved, primitive, matrix, tag):
    length_x, length_y = primitive.shape[1], primitive.shape[2]
    every = slice(None)
    routes = [
        ((1, 0, 0), 0, (every, slice(length_x - WIDTH, length_x)), 0, every),
        ((-1, 0, 0), 0, (every, slice(0, WIDTH)), 1, every),
        ((0, 1, 0), 0, (every, every, slice(length_y - WIDTH, length_y)), 2, every),
        ((0, -1, 0), 0, (every, every, slice(0, WIDTH)), 3, every),
    ]
    face_x = (primitive.shape[0], WIDTH) + primitive.shape[2:]
    face_y = primitive.shape[:2] + (WIDTH,) + primitive.shape[3:]
    out_shapes = [jax.ShapeDtypeStruct(face, primitive.dtype) for face in (face_x, face_x, face_y, face_y)]
    before_x, after_x, before_y, after_y, swept = exchange(
        [], routes, out_shapes, tag, (primitive, matrix), conserved
    )
    return (
        jnp.concatenate([before_x, primitive, after_x], axis=1),
        jnp.concatenate([before_y, primitive, after_y], axis=2),
        swept,
    )


def exchange_plane(value, tag):
    length_x, length_y = value.shape[1], value.shape[2]
    faces_y = jnp.stack(
        [
            lax.slice_in_dim(value, length_y - WIDTH, length_y, axis=2),
            lax.slice_in_dim(value, 0, WIDTH, axis=2),
        ]
    )
    last_x, first_x = slice(length_x - WIDTH, length_x), slice(0, WIDTH)
    every = slice(None)
    routes = [
        ((1, 0, 0), 0, (every, last_x), 0, 0),
        ((-1, 0, 0), 0, (every, first_x), 0, 1),
        ((0, 1, 0), 1, 0, 1, 0),
        ((0, -1, 0), 1, 1, 1, 1),
        ((1, 1, 0), 1, (0, every, last_x), 2, (0, 0)),
        ((-1, 1, 0), 1, (0, every, first_x), 2, (0, 1)),
        ((1, -1, 0), 1, (1, every, last_x), 2, (1, 0)),
        ((-1, -1, 0), 1, (1, every, first_x), 2, (1, 1)),
    ]
    fields, depth = value.shape[0], value.shape[3]
    out_shapes = [
        jax.ShapeDtypeStruct((2, fields, WIDTH, length_y, depth), value.dtype),
        jax.ShapeDtypeStruct((2, fields, length_x, WIDTH, depth), value.dtype),
        jax.ShapeDtypeStruct((2, 2, fields, WIDTH, WIDTH, depth), value.dtype),
    ]
    along_x, along_y, edges = exchange([(value, pl.ANY), (faces_y, pl.ANY)], routes, out_shapes, tag)
    sections = [
        jnp.concatenate([edges[0, 0], along_x[0], edges[1, 0]], axis=2),
        jnp.concatenate([along_y[0], value, along_y[1]], axis=2),
        jnp.concatenate([edges[0, 1], along_x[1], edges[1, 1]], axis=2),
    ]
    return jnp.concatenate(sections, axis=1)


def sweep_zeta(value, matrix, tag):
    return exchange([], [], [], tag, (value, matrix))[-1]


def with_halo(value, sides, width):
    for axis, dim in sides:
        count, length = (lax.axis_size(axis), value.shape[dim])
        up = [(i, (i + 1) % count) for i in range(count)]
        down = [(j, i) for i, j in up]
        last = lax.slice_in_dim(value, length - width, length, axis=dim)
        initial = lax.slice_in_dim(value, 0, width, axis=dim)
        before = lax.ppermute(last, axis, up)
        after = lax.ppermute(initial, axis, down)
        value = jnp.concatenate([before, value, after], axis=dim)
    return value


def banded_solve(system, source):
    extent = system.shape[0]
    lower = np.zeros(extent)
    upper = np.zeros(extent)
    middle = np.array([float(system[index, index]) for index in range(extent)])
    for index in range(1, extent):
        lower[index] = system[index, index - 1]
        upper[index - 1] = system[index - 1, index]
    rights = np.array(source)
    for index in range(1, extent):
        factor = lower[index] / middle[index - 1]
        middle[index] = middle[index] - factor * upper[index - 1]
        rights[index] = rights[index] - factor * rights[index - 1]
    answer = np.zeros(rights.shape)
    answer[extent - 1] = rights[extent - 1] / middle[extent - 1]
    for index in range(extent - 2, -1, -1):
        answer[index] = (rights[index] - upper[index] * answer[index + 1]) / middle[index]
    return answer


def derivative_table(length):
    extent = length + 2 * WIDTH
    system = np.eye(extent)
    source = np.zeros((extent, extent))
    for position in range(2, extent - 2):
        system[position, position - 1] = 1.0 / 3.0
        system[position, position + 1] = 1.0 / 3.0
        source[position, position + 1] = 7.0 / 9.0
        source[position, position - 1] = -7.0 / 9.0
        source[position, position + 2] = 1.0 / 36.0
        source[position, position - 2] = -1.0 / 36.0
    source[1, 2] = 0.5
    source[1, 0] = -0.5
    source[extent - 2, extent - 1] = 0.5
    source[extent - 2, extent - 3] = -0.5
    source[0, 1] = 1.0
    source[0, 0] = -1.0
    source[extent - 1, extent - 1] = 1.0
    source[extent - 1, extent - 2] = -1.0
    return banded_solve(system, source)[WIDTH : WIDTH + length]


def filter_table(length):
    strength = 0.4
    coeffs = [
        (193.0 + 126.0 * strength) / 256.0,
        (105.0 + 302.0 * strength) / 256.0,
        15.0 * (2.0 * strength - 1.0) / 64.0,
        45.0 * (1.0 - 2.0 * strength) / 512.0,
        5.0 * (2.0 * strength - 1.0) / 256.0,
        (1.0 - 2.0 * strength) / 512.0,
    ]
    extent = length + 2 * WIDTH
    system = np.eye(extent)
    source = np.eye(extent)
    for position in range(5, extent - 5):
        system[position, position - 1] = strength
        system[position, position + 1] = strength
        source[position, position] = coeffs[0]
        for offset in range(1, 6):
            source[position, position + offset] = coeffs[offset] / 2.0
            source[position, position - offset] = coeffs[offset] / 2.0
    return banded_solve(system, source)[WIDTH : WIDTH + length]


def sweep_lines(padded, matrix, dim):
    return jnp.einsum(line_forms[dim], matrix, padded, precision=lax.Precision.HIGHEST)


def faces_xi(values):
    return with_halo(values, (("xi", 1),), WIDTH)


def faces_eta(values):
    return with_halo(values, (("eta", 2),), WIDTH)


def faces_zeta(values):
    return with_halo(values, (("zeta", 3),), WIDTH)


def basic_quantities(conserved_solution):
    density = conserved_solution[0]
    fluid_speed_vector = conserved_solution[1:4] / density
    thermodynamic_stress_scalar = 0.4 * (
        conserved_solution[4] - 0.5 * jnp.sum(conserved_solution[1:4] * fluid_speed_vector, axis=0)
    )
    return (fluid_speed_vector, thermodynamic_stress_scalar, thermodynamic_stress_scalar / density)


def fluxes(
    conserved_solution, fluid_speed_vector, thermodynamic_stress_scalar, slopes, metrics, jacobian
):
    physical = [
        [
            jacobian
            * (
                metrics[0, column] * slopes[0][member]
                + metrics[1, column] * slopes[1][member]
                + metrics[2, column] * slopes[2][member]
            )
            for column in range(3)
        ]
        for member in range(4)
    ]
    spread = physical[0][0] + physical[1][1] + physical[2][2]
    totals = []
    for column in range(3):
        stress = [
            viscosity * (physical[member][column] + physical[column][member]) for member in range(3)
        ]
        stress[column] = stress[column] - 2.0 / 3.0 * viscosity * spread
        subdomain_parts = [conserved_solution[1 + column]]
        for member in range(3):
            carried = conserved_solution[1 + member] * fluid_speed_vector[column] - stress[member]
            if member == column:
                carried = carried + thermodynamic_stress_scalar
            subdomain_parts.append(carried)
        worked = (
            fluid_speed_vector[0] * stress[0]
            + fluid_speed_vector[1] * stress[1]
            + fluid_speed_vector[2] * stress[2]
        )
        subdomain_parts.append(
            (conserved_solution[4] + thermodynamic_stress_scalar) * fluid_speed_vector[column]
            - worked
            - conduction * physical[3][column]
        )
        totals.append(jnp.stack(subdomain_parts))
    return [
        metrics[direction, 0] * totals[0]
        + metrics[direction, 1] * totals[1]
        + metrics[direction, 2] * totals[2]
        for direction in range(3)
    ]


def local(conserved_solution, metrics, jacobian):
    lengths = conserved_solution.shape[1:]
    derive = [jnp.asarray(derivative_table(length), dtype=jnp.float32) for length in lengths]
    smooth = [jnp.asarray(filter_table(length), dtype=jnp.float32) for length in lengths]
    fluid_speed_vector, thermodynamic_stress_scalar, thermal_level = basic_quantities(
        conserved_solution
    )
    basic_quantity = jnp.concatenate([fluid_speed_vector, thermal_level[None]], axis=0)
    padded = exchange_primitive(conserved_solution, basic_quantity, derive[2], 0)
    slopes = [sweep_lines(padded[k], derive[k], k + 1) for k in range(2)] + [padded[2]]
    contra = fluxes(
        conserved_solution,
        fluid_speed_vector,
        thermodynamic_stress_scalar,
        slopes,
        metrics,
        jacobian,
    )
    padded = exchange_faces([(contra[0], "xi", 1), (contra[1], "eta", 2)], 1, (contra[2], derive[2]))
    divergence = sweep_lines(padded[0], derive[0], 1)
    divergence = divergence + sweep_lines(padded[1], derive[1], 2)
    divergence = divergence + padded[2]
    sectioned = conserved_solution - step_duration * jacobian * divergence
    result = sweep_lines(exchange_plane(sectioned, 2), smooth[0], 1)
    result = sweep_lines(result, smooth[1], 2)
    result = sweep_zeta(result, smooth[2], 4)
    return result


def solution(mesh):
    in_specs = (
        P(None, "xi", "eta", "zeta"),
        P(None, None, "xi", "eta", "zeta"),
        P("xi", "eta", "zeta"),
    )
    out_specs = P(None, "xi", "eta", "zeta")
    return jax.shard_map(local, mesh=mesh, in_specs=in_specs, out_specs=out_specs, check_vma=False)
```

```python
import functools

import jax
import jax.numpy as jnp
import numpy as np
from jax import lax
from jax.experimental import pallas as pl
from jax.experimental.pallas import tpu as pltpu
from jax.sharding import PartitionSpec as P

WIDTH = 5


viscosity = 0.15
conduction = 0.15 * 1.4 / (0.4 * 0.72)
step_duration = 0.08
line_forms = ("", "al,flyz->fayz", "al,fxlz->fxaz", "al,fxyl->fxya")
MESH = pl.DeviceIdType.MESH
AXES = ("xi", "eta", "zeta")


def primitive_state(conserved):
    density = conserved[0]
    speed = conserved[1:4] / density
    pressure = 0.4 * (conserved[4] - 0.5 * jnp.sum(conserved[1:4] * speed, axis=0))
    return speed, pressure, pressure / density


def exchange_kernel(routes, sizes, count, zeta, prepare, *refs):
    sources = list(refs[:count])
    refs = refs[count:]
    if prepare:
        conserved_ref = sources.pop()
    if zeta:
        if not prepare:
            block_ref = refs[0]
            refs = refs[1:]
        middle_ref, lower_ref, upper_ref = refs[:3]
        refs = refs[3:]
    extra = (1 if zeta else 0) + (2 if prepare else 0)
    targets = refs[: len(refs) - 2 - (3 if zeta else 0) - extra]
    refs = refs[len(targets) :]
    if zeta:
        out_ref = refs[0]
        refs = refs[1:]
    if prepare:
        made, pressure_ref = refs[:2]
        refs = refs[2:]
        sources.append(made)
        if zeta:
            block_ref = made
    if zeta:
        turned, before, after = refs[:3]
        refs = refs[3:]
    send_sems, recv_sems = refs
    here = [lax.axis_index(axis) for axis in AXES]

    def device(offset):
        return tuple(
            lax.rem(here[slot] + offset[slot] + sizes[slot], sizes[slot]) for slot in range(3)
        )

    offsets = [route[0] for route in routes] + ([(0, 0, 1), (0, 0, -1)] if zeta else [])
    partners = []
    for offset in offsets:
        for way in (offset, tuple(-step for step in offset)):
            if way not in partners:
                partners.append(way)
    barrier = pltpu.get_barrier_semaphore()
    for offset in partners:
        pl.semaphore_signal(barrier, inc=1, device_id=device(offset), device_id_type=MESH)
    if prepare:
        speed, pressure, temperature = primitive_state(conserved_ref[...])
        made[0:3] = speed
        made[3] = temperature
        pressure_ref[...] = pressure
    if zeta:
        fields, length_x, length_y, depth = block_ref.shape
        rows = fields * length_x * length_y
        turned[...] = block_ref[...].reshape(rows, depth).T
    pl.semaphore_wait(barrier, len(partners))
    copies = []
    for index, (offset, source, source_at, target, target_at) in enumerate(routes):
        copies.append(
            pltpu.make_async_remote_copy(
                src_ref=sources[source].at[source_at],
                dst_ref=targets[target].at[target_at],
                send_sem=send_sems.at[index],
                recv_sem=recv_sems.at[index],
                device_id=device(offset),
                device_id_type=MESH,
            )
        )
    if zeta:
        for index, (rows_at, landing, offset) in enumerate(
            ((pl.ds(depth - 8, 8), before, (0, 0, 1)), (pl.ds(0, 8), after, (0, 0, -1)))
        ):
            copies.append(
                pltpu.make_async_remote_copy(
                    src_ref=turned.at[rows_at],
                    dst_ref=landing,
                    send_sem=send_sems.at[len(routes) + index],
                    recv_sem=recv_sems.at[len(routes) + index],
                    device_id=device(offset),
                    device_id_type=MESH,
                )
            )
    for copy in copies:
        copy.start()
    if zeta:
        total = jnp.dot(middle_ref[...], turned[...], precision=lax.Precision.HIGHEST,
                        preferred_element_type=jnp.float32)
    for copy in copies:
        copy.wait()
    if zeta:
        total = total + jnp.dot(lower_ref[...], before[...], precision=lax.Precision.HIGHEST,
                                preferred_element_type=jnp.float32)
        total = total + jnp.dot(upper_ref[...], after[...], precision=lax.Precision.HIGHEST,
                                preferred_element_type=jnp.float32)
        out_ref[...] = total.T.reshape(fields, length_x, length_y, depth)


def exchange(arrays, routes, out_shapes, tag, zeta=None, prepare=None):
    sizes = tuple(lax.axis_size(axis) for axis in AXES)
    operands = [array for array, _ in arrays]
    in_specs = [pl.BlockSpec(memory_space=space) for _, space in arrays]
    out_specs = [pl.BlockSpec(memory_space=pl.ANY)] * len(out_shapes)
    out_shapes = list(out_shapes)
    scratch = []
    copies = len(routes)
    if prepare is not None:
        operands.append(prepare)
        in_specs.append(pl.BlockSpec(memory_space=pltpu.VMEM))
    if zeta is not None:
        value, matrix = zeta
        fields, length_x, length_y, depth = value.shape
        rows = fields * length_x * length_y
        padding = jnp.zeros((depth, 8 - WIDTH), matrix.dtype)
        if prepare is None:
            operands.append(value)
            in_specs.append(pl.BlockSpec(memory_space=pltpu.VMEM))
        operands += [
            matrix[:, WIDTH : WIDTH + depth],
            jnp.concatenate([padding, matrix[:, :WIDTH]], axis=1),
            jnp.concatenate([matrix[:, WIDTH + depth :], padding], axis=1),
        ]
        in_specs += [pl.BlockSpec(memory_space=pltpu.VMEM)] * 3
        out_shapes.append(jax.ShapeDtypeStruct(value.shape, value.dtype))
        out_specs.append(pl.BlockSpec(memory_space=pltpu.VMEM))
        scratch = [pltpu.VMEM((depth, rows), jnp.float32), pltpu.VMEM((8, rows), jnp.float32),
                   pltpu.VMEM((8, rows), jnp.float32)]
        copies += 2
    if prepare is not None:
        out_shapes += [
            jax.ShapeDtypeStruct(zeta[0].shape, jnp.float32),
            jax.ShapeDtypeStruct(prepare.shape[1:], jnp.float32),
        ]
        out_specs += [pl.BlockSpec(memory_space=pltpu.VMEM)] * 2
    return pl.pallas_call(
        functools.partial(
            exchange_kernel, tuple(routes), sizes, len(arrays) + (prepare is not None),
            zeta is not None, prepare is not None,
        ),
        out_shape=out_shapes,
        in_specs=in_specs,
        out_specs=out_specs,
        scratch_shapes=scratch + [
            pltpu.SemaphoreType.DMA((copies,)),
            pltpu.SemaphoreType.DMA((copies,)),
        ],
        compiler_params=pltpu.CompilerParams(collective_id=tag, has_side_effects=True),
    )(*operands)


def offset_along(axis, step):
    return tuple(step if name == axis else 0 for name in AXES)


def window(ndim, dim, start, stop):
    return tuple(slice(start, stop) if axis == dim else slice(None) for axis in range(ndim))


def exchange_faces(items, tag, zeta=None):
    arrays, routes, out_shapes = [], [], []
    for value, axis, dim in items:
        ndim, length = value.ndim, value.shape[dim]
        if dim == ndim - 1:
            both = jnp.stack(
                [
                    lax.slice_in_dim(value, length - WIDTH, length, axis=dim),
                    lax.slice_in_dim(value, 0, WIDTH, axis=dim),
                ]
            )
            both = jnp.moveaxis(both, dim + 1, 2).reshape(2, value.shape[0], WIDTH, -1)
            arrays.append((both, pl.ANY))
            out_shapes.append(jax.ShapeDtypeStruct(both.shape, both.dtype))
            source, target = len(arrays) - 1, len(out_shapes) - 1
            routes.append((offset_along(axis, 1), source, 0, target, 0))
            routes.append((offset_along(axis, -1), source, 1, target, 1))
        elif dim == ndim - 2:
            face = value.shape[:dim] + (WIDTH,) + value.shape[dim + 1 :]
            arrays.append((value, pltpu.VMEM))
            out_shapes += [jax.ShapeDtypeStruct(face, value.dtype)] * 2
            source, target = len(arrays) - 1, len(out_shapes) - 2
            whole = window(ndim, dim, None, None)
            last, first = window(ndim, dim, length - WIDTH, length), window(ndim, dim, 0, WIDTH)
            routes.append((offset_along(axis, 1), source, last, target, whole))
            routes.append((offset_along(axis, -1), source, first, target + 1, whole))
        else:
            arrays.append((value, pl.ANY))
            face = value.shape[:dim] + (WIDTH,) + value.shape[dim + 1 :]
            out_shapes += [jax.ShapeDtypeStruct(face, value.dtype)] * 2
            source, target = len(arrays) - 1, len(out_shapes) - 2
            whole = window(ndim, dim, None, None)
            last, first = window(ndim, dim, length - WIDTH, length), window(ndim, dim, 0, WIDTH)
            routes.append((offset_along(axis, 1), source, last, target, whole))
            routes.append((offset_along(axis, -1), source, first, target + 1, whole))
    received = exchange(arrays, routes, out_shapes, tag, zeta)
    padded, place = [], 0
    for value, axis, dim in items:
        if dim == value.ndim - 1:
            both = received[place].reshape((2, value.shape[0], WIDTH) + value.shape[1:dim])
            both = jnp.moveaxis(both, 2, dim + 1)
            before, after = both[0], both[1]
            place += 1
        else:
            before, after = received[place], received[place + 1]
            place += 2
        padded.append(jnp.concatenate([before, value, after], axis=dim))
    if zeta is not None:
        padded.append(received[-1])
    return padded


def exchange_primitive(conserved, matrix, tag):
    primitive = jax.ShapeDtypeStruct((4,) + conserved.shape[1:], conserved.dtype)
    length_x, length_y = primitive.shape[1], primitive.shape[2]
    every = slice(None)
    routes = [
        ((1, 0, 0), 0, (every, slice(length_x - WIDTH, length_x)), 0, every),
        ((-1, 0, 0), 0, (every, slice(0, WIDTH)), 1, every),
        ((0, 1, 0), 0, (every, every, slice(length_y - WIDTH, length_y)), 2, every),
        ((0, -1, 0), 0, (every, every, slice(0, WIDTH)), 3, every),
    ]
    face_x = (primitive.shape[0], WIDTH) + primitive.shape[2:]
    face_y = primitive.shape[:2] + (WIDTH,) + primitive.shape[3:]
    out_shapes = [jax.ShapeDtypeStruct(face, primitive.dtype) for face in (face_x, face_x, face_y, face_y)]
    before_x, after_x, before_y, after_y, swept, primitive, pressure = exchange(
        [], routes, out_shapes, tag, (primitive, matrix), conserved
    )
    return (
        jnp.concatenate([before_x, primitive, after_x], axis=1),
        jnp.concatenate([before_y, primitive, after_y], axis=2),
        swept,
        primitive,
        pressure,
    )


def exchange_plane(value, tag):
    length_x, length_y = value.shape[1], value.shape[2]
    faces_y = jnp.stack(
        [
            lax.slice_in_dim(value, length_y - WIDTH, length_y, axis=2),
            lax.slice_in_dim(value, 0, WIDTH, axis=2),
        ]
    )
    last_x, first_x = slice(length_x - WIDTH, length_x), slice(0, WIDTH)
    every = slice(None)
    routes = [
        ((1, 0, 0), 0, (every, last_x), 0, 0),
        ((-1, 0, 0), 0, (every, first_x), 0, 1),
        ((0, 1, 0), 1, 0, 1, 0),
        ((0, -1, 0), 1, 1, 1, 1),
        ((1, 1, 0), 1, (0, every, last_x), 2, (0, 0)),
        ((-1, 1, 0), 1, (0, every, first_x), 2, (0, 1)),
        ((1, -1, 0), 1, (1, every, last_x), 2, (1, 0)),
        ((-1, -1, 0), 1, (1, every, first_x), 2, (1, 1)),
    ]
    fields, depth = value.shape[0], value.shape[3]
    out_shapes = [
        jax.ShapeDtypeStruct((2, fields, WIDTH, length_y, depth), value.dtype),
        jax.ShapeDtypeStruct((2, fields, length_x, WIDTH, depth), value.dtype),
        jax.ShapeDtypeStruct((2, 2, fields, WIDTH, WIDTH, depth), value.dtype),
    ]
    along_x, along_y, edges = exchange([(value, pl.ANY), (faces_y, pl.ANY)], routes, out_shapes, tag)
    sections = [
        jnp.concatenate([edges[0, 0], along_x[0], edges[1, 0]], axis=2),
        jnp.concatenate([along_y[0], value, along_y[1]], axis=2),
        jnp.concatenate([edges[0, 1], along_x[1], edges[1, 1]], axis=2),
    ]
    return jnp.concatenate(sections, axis=1)


def sweep_zeta(value, matrix, tag):
    return exchange([], [], [], tag, (value, matrix))[-1]


def with_halo(value, sides, width):
    for axis, dim in sides:
        count, length = (lax.axis_size(axis), value.shape[dim])
        up = [(i, (i + 1) % count) for i in range(count)]
        down = [(j, i) for i, j in up]
        last = lax.slice_in_dim(value, length - width, length, axis=dim)
        initial = lax.slice_in_dim(value, 0, width, axis=dim)
        before = lax.ppermute(last, axis, up)
        after = lax.ppermute(initial, axis, down)
        value = jnp.concatenate([before, value, after], axis=dim)
    return value


def banded_solve(system, source):
    extent = system.shape[0]
    lower = np.zeros(extent)
    upper = np.zeros(extent)
    middle = np.array([float(system[index, index]) for index in range(extent)])
    for index in range(1, extent):
        lower[index] = system[index, index - 1]
        upper[index - 1] = system[index - 1, index]
    rights = np.array(source)
    for index in range(1, extent):
        factor = lower[index] / middle[index - 1]
        middle[index] = middle[index] - factor * upper[index - 1]
        rights[index] = rights[index] - factor * rights[index - 1]
    answer = np.zeros(rights.shape)
    answer[extent - 1] = rights[extent - 1] / middle[extent - 1]
    for index in range(extent - 2, -1, -1):
        answer[index] = (rights[index] - upper[index] * answer[index + 1]) / middle[index]
    return answer


def derivative_table(length):
    extent = length + 2 * WIDTH
    system = np.eye(extent)
    source = np.zeros((extent, extent))
    for position in range(2, extent - 2):
        system[position, position - 1] = 1.0 / 3.0
        system[position, position + 1] = 1.0 / 3.0
        source[position, position + 1] = 7.0 / 9.0
        source[position, position - 1] = -7.0 / 9.0
        source[position, position + 2] = 1.0 / 36.0
        source[position, position - 2] = -1.0 / 36.0
    source[1, 2] = 0.5
    source[1, 0] = -0.5
    source[extent - 2, extent - 1] = 0.5
    source[extent - 2, extent - 3] = -0.5
    source[0, 1] = 1.0
    source[0, 0] = -1.0
    source[extent - 1, extent - 1] = 1.0
    source[extent - 1, extent - 2] = -1.0
    return banded_solve(system, source)[WIDTH : WIDTH + length]


def filter_table(length):
    strength = 0.4
    coeffs = [
        (193.0 + 126.0 * strength) / 256.0,
        (105.0 + 302.0 * strength) / 256.0,
        15.0 * (2.0 * strength - 1.0) / 64.0,
        45.0 * (1.0 - 2.0 * strength) / 512.0,
        5.0 * (2.0 * strength - 1.0) / 256.0,
        (1.0 - 2.0 * strength) / 512.0,
    ]
    extent = length + 2 * WIDTH
    system = np.eye(extent)
    source = np.eye(extent)
    for position in range(5, extent - 5):
        system[position, position - 1] = strength
        system[position, position + 1] = strength
        source[position, position] = coeffs[0]
        for offset in range(1, 6):
            source[position, position + offset] = coeffs[offset] / 2.0
            source[position, position - offset] = coeffs[offset] / 2.0
    return banded_solve(system, source)[WIDTH : WIDTH + length]


def sweep_lines(padded, matrix, dim):
    return jnp.einsum(line_forms[dim], matrix, padded, precision=lax.Precision.HIGHEST)


def faces_xi(values):
    return with_halo(values, (("xi", 1),), WIDTH)


def faces_eta(values):
    return with_halo(values, (("eta", 2),), WIDTH)


def faces_zeta(values):
    return with_halo(values, (("zeta", 3),), WIDTH)


def basic_quantities(conserved_solution):
    density = conserved_solution[0]
    fluid_speed_vector = conserved_solution[1:4] / density
    thermodynamic_stress_scalar = 0.4 * (
        conserved_solution[4] - 0.5 * jnp.sum(conserved_solution[1:4] * fluid_speed_vector, axis=0)
    )
    return (fluid_speed_vector, thermodynamic_stress_scalar, thermodynamic_stress_scalar / density)


def fluxes(
    conserved_solution, fluid_speed_vector, thermodynamic_stress_scalar, slopes, metrics, jacobian
):
    physical = [
        [
            jacobian
            * (
                metrics[0, column] * slopes[0][member]
                + metrics[1, column] * slopes[1][member]
                + metrics[2, column] * slopes[2][member]
            )
            for column in range(3)
        ]
        for member in range(4)
    ]
    spread = physical[0][0] + physical[1][1] + physical[2][2]
    totals = []
    for column in range(3):
        stress = [
            viscosity * (physical[member][column] + physical[column][member]) for member in range(3)
        ]
        stress[column] = stress[column] - 2.0 / 3.0 * viscosity * spread
        subdomain_parts = [conserved_solution[1 + column]]
        for member in range(3):
            carried = conserved_solution[1 + member] * fluid_speed_vector[column] - stress[member]
            if member == column:
                carried = carried + thermodynamic_stress_scalar
            subdomain_parts.append(carried)
        worked = (
            fluid_speed_vector[0] * stress[0]
            + fluid_speed_vector[1] * stress[1]
            + fluid_speed_vector[2] * stress[2]
        )
        subdomain_parts.append(
            (conserved_solution[4] + thermodynamic_stress_scalar) * fluid_speed_vector[column]
            - worked
            - conduction * physical[3][column]
        )
        totals.append(jnp.stack(subdomain_parts))
    return [
        metrics[direction, 0] * totals[0]
        + metrics[direction, 1] * totals[1]
        + metrics[direction, 2] * totals[2]
        for direction in range(3)
    ]


def local(conserved_solution, metrics, jacobian):
    lengths = conserved_solution.shape[1:]
    derive = [jnp.asarray(derivative_table(length), dtype=jnp.float32) for length in lengths]
    smooth = [jnp.asarray(filter_table(length), dtype=jnp.float32) for length in lengths]
    padded = exchange_primitive(conserved_solution, derive[2], 0)
    slopes = [sweep_lines(padded[k], derive[k], k + 1) for k in range(2)] + [padded[2]]
    fluid_speed_vector, thermodynamic_stress_scalar = padded[3][0:3], padded[4]
    contra = fluxes(
        conserved_solution,
        fluid_speed_vector,
        thermodynamic_stress_scalar,
        slopes,
        metrics,
        jacobian,
    )
    padded = exchange_faces([(contra[0], "xi", 1), (contra[1], "eta", 2)], 1, (contra[2], derive[2]))
    divergence = sweep_lines(padded[0], derive[0], 1)
    divergence = divergence + sweep_lines(padded[1], derive[1], 2)
    divergence = divergence + padded[2]
    sectioned = conserved_solution - step_duration * jacobian * divergence
    result = sweep_lines(exchange_plane(sectioned, 2), smooth[0], 1)
    result = sweep_lines(result, smooth[1], 2)
    result = sweep_zeta(result, smooth[2], 4)
    return result


def solution(mesh):
    in_specs = (
        P(None, "xi", "eta", "zeta"),
        P(None, None, "xi", "eta", "zeta"),
        P("xi", "eta", "zeta"),
    )
    out_specs = P(None, "xi", "eta", "zeta")
    return jax.shard_map(local, mesh=mesh, in_specs=in_specs, out_specs=out_specs, check_vma=False)
```

```python
import functools

import jax
import jax.numpy as jnp
import numpy as np
from jax import lax
from jax.experimental import pallas as pl
from jax.experimental.pallas import tpu as pltpu
from jax.sharding import PartitionSpec as P

WIDTH = 5


viscosity = 0.15
conduction = 0.15 * 1.4 / (0.4 * 0.72)
step_duration = 0.08
line_forms = ("", "al,flyz->fayz", "al,fxlz->fxaz", "al,fxyl->fxya")
MESH = pl.DeviceIdType.MESH
AXES = ("xi", "eta", "zeta")


def primitive_state(conserved):
    density = conserved[0]
    speed = conserved[1:4] / density
    pressure = 0.4 * (conserved[4] - 0.5 * jnp.sum(conserved[1:4] * speed, axis=0))
    return speed, pressure, pressure / density


def exchange_kernel(routes, sizes, count, zeta, prepare, *refs):
    sources = list(refs[:count])
    refs = refs[count:]
    if prepare:
        conserved_ref = sources.pop()
    if zeta:
        if not prepare:
            block_ref = refs[0]
            refs = refs[1:]
        middle_ref, lower_ref, upper_ref = refs[:3]
        refs = refs[3:]
    extra = (1 if zeta else 0) + (2 if prepare else 0)
    targets = refs[: len(refs) - 2 - (3 if zeta else 0) - extra]
    refs = refs[len(targets) :]
    if zeta:
        out_ref = refs[0]
        refs = refs[1:]
    if prepare:
        made, pressure_ref = refs[:2]
        refs = refs[2:]
        sources.append(made)
        if zeta:
            block_ref = made
    if zeta:
        turned, before, after = refs[:3]
        refs = refs[3:]
    send_sems, recv_sems = refs
    here = [lax.axis_index(axis) for axis in AXES]

    def device(offset):
        return tuple(
            lax.rem(here[slot] + offset[slot] + sizes[slot], sizes[slot]) for slot in range(3)
        )

    offsets = [route[0] for route in routes] + ([(0, 0, 1), (0, 0, -1)] if zeta else [])
    partners = []
    for offset in offsets:
        for way in (offset, tuple(-step for step in offset)):
            if way not in partners:
                partners.append(way)
    barrier = pltpu.get_barrier_semaphore()
    for offset in partners:
        pl.semaphore_signal(barrier, inc=1, device_id=device(offset), device_id_type=MESH)
    if prepare:
        speed, pressure, temperature = primitive_state(conserved_ref[...])
        made[0:3] = speed
        made[3] = temperature
        pressure_ref[...] = pressure
    if zeta:
        fields, length_x, length_y, depth = block_ref.shape
        rows = fields * length_x * length_y
        turned[...] = block_ref[...].reshape(rows, depth).T
    pl.semaphore_wait(barrier, len(partners))
    copies = []
    for index, (offset, source, source_at, target, target_at) in enumerate(routes):
        copies.append(
            pltpu.make_async_remote_copy(
                src_ref=sources[source].at[source_at],
                dst_ref=targets[target].at[target_at],
                send_sem=send_sems.at[index],
                recv_sem=recv_sems.at[index],
                device_id=device(offset),
                device_id_type=MESH,
            )
        )
    if zeta:
        for index, (rows_at, landing, offset) in enumerate(
            ((pl.ds(depth - 8, 8), before, (0, 0, 1)), (pl.ds(0, 8), after, (0, 0, -1)))
        ):
            copies.append(
                pltpu.make_async_remote_copy(
                    src_ref=turned.at[rows_at],
                    dst_ref=landing,
                    send_sem=send_sems.at[len(routes) + index],
                    recv_sem=recv_sems.at[len(routes) + index],
                    device_id=device(offset),
                    device_id_type=MESH,
                )
            )
    for copy in copies:
        copy.start()
    if zeta:
        total = jnp.dot(middle_ref[...], turned[...], precision=lax.Precision.HIGHEST,
                        preferred_element_type=jnp.float32)
    for copy in copies:
        copy.wait()
    if zeta:
        total = total + jnp.dot(lower_ref[...], before[...], precision=lax.Precision.HIGHEST,
                                preferred_element_type=jnp.float32)
        total = total + jnp.dot(upper_ref[...], after[...], precision=lax.Precision.HIGHEST,
                                preferred_element_type=jnp.float32)
        out_ref[...] = total.T.reshape(fields, length_x, length_y, depth)


def exchange(arrays, routes, out_shapes, tag, zeta=None, prepare=None):
    sizes = tuple(lax.axis_size(axis) for axis in AXES)
    operands = [array for array, _ in arrays]
    in_specs = [pl.BlockSpec(memory_space=space) for _, space in arrays]
    out_specs = [pl.BlockSpec(memory_space=pl.ANY)] * len(out_shapes)
    out_shapes = list(out_shapes)
    scratch = []
    copies = len(routes)
    if prepare is not None:
        operands.append(prepare)
        in_specs.append(pl.BlockSpec(memory_space=pltpu.VMEM))
    if zeta is not None:
        value, matrix = zeta
        fields, length_x, length_y, depth = value.shape
        rows = fields * length_x * length_y
        padding = jnp.zeros((depth, 8 - WIDTH), matrix.dtype)
        if prepare is None:
            operands.append(value)
            in_specs.append(pl.BlockSpec(memory_space=pltpu.VMEM))
        operands += [
            matrix[:, WIDTH : WIDTH + depth],
            jnp.concatenate([padding, matrix[:, :WIDTH]], axis=1),
            jnp.concatenate([matrix[:, WIDTH + depth :], padding], axis=1),
        ]
        in_specs += [pl.BlockSpec(memory_space=pltpu.VMEM)] * 3
        out_shapes.append(jax.ShapeDtypeStruct(value.shape, value.dtype))
        out_specs.append(pl.BlockSpec(memory_space=pltpu.VMEM))
        scratch = [pltpu.VMEM((depth, rows), jnp.float32), pltpu.VMEM((8, rows), jnp.float32),
                   pltpu.VMEM((8, rows), jnp.float32)]
        copies += 2
    if prepare is not None:
        out_shapes += [
            jax.ShapeDtypeStruct(zeta[0].shape, jnp.float32),
            jax.ShapeDtypeStruct(prepare.shape[1:], jnp.float32),
        ]
        out_specs += [pl.BlockSpec(memory_space=pltpu.VMEM)] * 2
    return pl.pallas_call(
        functools.partial(
            exchange_kernel, tuple(routes), sizes, len(arrays) + (prepare is not None),
            zeta is not None, prepare is not None,
        ),
        out_shape=out_shapes,
        in_specs=in_specs,
        out_specs=out_specs,
        scratch_shapes=scratch + [
            pltpu.SemaphoreType.DMA((copies,)),
            pltpu.SemaphoreType.DMA((copies,)),
        ],
        compiler_params=pltpu.CompilerParams(collective_id=tag, has_side_effects=True),
    )(*operands)


def offset_along(axis, step):
    return tuple(step if name == axis else 0 for name in AXES)


def window(ndim, dim, start, stop):
    return tuple(slice(start, stop) if axis == dim else slice(None) for axis in range(ndim))


def exchange_faces(items, tag, zeta=None):
    arrays, routes, out_shapes = [], [], []
    for value, axis, dim in items:
        ndim, length = value.ndim, value.shape[dim]
        if dim == ndim - 1:
            both = jnp.stack(
                [
                    lax.slice_in_dim(value, length - WIDTH, length, axis=dim),
                    lax.slice_in_dim(value, 0, WIDTH, axis=dim),
                ]
            )
            both = jnp.moveaxis(both, dim + 1, 2).reshape(2, value.shape[0], WIDTH, -1)
            arrays.append((both, pl.ANY))
            out_shapes.append(jax.ShapeDtypeStruct(both.shape, both.dtype))
            source, target = len(arrays) - 1, len(out_shapes) - 1
            routes.append((offset_along(axis, 1), source, 0, target, 0))
            routes.append((offset_along(axis, -1), source, 1, target, 1))
        elif dim == ndim - 2:
            face = value.shape[:dim] + (WIDTH,) + value.shape[dim + 1 :]
            arrays.append((value, pltpu.VMEM))
            out_shapes += [jax.ShapeDtypeStruct(face, value.dtype)] * 2
            source, target = len(arrays) - 1, len(out_shapes) - 2
            whole = window(ndim, dim, None, None)
            last, first = window(ndim, dim, length - WIDTH, length), window(ndim, dim, 0, WIDTH)
            routes.append((offset_along(axis, 1), source, last, target, whole))
            routes.append((offset_along(axis, -1), source, first, target + 1, whole))
        else:
            arrays.append((value, pl.ANY))
            face = value.shape[:dim] + (WIDTH,) + value.shape[dim + 1 :]
            out_shapes += [jax.ShapeDtypeStruct(face, value.dtype)] * 2
            source, target = len(arrays) - 1, len(out_shapes) - 2
            whole = window(ndim, dim, None, None)
            last, first = window(ndim, dim, length - WIDTH, length), window(ndim, dim, 0, WIDTH)
            routes.append((offset_along(axis, 1), source, last, target, whole))
            routes.append((offset_along(axis, -1), source, first, target + 1, whole))
    received = exchange(arrays, routes, out_shapes, tag, zeta)
    padded, place = [], 0
    for value, axis, dim in items:
        if dim == value.ndim - 1:
            both = received[place].reshape((2, value.shape[0], WIDTH) + value.shape[1:dim])
            both = jnp.moveaxis(both, 2, dim + 1)
            before, after = both[0], both[1]
            place += 1
        else:
            before, after = received[place], received[place + 1]
            place += 2
        padded.append(jnp.concatenate([before, value, after], axis=dim))
    if zeta is not None:
        padded.append(received[-1])
    return padded


def exchange_primitive(conserved, matrix, tag):
    primitive = jax.ShapeDtypeStruct((4,) + conserved.shape[1:], conserved.dtype)
    length_x, length_y = primitive.shape[1], primitive.shape[2]
    every = slice(None)
    routes = [
        ((1, 0, 0), 0, (every, slice(length_x - WIDTH, length_x)), 0, every),
        ((-1, 0, 0), 0, (every, slice(0, WIDTH)), 1, every),
        ((0, 1, 0), 0, (every, every, slice(length_y - WIDTH, length_y)), 2, every),
        ((0, -1, 0), 0, (every, every, slice(0, WIDTH)), 3, every),
    ]
    face_x = (primitive.shape[0], WIDTH) + primitive.shape[2:]
    face_y = primitive.shape[:2] + (WIDTH,) + primitive.shape[3:]
    out_shapes = [jax.ShapeDtypeStruct(face, primitive.dtype) for face in (face_x, face_x, face_y, face_y)]
    before_x, after_x, before_y, after_y, swept, primitive, pressure = exchange(
        [], routes, out_shapes, tag, (primitive, matrix), conserved
    )
    return (
        jnp.concatenate([before_x, primitive, after_x], axis=1),
        jnp.concatenate([before_y, primitive, after_y], axis=2),
        swept,
        primitive,
        pressure,
    )


def plane_kernel(sizes, value_ref, extended, across, send_sems, recv_sems):
    length_x, length_y = value_ref.shape[1], value_ref.shape[2]
    here = [lax.axis_index(axis) for axis in AXES]

    def device(offset):
        return tuple(
            lax.rem(here[slot] + offset[slot] + sizes[slot], sizes[slot]) for slot in range(3)
        )

    barrier = pltpu.get_barrier_semaphore()
    for offset in ((1, 0, 0), (-1, 0, 0), (0, 1, 0), (0, -1, 0)):
        pl.semaphore_signal(barrier, inc=1, device_id=device(offset), device_id_type=MESH)
    extended[:, WIDTH : WIDTH + length_x] = value_ref[...]
    pl.semaphore_wait(barrier, 4)
    along_x = [
        pltpu.make_async_remote_copy(
            src_ref=value_ref.at[:, pl.ds(length_x - WIDTH, WIDTH)],
            dst_ref=extended.at[:, pl.ds(0, WIDTH)],
            send_sem=send_sems.at[0], recv_sem=recv_sems.at[0],
            device_id=device((1, 0, 0)), device_id_type=MESH,
        ),
        pltpu.make_async_remote_copy(
            src_ref=value_ref.at[:, pl.ds(0, WIDTH)],
            dst_ref=extended.at[:, pl.ds(WIDTH + length_x, WIDTH)],
            send_sem=send_sems.at[1], recv_sem=recv_sems.at[1],
            device_id=device((-1, 0, 0)), device_id_type=MESH,
        ),
    ]
    for copy in along_x:
        copy.start()
    for copy in along_x:
        copy.wait()
    along_y = [
        pltpu.make_async_remote_copy(
            src_ref=extended.at[:, :, pl.ds(length_y - WIDTH, WIDTH)],
            dst_ref=across.at[0],
            send_sem=send_sems.at[2], recv_sem=recv_sems.at[2],
            device_id=device((0, 1, 0)), device_id_type=MESH,
        ),
        pltpu.make_async_remote_copy(
            src_ref=extended.at[:, :, pl.ds(0, WIDTH)],
            dst_ref=across.at[1],
            send_sem=send_sems.at[3], recv_sem=recv_sems.at[3],
            device_id=device((0, -1, 0)), device_id_type=MESH,
        ),
    ]
    for copy in along_y:
        copy.start()
    for copy in along_y:
        copy.wait()


def exchange_plane(value, tag):
    sizes = tuple(lax.axis_size(axis) for axis in AXES)
    fields, length_x, length_y, depth = value.shape
    extended, across = pl.pallas_call(
        functools.partial(plane_kernel, sizes),
        out_shape=[
            jax.ShapeDtypeStruct((fields, length_x + 2 * WIDTH, length_y, depth), value.dtype),
            jax.ShapeDtypeStruct((2, fields, length_x + 2 * WIDTH, WIDTH, depth), value.dtype),
        ],
        in_specs=[pl.BlockSpec(memory_space=pltpu.VMEM)],
        out_specs=[pl.BlockSpec(memory_space=pltpu.VMEM), pl.BlockSpec(memory_space=pl.ANY)],
        scratch_shapes=[pltpu.SemaphoreType.DMA((4,)), pltpu.SemaphoreType.DMA((4,))],
        compiler_params=pltpu.CompilerParams(collective_id=tag, has_side_effects=True),
    )(value)
    return jnp.concatenate([across[0], extended, across[1]], axis=2)


def exchange_plane_edges(value, tag):
    length_x, length_y = value.shape[1], value.shape[2]
    faces_y = jnp.stack(
        [
            lax.slice_in_dim(value, length_y - WIDTH, length_y, axis=2),
            lax.slice_in_dim(value, 0, WIDTH, axis=2),
        ]
    )
    last_x, first_x = slice(length_x - WIDTH, length_x), slice(0, WIDTH)
    every = slice(None)
    routes = [
        ((1, 0, 0), 0, (every, last_x), 0, 0),
        ((-1, 0, 0), 0, (every, first_x), 0, 1),
        ((0, 1, 0), 1, 0, 1, 0),
        ((0, -1, 0), 1, 1, 1, 1),
        ((1, 1, 0), 1, (0, every, last_x), 2, (0, 0)),
        ((-1, 1, 0), 1, (0, every, first_x), 2, (0, 1)),
        ((1, -1, 0), 1, (1, every, last_x), 2, (1, 0)),
        ((-1, -1, 0), 1, (1, every, first_x), 2, (1, 1)),
    ]
    fields, depth = value.shape[0], value.shape[3]
    out_shapes = [
        jax.ShapeDtypeStruct((2, fields, WIDTH, length_y, depth), value.dtype),
        jax.ShapeDtypeStruct((2, fields, length_x, WIDTH, depth), value.dtype),
        jax.ShapeDtypeStruct((2, 2, fields, WIDTH, WIDTH, depth), value.dtype),
    ]
    along_x, along_y, edges = exchange([(value, pl.ANY), (faces_y, pl.ANY)], routes, out_shapes, tag)
    sections = [
        jnp.concatenate([edges[0, 0], along_x[0], edges[1, 0]], axis=2),
        jnp.concatenate([along_y[0], value, along_y[1]], axis=2),
        jnp.concatenate([edges[0, 1], along_x[1], edges[1, 1]], axis=2),
    ]
    return jnp.concatenate(sections, axis=1)


def sweep_zeta(value, matrix, tag):
    return exchange([], [], [], tag, (value, matrix))[-1]


def with_halo(value, sides, width):
    for axis, dim in sides:
        count, length = (lax.axis_size(axis), value.shape[dim])
        up = [(i, (i + 1) % count) for i in range(count)]
        down = [(j, i) for i, j in up]
        last = lax.slice_in_dim(value, length - width, length, axis=dim)
        initial = lax.slice_in_dim(value, 0, width, axis=dim)
        before = lax.ppermute(last, axis, up)
        after = lax.ppermute(initial, axis, down)
        value = jnp.concatenate([before, value, after], axis=dim)
    return value


def banded_solve(system, source):
    extent = system.shape[0]
    lower = np.zeros(extent)
    upper = np.zeros(extent)
    middle = np.array([float(system[index, index]) for index in range(extent)])
    for index in range(1, extent):
        lower[index] = system[index, index - 1]
        upper[index - 1] = system[index - 1, index]
    rights = np.array(source)
    for index in range(1, extent):
        factor = lower[index] / middle[index - 1]
        middle[index] = middle[index] - factor * upper[index - 1]
        rights[index] = rights[index] - factor * rights[index - 1]
    answer = np.zeros(rights.shape)
    answer[extent - 1] = rights[extent - 1] / middle[extent - 1]
    for index in range(extent - 2, -1, -1):
        answer[index] = (rights[index] - upper[index] * answer[index + 1]) / middle[index]
    return answer


def derivative_table(length):
    extent = length + 2 * WIDTH
    system = np.eye(extent)
    source = np.zeros((extent, extent))
    for position in range(2, extent - 2):
        system[position, position - 1] = 1.0 / 3.0
        system[position, position + 1] = 1.0 / 3.0
        source[position, position + 1] = 7.0 / 9.0
        source[position, position - 1] = -7.0 / 9.0
        source[position, position + 2] = 1.0 / 36.0
        source[position, position - 2] = -1.0 / 36.0
    source[1, 2] = 0.5
    source[1, 0] = -0.5
    source[extent - 2, extent - 1] = 0.5
    source[extent - 2, extent - 3] = -0.5
    source[0, 1] = 1.0
    source[0, 0] = -1.0
    source[extent - 1, extent - 1] = 1.0
    source[extent - 1, extent - 2] = -1.0
    return banded_solve(system, source)[WIDTH : WIDTH + length]


def filter_table(length):
    strength = 0.4
    coeffs = [
        (193.0 + 126.0 * strength) / 256.0,
        (105.0 + 302.0 * strength) / 256.0,
        15.0 * (2.0 * strength - 1.0) / 64.0,
        45.0 * (1.0 - 2.0 * strength) / 512.0,
        5.0 * (2.0 * strength - 1.0) / 256.0,
        (1.0 - 2.0 * strength) / 512.0,
    ]
    extent = length + 2 * WIDTH
    system = np.eye(extent)
    source = np.eye(extent)
    for position in range(5, extent - 5):
        system[position, position - 1] = strength
        system[position, position + 1] = strength
        source[position, position] = coeffs[0]
        for offset in range(1, 6):
            source[position, position + offset] = coeffs[offset] / 2.0
            source[position, position - offset] = coeffs[offset] / 2.0
    return banded_solve(system, source)[WIDTH : WIDTH + length]


def sweep_lines(padded, matrix, dim):
    return jnp.einsum(line_forms[dim], matrix, padded, precision=lax.Precision.HIGHEST)


def faces_xi(values):
    return with_halo(values, (("xi", 1),), WIDTH)


def faces_eta(values):
    return with_halo(values, (("eta", 2),), WIDTH)


def faces_zeta(values):
    return with_halo(values, (("zeta", 3),), WIDTH)


def basic_quantities(conserved_solution):
    density = conserved_solution[0]
    fluid_speed_vector = conserved_solution[1:4] / density
    thermodynamic_stress_scalar = 0.4 * (
        conserved_solution[4] - 0.5 * jnp.sum(conserved_solution[1:4] * fluid_speed_vector, axis=0)
    )
    return (fluid_speed_vector, thermodynamic_stress_scalar, thermodynamic_stress_scalar / density)


def fluxes(
    conserved_solution, fluid_speed_vector, thermodynamic_stress_scalar, slopes, metrics, jacobian
):
    physical = [
        [
            jacobian
            * (
                metrics[0, column] * slopes[0][member]
                + metrics[1, column] * slopes[1][member]
                + metrics[2, column] * slopes[2][member]
            )
            for column in range(3)
        ]
        for member in range(4)
    ]
    spread = physical[0][0] + physical[1][1] + physical[2][2]
    totals = []
    for column in range(3):
        stress = [
            viscosity * (physical[member][column] + physical[column][member]) for member in range(3)
        ]
        stress[column] = stress[column] - 2.0 / 3.0 * viscosity * spread
        subdomain_parts = [conserved_solution[1 + column]]
        for member in range(3):
            carried = conserved_solution[1 + member] * fluid_speed_vector[column] - stress[member]
            if member == column:
                carried = carried + thermodynamic_stress_scalar
            subdomain_parts.append(carried)
        worked = (
            fluid_speed_vector[0] * stress[0]
            + fluid_speed_vector[1] * stress[1]
            + fluid_speed_vector[2] * stress[2]
        )
        subdomain_parts.append(
            (conserved_solution[4] + thermodynamic_stress_scalar) * fluid_speed_vector[column]
            - worked
            - conduction * physical[3][column]
        )
        totals.append(jnp.stack(subdomain_parts))
    return [
        metrics[direction, 0] * totals[0]
        + metrics[direction, 1] * totals[1]
        + metrics[direction, 2] * totals[2]
        for direction in range(3)
    ]


def local(conserved_solution, metrics, jacobian):
    lengths = conserved_solution.shape[1:]
    derive = [jnp.asarray(derivative_table(length), dtype=jnp.float32) for length in lengths]
    smooth = [jnp.asarray(filter_table(length), dtype=jnp.float32) for length in lengths]
    padded = exchange_primitive(conserved_solution, derive[2], 0)
    slopes = [sweep_lines(padded[k], derive[k], k + 1) for k in range(2)] + [padded[2]]
    fluid_speed_vector, thermodynamic_stress_scalar = padded[3][0:3], padded[4]
    contra = fluxes(
        conserved_solution,
        fluid_speed_vector,
        thermodynamic_stress_scalar,
        slopes,
        metrics,
        jacobian,
    )
    padded = exchange_faces([(contra[0], "xi", 1), (contra[1], "eta", 2)], 1, (contra[2], derive[2]))
    divergence = sweep_lines(padded[0], derive[0], 1)
    divergence = divergence + sweep_lines(padded[1], derive[1], 2)
    divergence = divergence + padded[2]
    sectioned = conserved_solution - step_duration * jacobian * divergence
    result = sweep_lines(exchange_plane(sectioned, 2), smooth[0], 1)
    result = sweep_lines(result, smooth[1], 2)
    result = sweep_zeta(result, smooth[2], 4)
    return result


def solution(mesh):
    in_specs = (
        P(None, "xi", "eta", "zeta"),
        P(None, None, "xi", "eta", "zeta"),
        P("xi", "eta", "zeta"),
    )
    out_specs = P(None, "xi", "eta", "zeta")
    return jax.shard_map(local, mesh=mesh, in_specs=in_specs, out_specs=out_specs, check_vma=False)
```

```python
import functools

import jax
import jax.numpy as jnp
import numpy as np
from jax import lax
from jax.experimental import pallas as pl
from jax.experimental.pallas import tpu as pltpu
from jax.sharding import PartitionSpec as P

WIDTH = 5


viscosity = 0.15
conduction = 0.15 * 1.4 / (0.4 * 0.72)
step_duration = 0.08
line_forms = ("", "al,flyz->fayz", "al,fxlz->fxaz", "al,fxyl->fxya")
MESH = pl.DeviceIdType.MESH
AXES = ("xi", "eta", "zeta")


def primitive_state(conserved):
    density = conserved[0]
    speed = conserved[1:4] / density
    pressure = 0.4 * (conserved[4] - 0.5 * jnp.sum(conserved[1:4] * speed, axis=0))
    return speed, pressure, pressure / density


def exchange_kernel(routes, sizes, count, zeta, prepare, *refs):
    sources = list(refs[:count])
    refs = refs[count:]
    if prepare:
        conserved_ref = sources.pop()
    if zeta:
        if not prepare:
            block_ref = refs[0]
            refs = refs[1:]
        middle_ref, lower_ref, upper_ref = refs[:3]
        refs = refs[3:]
    extra = (1 if zeta else 0) + (2 if prepare else 0)
    targets = refs[: len(refs) - 2 - (3 if zeta else 0) - extra]
    refs = refs[len(targets) :]
    if zeta:
        out_ref = refs[0]
        refs = refs[1:]
    if prepare:
        made, pressure_ref = refs[:2]
        refs = refs[2:]
        sources.append(made)
        if zeta:
            block_ref = made
    if zeta:
        turned, before, after = refs[:3]
        refs = refs[3:]
    send_sems, recv_sems = refs
    here = [lax.axis_index(axis) for axis in AXES]

    def device(offset):
        return tuple(
            lax.rem(here[slot] + offset[slot] + sizes[slot], sizes[slot]) for slot in range(3)
        )

    offsets = [route[0] for route in routes] + ([(0, 0, 1), (0, 0, -1)] if zeta else [])
    partners = []
    for offset in offsets:
        for way in (offset, tuple(-step for step in offset)):
            if way not in partners:
                partners.append(way)
    barrier = pltpu.get_barrier_semaphore()
    for offset in partners:
        pl.semaphore_signal(barrier, inc=1, device_id=device(offset), device_id_type=MESH)
    if prepare:
        speed, pressure, temperature = primitive_state(conserved_ref[...])
        made[0:3] = speed
        made[3] = temperature
        pressure_ref[...] = pressure
    if zeta:
        fields, length_x, length_y, depth = block_ref.shape
        rows = fields * length_x * length_y
        turned[...] = block_ref[...].reshape(rows, depth).T
    pl.semaphore_wait(barrier, len(partners))
    copies = []
    for index, (offset, source, source_at, target, target_at) in enumerate(routes):
        copies.append(
            pltpu.make_async_remote_copy(
                src_ref=sources[source].at[source_at],
                dst_ref=targets[target].at[target_at],
                send_sem=send_sems.at[index],
                recv_sem=recv_sems.at[index],
                device_id=device(offset),
                device_id_type=MESH,
            )
        )
    if zeta:
        for index, (rows_at, landing, offset) in enumerate(
            ((pl.ds(depth - 8, 8), before, (0, 0, 1)), (pl.ds(0, 8), after, (0, 0, -1)))
        ):
            copies.append(
                pltpu.make_async_remote_copy(
                    src_ref=turned.at[rows_at],
                    dst_ref=landing,
                    send_sem=send_sems.at[len(routes) + index],
                    recv_sem=recv_sems.at[len(routes) + index],
                    device_id=device(offset),
                    device_id_type=MESH,
                )
            )
    for copy in copies:
        copy.start()
    if zeta:
        total = jnp.dot(middle_ref[...], turned[...], precision=lax.Precision.HIGHEST,
                        preferred_element_type=jnp.float32)
    for copy in copies:
        copy.wait()
    if zeta:
        total = total + jnp.dot(lower_ref[...], before[...], precision=lax.Precision.HIGHEST,
                                preferred_element_type=jnp.float32)
        total = total + jnp.dot(upper_ref[...], after[...], precision=lax.Precision.HIGHEST,
                                preferred_element_type=jnp.float32)
        out_ref[...] = total.T.reshape(fields, length_x, length_y, depth)


def exchange(arrays, routes, out_shapes, tag, zeta=None, prepare=None):
    sizes = tuple(lax.axis_size(axis) for axis in AXES)
    operands = [array for array, _ in arrays]
    in_specs = [pl.BlockSpec(memory_space=space) for _, space in arrays]
    out_specs = [pl.BlockSpec(memory_space=pl.ANY)] * len(out_shapes)
    out_shapes = list(out_shapes)
    scratch = []
    copies = len(routes)
    if prepare is not None:
        operands.append(prepare)
        in_specs.append(pl.BlockSpec(memory_space=pltpu.VMEM))
    if zeta is not None:
        value, matrix = zeta
        fields, length_x, length_y, depth = value.shape
        rows = fields * length_x * length_y
        padding = jnp.zeros((depth, 8 - WIDTH), matrix.dtype)
        if prepare is None:
            operands.append(value)
            in_specs.append(pl.BlockSpec(memory_space=pltpu.VMEM))
        operands += [
            matrix[:, WIDTH : WIDTH + depth],
            jnp.concatenate([padding, matrix[:, :WIDTH]], axis=1),
            jnp.concatenate([matrix[:, WIDTH + depth :], padding], axis=1),
        ]
        in_specs += [pl.BlockSpec(memory_space=pltpu.VMEM)] * 3
        out_shapes.append(jax.ShapeDtypeStruct(value.shape, value.dtype))
        out_specs.append(pl.BlockSpec(memory_space=pltpu.VMEM))
        scratch = [pltpu.VMEM((depth, rows), jnp.float32), pltpu.VMEM((8, rows), jnp.float32),
                   pltpu.VMEM((8, rows), jnp.float32)]
        copies += 2
    if prepare is not None:
        out_shapes += [
            jax.ShapeDtypeStruct(zeta[0].shape, jnp.float32),
            jax.ShapeDtypeStruct(prepare.shape[1:], jnp.float32),
        ]
        out_specs += [pl.BlockSpec(memory_space=pltpu.VMEM)] * 2
    return pl.pallas_call(
        functools.partial(
            exchange_kernel, tuple(routes), sizes, len(arrays) + (prepare is not None),
            zeta is not None, prepare is not None,
        ),
        out_shape=out_shapes,
        in_specs=in_specs,
        out_specs=out_specs,
        scratch_shapes=scratch + [
            pltpu.SemaphoreType.DMA((copies,)),
            pltpu.SemaphoreType.DMA((copies,)),
        ],
        compiler_params=pltpu.CompilerParams(collective_id=tag, has_side_effects=True),
    )(*operands)


def offset_along(axis, step):
    return tuple(step if name == axis else 0 for name in AXES)


def window(ndim, dim, start, stop):
    return tuple(slice(start, stop) if axis == dim else slice(None) for axis in range(ndim))


def exchange_faces(items, tag, zeta=None):
    arrays, routes, out_shapes = [], [], []
    for value, axis, dim in items:
        ndim, length = value.ndim, value.shape[dim]
        if dim == ndim - 1:
            both = jnp.stack(
                [
                    lax.slice_in_dim(value, length - WIDTH, length, axis=dim),
                    lax.slice_in_dim(value, 0, WIDTH, axis=dim),
                ]
            )
            both = jnp.moveaxis(both, dim + 1, 2).reshape(2, value.shape[0], WIDTH, -1)
            arrays.append((both, pl.ANY))
            out_shapes.append(jax.ShapeDtypeStruct(both.shape, both.dtype))
            source, target = len(arrays) - 1, len(out_shapes) - 1
            routes.append((offset_along(axis, 1), source, 0, target, 0))
            routes.append((offset_along(axis, -1), source, 1, target, 1))
        elif dim == ndim - 2:
            face = value.shape[:dim] + (WIDTH,) + value.shape[dim + 1 :]
            arrays.append((value, pltpu.VMEM))
            out_shapes += [jax.ShapeDtypeStruct(face, value.dtype)] * 2
            source, target = len(arrays) - 1, len(out_shapes) - 2
            whole = window(ndim, dim, None, None)
            last, first = window(ndim, dim, length - WIDTH, length), window(ndim, dim, 0, WIDTH)
            routes.append((offset_along(axis, 1), source, last, target, whole))
            routes.append((offset_along(axis, -1), source, first, target + 1, whole))
        else:
            arrays.append((value, pl.ANY))
            face = value.shape[:dim] + (WIDTH,) + value.shape[dim + 1 :]
            out_shapes += [jax.ShapeDtypeStruct(face, value.dtype)] * 2
            source, target = len(arrays) - 1, len(out_shapes) - 2
            whole = window(ndim, dim, None, None)
            last, first = window(ndim, dim, length - WIDTH, length), window(ndim, dim, 0, WIDTH)
            routes.append((offset_along(axis, 1), source, last, target, whole))
            routes.append((offset_along(axis, -1), source, first, target + 1, whole))
    received = exchange(arrays, routes, out_shapes, tag, zeta)
    padded, place = [], 0
    for value, axis, dim in items:
        if dim == value.ndim - 1:
            both = received[place].reshape((2, value.shape[0], WIDTH) + value.shape[1:dim])
            both = jnp.moveaxis(both, 2, dim + 1)
            before, after = both[0], both[1]
            place += 1
        else:
            before, after = received[place], received[place + 1]
            place += 2
        padded.append(jnp.concatenate([before, value, after], axis=dim))
    if zeta is not None:
        padded.append(received[-1])
    return padded


def exchange_primitive(conserved, matrix, tag):
    primitive = jax.ShapeDtypeStruct((4,) + conserved.shape[1:], conserved.dtype)
    length_x, length_y = primitive.shape[1], primitive.shape[2]
    every = slice(None)
    routes = [
        ((1, 0, 0), 0, (every, slice(length_x - WIDTH, length_x)), 0, every),
        ((-1, 0, 0), 0, (every, slice(0, WIDTH)), 1, every),
        ((0, 1, 0), 0, (every, every, slice(length_y - WIDTH, length_y)), 2, every),
        ((0, -1, 0), 0, (every, every, slice(0, WIDTH)), 3, every),
    ]
    face_x = (primitive.shape[0], WIDTH) + primitive.shape[2:]
    face_y = primitive.shape[:2] + (WIDTH,) + primitive.shape[3:]
    out_shapes = [jax.ShapeDtypeStruct(face, primitive.dtype) for face in (face_x, face_x, face_y, face_y)]
    before_x, after_x, before_y, after_y, swept, primitive, pressure = exchange(
        [], routes, out_shapes, tag, (primitive, matrix), conserved
    )
    return (
        jnp.concatenate([before_x, primitive, after_x], axis=1),
        jnp.concatenate([before_y, primitive, after_y], axis=2),
        swept,
        primitive,
        pressure,
    )


def exchange_plane(value, tag):
    length_x, length_y = value.shape[1], value.shape[2]
    faces_y = jnp.stack(
        [
            lax.slice_in_dim(value, length_y - WIDTH, length_y, axis=2),
            lax.slice_in_dim(value, 0, WIDTH, axis=2),
        ]
    )
    last_x, first_x = slice(length_x - WIDTH, length_x), slice(0, WIDTH)
    every = slice(None)
    routes = [
        ((1, 0, 0), 0, (every, last_x), 0, 0),
        ((-1, 0, 0), 0, (every, first_x), 0, 1),
        ((0, 1, 0), 1, 0, 1, 0),
        ((0, -1, 0), 1, 1, 1, 1),
        ((1, 1, 0), 1, (0, every, last_x), 2, (0, 0)),
        ((-1, 1, 0), 1, (0, every, first_x), 2, (0, 1)),
        ((1, -1, 0), 1, (1, every, last_x), 2, (1, 0)),
        ((-1, -1, 0), 1, (1, every, first_x), 2, (1, 1)),
    ]
    fields, depth = value.shape[0], value.shape[3]
    out_shapes = [
        jax.ShapeDtypeStruct((2, fields, WIDTH, length_y, depth), value.dtype),
        jax.ShapeDtypeStruct((2, fields, length_x, WIDTH, depth), value.dtype),
        jax.ShapeDtypeStruct((2, 2, fields, WIDTH, WIDTH, depth), value.dtype),
    ]
    along_x, along_y, edges = exchange([(value, pl.ANY), (faces_y, pl.ANY)], routes, out_shapes, tag)
    sections = [
        jnp.concatenate([edges[0, 0], along_x[0], edges[1, 0]], axis=2),
        jnp.concatenate([along_y[0], value, along_y[1]], axis=2),
        jnp.concatenate([edges[0, 1], along_x[1], edges[1, 1]], axis=2),
    ]
    return jnp.concatenate(sections, axis=1)


def sweep_zeta(value, matrix, tag):
    return exchange([], [], [], tag, (value, matrix))[-1]


def with_halo(value, sides, width):
    for axis, dim in sides:
        count, length = (lax.axis_size(axis), value.shape[dim])
        up = [(i, (i + 1) % count) for i in range(count)]
        down = [(j, i) for i, j in up]
        last = lax.slice_in_dim(value, length - width, length, axis=dim)
        initial = lax.slice_in_dim(value, 0, width, axis=dim)
        before = lax.ppermute(last, axis, up)
        after = lax.ppermute(initial, axis, down)
        value = jnp.concatenate([before, value, after], axis=dim)
    return value


def banded_solve(system, source):
    extent = system.shape[0]
    lower = np.zeros(extent)
    upper = np.zeros(extent)
    middle = np.array([float(system[index, index]) for index in range(extent)])
    for index in range(1, extent):
        lower[index] = system[index, index - 1]
        upper[index - 1] = system[index - 1, index]
    rights = np.array(source)
    for index in range(1, extent):
        factor = lower[index] / middle[index - 1]
        middle[index] = middle[index] - factor * upper[index - 1]
        rights[index] = rights[index] - factor * rights[index - 1]
    answer = np.zeros(rights.shape)
    answer[extent - 1] = rights[extent - 1] / middle[extent - 1]
    for index in range(extent - 2, -1, -1):
        answer[index] = (rights[index] - upper[index] * answer[index + 1]) / middle[index]
    return answer


def derivative_table(length):
    extent = length + 2 * WIDTH
    system = np.eye(extent)
    source = np.zeros((extent, extent))
    for position in range(2, extent - 2):
        system[position, position - 1] = 1.0 / 3.0
        system[position, position + 1] = 1.0 / 3.0
        source[position, position + 1] = 7.0 / 9.0
        source[position, position - 1] = -7.0 / 9.0
        source[position, position + 2] = 1.0 / 36.0
        source[position, position - 2] = -1.0 / 36.0
    source[1, 2] = 0.5
    source[1, 0] = -0.5
    source[extent - 2, extent - 1] = 0.5
    source[extent - 2, extent - 3] = -0.5
    source[0, 1] = 1.0
    source[0, 0] = -1.0
    source[extent - 1, extent - 1] = 1.0
    source[extent - 1, extent - 2] = -1.0
    return banded_solve(system, source)[WIDTH : WIDTH + length]


def filter_table(length):
    strength = 0.4
    coeffs = [
        (193.0 + 126.0 * strength) / 256.0,
        (105.0 + 302.0 * strength) / 256.0,
        15.0 * (2.0 * strength - 1.0) / 64.0,
        45.0 * (1.0 - 2.0 * strength) / 512.0,
        5.0 * (2.0 * strength - 1.0) / 256.0,
        (1.0 - 2.0 * strength) / 512.0,
    ]
    extent = length + 2 * WIDTH
    system = np.eye(extent)
    source = np.eye(extent)
    for position in range(5, extent - 5):
        system[position, position - 1] = strength
        system[position, position + 1] = strength
        source[position, position] = coeffs[0]
        for offset in range(1, 6):
            source[position, position + offset] = coeffs[offset] / 2.0
            source[position, position - offset] = coeffs[offset] / 2.0
    return banded_solve(system, source)[WIDTH : WIDTH + length]


def sweep_lines(padded, matrix, dim):
    return jnp.einsum(line_forms[dim], matrix, padded, precision=lax.Precision.HIGHEST)


def faces_xi(values):
    return with_halo(values, (("xi", 1),), WIDTH)


def faces_eta(values):
    return with_halo(values, (("eta", 2),), WIDTH)


def faces_zeta(values):
    return with_halo(values, (("zeta", 3),), WIDTH)


def basic_quantities(conserved_solution):
    density = conserved_solution[0]
    fluid_speed_vector = conserved_solution[1:4] / density
    thermodynamic_stress_scalar = 0.4 * (
        conserved_solution[4] - 0.5 * jnp.sum(conserved_solution[1:4] * fluid_speed_vector, axis=0)
    )
    return (fluid_speed_vector, thermodynamic_stress_scalar, thermodynamic_stress_scalar / density)


def fluxes(
    conserved_solution, fluid_speed_vector, thermodynamic_stress_scalar, slopes, metrics, jacobian
):
    physical = [
        [
            jacobian
            * (
                metrics[0, column] * slopes[0][member]
                + metrics[1, column] * slopes[1][member]
                + metrics[2, column] * slopes[2][member]
            )
            for column in range(3)
        ]
        for member in range(4)
    ]
    spread = physical[0][0] + physical[1][1] + physical[2][2]
    totals = []
    for column in range(3):
        stress = [
            viscosity * (physical[member][column] + physical[column][member]) for member in range(3)
        ]
        stress[column] = stress[column] - 2.0 / 3.0 * viscosity * spread
        subdomain_parts = [conserved_solution[1 + column]]
        for member in range(3):
            carried = conserved_solution[1 + member] * fluid_speed_vector[column] - stress[member]
            if member == column:
                carried = carried + thermodynamic_stress_scalar
            subdomain_parts.append(carried)
        worked = (
            fluid_speed_vector[0] * stress[0]
            + fluid_speed_vector[1] * stress[1]
            + fluid_speed_vector[2] * stress[2]
        )
        subdomain_parts.append(
            (conserved_solution[4] + thermodynamic_stress_scalar) * fluid_speed_vector[column]
            - worked
            - conduction * physical[3][column]
        )
        totals.append(jnp.stack(subdomain_parts))
    return [
        metrics[direction, 0] * totals[0]
        + metrics[direction, 1] * totals[1]
        + metrics[direction, 2] * totals[2]
        for direction in range(3)
    ]


def local(conserved_solution, metrics, jacobian):
    lengths = conserved_solution.shape[1:]
    derive = [jnp.asarray(derivative_table(length), dtype=jnp.float32) for length in lengths]
    smooth = [jnp.asarray(filter_table(length), dtype=jnp.float32) for length in lengths]
    padded = exchange_primitive(conserved_solution, derive[2], 0)
    slopes = [sweep_lines(padded[k], derive[k], k + 1) for k in range(2)] + [padded[2]]
    fluid_speed_vector, thermodynamic_stress_scalar = padded[3][0:3], padded[4]
    contra = fluxes(
        conserved_solution,
        fluid_speed_vector,
        thermodynamic_stress_scalar,
        slopes,
        metrics,
        jacobian,
    )
    padded = exchange_faces([(contra[0], "xi", 1), (contra[1], "eta", 2)], 1, (contra[2], derive[2]))
    divergence = sweep_lines(padded[0], derive[0], 1)
    divergence = divergence + sweep_lines(padded[1], derive[1], 2)
    divergence = divergence + padded[2]
    sectioned = conserved_solution - step_duration * jacobian * divergence
    result = sweep_zeta(sectioned, smooth[2], 4)
    result = sweep_lines(exchange_plane(result, 2), smooth[0], 1)
    result = sweep_lines(result, smooth[1], 2)
    return result


def solution(mesh):
    in_specs = (
        P(None, "xi", "eta", "zeta"),
        P(None, None, "xi", "eta", "zeta"),
        P("xi", "eta", "zeta"),
    )
    out_specs = P(None, "xi", "eta", "zeta")
    return jax.shard_map(local, mesh=mesh, in_specs=in_specs, out_specs=out_specs, check_vma=False)
```

```python
import functools

import jax
import jax.numpy as jnp
import numpy as np
from jax import lax
from jax.experimental import pallas as pl
from jax.experimental.pallas import tpu as pltpu
from jax.sharding import PartitionSpec as P

WIDTH = 5


viscosity = 0.15
conduction = 0.15 * 1.4 / (0.4 * 0.72)
step_duration = 0.08
line_forms = ("", "al,flyz->fayz", "al,fxlz->fxaz", "al,fxyl->fxya")
MESH = pl.DeviceIdType.MESH
AXES = ("xi", "eta", "zeta")


def primitive_state(conserved):
    density = conserved[0]
    speed = conserved[1:4] / density
    pressure = 0.4 * (conserved[4] - 0.5 * jnp.sum(conserved[1:4] * speed, axis=0))
    return speed, pressure, pressure / density


def exchange_kernel(routes, sizes, count, zeta, prepare, *refs):
    sources = list(refs[:count])
    refs = refs[count:]
    if prepare:
        conserved_ref = sources.pop()
    if zeta:
        if not prepare:
            block_ref = refs[0]
            refs = refs[1:]
        middle_ref, lower_ref, upper_ref = refs[:3]
        refs = refs[3:]
    extra = (1 if zeta else 0) + (2 if prepare else 0)
    targets = refs[: len(refs) - 2 - (3 if zeta else 0) - extra]
    refs = refs[len(targets) :]
    if zeta:
        out_ref = refs[0]
        refs = refs[1:]
    if prepare:
        made, pressure_ref = refs[:2]
        refs = refs[2:]
        sources.append(made)
        if zeta:
            block_ref = made
    if zeta:
        turned, before, after = refs[:3]
        refs = refs[3:]
    send_sems, recv_sems = refs
    here = [lax.axis_index(axis) for axis in AXES]

    def device(offset):
        return tuple(
            lax.rem(here[slot] + offset[slot] + sizes[slot], sizes[slot]) for slot in range(3)
        )

    offsets = [route[0] for route in routes] + ([(0, 0, 1), (0, 0, -1)] if zeta else [])
    partners = []
    for offset in offsets:
        for way in (offset, tuple(-step for step in offset)):
            if way not in partners:
                partners.append(way)
    barrier = pltpu.get_barrier_semaphore()
    for offset in partners:
        pl.semaphore_signal(barrier, inc=1, device_id=device(offset), device_id_type=MESH)
    if prepare:
        speed, pressure, temperature = primitive_state(conserved_ref[...])
        made[0:3] = speed
        made[3] = temperature
        pressure_ref[...] = pressure
    if zeta:
        fields, length_x, length_y, depth = block_ref.shape
        rows = fields * length_x * length_y
        turned[...] = block_ref[...].reshape(rows, depth).T
    pl.semaphore_wait(barrier, len(partners))
    copies = []
    for index, (offset, source, source_at, target, target_at) in enumerate(routes):
        copies.append(
            pltpu.make_async_remote_copy(
                src_ref=sources[source].at[source_at],
                dst_ref=targets[target].at[target_at],
                send_sem=send_sems.at[index],
                recv_sem=recv_sems.at[index],
                device_id=device(offset),
                device_id_type=MESH,
            )
        )
    if zeta:
        for index, (rows_at, landing, offset) in enumerate(
            ((pl.ds(depth - 8, 8), before, (0, 0, 1)), (pl.ds(0, 8), after, (0, 0, -1)))
        ):
            copies.append(
                pltpu.make_async_remote_copy(
                    src_ref=turned.at[rows_at],
                    dst_ref=landing,
                    send_sem=send_sems.at[len(routes) + index],
                    recv_sem=recv_sems.at[len(routes) + index],
                    device_id=device(offset),
                    device_id_type=MESH,
                )
            )
    for copy in copies:
        copy.start()
    if zeta:
        total = jnp.dot(middle_ref[...], turned[...], precision=lax.Precision.HIGH,
                        preferred_element_type=jnp.float32)
    for copy in copies:
        copy.wait()
    if zeta:
        total = total + jnp.dot(lower_ref[...], before[...], precision=lax.Precision.HIGH,
                                preferred_element_type=jnp.float32)
        total = total + jnp.dot(upper_ref[...], after[...], precision=lax.Precision.HIGH,
                                preferred_element_type=jnp.float32)
        out_ref[...] = total.T.reshape(fields, length_x, length_y, depth)


def exchange(arrays, routes, out_shapes, tag, zeta=None, prepare=None):
    sizes = tuple(lax.axis_size(axis) for axis in AXES)
    operands = [array for array, _ in arrays]
    in_specs = [pl.BlockSpec(memory_space=space) for _, space in arrays]
    out_specs = [pl.BlockSpec(memory_space=pl.ANY)] * len(out_shapes)
    out_shapes = list(out_shapes)
    scratch = []
    copies = len(routes)
    if prepare is not None:
        operands.append(prepare)
        in_specs.append(pl.BlockSpec(memory_space=pltpu.VMEM))
    if zeta is not None:
        value, matrix = zeta
        fields, length_x, length_y, depth = value.shape
        rows = fields * length_x * length_y
        padding = jnp.zeros((depth, 8 - WIDTH), matrix.dtype)
        if prepare is None:
            operands.append(value)
            in_specs.append(pl.BlockSpec(memory_space=pltpu.VMEM))
        operands += [
            matrix[:, WIDTH : WIDTH + depth],
            jnp.concatenate([padding, matrix[:, :WIDTH]], axis=1),
            jnp.concatenate([matrix[:, WIDTH + depth :], padding], axis=1),
        ]
        in_specs += [pl.BlockSpec(memory_space=pltpu.VMEM)] * 3
        out_shapes.append(jax.ShapeDtypeStruct(value.shape, value.dtype))
        out_specs.append(pl.BlockSpec(memory_space=pltpu.VMEM))
        scratch = [pltpu.VMEM((depth, rows), jnp.float32), pltpu.VMEM((8, rows), jnp.float32),
                   pltpu.VMEM((8, rows), jnp.float32)]
        copies += 2
    if prepare is not None:
        out_shapes += [
            jax.ShapeDtypeStruct(zeta[0].shape, jnp.float32),
            jax.ShapeDtypeStruct(prepare.shape[1:], jnp.float32),
        ]
        out_specs += [pl.BlockSpec(memory_space=pltpu.VMEM)] * 2
    return pl.pallas_call(
        functools.partial(
            exchange_kernel, tuple(routes), sizes, len(arrays) + (prepare is not None),
            zeta is not None, prepare is not None,
        ),
        out_shape=out_shapes,
        in_specs=in_specs,
        out_specs=out_specs,
        scratch_shapes=scratch + [
            pltpu.SemaphoreType.DMA((copies,)),
            pltpu.SemaphoreType.DMA((copies,)),
        ],
        compiler_params=pltpu.CompilerParams(collective_id=tag, has_side_effects=True),
    )(*operands)


def offset_along(axis, step):
    return tuple(step if name == axis else 0 for name in AXES)


def window(ndim, dim, start, stop):
    return tuple(slice(start, stop) if axis == dim else slice(None) for axis in range(ndim))


def exchange_faces(items, tag, zeta=None):
    arrays, routes, out_shapes = [], [], []
    for value, axis, dim in items:
        ndim, length = value.ndim, value.shape[dim]
        if dim == ndim - 1:
            both = jnp.stack(
                [
                    lax.slice_in_dim(value, length - WIDTH, length, axis=dim),
                    lax.slice_in_dim(value, 0, WIDTH, axis=dim),
                ]
            )
            both = jnp.moveaxis(both, dim + 1, 2).reshape(2, value.shape[0], WIDTH, -1)
            arrays.append((both, pl.ANY))
            out_shapes.append(jax.ShapeDtypeStruct(both.shape, both.dtype))
            source, target = len(arrays) - 1, len(out_shapes) - 1
            routes.append((offset_along(axis, 1), source, 0, target, 0))
            routes.append((offset_along(axis, -1), source, 1, target, 1))
        elif dim == ndim - 2:
            face = value.shape[:dim] + (WIDTH,) + value.shape[dim + 1 :]
            arrays.append((value, pltpu.VMEM))
            out_shapes += [jax.ShapeDtypeStruct(face, value.dtype)] * 2
            source, target = len(arrays) - 1, len(out_shapes) - 2
            whole = window(ndim, dim, None, None)
            last, first = window(ndim, dim, length - WIDTH, length), window(ndim, dim, 0, WIDTH)
            routes.append((offset_along(axis, 1), source, last, target, whole))
            routes.append((offset_along(axis, -1), source, first, target + 1, whole))
        else:
            arrays.append((value, pl.ANY))
            face = value.shape[:dim] + (WIDTH,) + value.shape[dim + 1 :]
            out_shapes += [jax.ShapeDtypeStruct(face, value.dtype)] * 2
            source, target = len(arrays) - 1, len(out_shapes) - 2
            whole = window(ndim, dim, None, None)
            last, first = window(ndim, dim, length - WIDTH, length), window(ndim, dim, 0, WIDTH)
            routes.append((offset_along(axis, 1), source, last, target, whole))
            routes.append((offset_along(axis, -1), source, first, target + 1, whole))
    received = exchange(arrays, routes, out_shapes, tag, zeta)
    padded, place = [], 0
    for value, axis, dim in items:
        if dim == value.ndim - 1:
            both = received[place].reshape((2, value.shape[0], WIDTH) + value.shape[1:dim])
            both = jnp.moveaxis(both, 2, dim + 1)
            before, after = both[0], both[1]
            place += 1
        else:
            before, after = received[place], received[place + 1]
            place += 2
        padded.append(jnp.concatenate([before, value, after], axis=dim))
    if zeta is not None:
        padded.append(received[-1])
    return padded


def exchange_primitive(conserved, matrix, tag):
    primitive = jax.ShapeDtypeStruct((4,) + conserved.shape[1:], conserved.dtype)
    length_x, length_y = primitive.shape[1], primitive.shape[2]
    every = slice(None)
    routes = [
        ((1, 0, 0), 0, (every, slice(length_x - WIDTH, length_x)), 0, every),
        ((-1, 0, 0), 0, (every, slice(0, WIDTH)), 1, every),
        ((0, 1, 0), 0, (every, every, slice(length_y - WIDTH, length_y)), 2, every),
        ((0, -1, 0), 0, (every, every, slice(0, WIDTH)), 3, every),
    ]
    face_x = (primitive.shape[0], WIDTH) + primitive.shape[2:]
    face_y = primitive.shape[:2] + (WIDTH,) + primitive.shape[3:]
    out_shapes = [jax.ShapeDtypeStruct(face, primitive.dtype) for face in (face_x, face_x, face_y, face_y)]
    before_x, after_x, before_y, after_y, swept, primitive, pressure = exchange(
        [], routes, out_shapes, tag, (primitive, matrix), conserved
    )
    return (
        jnp.concatenate([before_x, primitive, after_x], axis=1),
        jnp.concatenate([before_y, primitive, after_y], axis=2),
        swept,
        primitive,
        pressure,
    )


def exchange_plane(value, tag):
    length_x, length_y = value.shape[1], value.shape[2]
    faces_y = jnp.stack(
        [
            lax.slice_in_dim(value, length_y - WIDTH, length_y, axis=2),
            lax.slice_in_dim(value, 0, WIDTH, axis=2),
        ]
    )
    last_x, first_x = slice(length_x - WIDTH, length_x), slice(0, WIDTH)
    every = slice(None)
    routes = [
        ((1, 0, 0), 0, (every, last_x), 0, 0),
        ((-1, 0, 0), 0, (every, first_x), 0, 1),
        ((0, 1, 0), 1, 0, 1, 0),
        ((0, -1, 0), 1, 1, 1, 1),
        ((1, 1, 0), 1, (0, every, last_x), 2, (0, 0)),
        ((-1, 1, 0), 1, (0, every, first_x), 2, (0, 1)),
        ((1, -1, 0), 1, (1, every, last_x), 2, (1, 0)),
        ((-1, -1, 0), 1, (1, every, first_x), 2, (1, 1)),
    ]
    fields, depth = value.shape[0], value.shape[3]
    out_shapes = [
        jax.ShapeDtypeStruct((2, fields, WIDTH, length_y, depth), value.dtype),
        jax.ShapeDtypeStruct((2, fields, length_x, WIDTH, depth), value.dtype),
        jax.ShapeDtypeStruct((2, 2, fields, WIDTH, WIDTH, depth), value.dtype),
    ]
    along_x, along_y, edges = exchange([(value, pl.ANY), (faces_y, pl.ANY)], routes, out_shapes, tag)
    sections = [
        jnp.concatenate([edges[0, 0], along_x[0], edges[1, 0]], axis=2),
        jnp.concatenate([along_y[0], value, along_y[1]], axis=2),
        jnp.concatenate([edges[0, 1], along_x[1], edges[1, 1]], axis=2),
    ]
    return jnp.concatenate(sections, axis=1)


def sweep_zeta(value, matrix, tag):
    return exchange([], [], [], tag, (value, matrix))[-1]


def with_halo(value, sides, width):
    for axis, dim in sides:
        count, length = (lax.axis_size(axis), value.shape[dim])
        up = [(i, (i + 1) % count) for i in range(count)]
        down = [(j, i) for i, j in up]
        last = lax.slice_in_dim(value, length - width, length, axis=dim)
        initial = lax.slice_in_dim(value, 0, width, axis=dim)
        before = lax.ppermute(last, axis, up)
        after = lax.ppermute(initial, axis, down)
        value = jnp.concatenate([before, value, after], axis=dim)
    return value


def banded_solve(system, source):
    extent = system.shape[0]
    lower = np.zeros(extent)
    upper = np.zeros(extent)
    middle = np.array([float(system[index, index]) for index in range(extent)])
    for index in range(1, extent):
        lower[index] = system[index, index - 1]
        upper[index - 1] = system[index - 1, index]
    rights = np.array(source)
    for index in range(1, extent):
        factor = lower[index] / middle[index - 1]
        middle[index] = middle[index] - factor * upper[index - 1]
        rights[index] = rights[index] - factor * rights[index - 1]
    answer = np.zeros(rights.shape)
    answer[extent - 1] = rights[extent - 1] / middle[extent - 1]
    for index in range(extent - 2, -1, -1):
        answer[index] = (rights[index] - upper[index] * answer[index + 1]) / middle[index]
    return answer


def derivative_table(length):
    extent = length + 2 * WIDTH
    system = np.eye(extent)
    source = np.zeros((extent, extent))
    for position in range(2, extent - 2):
        system[position, position - 1] = 1.0 / 3.0
        system[position, position + 1] = 1.0 / 3.0
        source[position, position + 1] = 7.0 / 9.0
        source[position, position - 1] = -7.0 / 9.0
        source[position, position + 2] = 1.0 / 36.0
        source[position, position - 2] = -1.0 / 36.0
    source[1, 2] = 0.5
    source[1, 0] = -0.5
    source[extent - 2, extent - 1] = 0.5
    source[extent - 2, extent - 3] = -0.5
    source[0, 1] = 1.0
    source[0, 0] = -1.0
    source[extent - 1, extent - 1] = 1.0
    source[extent - 1, extent - 2] = -1.0
    return banded_solve(system, source)[WIDTH : WIDTH + length]


def filter_table(length):
    strength = 0.4
    coeffs = [
        (193.0 + 126.0 * strength) / 256.0,
        (105.0 + 302.0 * strength) / 256.0,
        15.0 * (2.0 * strength - 1.0) / 64.0,
        45.0 * (1.0 - 2.0 * strength) / 512.0,
        5.0 * (2.0 * strength - 1.0) / 256.0,
        (1.0 - 2.0 * strength) / 512.0,
    ]
    extent = length + 2 * WIDTH
    system = np.eye(extent)
    source = np.eye(extent)
    for position in range(5, extent - 5):
        system[position, position - 1] = strength
        system[position, position + 1] = strength
        source[position, position] = coeffs[0]
        for offset in range(1, 6):
            source[position, position + offset] = coeffs[offset] / 2.0
            source[position, position - offset] = coeffs[offset] / 2.0
    return banded_solve(system, source)[WIDTH : WIDTH + length]


def sweep_lines(padded, matrix, dim):
    return jnp.einsum(line_forms[dim], matrix, padded, precision=lax.Precision.HIGHEST)


def faces_xi(values):
    return with_halo(values, (("xi", 1),), WIDTH)


def faces_eta(values):
    return with_halo(values, (("eta", 2),), WIDTH)


def faces_zeta(values):
    return with_halo(values, (("zeta", 3),), WIDTH)


def basic_quantities(conserved_solution):
    density = conserved_solution[0]
    fluid_speed_vector = conserved_solution[1:4] / density
    thermodynamic_stress_scalar = 0.4 * (
        conserved_solution[4] - 0.5 * jnp.sum(conserved_solution[1:4] * fluid_speed_vector, axis=0)
    )
    return (fluid_speed_vector, thermodynamic_stress_scalar, thermodynamic_stress_scalar / density)


def fluxes(
    conserved_solution, fluid_speed_vector, thermodynamic_stress_scalar, slopes, metrics, jacobian
):
    physical = [
        [
            jacobian
            * (
                metrics[0, column] * slopes[0][member]
                + metrics[1, column] * slopes[1][member]
                + metrics[2, column] * slopes[2][member]
            )
            for column in range(3)
        ]
        for member in range(4)
    ]
    spread = physical[0][0] + physical[1][1] + physical[2][2]
    totals = []
    for column in range(3):
        stress = [
            viscosity * (physical[member][column] + physical[column][member]) for member in range(3)
        ]
        stress[column] = stress[column] - 2.0 / 3.0 * viscosity * spread
        subdomain_parts = [conserved_solution[1 + column]]
        for member in range(3):
            carried = conserved_solution[1 + member] * fluid_speed_vector[column] - stress[member]
            if member == column:
                carried = carried + thermodynamic_stress_scalar
            subdomain_parts.append(carried)
        worked = (
            fluid_speed_vector[0] * stress[0]
            + fluid_speed_vector[1] * stress[1]
            + fluid_speed_vector[2] * stress[2]
        )
        subdomain_parts.append(
            (conserved_solution[4] + thermodynamic_stress_scalar) * fluid_speed_vector[column]
            - worked
            - conduction * physical[3][column]
        )
        totals.append(jnp.stack(subdomain_parts))
    return [
        metrics[direction, 0] * totals[0]
        + metrics[direction, 1] * totals[1]
        + metrics[direction, 2] * totals[2]
        for direction in range(3)
    ]


def local(conserved_solution, metrics, jacobian):
    lengths = conserved_solution.shape[1:]
    derive = [jnp.asarray(derivative_table(length), dtype=jnp.float32) for length in lengths]
    smooth = [jnp.asarray(filter_table(length), dtype=jnp.float32) for length in lengths]
    padded = exchange_primitive(conserved_solution, derive[2], 0)
    slopes = [sweep_lines(padded[k], derive[k], k + 1) for k in range(2)] + [padded[2]]
    fluid_speed_vector, thermodynamic_stress_scalar = padded[3][0:3], padded[4]
    contra = fluxes(
        conserved_solution,
        fluid_speed_vector,
        thermodynamic_stress_scalar,
        slopes,
        metrics,
        jacobian,
    )
    padded = exchange_faces([(contra[0], "xi", 1), (contra[1], "eta", 2)], 1, (contra[2], derive[2]))
    divergence = sweep_lines(padded[0], derive[0], 1)
    divergence = divergence + sweep_lines(padded[1], derive[1], 2)
    divergence = divergence + padded[2]
    sectioned = conserved_solution - step_duration * jacobian * divergence
    result = sweep_lines(exchange_plane(sectioned, 2), smooth[0], 1)
    result = sweep_lines(result, smooth[1], 2)
    result = sweep_zeta(result, smooth[2], 4)
    return result


def solution(mesh):
    in_specs = (
        P(None, "xi", "eta", "zeta"),
        P(None, None, "xi", "eta", "zeta"),
        P("xi", "eta", "zeta"),
    )
    out_specs = P(None, "xi", "eta", "zeta")
    return jax.shard_map(local, mesh=mesh, in_specs=in_specs, out_specs=out_specs, check_vma=False)
```

```python
import functools

import jax
import jax.numpy as jnp
import numpy as np
from jax import lax
from jax.experimental import pallas as pl
from jax.experimental.pallas import tpu as pltpu
from jax.sharding import PartitionSpec as P

WIDTH = 5


viscosity = 0.15
conduction = 0.15 * 1.4 / (0.4 * 0.72)
step_duration = 0.08
line_forms = ("", "al,flyz->fayz", "al,fxlz->fxaz", "al,fxyl->fxya")
MESH = pl.DeviceIdType.MESH
AXES = ("xi", "eta", "zeta")


def primitive_state(conserved):
    density = conserved[0]
    speed = conserved[1:4] / density
    pressure = 0.4 * (conserved[4] - 0.5 * jnp.sum(conserved[1:4] * speed, axis=0))
    return speed, pressure, pressure / density


def exchange_kernel(routes, sizes, count, zeta, prepare, precision, *refs):
    sources = list(refs[:count])
    refs = refs[count:]
    if prepare:
        conserved_ref = sources.pop()
    if zeta:
        if not prepare:
            block_ref = refs[0]
            refs = refs[1:]
        middle_ref, lower_ref, upper_ref = refs[:3]
        refs = refs[3:]
    extra = (1 if zeta else 0) + (2 if prepare else 0)
    targets = refs[: len(refs) - 2 - (3 if zeta else 0) - extra]
    refs = refs[len(targets) :]
    if zeta:
        out_ref = refs[0]
        refs = refs[1:]
    if prepare:
        made, pressure_ref = refs[:2]
        refs = refs[2:]
        sources.append(made)
        if zeta:
            block_ref = made
    if zeta:
        turned, before, after = refs[:3]
        refs = refs[3:]
    send_sems, recv_sems = refs
    here = [lax.axis_index(axis) for axis in AXES]

    def device(offset):
        return tuple(
            lax.rem(here[slot] + offset[slot] + sizes[slot], sizes[slot]) for slot in range(3)
        )

    offsets = [route[0] for route in routes] + ([(0, 0, 1), (0, 0, -1)] if zeta else [])
    partners = []
    for offset in offsets:
        for way in (offset, tuple(-step for step in offset)):
            if way not in partners:
                partners.append(way)
    barrier = pltpu.get_barrier_semaphore()
    for offset in partners:
        pl.semaphore_signal(barrier, inc=1, device_id=device(offset), device_id_type=MESH)
    if prepare:
        speed, pressure, temperature = primitive_state(conserved_ref[...])
        made[0:3] = speed
        made[3] = temperature
        pressure_ref[...] = pressure
    if zeta:
        fields, length_x, length_y, depth = block_ref.shape
        rows = fields * length_x * length_y
        turned[...] = block_ref[...].reshape(rows, depth).T
    pl.semaphore_wait(barrier, len(partners))
    copies = []
    for index, (offset, source, source_at, target, target_at) in enumerate(routes):
        copies.append(
            pltpu.make_async_remote_copy(
                src_ref=sources[source].at[source_at],
                dst_ref=targets[target].at[target_at],
                send_sem=send_sems.at[index],
                recv_sem=recv_sems.at[index],
                device_id=device(offset),
                device_id_type=MESH,
            )
        )
    if zeta:
        for index, (rows_at, landing, offset) in enumerate(
            ((pl.ds(depth - 8, 8), before, (0, 0, 1)), (pl.ds(0, 8), after, (0, 0, -1)))
        ):
            copies.append(
                pltpu.make_async_remote_copy(
                    src_ref=turned.at[rows_at],
                    dst_ref=landing,
                    send_sem=send_sems.at[len(routes) + index],
                    recv_sem=recv_sems.at[len(routes) + index],
                    device_id=device(offset),
                    device_id_type=MESH,
                )
            )
    for copy in copies:
        copy.start()
    if zeta:
        total = jnp.dot(middle_ref[...], turned[...], precision=precision,
                        preferred_element_type=jnp.float32)
    for copy in copies:
        copy.wait()
    if zeta:
        total = total + jnp.dot(lower_ref[...], before[...], precision=precision,
                                preferred_element_type=jnp.float32)
        total = total + jnp.dot(upper_ref[...], after[...], precision=precision,
                                preferred_element_type=jnp.float32)
        out_ref[...] = total.T.reshape(fields, length_x, length_y, depth)


def exchange(arrays, routes, out_shapes, tag, zeta=None, prepare=None,
             precision=lax.Precision.HIGH):
    sizes = tuple(lax.axis_size(axis) for axis in AXES)
    operands = [array for array, _ in arrays]
    in_specs = [pl.BlockSpec(memory_space=space) for _, space in arrays]
    out_specs = [pl.BlockSpec(memory_space=pl.ANY)] * len(out_shapes)
    out_shapes = list(out_shapes)
    scratch = []
    copies = len(routes)
    if prepare is not None:
        operands.append(prepare)
        in_specs.append(pl.BlockSpec(memory_space=pltpu.VMEM))
    if zeta is not None:
        value, matrix = zeta
        fields, length_x, length_y, depth = value.shape
        rows = fields * length_x * length_y
        padding = jnp.zeros((depth, 8 - WIDTH), matrix.dtype)
        if prepare is None:
            operands.append(value)
            in_specs.append(pl.BlockSpec(memory_space=pltpu.VMEM))
        operands += [
            matrix[:, WIDTH : WIDTH + depth],
            jnp.concatenate([padding, matrix[:, :WIDTH]], axis=1),
            jnp.concatenate([matrix[:, WIDTH + depth :], padding], axis=1),
        ]
        in_specs += [pl.BlockSpec(memory_space=pltpu.VMEM)] * 3
        out_shapes.append(jax.ShapeDtypeStruct(value.shape, value.dtype))
        out_specs.append(pl.BlockSpec(memory_space=pltpu.VMEM))
        scratch = [pltpu.VMEM((depth, rows), jnp.float32), pltpu.VMEM((8, rows), jnp.float32),
                   pltpu.VMEM((8, rows), jnp.float32)]
        copies += 2
    if prepare is not None:
        out_shapes += [
            jax.ShapeDtypeStruct(zeta[0].shape, jnp.float32),
            jax.ShapeDtypeStruct(prepare.shape[1:], jnp.float32),
        ]
        out_specs += [pl.BlockSpec(memory_space=pltpu.VMEM)] * 2
    return pl.pallas_call(
        functools.partial(
            exchange_kernel, tuple(routes), sizes, len(arrays) + (prepare is not None),
            zeta is not None, prepare is not None, precision,
        ),
        out_shape=out_shapes,
        in_specs=in_specs,
        out_specs=out_specs,
        scratch_shapes=scratch + [
            pltpu.SemaphoreType.DMA((copies,)),
            pltpu.SemaphoreType.DMA((copies,)),
        ],
        compiler_params=pltpu.CompilerParams(collective_id=tag, has_side_effects=True),
    )(*operands)


def offset_along(axis, step):
    return tuple(step if name == axis else 0 for name in AXES)


def window(ndim, dim, start, stop):
    return tuple(slice(start, stop) if axis == dim else slice(None) for axis in range(ndim))


def exchange_faces(items, tag, zeta=None):
    arrays, routes, out_shapes = [], [], []
    for value, axis, dim in items:
        ndim, length = value.ndim, value.shape[dim]
        if dim == ndim - 1:
            both = jnp.stack(
                [
                    lax.slice_in_dim(value, length - WIDTH, length, axis=dim),
                    lax.slice_in_dim(value, 0, WIDTH, axis=dim),
                ]
            )
            both = jnp.moveaxis(both, dim + 1, 2).reshape(2, value.shape[0], WIDTH, -1)
            arrays.append((both, pl.ANY))
            out_shapes.append(jax.ShapeDtypeStruct(both.shape, both.dtype))
            source, target = len(arrays) - 1, len(out_shapes) - 1
            routes.append((offset_along(axis, 1), source, 0, target, 0))
            routes.append((offset_along(axis, -1), source, 1, target, 1))
        elif dim == ndim - 2:
            face = value.shape[:dim] + (WIDTH,) + value.shape[dim + 1 :]
            arrays.append((value, pltpu.VMEM))
            out_shapes += [jax.ShapeDtypeStruct(face, value.dtype)] * 2
            source, target = len(arrays) - 1, len(out_shapes) - 2
            whole = window(ndim, dim, None, None)
            last, first = window(ndim, dim, length - WIDTH, length), window(ndim, dim, 0, WIDTH)
            routes.append((offset_along(axis, 1), source, last, target, whole))
            routes.append((offset_along(axis, -1), source, first, target + 1, whole))
        else:
            arrays.append((value, pl.ANY))
            face = value.shape[:dim] + (WIDTH,) + value.shape[dim + 1 :]
            out_shapes += [jax.ShapeDtypeStruct(face, value.dtype)] * 2
            source, target = len(arrays) - 1, len(out_shapes) - 2
            whole = window(ndim, dim, None, None)
            last, first = window(ndim, dim, length - WIDTH, length), window(ndim, dim, 0, WIDTH)
            routes.append((offset_along(axis, 1), source, last, target, whole))
            routes.append((offset_along(axis, -1), source, first, target + 1, whole))
    received = exchange(arrays, routes, out_shapes, tag, zeta)
    padded, place = [], 0
    for value, axis, dim in items:
        if dim == value.ndim - 1:
            both = received[place].reshape((2, value.shape[0], WIDTH) + value.shape[1:dim])
            both = jnp.moveaxis(both, 2, dim + 1)
            before, after = both[0], both[1]
            place += 1
        else:
            before, after = received[place], received[place + 1]
            place += 2
        padded.append(jnp.concatenate([before, value, after], axis=dim))
    if zeta is not None:
        padded.append(received[-1])
    return padded


def exchange_primitive(conserved, matrix, tag):
    primitive = jax.ShapeDtypeStruct((4,) + conserved.shape[1:], conserved.dtype)
    length_x, length_y = primitive.shape[1], primitive.shape[2]
    every = slice(None)
    routes = [
        ((1, 0, 0), 0, (every, slice(length_x - WIDTH, length_x)), 0, every),
        ((-1, 0, 0), 0, (every, slice(0, WIDTH)), 1, every),
        ((0, 1, 0), 0, (every, every, slice(length_y - WIDTH, length_y)), 2, every),
        ((0, -1, 0), 0, (every, every, slice(0, WIDTH)), 3, every),
    ]
    face_x = (primitive.shape[0], WIDTH) + primitive.shape[2:]
    face_y = primitive.shape[:2] + (WIDTH,) + primitive.shape[3:]
    out_shapes = [jax.ShapeDtypeStruct(face, primitive.dtype) for face in (face_x, face_x, face_y, face_y)]
    before_x, after_x, before_y, after_y, swept, primitive, pressure = exchange(
        [], routes, out_shapes, tag, (primitive, matrix), conserved
    )
    return (
        jnp.concatenate([before_x, primitive, after_x], axis=1),
        jnp.concatenate([before_y, primitive, after_y], axis=2),
        swept,
        primitive,
        pressure,
    )


def exchange_plane(value, tag):
    length_x, length_y = value.shape[1], value.shape[2]
    faces_y = jnp.stack(
        [
            lax.slice_in_dim(value, length_y - WIDTH, length_y, axis=2),
            lax.slice_in_dim(value, 0, WIDTH, axis=2),
        ]
    )
    last_x, first_x = slice(length_x - WIDTH, length_x), slice(0, WIDTH)
    every = slice(None)
    routes = [
        ((1, 0, 0), 0, (every, last_x), 0, 0),
        ((-1, 0, 0), 0, (every, first_x), 0, 1),
        ((0, 1, 0), 1, 0, 1, 0),
        ((0, -1, 0), 1, 1, 1, 1),
        ((1, 1, 0), 1, (0, every, last_x), 2, (0, 0)),
        ((-1, 1, 0), 1, (0, every, first_x), 2, (0, 1)),
        ((1, -1, 0), 1, (1, every, last_x), 2, (1, 0)),
        ((-1, -1, 0), 1, (1, every, first_x), 2, (1, 1)),
    ]
    fields, depth = value.shape[0], value.shape[3]
    out_shapes = [
        jax.ShapeDtypeStruct((2, fields, WIDTH, length_y, depth), value.dtype),
        jax.ShapeDtypeStruct((2, fields, length_x, WIDTH, depth), value.dtype),
        jax.ShapeDtypeStruct((2, 2, fields, WIDTH, WIDTH, depth), value.dtype),
    ]
    along_x, along_y, edges = exchange([(value, pl.ANY), (faces_y, pl.ANY)], routes, out_shapes, tag)
    sections = [
        jnp.concatenate([edges[0, 0], along_x[0], edges[1, 0]], axis=2),
        jnp.concatenate([along_y[0], value, along_y[1]], axis=2),
        jnp.concatenate([edges[0, 1], along_x[1], edges[1, 1]], axis=2),
    ]
    return jnp.concatenate(sections, axis=1)


def sweep_zeta(value, matrix, tag):
    return exchange([], [], [], tag, (value, matrix), precision=lax.Precision.HIGHEST)[-1]


def with_halo(value, sides, width):
    for axis, dim in sides:
        count, length = (lax.axis_size(axis), value.shape[dim])
        up = [(i, (i + 1) % count) for i in range(count)]
        down = [(j, i) for i, j in up]
        last = lax.slice_in_dim(value, length - width, length, axis=dim)
        initial = lax.slice_in_dim(value, 0, width, axis=dim)
        before = lax.ppermute(last, axis, up)
        after = lax.ppermute(initial, axis, down)
        value = jnp.concatenate([before, value, after], axis=dim)
    return value


def banded_solve(system, source):
    extent = system.shape[0]
    lower = np.zeros(extent)
    upper = np.zeros(extent)
    middle = np.array([float(system[index, index]) for index in range(extent)])
    for index in range(1, extent):
        lower[index] = system[index, index - 1]
        upper[index - 1] = system[index - 1, index]
    rights = np.array(source)
    for index in range(1, extent):
        factor = lower[index] / middle[index - 1]
        middle[index] = middle[index] - factor * upper[index - 1]
        rights[index] = rights[index] - factor * rights[index - 1]
    answer = np.zeros(rights.shape)
    answer[extent - 1] = rights[extent - 1] / middle[extent - 1]
    for index in range(extent - 2, -1, -1):
        answer[index] = (rights[index] - upper[index] * answer[index + 1]) / middle[index]
    return answer


def derivative_table(length):
    extent = length + 2 * WIDTH
    system = np.eye(extent)
    source = np.zeros((extent, extent))
    for position in range(2, extent - 2):
        system[position, position - 1] = 1.0 / 3.0
        system[position, position + 1] = 1.0 / 3.0
        source[position, position + 1] = 7.0 / 9.0
        source[position, position - 1] = -7.0 / 9.0
        source[position, position + 2] = 1.0 / 36.0
        source[position, position - 2] = -1.0 / 36.0
    source[1, 2] = 0.5
    source[1, 0] = -0.5
    source[extent - 2, extent - 1] = 0.5
    source[extent - 2, extent - 3] = -0.5
    source[0, 1] = 1.0
    source[0, 0] = -1.0
    source[extent - 1, extent - 1] = 1.0
    source[extent - 1, extent - 2] = -1.0
    return banded_solve(system, source)[WIDTH : WIDTH + length]


def filter_table(length):
    strength = 0.4
    coeffs = [
        (193.0 + 126.0 * strength) / 256.0,
        (105.0 + 302.0 * strength) / 256.0,
        15.0 * (2.0 * strength - 1.0) / 64.0,
        45.0 * (1.0 - 2.0 * strength) / 512.0,
        5.0 * (2.0 * strength - 1.0) / 256.0,
        (1.0 - 2.0 * strength) / 512.0,
    ]
    extent = length + 2 * WIDTH
    system = np.eye(extent)
    source = np.eye(extent)
    for position in range(5, extent - 5):
        system[position, position - 1] = strength
        system[position, position + 1] = strength
        source[position, position] = coeffs[0]
        for offset in range(1, 6):
            source[position, position + offset] = coeffs[offset] / 2.0
            source[position, position - offset] = coeffs[offset] / 2.0
    return banded_solve(system, source)[WIDTH : WIDTH + length]


def sweep_lines(padded, matrix, dim):
    return jnp.einsum(line_forms[dim], matrix, padded, precision=lax.Precision.HIGHEST)


def faces_xi(values):
    return with_halo(values, (("xi", 1),), WIDTH)


def faces_eta(values):
    return with_halo(values, (("eta", 2),), WIDTH)


def faces_zeta(values):
    return with_halo(values, (("zeta", 3),), WIDTH)


def basic_quantities(conserved_solution):
    density = conserved_solution[0]
    fluid_speed_vector = conserved_solution[1:4] / density
    thermodynamic_stress_scalar = 0.4 * (
        conserved_solution[4] - 0.5 * jnp.sum(conserved_solution[1:4] * fluid_speed_vector, axis=0)
    )
    return (fluid_speed_vector, thermodynamic_stress_scalar, thermodynamic_stress_scalar / density)


def fluxes(
    conserved_solution, fluid_speed_vector, thermodynamic_stress_scalar, slopes, metrics, jacobian
):
    physical = [
        [
            jacobian
            * (
                metrics[0, column] * slopes[0][member]
                + metrics[1, column] * slopes[1][member]
                + metrics[2, column] * slopes[2][member]
            )
            for column in range(3)
        ]
        for member in range(4)
    ]
    spread = physical[0][0] + physical[1][1] + physical[2][2]
    totals = []
    for column in range(3):
        stress = [
            viscosity * (physical[member][column] + physical[column][member]) for member in range(3)
        ]
        stress[column] = stress[column] - 2.0 / 3.0 * viscosity * spread
        subdomain_parts = [conserved_solution[1 + column]]
        for member in range(3):
            carried = conserved_solution[1 + member] * fluid_speed_vector[column] - stress[member]
            if member == column:
                carried = carried + thermodynamic_stress_scalar
            subdomain_parts.append(carried)
        worked = (
            fluid_speed_vector[0] * stress[0]
            + fluid_speed_vector[1] * stress[1]
            + fluid_speed_vector[2] * stress[2]
        )
        subdomain_parts.append(
            (conserved_solution[4] + thermodynamic_stress_scalar) * fluid_speed_vector[column]
            - worked
            - conduction * physical[3][column]
        )
        totals.append(jnp.stack(subdomain_parts))
    return [
        metrics[direction, 0] * totals[0]
        + metrics[direction, 1] * totals[1]
        + metrics[direction, 2] * totals[2]
        for direction in range(3)
    ]


def local(conserved_solution, metrics, jacobian):
    lengths = conserved_solution.shape[1:]
    derive = [jnp.asarray(derivative_table(length), dtype=jnp.float32) for length in lengths]
    smooth = [jnp.asarray(filter_table(length), dtype=jnp.float32) for length in lengths]
    padded = exchange_primitive(conserved_solution, derive[2], 0)
    slopes = [sweep_lines(padded[k], derive[k], k + 1) for k in range(2)] + [padded[2]]
    fluid_speed_vector, thermodynamic_stress_scalar = padded[3][0:3], padded[4]
    contra = fluxes(
        conserved_solution,
        fluid_speed_vector,
        thermodynamic_stress_scalar,
        slopes,
        metrics,
        jacobian,
    )
    padded = exchange_faces([(contra[0], "xi", 1), (contra[1], "eta", 2)], 1, (contra[2], derive[2]))
    divergence = sweep_lines(padded[0], derive[0], 1)
    divergence = divergence + sweep_lines(padded[1], derive[1], 2)
    divergence = divergence + padded[2]
    sectioned = conserved_solution - step_duration * jacobian * divergence
    result = sweep_lines(exchange_plane(sectioned, 2), smooth[0], 1)
    result = sweep_lines(result, smooth[1], 2)
    result = sweep_zeta(result, smooth[2], 4)
    return result


def solution(mesh):
    in_specs = (
        P(None, "xi", "eta", "zeta"),
        P(None, None, "xi", "eta", "zeta"),
        P("xi", "eta", "zeta"),
    )
    out_specs = P(None, "xi", "eta", "zeta")
    return jax.shard_map(local, mesh=mesh, in_specs=in_specs, out_specs=out_specs, check_vma=False)
```

```python
import functools

import jax
import jax.numpy as jnp
import numpy as np
from jax import lax
from jax.experimental import pallas as pl
from jax.experimental.pallas import tpu as pltpu
from jax.sharding import PartitionSpec as P

WIDTH = 5


viscosity = 0.15
conduction = 0.15 * 1.4 / (0.4 * 0.72)
step_duration = 0.08
line_forms = ("", "al,flyz->fayz", "al,fxlz->fxaz", "al,fxyl->fxya")
MESH = pl.DeviceIdType.MESH
AXES = ("xi", "eta", "zeta")


def primitive_state(conserved):
    density = conserved[0]
    speed = conserved[1:4] / density
    pressure = 0.4 * (conserved[4] - 0.5 * jnp.sum(conserved[1:4] * speed, axis=0))
    return speed, pressure, pressure / density


def exchange_kernel(routes, sizes, count, zeta, prepare, precision, *refs):
    sources = list(refs[:count])
    refs = refs[count:]
    if prepare:
        conserved_ref = sources.pop()
    if zeta:
        if not prepare:
            block_ref = refs[0]
            refs = refs[1:]
        middle_ref, lower_ref, upper_ref = refs[:3]
        refs = refs[3:]
    extra = (1 if zeta else 0) + (2 if prepare else 0)
    targets = refs[: len(refs) - 2 - (3 if zeta else 0) - extra]
    refs = refs[len(targets) :]
    if zeta:
        out_ref = refs[0]
        refs = refs[1:]
    if prepare:
        made, pressure_ref = refs[:2]
        refs = refs[2:]
        sources.append(made)
        if zeta:
            block_ref = made
    if zeta:
        turned, before, after = refs[:3]
        refs = refs[3:]
    send_sems, recv_sems = refs
    here = [lax.axis_index(axis) for axis in AXES]

    def device(offset):
        return tuple(
            lax.rem(here[slot] + offset[slot] + sizes[slot], sizes[slot]) for slot in range(3)
        )

    offsets = [route[0] for route in routes] + ([(0, 0, 1), (0, 0, -1)] if zeta else [])
    partners = []
    for offset in offsets:
        for way in (offset, tuple(-step for step in offset)):
            if way not in partners:
                partners.append(way)
    barrier = pltpu.get_barrier_semaphore()
    for offset in partners:
        pl.semaphore_signal(barrier, inc=1, device_id=device(offset), device_id_type=MESH)
    if prepare:
        speed, pressure, temperature = primitive_state(conserved_ref[...])
        made[0:3] = speed
        made[3] = temperature
        pressure_ref[...] = pressure
    if zeta:
        fields, length_x, length_y, depth = block_ref.shape
        rows = fields * length_x * length_y
        turned[...] = block_ref[...].reshape(rows, depth).T
    pl.semaphore_wait(barrier, len(partners))
    copies = []
    for index, (offset, source, source_at, target, target_at) in enumerate(routes):
        copies.append(
            pltpu.make_async_remote_copy(
                src_ref=sources[source].at[source_at],
                dst_ref=targets[target].at[target_at],
                send_sem=send_sems.at[index],
                recv_sem=recv_sems.at[index],
                device_id=device(offset),
                device_id_type=MESH,
            )
        )
    if zeta:
        for index, (rows_at, landing, offset) in enumerate(
            ((pl.ds(depth - 8, 8), before, (0, 0, 1)), (pl.ds(0, 8), after, (0, 0, -1)))
        ):
            copies.append(
                pltpu.make_async_remote_copy(
                    src_ref=turned.at[rows_at],
                    dst_ref=landing,
                    send_sem=send_sems.at[len(routes) + index],
                    recv_sem=recv_sems.at[len(routes) + index],
                    device_id=device(offset),
                    device_id_type=MESH,
                )
            )
    for copy in copies:
        copy.start()
    if zeta:
        total = jnp.dot(middle_ref[...], turned[...], precision=precision,
                        preferred_element_type=jnp.float32)
    for copy in copies:
        copy.wait()
    if zeta:
        total = total + jnp.dot(lower_ref[...], before[...], precision=precision,
                                preferred_element_type=jnp.float32)
        total = total + jnp.dot(upper_ref[...], after[...], precision=precision,
                                preferred_element_type=jnp.float32)
        out_ref[...] = total.T.reshape(fields, length_x, length_y, depth)


def exchange(arrays, routes, out_shapes, tag, zeta=None, prepare=None,
             precision=lax.Precision.HIGH):
    sizes = tuple(lax.axis_size(axis) for axis in AXES)
    operands = [array for array, _ in arrays]
    in_specs = [pl.BlockSpec(memory_space=space) for _, space in arrays]
    out_specs = [pl.BlockSpec(memory_space=pl.ANY)] * len(out_shapes)
    out_shapes = list(out_shapes)
    scratch = []
    copies = len(routes)
    if prepare is not None:
        operands.append(prepare)
        in_specs.append(pl.BlockSpec(memory_space=pltpu.VMEM))
    if zeta is not None:
        value, matrix = zeta
        fields, length_x, length_y, depth = value.shape
        rows = fields * length_x * length_y
        padding = jnp.zeros((depth, 8 - WIDTH), matrix.dtype)
        if prepare is None:
            operands.append(value)
            in_specs.append(pl.BlockSpec(memory_space=pltpu.VMEM))
        operands += [
            matrix[:, WIDTH : WIDTH + depth],
            jnp.concatenate([padding, matrix[:, :WIDTH]], axis=1),
            jnp.concatenate([matrix[:, WIDTH + depth :], padding], axis=1),
        ]
        in_specs += [pl.BlockSpec(memory_space=pltpu.VMEM)] * 3
        out_shapes.append(jax.ShapeDtypeStruct(value.shape, value.dtype))
        out_specs.append(pl.BlockSpec(memory_space=pltpu.VMEM))
        scratch = [pltpu.VMEM((depth, rows), jnp.float32), pltpu.VMEM((8, rows), jnp.float32),
                   pltpu.VMEM((8, rows), jnp.float32)]
        copies += 2
    if prepare is not None:
        out_shapes += [
            jax.ShapeDtypeStruct(zeta[0].shape, jnp.float32),
            jax.ShapeDtypeStruct(prepare.shape[1:], jnp.float32),
        ]
        out_specs += [pl.BlockSpec(memory_space=pltpu.VMEM)] * 2
    return pl.pallas_call(
        functools.partial(
            exchange_kernel, tuple(routes), sizes, len(arrays) + (prepare is not None),
            zeta is not None, prepare is not None, precision,
        ),
        out_shape=out_shapes,
        in_specs=in_specs,
        out_specs=out_specs,
        scratch_shapes=scratch + [
            pltpu.SemaphoreType.DMA((copies,)),
            pltpu.SemaphoreType.DMA((copies,)),
        ],
        compiler_params=pltpu.CompilerParams(collective_id=tag, has_side_effects=True),
    )(*operands)


def offset_along(axis, step):
    return tuple(step if name == axis else 0 for name in AXES)


def window(ndim, dim, start, stop):
    return tuple(slice(start, stop) if axis == dim else slice(None) for axis in range(ndim))


def exchange_faces(items, tag, zeta=None):
    arrays, routes, out_shapes = [], [], []
    for value, axis, dim in items:
        ndim, length = value.ndim, value.shape[dim]
        if dim == ndim - 1:
            both = jnp.stack(
                [
                    lax.slice_in_dim(value, length - WIDTH, length, axis=dim),
                    lax.slice_in_dim(value, 0, WIDTH, axis=dim),
                ]
            )
            both = jnp.moveaxis(both, dim + 1, 2).reshape(2, value.shape[0], WIDTH, -1)
            arrays.append((both, pl.ANY))
            out_shapes.append(jax.ShapeDtypeStruct(both.shape, both.dtype))
            source, target = len(arrays) - 1, len(out_shapes) - 1
            routes.append((offset_along(axis, 1), source, 0, target, 0))
            routes.append((offset_along(axis, -1), source, 1, target, 1))
        elif dim == ndim - 2:
            face = value.shape[:dim] + (WIDTH,) + value.shape[dim + 1 :]
            arrays.append((value, pltpu.VMEM))
            out_shapes += [jax.ShapeDtypeStruct(face, value.dtype)] * 2
            source, target = len(arrays) - 1, len(out_shapes) - 2
            whole = window(ndim, dim, None, None)
            last, first = window(ndim, dim, length - WIDTH, length), window(ndim, dim, 0, WIDTH)
            routes.append((offset_along(axis, 1), source, last, target, whole))
            routes.append((offset_along(axis, -1), source, first, target + 1, whole))
        else:
            arrays.append((value, pl.ANY))
            face = value.shape[:dim] + (WIDTH,) + value.shape[dim + 1 :]
            out_shapes += [jax.ShapeDtypeStruct(face, value.dtype)] * 2
            source, target = len(arrays) - 1, len(out_shapes) - 2
            whole = window(ndim, dim, None, None)
            last, first = window(ndim, dim, length - WIDTH, length), window(ndim, dim, 0, WIDTH)
            routes.append((offset_along(axis, 1), source, last, target, whole))
            routes.append((offset_along(axis, -1), source, first, target + 1, whole))
    received = exchange(arrays, routes, out_shapes, tag, zeta)
    padded, place = [], 0
    for value, axis, dim in items:
        if dim == value.ndim - 1:
            both = received[place].reshape((2, value.shape[0], WIDTH) + value.shape[1:dim])
            both = jnp.moveaxis(both, 2, dim + 1)
            before, after = both[0], both[1]
            place += 1
        else:
            before, after = received[place], received[place + 1]
            place += 2
        padded.append(jnp.concatenate([before, value, after], axis=dim))
    if zeta is not None:
        padded.append(received[-1])
    return padded


def exchange_primitive(conserved, matrix, tag):
    primitive = jax.ShapeDtypeStruct((4,) + conserved.shape[1:], conserved.dtype)
    length_x, length_y = primitive.shape[1], primitive.shape[2]
    every = slice(None)
    routes = [
        ((1, 0, 0), 0, (every, slice(length_x - WIDTH, length_x)), 0, every),
        ((-1, 0, 0), 0, (every, slice(0, WIDTH)), 1, every),
        ((0, 1, 0), 0, (every, every, slice(length_y - WIDTH, length_y)), 2, every),
        ((0, -1, 0), 0, (every, every, slice(0, WIDTH)), 3, every),
    ]
    face_x = (primitive.shape[0], WIDTH) + primitive.shape[2:]
    face_y = primitive.shape[:2] + (WIDTH,) + primitive.shape[3:]
    out_shapes = [jax.ShapeDtypeStruct(face, primitive.dtype) for face in (face_x, face_x, face_y, face_y)]
    before_x, after_x, before_y, after_y, swept, primitive, pressure = exchange(
        [], routes, out_shapes, tag, (primitive, matrix), conserved
    )
    return (
        jnp.concatenate([before_x, primitive, after_x], axis=1),
        jnp.concatenate([before_y, primitive, after_y], axis=2),
        swept,
        primitive,
        pressure,
    )


def exchange_plane(value, tag):
    length_x, length_y = value.shape[1], value.shape[2]
    faces_y = jnp.stack(
        [
            lax.slice_in_dim(value, length_y - WIDTH, length_y, axis=2),
            lax.slice_in_dim(value, 0, WIDTH, axis=2),
        ]
    )
    last_x, first_x = slice(length_x - WIDTH, length_x), slice(0, WIDTH)
    every = slice(None)
    routes = [
        ((1, 0, 0), 0, (every, last_x), 0, 0),
        ((-1, 0, 0), 0, (every, first_x), 0, 1),
        ((0, 1, 0), 1, 0, 1, 0),
        ((0, -1, 0), 1, 1, 1, 1),
        ((1, 1, 0), 1, (0, every, last_x), 2, (0, 0)),
        ((-1, 1, 0), 1, (0, every, first_x), 2, (0, 1)),
        ((1, -1, 0), 1, (1, every, last_x), 2, (1, 0)),
        ((-1, -1, 0), 1, (1, every, first_x), 2, (1, 1)),
    ]
    fields, depth = value.shape[0], value.shape[3]
    out_shapes = [
        jax.ShapeDtypeStruct((2, fields, WIDTH, length_y, depth), value.dtype),
        jax.ShapeDtypeStruct((2, fields, length_x, WIDTH, depth), value.dtype),
        jax.ShapeDtypeStruct((2, 2, fields, WIDTH, WIDTH, depth), value.dtype),
    ]
    along_x, along_y, edges = exchange([(value, pl.ANY), (faces_y, pl.ANY)], routes, out_shapes, tag)
    sections = [
        jnp.concatenate([edges[0, 0], along_x[0], edges[1, 0]], axis=2),
        jnp.concatenate([along_y[0], value, along_y[1]], axis=2),
        jnp.concatenate([edges[0, 1], along_x[1], edges[1, 1]], axis=2),
    ]
    return jnp.concatenate(sections, axis=1)


def sweep_zeta(value, matrix, tag):
    return exchange([], [], [], tag, (value, matrix), precision=lax.Precision.HIGHEST)[-1]


def with_halo(value, sides, width):
    for axis, dim in sides:
        count, length = (lax.axis_size(axis), value.shape[dim])
        up = [(i, (i + 1) % count) for i in range(count)]
        down = [(j, i) for i, j in up]
        last = lax.slice_in_dim(value, length - width, length, axis=dim)
        initial = lax.slice_in_dim(value, 0, width, axis=dim)
        before = lax.ppermute(last, axis, up)
        after = lax.ppermute(initial, axis, down)
        value = jnp.concatenate([before, value, after], axis=dim)
    return value


def banded_solve(system, source):
    extent = system.shape[0]
    lower = np.zeros(extent)
    upper = np.zeros(extent)
    middle = np.array([float(system[index, index]) for index in range(extent)])
    for index in range(1, extent):
        lower[index] = system[index, index - 1]
        upper[index - 1] = system[index - 1, index]
    rights = np.array(source)
    for index in range(1, extent):
        factor = lower[index] / middle[index - 1]
        middle[index] = middle[index] - factor * upper[index - 1]
        rights[index] = rights[index] - factor * rights[index - 1]
    answer = np.zeros(rights.shape)
    answer[extent - 1] = rights[extent - 1] / middle[extent - 1]
    for index in range(extent - 2, -1, -1):
        answer[index] = (rights[index] - upper[index] * answer[index + 1]) / middle[index]
    return answer


def derivative_table(length):
    extent = length + 2 * WIDTH
    system = np.eye(extent)
    source = np.zeros((extent, extent))
    for position in range(2, extent - 2):
        system[position, position - 1] = 1.0 / 3.0
        system[position, position + 1] = 1.0 / 3.0
        source[position, position + 1] = 7.0 / 9.0
        source[position, position - 1] = -7.0 / 9.0
        source[position, position + 2] = 1.0 / 36.0
        source[position, position - 2] = -1.0 / 36.0
    source[1, 2] = 0.5
    source[1, 0] = -0.5
    source[extent - 2, extent - 1] = 0.5
    source[extent - 2, extent - 3] = -0.5
    source[0, 1] = 1.0
    source[0, 0] = -1.0
    source[extent - 1, extent - 1] = 1.0
    source[extent - 1, extent - 2] = -1.0
    return banded_solve(system, source)[WIDTH : WIDTH + length]


def filter_table(length):
    strength = 0.4
    coeffs = [
        (193.0 + 126.0 * strength) / 256.0,
        (105.0 + 302.0 * strength) / 256.0,
        15.0 * (2.0 * strength - 1.0) / 64.0,
        45.0 * (1.0 - 2.0 * strength) / 512.0,
        5.0 * (2.0 * strength - 1.0) / 256.0,
        (1.0 - 2.0 * strength) / 512.0,
    ]
    extent = length + 2 * WIDTH
    system = np.eye(extent)
    source = np.eye(extent)
    for position in range(5, extent - 5):
        system[position, position - 1] = strength
        system[position, position + 1] = strength
        source[position, position] = coeffs[0]
        for offset in range(1, 6):
            source[position, position + offset] = coeffs[offset] / 2.0
            source[position, position - offset] = coeffs[offset] / 2.0
    return banded_solve(system, source)[WIDTH : WIDTH + length]


def sweep_lines(padded, matrix, dim, precision=lax.Precision.HIGHEST):
    return jnp.einsum(line_forms[dim], matrix, padded, precision=precision)


def faces_xi(values):
    return with_halo(values, (("xi", 1),), WIDTH)


def faces_eta(values):
    return with_halo(values, (("eta", 2),), WIDTH)


def faces_zeta(values):
    return with_halo(values, (("zeta", 3),), WIDTH)


def basic_quantities(conserved_solution):
    density = conserved_solution[0]
    fluid_speed_vector = conserved_solution[1:4] / density
    thermodynamic_stress_scalar = 0.4 * (
        conserved_solution[4] - 0.5 * jnp.sum(conserved_solution[1:4] * fluid_speed_vector, axis=0)
    )
    return (fluid_speed_vector, thermodynamic_stress_scalar, thermodynamic_stress_scalar / density)


def fluxes(
    conserved_solution, fluid_speed_vector, thermodynamic_stress_scalar, slopes, metrics, jacobian
):
    physical = [
        [
            jacobian
            * (
                metrics[0, column] * slopes[0][member]
                + metrics[1, column] * slopes[1][member]
                + metrics[2, column] * slopes[2][member]
            )
            for column in range(3)
        ]
        for member in range(4)
    ]
    spread = physical[0][0] + physical[1][1] + physical[2][2]
    totals = []
    for column in range(3):
        stress = [
            viscosity * (physical[member][column] + physical[column][member]) for member in range(3)
        ]
        stress[column] = stress[column] - 2.0 / 3.0 * viscosity * spread
        subdomain_parts = [conserved_solution[1 + column]]
        for member in range(3):
            carried = conserved_solution[1 + member] * fluid_speed_vector[column] - stress[member]
            if member == column:
                carried = carried + thermodynamic_stress_scalar
            subdomain_parts.append(carried)
        worked = (
            fluid_speed_vector[0] * stress[0]
            + fluid_speed_vector[1] * stress[1]
            + fluid_speed_vector[2] * stress[2]
        )
        subdomain_parts.append(
            (conserved_solution[4] + thermodynamic_stress_scalar) * fluid_speed_vector[column]
            - worked
            - conduction * physical[3][column]
        )
        totals.append(jnp.stack(subdomain_parts))
    return [
        metrics[direction, 0] * totals[0]
        + metrics[direction, 1] * totals[1]
        + metrics[direction, 2] * totals[2]
        for direction in range(3)
    ]


def local(conserved_solution, metrics, jacobian):
    lengths = conserved_solution.shape[1:]
    derive = [jnp.asarray(derivative_table(length), dtype=jnp.float32) for length in lengths]
    smooth = [jnp.asarray(filter_table(length), dtype=jnp.float32) for length in lengths]
    padded = exchange_primitive(conserved_solution, derive[2], 0)
    slopes = [sweep_lines(padded[k], derive[k], k + 1, lax.Precision.HIGH) for k in range(2)]
    slopes.append(padded[2])
    fluid_speed_vector, thermodynamic_stress_scalar = padded[3][0:3], padded[4]
    contra = fluxes(
        conserved_solution,
        fluid_speed_vector,
        thermodynamic_stress_scalar,
        slopes,
        metrics,
        jacobian,
    )
    padded = exchange_faces([(contra[0], "xi", 1), (contra[1], "eta", 2)], 1, (contra[2], derive[2]))
    divergence = sweep_lines(padded[0], derive[0], 1, lax.Precision.HIGH)
    divergence = divergence + sweep_lines(padded[1], derive[1], 2, lax.Precision.HIGH)
    divergence = divergence + padded[2]
    sectioned = conserved_solution - step_duration * jacobian * divergence
    result = sweep_lines(exchange_plane(sectioned, 2), smooth[0], 1)
    result = sweep_lines(result, smooth[1], 2)
    result = sweep_zeta(result, smooth[2], 4)
    return result


def solution(mesh):
    in_specs = (
        P(None, "xi", "eta", "zeta"),
        P(None, None, "xi", "eta", "zeta"),
        P("xi", "eta", "zeta"),
    )
    out_specs = P(None, "xi", "eta", "zeta")
    return jax.shard_map(local, mesh=mesh, in_specs=in_specs, out_specs=out_specs, check_vma=False)
```

```python
import functools

import jax
import jax.numpy as jnp
import numpy as np
from jax import lax
from jax.experimental import pallas as pl
from jax.experimental.pallas import tpu as pltpu
from jax.sharding import PartitionSpec as P

WIDTH = 5


viscosity = 0.15
conduction = 0.15 * 1.4 / (0.4 * 0.72)
step_duration = 0.08
line_forms = ("", "al,flyz->fayz", "al,fxlz->fxaz", "al,fxyl->fxya")
MESH = pl.DeviceIdType.MESH
AXES = ("xi", "eta", "zeta")


def primitive_state(conserved):
    density = conserved[0]
    speed = conserved[1:4] / density
    pressure = 0.4 * (conserved[4] - 0.5 * jnp.sum(conserved[1:4] * speed, axis=0))
    return speed, pressure, pressure / density


def exchange_kernel(routes, sizes, count, zeta, prepare, precision, *refs):
    sources = list(refs[:count])
    refs = refs[count:]
    if prepare:
        conserved_ref = sources.pop()
    if zeta:
        if not prepare:
            block_ref = refs[0]
            refs = refs[1:]
        middle_ref, lower_ref, upper_ref = refs[:3]
        refs = refs[3:]
    extra = (1 if zeta else 0) + (2 if prepare else 0)
    targets = refs[: len(refs) - 2 - (3 if zeta else 0) - extra]
    refs = refs[len(targets) :]
    if zeta:
        out_ref = refs[0]
        refs = refs[1:]
    if prepare:
        made, pressure_ref = refs[:2]
        refs = refs[2:]
        sources.append(made)
        if zeta:
            block_ref = made
    if zeta:
        turned, before, after = refs[:3]
        refs = refs[3:]
    send_sems, recv_sems = refs
    here = [lax.axis_index(axis) for axis in AXES]

    def device(offset):
        return tuple(
            lax.rem(here[slot] + offset[slot] + sizes[slot], sizes[slot]) for slot in range(3)
        )

    offsets = [route[0] for route in routes] + ([(0, 0, 1), (0, 0, -1)] if zeta else [])
    partners = []
    for offset in offsets:
        for way in (offset, tuple(-step for step in offset)):
            if way not in partners:
                partners.append(way)
    barrier = pltpu.get_barrier_semaphore()
    for offset in partners:
        pl.semaphore_signal(barrier, inc=1, device_id=device(offset), device_id_type=MESH)
    if prepare:
        speed, pressure, temperature = primitive_state(conserved_ref[...])
        made[0:3] = speed
        made[3] = temperature
        pressure_ref[...] = pressure
    if zeta:
        fields, length_x, length_y, depth = block_ref.shape
        rows = fields * length_x * length_y
        turned[...] = block_ref[...].reshape(rows, depth).T
    pl.semaphore_wait(barrier, len(partners))
    copies = []
    for index, (offset, source, source_at, target, target_at) in enumerate(routes):
        copies.append(
            pltpu.make_async_remote_copy(
                src_ref=sources[source].at[source_at],
                dst_ref=targets[target].at[target_at],
                send_sem=send_sems.at[index],
                recv_sem=recv_sems.at[index],
                device_id=device(offset),
                device_id_type=MESH,
            )
        )
    if zeta:
        for index, (rows_at, landing, offset) in enumerate(
            ((pl.ds(depth - 8, 8), before, (0, 0, 1)), (pl.ds(0, 8), after, (0, 0, -1)))
        ):
            copies.append(
                pltpu.make_async_remote_copy(
                    src_ref=turned.at[rows_at],
                    dst_ref=landing,
                    send_sem=send_sems.at[len(routes) + index],
                    recv_sem=recv_sems.at[len(routes) + index],
                    device_id=device(offset),
                    device_id_type=MESH,
                )
            )
    for copy in copies:
        copy.start()
    if zeta:
        total = jnp.dot(middle_ref[...], turned[...], precision=precision,
                        preferred_element_type=jnp.float32)
    for copy in copies:
        copy.wait()
    if zeta:
        total = total + jnp.dot(lower_ref[...], before[...], precision=precision,
                                preferred_element_type=jnp.float32)
        total = total + jnp.dot(upper_ref[...], after[...], precision=precision,
                                preferred_element_type=jnp.float32)
        out_ref[...] = total.T.reshape(fields, length_x, length_y, depth)


def exchange(arrays, routes, out_shapes, tag, zeta=None, prepare=None,
             precision=lax.Precision.HIGH):
    sizes = tuple(lax.axis_size(axis) for axis in AXES)
    operands = [array for array, _ in arrays]
    in_specs = [pl.BlockSpec(memory_space=space) for _, space in arrays]
    out_specs = [pl.BlockSpec(memory_space=pl.ANY)] * len(out_shapes)
    out_shapes = list(out_shapes)
    scratch = []
    copies = len(routes)
    if prepare is not None:
        operands.append(prepare)
        in_specs.append(pl.BlockSpec(memory_space=pltpu.VMEM))
    if zeta is not None:
        value, matrix = zeta
        fields, length_x, length_y, depth = value.shape
        rows = fields * length_x * length_y
        padding = jnp.zeros((depth, 8 - WIDTH), matrix.dtype)
        if prepare is None:
            operands.append(value)
            in_specs.append(pl.BlockSpec(memory_space=pltpu.VMEM))
        operands += [
            matrix[:, WIDTH : WIDTH + depth],
            jnp.concatenate([padding, matrix[:, :WIDTH]], axis=1),
            jnp.concatenate([matrix[:, WIDTH + depth :], padding], axis=1),
        ]
        in_specs += [pl.BlockSpec(memory_space=pltpu.VMEM)] * 3
        out_shapes.append(jax.ShapeDtypeStruct(value.shape, value.dtype))
        out_specs.append(pl.BlockSpec(memory_space=pltpu.VMEM))
        scratch = [pltpu.VMEM((depth, rows), jnp.float32), pltpu.VMEM((8, rows), jnp.float32),
                   pltpu.VMEM((8, rows), jnp.float32)]
        copies += 2
    if prepare is not None:
        out_shapes += [
            jax.ShapeDtypeStruct(zeta[0].shape, jnp.float32),
            jax.ShapeDtypeStruct(prepare.shape[1:], jnp.float32),
        ]
        out_specs += [pl.BlockSpec(memory_space=pltpu.VMEM)] * 2
    return pl.pallas_call(
        functools.partial(
            exchange_kernel, tuple(routes), sizes, len(arrays) + (prepare is not None),
            zeta is not None, prepare is not None, precision,
        ),
        out_shape=out_shapes,
        in_specs=in_specs,
        out_specs=out_specs,
        scratch_shapes=scratch + [
            pltpu.SemaphoreType.DMA((copies,)),
            pltpu.SemaphoreType.DMA((copies,)),
        ],
        compiler_params=pltpu.CompilerParams(collective_id=tag, has_side_effects=True),
    )(*operands)


def offset_along(axis, step):
    return tuple(step if name == axis else 0 for name in AXES)


def window(ndim, dim, start, stop):
    return tuple(slice(start, stop) if axis == dim else slice(None) for axis in range(ndim))


def exchange_faces(items, tag, zeta=None):
    arrays, routes, out_shapes = [], [], []
    for value, axis, dim in items:
        ndim, length = value.ndim, value.shape[dim]
        if dim == ndim - 1:
            both = jnp.stack(
                [
                    lax.slice_in_dim(value, length - WIDTH, length, axis=dim),
                    lax.slice_in_dim(value, 0, WIDTH, axis=dim),
                ]
            )
            both = jnp.moveaxis(both, dim + 1, 2).reshape(2, value.shape[0], WIDTH, -1)
            arrays.append((both, pl.ANY))
            out_shapes.append(jax.ShapeDtypeStruct(both.shape, both.dtype))
            source, target = len(arrays) - 1, len(out_shapes) - 1
            routes.append((offset_along(axis, 1), source, 0, target, 0))
            routes.append((offset_along(axis, -1), source, 1, target, 1))
        elif dim == ndim - 2:
            face = value.shape[:dim] + (WIDTH,) + value.shape[dim + 1 :]
            arrays.append((value, pltpu.VMEM))
            out_shapes += [jax.ShapeDtypeStruct(face, value.dtype)] * 2
            source, target = len(arrays) - 1, len(out_shapes) - 2
            whole = window(ndim, dim, None, None)
            last, first = window(ndim, dim, length - WIDTH, length), window(ndim, dim, 0, WIDTH)
            routes.append((offset_along(axis, 1), source, last, target, whole))
            routes.append((offset_along(axis, -1), source, first, target + 1, whole))
        else:
            arrays.append((value, pl.ANY))
            face = value.shape[:dim] + (WIDTH,) + value.shape[dim + 1 :]
            out_shapes += [jax.ShapeDtypeStruct(face, value.dtype)] * 2
            source, target = len(arrays) - 1, len(out_shapes) - 2
            whole = window(ndim, dim, None, None)
            last, first = window(ndim, dim, length - WIDTH, length), window(ndim, dim, 0, WIDTH)
            routes.append((offset_along(axis, 1), source, last, target, whole))
            routes.append((offset_along(axis, -1), source, first, target + 1, whole))
    received = exchange(arrays, routes, out_shapes, tag, zeta)
    padded, place = [], 0
    for value, axis, dim in items:
        if dim == value.ndim - 1:
            both = received[place].reshape((2, value.shape[0], WIDTH) + value.shape[1:dim])
            both = jnp.moveaxis(both, 2, dim + 1)
            before, after = both[0], both[1]
            place += 1
        else:
            before, after = received[place], received[place + 1]
            place += 2
        padded.append(jnp.concatenate([before, value, after], axis=dim))
    if zeta is not None:
        padded.append(received[-1])
    return padded


def exchange_primitive(conserved, matrix, tag):
    primitive = jax.ShapeDtypeStruct((4,) + conserved.shape[1:], conserved.dtype)
    length_x, length_y = primitive.shape[1], primitive.shape[2]
    every = slice(None)
    routes = [
        ((1, 0, 0), 0, (every, slice(length_x - WIDTH, length_x)), 0, every),
        ((-1, 0, 0), 0, (every, slice(0, WIDTH)), 1, every),
        ((0, 1, 0), 0, (every, every, slice(length_y - WIDTH, length_y)), 2, every),
        ((0, -1, 0), 0, (every, every, slice(0, WIDTH)), 3, every),
    ]
    face_x = (primitive.shape[0], WIDTH) + primitive.shape[2:]
    face_y = primitive.shape[:2] + (WIDTH,) + primitive.shape[3:]
    out_shapes = [jax.ShapeDtypeStruct(face, primitive.dtype) for face in (face_x, face_x, face_y, face_y)]
    before_x, after_x, before_y, after_y, swept, primitive, pressure = exchange(
        [], routes, out_shapes, tag, (primitive, matrix), conserved
    )
    return (
        jnp.concatenate([before_x, primitive, after_x], axis=1),
        jnp.concatenate([before_y, primitive, after_y], axis=2),
        swept,
        primitive,
        pressure,
    )


def exchange_plane(value, tag):
    length_x, length_y = value.shape[1], value.shape[2]
    faces_y = jnp.stack(
        [
            lax.slice_in_dim(value, length_y - WIDTH, length_y, axis=2),
            lax.slice_in_dim(value, 0, WIDTH, axis=2),
        ]
    )
    last_x, first_x = slice(length_x - WIDTH, length_x), slice(0, WIDTH)
    every = slice(None)
    routes = [
        ((1, 0, 0), 0, (every, last_x), 0, every),
        ((-1, 0, 0), 0, (every, first_x), 1, every),
        ((0, 1, 0), 1, 0, 2, every),
        ((0, -1, 0), 1, 1, 3, every),
        ((1, 1, 0), 1, (0, every, last_x), 4, every),
        ((-1, 1, 0), 1, (0, every, first_x), 5, every),
        ((1, -1, 0), 1, (1, every, last_x), 6, every),
        ((-1, -1, 0), 1, (1, every, first_x), 7, every),
    ]
    fields, depth = value.shape[0], value.shape[3]
    out_shapes = (
        [jax.ShapeDtypeStruct((fields, WIDTH, length_y, depth), value.dtype)] * 2
        + [jax.ShapeDtypeStruct((fields, length_x, WIDTH, depth), value.dtype)] * 2
        + [jax.ShapeDtypeStruct((fields, WIDTH, WIDTH, depth), value.dtype)] * 4
    )
    x_before, x_after, y_before, y_after, both_before, x_after_y_before, x_before_y_after, both_after = (
        exchange([(value, pl.ANY), (faces_y, pl.ANY)], routes, out_shapes, tag)
    )
    sections = [
        jnp.concatenate([both_before, x_before, x_before_y_after], axis=2),
        jnp.concatenate([y_before, value, y_after], axis=2),
        jnp.concatenate([x_after_y_before, x_after, both_after], axis=2),
    ]
    return jnp.concatenate(sections, axis=1)


def sweep_zeta(value, matrix, tag):
    return exchange([], [], [], tag, (value, matrix), precision=lax.Precision.HIGHEST)[-1]


def with_halo(value, sides, width):
    for axis, dim in sides:
        count, length = (lax.axis_size(axis), value.shape[dim])
        up = [(i, (i + 1) % count) for i in range(count)]
        down = [(j, i) for i, j in up]
        last = lax.slice_in_dim(value, length - width, length, axis=dim)
        initial = lax.slice_in_dim(value, 0, width, axis=dim)
        before = lax.ppermute(last, axis, up)
        after = lax.ppermute(initial, axis, down)
        value = jnp.concatenate([before, value, after], axis=dim)
    return value


def banded_solve(system, source):
    extent = system.shape[0]
    lower = np.zeros(extent)
    upper = np.zeros(extent)
    middle = np.array([float(system[index, index]) for index in range(extent)])
    for index in range(1, extent):
        lower[index] = system[index, index - 1]
        upper[index - 1] = system[index - 1, index]
    rights = np.array(source)
    for index in range(1, extent):
        factor = lower[index] / middle[index - 1]
        middle[index] = middle[index] - factor * upper[index - 1]
        rights[index] = rights[index] - factor * rights[index - 1]
    answer = np.zeros(rights.shape)
    answer[extent - 1] = rights[extent - 1] / middle[extent - 1]
    for index in range(extent - 2, -1, -1):
        answer[index] = (rights[index] - upper[index] * answer[index + 1]) / middle[index]
    return answer


def derivative_table(length):
    extent = length + 2 * WIDTH
    system = np.eye(extent)
    source = np.zeros((extent, extent))
    for position in range(2, extent - 2):
        system[position, position - 1] = 1.0 / 3.0
        system[position, position + 1] = 1.0 / 3.0
        source[position, position + 1] = 7.0 / 9.0
        source[position, position - 1] = -7.0 / 9.0
        source[position, position + 2] = 1.0 / 36.0
        source[position, position - 2] = -1.0 / 36.0
    source[1, 2] = 0.5
    source[1, 0] = -0.5
    source[extent - 2, extent - 1] = 0.5
    source[extent - 2, extent - 3] = -0.5
    source[0, 1] = 1.0
    source[0, 0] = -1.0
    source[extent - 1, extent - 1] = 1.0
    source[extent - 1, extent - 2] = -1.0
    return banded_solve(system, source)[WIDTH : WIDTH + length]


def filter_table(length):
    strength = 0.4
    coeffs = [
        (193.0 + 126.0 * strength) / 256.0,
        (105.0 + 302.0 * strength) / 256.0,
        15.0 * (2.0 * strength - 1.0) / 64.0,
        45.0 * (1.0 - 2.0 * strength) / 512.0,
        5.0 * (2.0 * strength - 1.0) / 256.0,
        (1.0 - 2.0 * strength) / 512.0,
    ]
    extent = length + 2 * WIDTH
    system = np.eye(extent)
    source = np.eye(extent)
    for position in range(5, extent - 5):
        system[position, position - 1] = strength
        system[position, position + 1] = strength
        source[position, position] = coeffs[0]
        for offset in range(1, 6):
            source[position, position + offset] = coeffs[offset] / 2.0
            source[position, position - offset] = coeffs[offset] / 2.0
    return banded_solve(system, source)[WIDTH : WIDTH + length]


def sweep_lines(padded, matrix, dim, precision=lax.Precision.HIGHEST):
    return jnp.einsum(line_forms[dim], matrix, padded, precision=precision)


def faces_xi(values):
    return with_halo(values, (("xi", 1),), WIDTH)


def faces_eta(values):
    return with_halo(values, (("eta", 2),), WIDTH)


def faces_zeta(values):
    return with_halo(values, (("zeta", 3),), WIDTH)


def basic_quantities(conserved_solution):
    density = conserved_solution[0]
    fluid_speed_vector = conserved_solution[1:4] / density
    thermodynamic_stress_scalar = 0.4 * (
        conserved_solution[4] - 0.5 * jnp.sum(conserved_solution[1:4] * fluid_speed_vector, axis=0)
    )
    return (fluid_speed_vector, thermodynamic_stress_scalar, thermodynamic_stress_scalar / density)


def fluxes(
    conserved_solution, fluid_speed_vector, thermodynamic_stress_scalar, slopes, metrics, jacobian
):
    physical = [
        [
            jacobian
            * (
                metrics[0, column] * slopes[0][member]
                + metrics[1, column] * slopes[1][member]
                + metrics[2, column] * slopes[2][member]
            )
            for column in range(3)
        ]
        for member in range(4)
    ]
    spread = physical[0][0] + physical[1][1] + physical[2][2]
    totals = []
    for column in range(3):
        stress = [
            viscosity * (physical[member][column] + physical[column][member]) for member in range(3)
        ]
        stress[column] = stress[column] - 2.0 / 3.0 * viscosity * spread
        subdomain_parts = [conserved_solution[1 + column]]
        for member in range(3):
            carried = conserved_solution[1 + member] * fluid_speed_vector[column] - stress[member]
            if member == column:
                carried = carried + thermodynamic_stress_scalar
            subdomain_parts.append(carried)
        worked = (
            fluid_speed_vector[0] * stress[0]
            + fluid_speed_vector[1] * stress[1]
            + fluid_speed_vector[2] * stress[2]
        )
        subdomain_parts.append(
            (conserved_solution[4] + thermodynamic_stress_scalar) * fluid_speed_vector[column]
            - worked
            - conduction * physical[3][column]
        )
        totals.append(jnp.stack(subdomain_parts))
    return [
        metrics[direction, 0] * totals[0]
        + metrics[direction, 1] * totals[1]
        + metrics[direction, 2] * totals[2]
        for direction in range(3)
    ]


def local(conserved_solution, metrics, jacobian):
    lengths = conserved_solution.shape[1:]
    derive = [jnp.asarray(derivative_table(length), dtype=jnp.float32) for length in lengths]
    smooth = [jnp.asarray(filter_table(length), dtype=jnp.float32) for length in lengths]
    padded = exchange_primitive(conserved_solution, derive[2], 0)
    slopes = [sweep_lines(padded[k], derive[k], k + 1, lax.Precision.HIGH) for k in range(2)]
    slopes.append(padded[2])
    fluid_speed_vector, thermodynamic_stress_scalar = padded[3][0:3], padded[4]
    contra = fluxes(
        conserved_solution,
        fluid_speed_vector,
        thermodynamic_stress_scalar,
        slopes,
        metrics,
        jacobian,
    )
    padded = exchange_faces([(contra[0], "xi", 1), (contra[1], "eta", 2)], 1, (contra[2], derive[2]))
    divergence = sweep_lines(padded[0], derive[0], 1, lax.Precision.HIGH)
    divergence = divergence + sweep_lines(padded[1], derive[1], 2, lax.Precision.HIGH)
    divergence = divergence + padded[2]
    sectioned = conserved_solution - step_duration * jacobian * divergence
    result = sweep_lines(exchange_plane(sectioned, 2), smooth[0], 1)
    result = sweep_lines(result, smooth[1], 2)
    result = sweep_zeta(result, smooth[2], 4)
    return result


def solution(mesh):
    in_specs = (
        P(None, "xi", "eta", "zeta"),
        P(None, None, "xi", "eta", "zeta"),
        P("xi", "eta", "zeta"),
    )
    out_specs = P(None, "xi", "eta", "zeta")
    return jax.shard_map(local, mesh=mesh, in_specs=in_specs, out_specs=out_specs, check_vma=False)
```

```python
import functools

import jax
import jax.numpy as jnp
import numpy as np
from jax import lax
from jax.experimental import pallas as pl
from jax.experimental.pallas import tpu as pltpu
from jax.sharding import PartitionSpec as P

WIDTH = 5


viscosity = 0.15
conduction = 0.15 * 1.4 / (0.4 * 0.72)
step_duration = 0.08
line_forms = ("", "al,flyz->fayz", "al,fxlz->fxaz", "al,fxyl->fxya")
MESH = pl.DeviceIdType.MESH
AXES = ("xi", "eta", "zeta")


def primitive_state(conserved):
    density = conserved[0]
    speed = conserved[1:4] / density
    pressure = 0.4 * (conserved[4] - 0.5 * jnp.sum(conserved[1:4] * speed, axis=0))
    return speed, pressure, pressure / density


def exchange_kernel(routes, sizes, count, zeta, prepare, precision, *refs):
    sources = list(refs[:count])
    refs = refs[count:]
    if prepare:
        conserved_ref = sources.pop()
    if zeta:
        if not prepare:
            block_ref = refs[0]
            refs = refs[1:]
        middle_ref, lower_ref, upper_ref = refs[:3]
        refs = refs[3:]
    extra = (1 if zeta else 0) + (2 if prepare else 0)
    targets = refs[: len(refs) - 2 - (3 if zeta else 0) - extra]
    refs = refs[len(targets) :]
    if zeta:
        out_ref = refs[0]
        refs = refs[1:]
    if prepare:
        made, pressure_ref = refs[:2]
        refs = refs[2:]
        sources.append(made)
        if zeta:
            block_ref = made
    if zeta:
        turned, before, after = refs[:3]
        refs = refs[3:]
    send_sems, recv_sems = refs
    here = [lax.axis_index(axis) for axis in AXES]

    def device(offset):
        return tuple(
            lax.rem(here[slot] + offset[slot] + sizes[slot], sizes[slot]) for slot in range(3)
        )

    offsets = [route[0] for route in routes] + ([(0, 0, 1), (0, 0, -1)] if zeta else [])
    partners = []
    for offset in offsets:
        for way in (offset, tuple(-step for step in offset)):
            if way not in partners:
                partners.append(way)
    barrier = pltpu.get_barrier_semaphore()
    for offset in partners:
        pl.semaphore_signal(barrier, inc=1, device_id=device(offset), device_id_type=MESH)
    if prepare:
        speed, pressure, temperature = primitive_state(conserved_ref[...])
        made[0:3] = speed
        made[3] = temperature
        pressure_ref[...] = pressure
    if zeta:
        fields, length_x, length_y, depth = block_ref.shape
        rows = fields * length_x * length_y
        turned[...] = block_ref[...].reshape(rows, depth).T
    pl.semaphore_wait(barrier, len(partners))
    copies = []
    for index, (offset, source, source_at, target, target_at) in enumerate(routes):
        copies.append(
            pltpu.make_async_remote_copy(
                src_ref=sources[source].at[source_at],
                dst_ref=targets[target].at[target_at],
                send_sem=send_sems.at[index],
                recv_sem=recv_sems.at[index],
                device_id=device(offset),
                device_id_type=MESH,
            )
        )
    if zeta:
        for index, (rows_at, landing, offset) in enumerate(
            ((pl.ds(depth - 8, 8), before, (0, 0, 1)), (pl.ds(0, 8), after, (0, 0, -1)))
        ):
            copies.append(
                pltpu.make_async_remote_copy(
                    src_ref=turned.at[rows_at],
                    dst_ref=landing,
                    send_sem=send_sems.at[len(routes) + index],
                    recv_sem=recv_sems.at[len(routes) + index],
                    device_id=device(offset),
                    device_id_type=MESH,
                )
            )
    for copy in copies:
        copy.start()
    if zeta:
        total = jnp.dot(middle_ref[...], turned[...], precision=precision,
                        preferred_element_type=jnp.float32)
    for copy in copies:
        copy.wait()
    if zeta:
        total = total + jnp.dot(lower_ref[...], before[...], precision=precision,
                                preferred_element_type=jnp.float32)
        total = total + jnp.dot(upper_ref[...], after[...], precision=precision,
                                preferred_element_type=jnp.float32)
        out_ref[...] = total.T.reshape(fields, length_x, length_y, depth)


def exchange(arrays, routes, out_shapes, tag, zeta=None, prepare=None,
             precision=lax.Precision.HIGH):
    sizes = tuple(lax.axis_size(axis) for axis in AXES)
    operands = [array for array, _ in arrays]
    in_specs = [pl.BlockSpec(memory_space=space) for _, space in arrays]
    out_specs = [pl.BlockSpec(memory_space=pl.ANY)] * len(out_shapes)
    out_shapes = list(out_shapes)
    scratch = []
    copies = len(routes)
    if prepare is not None:
        operands.append(prepare)
        in_specs.append(pl.BlockSpec(memory_space=pltpu.VMEM))
    if zeta is not None:
        value, matrix = zeta
        fields, length_x, length_y, depth = value.shape
        rows = fields * length_x * length_y
        padding = jnp.zeros((depth, 8 - WIDTH), matrix.dtype)
        if prepare is None:
            operands.append(value)
            in_specs.append(pl.BlockSpec(memory_space=pltpu.VMEM))
        operands += [
            matrix[:, WIDTH : WIDTH + depth],
            jnp.concatenate([padding, matrix[:, :WIDTH]], axis=1),
            jnp.concatenate([matrix[:, WIDTH + depth :], padding], axis=1),
        ]
        in_specs += [pl.BlockSpec(memory_space=pltpu.VMEM)] * 3
        out_shapes.append(jax.ShapeDtypeStruct(value.shape, value.dtype))
        out_specs.append(pl.BlockSpec(memory_space=pltpu.VMEM))
        scratch = [pltpu.VMEM((depth, rows), jnp.float32), pltpu.VMEM((8, rows), jnp.float32),
                   pltpu.VMEM((8, rows), jnp.float32)]
        copies += 2
    if prepare is not None:
        out_shapes += [
            jax.ShapeDtypeStruct(zeta[0].shape, jnp.float32),
            jax.ShapeDtypeStruct(prepare.shape[1:], jnp.float32),
        ]
        out_specs += [pl.BlockSpec(memory_space=pltpu.VMEM)] * 2
    return pl.pallas_call(
        functools.partial(
            exchange_kernel, tuple(routes), sizes, len(arrays) + (prepare is not None),
            zeta is not None, prepare is not None, precision,
        ),
        out_shape=out_shapes,
        in_specs=in_specs,
        out_specs=out_specs,
        scratch_shapes=scratch + [
            pltpu.SemaphoreType.DMA((copies,)),
            pltpu.SemaphoreType.DMA((copies,)),
        ],
        compiler_params=pltpu.CompilerParams(collective_id=tag, has_side_effects=True),
    )(*operands)


def offset_along(axis, step):
    return tuple(step if name == axis else 0 for name in AXES)


def window(ndim, dim, start, stop):
    return tuple(slice(start, stop) if axis == dim else slice(None) for axis in range(ndim))


def exchange_faces(items, tag, zeta=None):
    arrays, routes, out_shapes = [], [], []
    for value, axis, dim in items:
        ndim, length = value.ndim, value.shape[dim]
        if dim == ndim - 1:
            both = jnp.stack(
                [
                    lax.slice_in_dim(value, length - WIDTH, length, axis=dim),
                    lax.slice_in_dim(value, 0, WIDTH, axis=dim),
                ]
            )
            both = jnp.moveaxis(both, dim + 1, 2).reshape(2, value.shape[0], WIDTH, -1)
            arrays.append((both, pl.ANY))
            out_shapes.append(jax.ShapeDtypeStruct(both.shape, both.dtype))
            source, target = len(arrays) - 1, len(out_shapes) - 1
            routes.append((offset_along(axis, 1), source, 0, target, 0))
            routes.append((offset_along(axis, -1), source, 1, target, 1))
        elif dim == ndim - 2:
            face = value.shape[:dim] + (WIDTH,) + value.shape[dim + 1 :]
            arrays.append((value, pltpu.VMEM))
            out_shapes += [jax.ShapeDtypeStruct(face, value.dtype)] * 2
            source, target = len(arrays) - 1, len(out_shapes) - 2
            whole = window(ndim, dim, None, None)
            last, first = window(ndim, dim, length - WIDTH, length), window(ndim, dim, 0, WIDTH)
            routes.append((offset_along(axis, 1), source, last, target, whole))
            routes.append((offset_along(axis, -1), source, first, target + 1, whole))
        else:
            arrays.append((value, pltpu.VMEM))
            face = value.shape[:dim] + (WIDTH,) + value.shape[dim + 1 :]
            out_shapes += [jax.ShapeDtypeStruct(face, value.dtype)] * 2
            source, target = len(arrays) - 1, len(out_shapes) - 2
            whole = window(ndim, dim, None, None)
            last, first = window(ndim, dim, length - WIDTH, length), window(ndim, dim, 0, WIDTH)
            routes.append((offset_along(axis, 1), source, last, target, whole))
            routes.append((offset_along(axis, -1), source, first, target + 1, whole))
    received = exchange(arrays, routes, out_shapes, tag, zeta)
    padded, place = [], 0
    for value, axis, dim in items:
        if dim == value.ndim - 1:
            both = received[place].reshape((2, value.shape[0], WIDTH) + value.shape[1:dim])
            both = jnp.moveaxis(both, 2, dim + 1)
            before, after = both[0], both[1]
            place += 1
        else:
            before, after = received[place], received[place + 1]
            place += 2
        padded.append(jnp.concatenate([before, value, after], axis=dim))
    if zeta is not None:
        padded.append(received[-1])
    return padded


def exchange_primitive(conserved, matrix, tag):
    primitive = jax.ShapeDtypeStruct((4,) + conserved.shape[1:], conserved.dtype)
    length_x, length_y = primitive.shape[1], primitive.shape[2]
    every = slice(None)
    routes = [
        ((1, 0, 0), 0, (every, slice(length_x - WIDTH, length_x)), 0, every),
        ((-1, 0, 0), 0, (every, slice(0, WIDTH)), 1, every),
        ((0, 1, 0), 0, (every, every, slice(length_y - WIDTH, length_y)), 2, every),
        ((0, -1, 0), 0, (every, every, slice(0, WIDTH)), 3, every),
    ]
    face_x = (primitive.shape[0], WIDTH) + primitive.shape[2:]
    face_y = primitive.shape[:2] + (WIDTH,) + primitive.shape[3:]
    out_shapes = [jax.ShapeDtypeStruct(face, primitive.dtype) for face in (face_x, face_x, face_y, face_y)]
    before_x, after_x, before_y, after_y, swept, primitive, pressure = exchange(
        [], routes, out_shapes, tag, (primitive, matrix), conserved
    )
    return (
        jnp.concatenate([before_x, primitive, after_x], axis=1),
        jnp.concatenate([before_y, primitive, after_y], axis=2),
        swept,
        primitive,
        pressure,
    )


def exchange_plane(value, tag):
    length_x, length_y = value.shape[1], value.shape[2]
    faces_y = jnp.stack(
        [
            lax.slice_in_dim(value, length_y - WIDTH, length_y, axis=2),
            lax.slice_in_dim(value, 0, WIDTH, axis=2),
        ]
    )
    last_x, first_x = slice(length_x - WIDTH, length_x), slice(0, WIDTH)
    every = slice(None)
    routes = [
        ((1, 0, 0), 0, (every, last_x), 0, every),
        ((-1, 0, 0), 0, (every, first_x), 1, every),
        ((0, 1, 0), 1, 0, 2, every),
        ((0, -1, 0), 1, 1, 3, every),
        ((1, 1, 0), 1, (0, every, last_x), 4, every),
        ((-1, 1, 0), 1, (0, every, first_x), 5, every),
        ((1, -1, 0), 1, (1, every, last_x), 6, every),
        ((-1, -1, 0), 1, (1, every, first_x), 7, every),
    ]
    fields, depth = value.shape[0], value.shape[3]
    out_shapes = (
        [jax.ShapeDtypeStruct((fields, WIDTH, length_y, depth), value.dtype)] * 2
        + [jax.ShapeDtypeStruct((fields, length_x, WIDTH, depth), value.dtype)] * 2
        + [jax.ShapeDtypeStruct((fields, WIDTH, WIDTH, depth), value.dtype)] * 4
    )
    x_before, x_after, y_before, y_after, both_before, x_after_y_before, x_before_y_after, both_after = (
        exchange([(value, pltpu.VMEM), (faces_y, pl.ANY)], routes, out_shapes, tag)
    )
    sections = [
        jnp.concatenate([both_before, x_before, x_before_y_after], axis=2),
        jnp.concatenate([y_before, value, y_after], axis=2),
        jnp.concatenate([x_after_y_before, x_after, both_after], axis=2),
    ]
    return jnp.concatenate(sections, axis=1)


def sweep_zeta(value, matrix, tag):
    return exchange([], [], [], tag, (value, matrix), precision=lax.Precision.HIGHEST)[-1]


def with_halo(value, sides, width):
    for axis, dim in sides:
        count, length = (lax.axis_size(axis), value.shape[dim])
        up = [(i, (i + 1) % count) for i in range(count)]
        down = [(j, i) for i, j in up]
        last = lax.slice_in_dim(value, length - width, length, axis=dim)
        initial = lax.slice_in_dim(value, 0, width, axis=dim)
        before = lax.ppermute(last, axis, up)
        after = lax.ppermute(initial, axis, down)
        value = jnp.concatenate([before, value, after], axis=dim)
    return value


def banded_solve(system, source):
    extent = system.shape[0]
    lower = np.zeros(extent)
    upper = np.zeros(extent)
    middle = np.array([float(system[index, index]) for index in range(extent)])
    for index in range(1, extent):
        lower[index] = system[index, index - 1]
        upper[index - 1] = system[index - 1, index]
    rights = np.array(source)
    for index in range(1, extent):
        factor = lower[index] / middle[index - 1]
        middle[index] = middle[index] - factor * upper[index - 1]
        rights[index] = rights[index] - factor * rights[index - 1]
    answer = np.zeros(rights.shape)
    answer[extent - 1] = rights[extent - 1] / middle[extent - 1]
    for index in range(extent - 2, -1, -1):
        answer[index] = (rights[index] - upper[index] * answer[index + 1]) / middle[index]
    return answer


def derivative_table(length):
    extent = length + 2 * WIDTH
    system = np.eye(extent)
    source = np.zeros((extent, extent))
    for position in range(2, extent - 2):
        system[position, position - 1] = 1.0 / 3.0
        system[position, position + 1] = 1.0 / 3.0
        source[position, position + 1] = 7.0 / 9.0
        source[position, position - 1] = -7.0 / 9.0
        source[position, position + 2] = 1.0 / 36.0
        source[position, position - 2] = -1.0 / 36.0
    source[1, 2] = 0.5
    source[1, 0] = -0.5
    source[extent - 2, extent - 1] = 0.5
    source[extent - 2, extent - 3] = -0.5
    source[0, 1] = 1.0
    source[0, 0] = -1.0
    source[extent - 1, extent - 1] = 1.0
    source[extent - 1, extent - 2] = -1.0
    return banded_solve(system, source)[WIDTH : WIDTH + length]


def filter_table(length):
    strength = 0.4
    coeffs = [
        (193.0 + 126.0 * strength) / 256.0,
        (105.0 + 302.0 * strength) / 256.0,
        15.0 * (2.0 * strength - 1.0) / 64.0,
        45.0 * (1.0 - 2.0 * strength) / 512.0,
        5.0 * (2.0 * strength - 1.0) / 256.0,
        (1.0 - 2.0 * strength) / 512.0,
    ]
    extent = length + 2 * WIDTH
    system = np.eye(extent)
    source = np.eye(extent)
    for position in range(5, extent - 5):
        system[position, position - 1] = strength
        system[position, position + 1] = strength
        source[position, position] = coeffs[0]
        for offset in range(1, 6):
            source[position, position + offset] = coeffs[offset] / 2.0
            source[position, position - offset] = coeffs[offset] / 2.0
    return banded_solve(system, source)[WIDTH : WIDTH + length]


def sweep_lines(padded, matrix, dim, precision=lax.Precision.HIGHEST):
    return jnp.einsum(line_forms[dim], matrix, padded, precision=precision)


def faces_xi(values):
    return with_halo(values, (("xi", 1),), WIDTH)


def faces_eta(values):
    return with_halo(values, (("eta", 2),), WIDTH)


def faces_zeta(values):
    return with_halo(values, (("zeta", 3),), WIDTH)


def basic_quantities(conserved_solution):
    density = conserved_solution[0]
    fluid_speed_vector = conserved_solution[1:4] / density
    thermodynamic_stress_scalar = 0.4 * (
        conserved_solution[4] - 0.5 * jnp.sum(conserved_solution[1:4] * fluid_speed_vector, axis=0)
    )
    return (fluid_speed_vector, thermodynamic_stress_scalar, thermodynamic_stress_scalar / density)


def fluxes(
    conserved_solution, fluid_speed_vector, thermodynamic_stress_scalar, slopes, metrics, jacobian
):
    physical = [
        [
            jacobian
            * (
                metrics[0, column] * slopes[0][member]
                + metrics[1, column] * slopes[1][member]
                + metrics[2, column] * slopes[2][member]
            )
            for column in range(3)
        ]
        for member in range(4)
    ]
    spread = physical[0][0] + physical[1][1] + physical[2][2]
    totals = []
    for column in range(3):
        stress = [
            viscosity * (physical[member][column] + physical[column][member]) for member in range(3)
        ]
        stress[column] = stress[column] - 2.0 / 3.0 * viscosity * spread
        subdomain_parts = [conserved_solution[1 + column]]
        for member in range(3):
            carried = conserved_solution[1 + member] * fluid_speed_vector[column] - stress[member]
            if member == column:
                carried = carried + thermodynamic_stress_scalar
            subdomain_parts.append(carried)
        worked = (
            fluid_speed_vector[0] * stress[0]
            + fluid_speed_vector[1] * stress[1]
            + fluid_speed_vector[2] * stress[2]
        )
        subdomain_parts.append(
            (conserved_solution[4] + thermodynamic_stress_scalar) * fluid_speed_vector[column]
            - worked
            - conduction * physical[3][column]
        )
        totals.append(jnp.stack(subdomain_parts))
    return [
        metrics[direction, 0] * totals[0]
        + metrics[direction, 1] * totals[1]
        + metrics[direction, 2] * totals[2]
        for direction in range(3)
    ]


def local(conserved_solution, metrics, jacobian):
    lengths = conserved_solution.shape[1:]
    derive = [jnp.asarray(derivative_table(length), dtype=jnp.float32) for length in lengths]
    smooth = [jnp.asarray(filter_table(length), dtype=jnp.float32) for length in lengths]
    padded = exchange_primitive(conserved_solution, derive[2], 0)
    slopes = [sweep_lines(padded[k], derive[k], k + 1, lax.Precision.HIGH) for k in range(2)]
    slopes.append(padded[2])
    fluid_speed_vector, thermodynamic_stress_scalar = padded[3][0:3], padded[4]
    contra = fluxes(
        conserved_solution,
        fluid_speed_vector,
        thermodynamic_stress_scalar,
        slopes,
        metrics,
        jacobian,
    )
    padded = exchange_faces([(contra[0], "xi", 1), (contra[1], "eta", 2)], 1, (contra[2], derive[2]))
    divergence = sweep_lines(padded[0], derive[0], 1, lax.Precision.HIGH)
    divergence = divergence + sweep_lines(padded[1], derive[1], 2, lax.Precision.HIGH)
    divergence = divergence + padded[2]
    sectioned = conserved_solution - step_duration * jacobian * divergence
    result = sweep_lines(exchange_plane(sectioned, 2), smooth[0], 1)
    result = sweep_lines(result, smooth[1], 2)
    result = sweep_zeta(result, smooth[2], 4)
    return result


def solution(mesh):
    in_specs = (
        P(None, "xi", "eta", "zeta"),
        P(None, None, "xi", "eta", "zeta"),
        P("xi", "eta", "zeta"),
    )
    out_specs = P(None, "xi", "eta", "zeta")
    return jax.shard_map(local, mesh=mesh, in_specs=in_specs, out_specs=out_specs, check_vma=False)
```

```python
import functools

import jax
import jax.numpy as jnp
import numpy as np
from jax import lax
from jax.experimental import pallas as pl
from jax.experimental.pallas import tpu as pltpu
from jax.sharding import PartitionSpec as P

WIDTH = 5


viscosity = 0.15
conduction = 0.15 * 1.4 / (0.4 * 0.72)
step_duration = 0.08
line_forms = ("", "al,flyz->fayz", "al,fxlz->fxaz", "al,fxyl->fxya")
MESH = pl.DeviceIdType.MESH
AXES = ("xi", "eta", "zeta")


def primitive_state(conserved):
    density = conserved[0]
    speed = conserved[1:4] / density
    pressure = 0.4 * (conserved[4] - 0.5 * jnp.sum(conserved[1:4] * speed, axis=0))
    return speed, pressure, pressure / density


def exchange_kernel(routes, sizes, count, zeta, prepare, precision, moves, *refs):
    sources = list(refs[:count])
    refs = refs[count:]
    if prepare:
        conserved_ref = sources.pop()
    if zeta:
        if not prepare:
            block_ref = refs[0]
            refs = refs[1:]
        middle_ref, lower_ref, upper_ref = refs[:3]
        refs = refs[3:]
    extra = (1 if zeta else 0) + (2 if prepare else 0)
    targets = refs[: len(refs) - 3 - (3 if zeta else 0) - extra]
    refs = refs[len(targets) :]
    if zeta:
        out_ref = refs[0]
        refs = refs[1:]
    if prepare:
        made, pressure_ref = refs[:2]
        refs = refs[2:]
        sources.append(made)
        if zeta:
            block_ref = made
    if zeta:
        turned, before, after = refs[:3]
        refs = refs[3:]
    send_sems, recv_sems, move_sems = refs
    here = [lax.axis_index(axis) for axis in AXES]

    def device(offset):
        return tuple(
            lax.rem(here[slot] + offset[slot] + sizes[slot], sizes[slot]) for slot in range(3)
        )

    offsets = [route[0] for route in routes] + ([(0, 0, 1), (0, 0, -1)] if zeta else [])
    partners = []
    for offset in offsets:
        for way in (offset, tuple(-step for step in offset)):
            if way not in partners:
                partners.append(way)
    barrier = pltpu.get_barrier_semaphore()
    for offset in partners:
        pl.semaphore_signal(barrier, inc=1, device_id=device(offset), device_id_type=MESH)
    if prepare:
        speed, pressure, temperature = primitive_state(conserved_ref[...])
        made[0:3] = speed
        made[3] = temperature
        pressure_ref[...] = pressure
    if zeta:
        fields, length_x, length_y, depth = block_ref.shape
        rows = fields * length_x * length_y
        turned[...] = block_ref[...].reshape(rows, depth).T
    local = []
    for index, (source, source_at, target, target_at) in enumerate(moves):
        local.append(
            pltpu.make_async_copy(
                sources[source].at[source_at], targets[target].at[target_at], move_sems.at[index]
            )
        )
        local[-1].start()
    pl.semaphore_wait(barrier, len(partners))
    copies = []
    for index, (offset, source, source_at, target, target_at) in enumerate(routes):
        copies.append(
            pltpu.make_async_remote_copy(
                src_ref=sources[source].at[source_at],
                dst_ref=targets[target].at[target_at],
                send_sem=send_sems.at[index],
                recv_sem=recv_sems.at[index],
                device_id=device(offset),
                device_id_type=MESH,
            )
        )
    if zeta:
        for index, (rows_at, landing, offset) in enumerate(
            ((pl.ds(depth - 8, 8), before, (0, 0, 1)), (pl.ds(0, 8), after, (0, 0, -1)))
        ):
            copies.append(
                pltpu.make_async_remote_copy(
                    src_ref=turned.at[rows_at],
                    dst_ref=landing,
                    send_sem=send_sems.at[len(routes) + index],
                    recv_sem=recv_sems.at[len(routes) + index],
                    device_id=device(offset),
                    device_id_type=MESH,
                )
            )
    for copy in copies:
        copy.start()
    if zeta:
        total = jnp.dot(middle_ref[...], turned[...], precision=precision,
                        preferred_element_type=jnp.float32)
    for copy in copies + local:
        copy.wait()
    if zeta:
        total = total + jnp.dot(lower_ref[...], before[...], precision=precision,
                                preferred_element_type=jnp.float32)
        total = total + jnp.dot(upper_ref[...], after[...], precision=precision,
                                preferred_element_type=jnp.float32)
        out_ref[...] = total.T.reshape(fields, length_x, length_y, depth)


def exchange(arrays, routes, out_shapes, tag, zeta=None, prepare=None,
             precision=lax.Precision.HIGH, moves=()):
    sizes = tuple(lax.axis_size(axis) for axis in AXES)
    operands = [array for array, _ in arrays]
    in_specs = [pl.BlockSpec(memory_space=space) for _, space in arrays]
    out_specs = [pl.BlockSpec(memory_space=pl.ANY)] * len(out_shapes)
    out_shapes = list(out_shapes)
    scratch = []
    copies = len(routes)
    if prepare is not None:
        operands.append(prepare)
        in_specs.append(pl.BlockSpec(memory_space=pltpu.VMEM))
    if zeta is not None:
        value, matrix = zeta
        fields, length_x, length_y, depth = value.shape
        rows = fields * length_x * length_y
        padding = jnp.zeros((depth, 8 - WIDTH), matrix.dtype)
        if prepare is None:
            operands.append(value)
            in_specs.append(pl.BlockSpec(memory_space=pltpu.VMEM))
        operands += [
            matrix[:, WIDTH : WIDTH + depth],
            jnp.concatenate([padding, matrix[:, :WIDTH]], axis=1),
            jnp.concatenate([matrix[:, WIDTH + depth :], padding], axis=1),
        ]
        in_specs += [pl.BlockSpec(memory_space=pltpu.VMEM)] * 3
        out_shapes.append(jax.ShapeDtypeStruct(value.shape, value.dtype))
        out_specs.append(pl.BlockSpec(memory_space=pltpu.VMEM))
        scratch = [pltpu.VMEM((depth, rows), jnp.float32), pltpu.VMEM((8, rows), jnp.float32),
                   pltpu.VMEM((8, rows), jnp.float32)]
        copies += 2
    if prepare is not None:
        out_shapes += [
            jax.ShapeDtypeStruct(zeta[0].shape, jnp.float32),
            jax.ShapeDtypeStruct(prepare.shape[1:], jnp.float32),
        ]
        out_specs += [pl.BlockSpec(memory_space=pltpu.VMEM)] * 2
    return pl.pallas_call(
        functools.partial(
            exchange_kernel, tuple(routes), sizes, len(arrays) + (prepare is not None),
            zeta is not None, prepare is not None, precision, tuple(moves),
        ),
        out_shape=out_shapes,
        in_specs=in_specs,
        out_specs=out_specs,
        scratch_shapes=scratch + [
            pltpu.SemaphoreType.DMA((copies,)),
            pltpu.SemaphoreType.DMA((copies,)),
            pltpu.SemaphoreType.DMA((max(1, len(moves)),)),
        ],
        compiler_params=pltpu.CompilerParams(collective_id=tag, has_side_effects=True),
    )(*operands)


def offset_along(axis, step):
    return tuple(step if name == axis else 0 for name in AXES)


def window(ndim, dim, start, stop):
    return tuple(slice(start, stop) if axis == dim else slice(None) for axis in range(ndim))


def exchange_faces(items, tag, zeta=None):
    arrays, routes, out_shapes, moves = [], [], [], []
    for value, axis, dim in items:
        ndim, length = value.ndim, value.shape[dim]
        if dim == ndim - 1:
            both = jnp.stack(
                [
                    lax.slice_in_dim(value, length - WIDTH, length, axis=dim),
                    lax.slice_in_dim(value, 0, WIDTH, axis=dim),
                ]
            )
            both = jnp.moveaxis(both, dim + 1, 2).reshape(2, value.shape[0], WIDTH, -1)
            arrays.append((both, pl.ANY))
            out_shapes.append(jax.ShapeDtypeStruct(both.shape, both.dtype))
            source, target = len(arrays) - 1, len(out_shapes) - 1
            routes.append((offset_along(axis, 1), source, 0, target, 0))
            routes.append((offset_along(axis, -1), source, 1, target, 1))
        elif dim == ndim - 2:
            face = value.shape[:dim] + (WIDTH,) + value.shape[dim + 1 :]
            arrays.append((value, pltpu.VMEM))
            out_shapes += [jax.ShapeDtypeStruct(face, value.dtype)] * 2
            source, target = len(arrays) - 1, len(out_shapes) - 2
            whole = window(ndim, dim, None, None)
            last, first = window(ndim, dim, length - WIDTH, length), window(ndim, dim, 0, WIDTH)
            routes.append((offset_along(axis, 1), source, last, target, whole))
            routes.append((offset_along(axis, -1), source, first, target + 1, whole))
        else:
            arrays += [(value, pl.ANY), (value, pltpu.VMEM)]
            extended = value.shape[:dim] + (length + 2 * WIDTH,) + value.shape[dim + 1 :]
            out_shapes.append(jax.ShapeDtypeStruct(extended, value.dtype))
            source, target = len(arrays) - 2, len(out_shapes) - 1
            last, first = window(ndim, dim, length - WIDTH, length), window(ndim, dim, 0, WIDTH)
            ahead = window(ndim, dim, length + WIDTH, length + 2 * WIDTH)
            routes.append((offset_along(axis, 1), source, last, target, first))
            routes.append((offset_along(axis, -1), source, first, target, ahead))
            moves.append((source + 1, window(ndim, dim, None, None), target,
                          window(ndim, dim, WIDTH, length + WIDTH)))
    received = exchange(arrays, routes, out_shapes, tag, zeta, moves=moves)
    padded, place = [], 0
    for value, axis, dim in items:
        if dim == value.ndim - 1:
            both = received[place].reshape((2, value.shape[0], WIDTH) + value.shape[1:dim])
            both = jnp.moveaxis(both, 2, dim + 1)
            before, after = both[0], both[1]
            place += 1
        elif dim == value.ndim - 2:
            before, after = received[place], received[place + 1]
            place += 2
        else:
            padded.append(received[place])
            place += 1
            continue
        padded.append(jnp.concatenate([before, value, after], axis=dim))
    if zeta is not None:
        padded.append(received[-1])
    return padded


def exchange_primitive(conserved, matrix, tag):
    primitive = jax.ShapeDtypeStruct((4,) + conserved.shape[1:], conserved.dtype)
    length_x, length_y = primitive.shape[1], primitive.shape[2]
    every = slice(None)
    routes = [
        ((1, 0, 0), 0, (every, slice(length_x - WIDTH, length_x)), 0, (every, slice(0, WIDTH))),
        ((-1, 0, 0), 0, (every, slice(0, WIDTH)), 0, (every, slice(length_x + WIDTH, length_x + 2 * WIDTH))),
        ((0, 1, 0), 0, (every, every, slice(length_y - WIDTH, length_y)), 1, every),
        ((0, -1, 0), 0, (every, every, slice(0, WIDTH)), 2, every),
    ]
    moves = [(0, every, 0, (every, slice(WIDTH, length_x + WIDTH)))]
    extended_x = (primitive.shape[0], length_x + 2 * WIDTH) + primitive.shape[2:]
    face_y = primitive.shape[:2] + (WIDTH,) + primitive.shape[3:]
    out_shapes = [jax.ShapeDtypeStruct(face, primitive.dtype) for face in (extended_x, face_y, face_y)]
    padded_x, before_y, after_y, swept, primitive, pressure = exchange(
        [], routes, out_shapes, tag, (primitive, matrix), conserved, moves=moves
    )
    return (
        padded_x,
        jnp.concatenate([before_y, primitive, after_y], axis=2),
        swept,
        primitive,
        pressure,
    )


def exchange_plane(value, tag):
    length_x, length_y = value.shape[1], value.shape[2]
    faces_y = jnp.stack(
        [
            lax.slice_in_dim(value, length_y - WIDTH, length_y, axis=2),
            lax.slice_in_dim(value, 0, WIDTH, axis=2),
        ]
    )
    last_x, first_x = slice(length_x - WIDTH, length_x), slice(0, WIDTH)
    every = slice(None)
    routes = [
        ((1, 0, 0), 0, (every, last_x), 0, every),
        ((-1, 0, 0), 0, (every, first_x), 1, every),
        ((0, 1, 0), 1, 0, 2, every),
        ((0, -1, 0), 1, 1, 3, every),
        ((1, 1, 0), 1, (0, every, last_x), 4, every),
        ((-1, 1, 0), 1, (0, every, first_x), 5, every),
        ((1, -1, 0), 1, (1, every, last_x), 6, every),
        ((-1, -1, 0), 1, (1, every, first_x), 7, every),
    ]
    fields, depth = value.shape[0], value.shape[3]
    out_shapes = (
        [jax.ShapeDtypeStruct((fields, WIDTH, length_y, depth), value.dtype)] * 2
        + [jax.ShapeDtypeStruct((fields, length_x, WIDTH, depth), value.dtype)] * 2
        + [jax.ShapeDtypeStruct((fields, WIDTH, WIDTH, depth), value.dtype)] * 4
    )
    x_before, x_after, y_before, y_after, both_before, x_after_y_before, x_before_y_after, both_after = (
        exchange([(value, pl.ANY), (faces_y, pl.ANY)], routes, out_shapes, tag)
    )
    sections = [
        jnp.concatenate([both_before, x_before, x_before_y_after], axis=2),
        jnp.concatenate([y_before, value, y_after], axis=2),
        jnp.concatenate([x_after_y_before, x_after, both_after], axis=2),
    ]
    return jnp.concatenate(sections, axis=1)


def sweep_zeta(value, matrix, tag):
    return exchange([], [], [], tag, (value, matrix), precision=lax.Precision.HIGHEST)[-1]


def with_halo(value, sides, width):
    for axis, dim in sides:
        count, length = (lax.axis_size(axis), value.shape[dim])
        up = [(i, (i + 1) % count) for i in range(count)]
        down = [(j, i) for i, j in up]
        last = lax.slice_in_dim(value, length - width, length, axis=dim)
        initial = lax.slice_in_dim(value, 0, width, axis=dim)
        before = lax.ppermute(last, axis, up)
        after = lax.ppermute(initial, axis, down)
        value = jnp.concatenate([before, value, after], axis=dim)
    return value


def banded_solve(system, source):
    extent = system.shape[0]
    lower = np.zeros(extent)
    upper = np.zeros(extent)
    middle = np.array([float(system[index, index]) for index in range(extent)])
    for index in range(1, extent):
        lower[index] = system[index, index - 1]
        upper[index - 1] = system[index - 1, index]
    rights = np.array(source)
    for index in range(1, extent):
        factor = lower[index] / middle[index - 1]
        middle[index] = middle[index] - factor * upper[index - 1]
        rights[index] = rights[index] - factor * rights[index - 1]
    answer = np.zeros(rights.shape)
    answer[extent - 1] = rights[extent - 1] / middle[extent - 1]
    for index in range(extent - 2, -1, -1):
        answer[index] = (rights[index] - upper[index] * answer[index + 1]) / middle[index]
    return answer


def derivative_table(length):
    extent = length + 2 * WIDTH
    system = np.eye(extent)
    source = np.zeros((extent, extent))
    for position in range(2, extent - 2):
        system[position, position - 1] = 1.0 / 3.0
        system[position, position + 1] = 1.0 / 3.0
        source[position, position + 1] = 7.0 / 9.0
        source[position, position - 1] = -7.0 / 9.0
        source[position, position + 2] = 1.0 / 36.0
        source[position, position - 2] = -1.0 / 36.0
    source[1, 2] = 0.5
    source[1, 0] = -0.5
    source[extent - 2, extent - 1] = 0.5
    source[extent - 2, extent - 3] = -0.5
    source[0, 1] = 1.0
    source[0, 0] = -1.0
    source[extent - 1, extent - 1] = 1.0
    source[extent - 1, extent - 2] = -1.0
    return banded_solve(system, source)[WIDTH : WIDTH + length]


def filter_table(length):
    strength = 0.4
    coeffs = [
        (193.0 + 126.0 * strength) / 256.0,
        (105.0 + 302.0 * strength) / 256.0,
        15.0 * (2.0 * strength - 1.0) / 64.0,
        45.0 * (1.0 - 2.0 * strength) / 512.0,
        5.0 * (2.0 * strength - 1.0) / 256.0,
        (1.0 - 2.0 * strength) / 512.0,
    ]
    extent = length + 2 * WIDTH
    system = np.eye(extent)
    source = np.eye(extent)
    for position in range(5, extent - 5):
        system[position, position - 1] = strength
        system[position, position + 1] = strength
        source[position, position] = coeffs[0]
        for offset in range(1, 6):
            source[position, position + offset] = coeffs[offset] / 2.0
            source[position, position - offset] = coeffs[offset] / 2.0
    return banded_solve(system, source)[WIDTH : WIDTH + length]


def sweep_lines(padded, matrix, dim, precision=lax.Precision.HIGHEST):
    return jnp.einsum(line_forms[dim], matrix, padded, precision=precision)


def faces_xi(values):
    return with_halo(values, (("xi", 1),), WIDTH)


def faces_eta(values):
    return with_halo(values, (("eta", 2),), WIDTH)


def faces_zeta(values):
    return with_halo(values, (("zeta", 3),), WIDTH)


def basic_quantities(conserved_solution):
    density = conserved_solution[0]
    fluid_speed_vector = conserved_solution[1:4] / density
    thermodynamic_stress_scalar = 0.4 * (
        conserved_solution[4] - 0.5 * jnp.sum(conserved_solution[1:4] * fluid_speed_vector, axis=0)
    )
    return (fluid_speed_vector, thermodynamic_stress_scalar, thermodynamic_stress_scalar / density)


def fluxes(
    conserved_solution, fluid_speed_vector, thermodynamic_stress_scalar, slopes, metrics, jacobian
):
    physical = [
        [
            jacobian
            * (
                metrics[0, column] * slopes[0][member]
                + metrics[1, column] * slopes[1][member]
                + metrics[2, column] * slopes[2][member]
            )
            for column in range(3)
        ]
        for member in range(4)
    ]
    spread = physical[0][0] + physical[1][1] + physical[2][2]
    totals = []
    for column in range(3):
        stress = [
            viscosity * (physical[member][column] + physical[column][member]) for member in range(3)
        ]
        stress[column] = stress[column] - 2.0 / 3.0 * viscosity * spread
        subdomain_parts = [conserved_solution[1 + column]]
        for member in range(3):
            carried = conserved_solution[1 + member] * fluid_speed_vector[column] - stress[member]
            if member == column:
                carried = carried + thermodynamic_stress_scalar
            subdomain_parts.append(carried)
        worked = (
            fluid_speed_vector[0] * stress[0]
            + fluid_speed_vector[1] * stress[1]
            + fluid_speed_vector[2] * stress[2]
        )
        subdomain_parts.append(
            (conserved_solution[4] + thermodynamic_stress_scalar) * fluid_speed_vector[column]
            - worked
            - conduction * physical[3][column]
        )
        totals.append(jnp.stack(subdomain_parts))
    return [
        metrics[direction, 0] * totals[0]
        + metrics[direction, 1] * totals[1]
        + metrics[direction, 2] * totals[2]
        for direction in range(3)
    ]


def local(conserved_solution, metrics, jacobian):
    lengths = conserved_solution.shape[1:]
    derive = [jnp.asarray(derivative_table(length), dtype=jnp.float32) for length in lengths]
    smooth = [jnp.asarray(filter_table(length), dtype=jnp.float32) for length in lengths]
    padded = exchange_primitive(conserved_solution, derive[2], 0)
    slopes = [sweep_lines(padded[k], derive[k], k + 1, lax.Precision.HIGH) for k in range(2)]
    slopes.append(padded[2])
    fluid_speed_vector, thermodynamic_stress_scalar = padded[3][0:3], padded[4]
    contra = fluxes(
        conserved_solution,
        fluid_speed_vector,
        thermodynamic_stress_scalar,
        slopes,
        metrics,
        jacobian,
    )
    padded = exchange_faces([(contra[0], "xi", 1), (contra[1], "eta", 2)], 1, (contra[2], derive[2]))
    divergence = sweep_lines(padded[0], derive[0], 1, lax.Precision.HIGH)
    divergence = divergence + sweep_lines(padded[1], derive[1], 2, lax.Precision.HIGH)
    divergence = divergence + padded[2]
    sectioned = conserved_solution - step_duration * jacobian * divergence
    result = sweep_lines(exchange_plane(sectioned, 2), smooth[0], 1)
    result = sweep_lines(result, smooth[1], 2)
    result = sweep_zeta(result, smooth[2], 4)
    return result


def solution(mesh):
    in_specs = (
        P(None, "xi", "eta", "zeta"),
        P(None, None, "xi", "eta", "zeta"),
        P("xi", "eta", "zeta"),
    )
    out_specs = P(None, "xi", "eta", "zeta")
    return jax.shard_map(local, mesh=mesh, in_specs=in_specs, out_specs=out_specs, check_vma=False)
```

```python
import functools

import jax
import jax.numpy as jnp
import numpy as np
from jax import lax
from jax.experimental import pallas as pl
from jax.experimental.pallas import tpu as pltpu
from jax.sharding import PartitionSpec as P

WIDTH = 5


viscosity = 0.15
conduction = 0.15 * 1.4 / (0.4 * 0.72)
step_duration = 0.08
line_forms = ("", "al,flyz->fayz", "al,fxlz->fxaz", "al,fxyl->fxya")
MESH = pl.DeviceIdType.MESH
AXES = ("xi", "eta", "zeta")


def primitive_state(conserved):
    density = conserved[0]
    speed = conserved[1:4] / density
    pressure = 0.4 * (conserved[4] - 0.5 * jnp.sum(conserved[1:4] * speed, axis=0))
    return speed, pressure, pressure / density


def exchange_kernel(routes, sizes, count, zeta, prepare, precision, moves, *refs):
    sources = list(refs[:count])
    refs = refs[count:]
    if prepare:
        conserved_ref = sources.pop()
    if zeta:
        if not prepare:
            block_ref = refs[0]
            refs = refs[1:]
        middle_ref, lower_ref, upper_ref = refs[:3]
        refs = refs[3:]
    extra = (1 if zeta else 0) + (2 if prepare else 0)
    targets = refs[: len(refs) - 3 - (3 if zeta else 0) - extra]
    refs = refs[len(targets) :]
    if zeta:
        out_ref = refs[0]
        refs = refs[1:]
    if prepare:
        made, pressure_ref = refs[:2]
        refs = refs[2:]
        sources.append(made)
        if zeta:
            block_ref = made
    if zeta:
        turned, before, after = refs[:3]
        refs = refs[3:]
    send_sems, recv_sems, move_sems = refs
    here = [lax.axis_index(axis) for axis in AXES]

    def device(offset):
        return tuple(
            lax.rem(here[slot] + offset[slot] + sizes[slot], sizes[slot]) for slot in range(3)
        )

    offsets = [route[0] for route in routes] + ([(0, 0, 1), (0, 0, -1)] if zeta else [])
    partners = []
    for offset in offsets:
        for way in (offset, tuple(-step for step in offset)):
            if way not in partners:
                partners.append(way)
    barrier = pltpu.get_barrier_semaphore()
    for offset in partners:
        pl.semaphore_signal(barrier, inc=1, device_id=device(offset), device_id_type=MESH)
    if prepare:
        speed, pressure, temperature = primitive_state(conserved_ref[...])
        made[0:3] = speed
        made[3] = temperature
        pressure_ref[...] = pressure
    if zeta:
        fields, length_x, length_y, depth = block_ref.shape
        rows = fields * length_x * length_y
        turned[...] = block_ref[...].reshape(rows, depth).T
    local = []
    for index, (source, source_at, target, target_at) in enumerate(moves):
        local.append(
            pltpu.make_async_copy(
                sources[source].at[source_at], targets[target].at[target_at], move_sems.at[index]
            )
        )
        local[-1].start()
    pl.semaphore_wait(barrier, len(partners))
    copies = []
    for index, (offset, source, source_at, target, target_at) in enumerate(routes):
        copies.append(
            pltpu.make_async_remote_copy(
                src_ref=sources[source].at[source_at],
                dst_ref=targets[target].at[target_at],
                send_sem=send_sems.at[index],
                recv_sem=recv_sems.at[index],
                device_id=device(offset),
                device_id_type=MESH,
            )
        )
    if zeta:
        for index, (rows_at, landing, offset) in enumerate(
            ((pl.ds(depth - 8, 8), before, (0, 0, 1)), (pl.ds(0, 8), after, (0, 0, -1)))
        ):
            copies.append(
                pltpu.make_async_remote_copy(
                    src_ref=turned.at[rows_at],
                    dst_ref=landing,
                    send_sem=send_sems.at[len(routes) + index],
                    recv_sem=recv_sems.at[len(routes) + index],
                    device_id=device(offset),
                    device_id_type=MESH,
                )
            )
    for copy in copies:
        copy.start()
    if zeta:
        total = jnp.dot(middle_ref[...], turned[...], precision=precision,
                        preferred_element_type=jnp.float32)
    for copy in copies + local:
        copy.wait()
    if zeta:
        total = total + jnp.dot(lower_ref[...], before[...], precision=precision,
                                preferred_element_type=jnp.float32)
        total = total + jnp.dot(upper_ref[...], after[...], precision=precision,
                                preferred_element_type=jnp.float32)
        out_ref[...] = total.T.reshape(fields, length_x, length_y, depth)


def exchange(arrays, routes, out_shapes, tag, zeta=None, prepare=None,
             precision=lax.Precision.HIGH, moves=(), near=()):
    sizes = tuple(lax.axis_size(axis) for axis in AXES)
    operands = [array for array, _ in arrays]
    in_specs = [pl.BlockSpec(memory_space=space) for _, space in arrays]
    out_specs = [
        pl.BlockSpec(memory_space=pltpu.VMEM if index in near else pl.ANY)
        for index in range(len(out_shapes))
    ]
    out_shapes = list(out_shapes)
    scratch = []
    copies = len(routes)
    if prepare is not None:
        operands.append(prepare)
        in_specs.append(pl.BlockSpec(memory_space=pltpu.VMEM))
    if zeta is not None:
        value, matrix = zeta
        fields, length_x, length_y, depth = value.shape
        rows = fields * length_x * length_y
        padding = jnp.zeros((depth, 8 - WIDTH), matrix.dtype)
        if prepare is None:
            operands.append(value)
            in_specs.append(pl.BlockSpec(memory_space=pltpu.VMEM))
        operands += [
            matrix[:, WIDTH : WIDTH + depth],
            jnp.concatenate([padding, matrix[:, :WIDTH]], axis=1),
            jnp.concatenate([matrix[:, WIDTH + depth :], padding], axis=1),
        ]
        in_specs += [pl.BlockSpec(memory_space=pltpu.VMEM)] * 3
        out_shapes.append(jax.ShapeDtypeStruct(value.shape, value.dtype))
        out_specs.append(pl.BlockSpec(memory_space=pltpu.VMEM))
        scratch = [pltpu.VMEM((depth, rows), jnp.float32), pltpu.VMEM((8, rows), jnp.float32),
                   pltpu.VMEM((8, rows), jnp.float32)]
        copies += 2
    if prepare is not None:
        out_shapes += [
            jax.ShapeDtypeStruct(zeta[0].shape, jnp.float32),
            jax.ShapeDtypeStruct(prepare.shape[1:], jnp.float32),
        ]
        out_specs += [pl.BlockSpec(memory_space=pltpu.VMEM)] * 2
    return pl.pallas_call(
        functools.partial(
            exchange_kernel, tuple(routes), sizes, len(arrays) + (prepare is not None),
            zeta is not None, prepare is not None, precision, tuple(moves),
        ),
        out_shape=out_shapes,
        in_specs=in_specs,
        out_specs=out_specs,
        scratch_shapes=scratch + [
            pltpu.SemaphoreType.DMA((copies,)),
            pltpu.SemaphoreType.DMA((copies,)),
            pltpu.SemaphoreType.DMA((max(1, len(moves)),)),
        ],
        compiler_params=pltpu.CompilerParams(collective_id=tag, has_side_effects=True),
    )(*operands)


def offset_along(axis, step):
    return tuple(step if name == axis else 0 for name in AXES)


def window(ndim, dim, start, stop):
    return tuple(slice(start, stop) if axis == dim else slice(None) for axis in range(ndim))


def exchange_faces(items, tag, zeta=None):
    arrays, routes, out_shapes, moves = [], [], [], []
    for value, axis, dim in items:
        ndim, length = value.ndim, value.shape[dim]
        if dim == ndim - 1:
            both = jnp.stack(
                [
                    lax.slice_in_dim(value, length - WIDTH, length, axis=dim),
                    lax.slice_in_dim(value, 0, WIDTH, axis=dim),
                ]
            )
            both = jnp.moveaxis(both, dim + 1, 2).reshape(2, value.shape[0], WIDTH, -1)
            arrays.append((both, pl.ANY))
            out_shapes.append(jax.ShapeDtypeStruct(both.shape, both.dtype))
            source, target = len(arrays) - 1, len(out_shapes) - 1
            routes.append((offset_along(axis, 1), source, 0, target, 0))
            routes.append((offset_along(axis, -1), source, 1, target, 1))
        elif dim == ndim - 2:
            face = value.shape[:dim] + (WIDTH,) + value.shape[dim + 1 :]
            arrays.append((value, pltpu.VMEM))
            out_shapes += [jax.ShapeDtypeStruct(face, value.dtype)] * 2
            source, target = len(arrays) - 1, len(out_shapes) - 2
            whole = window(ndim, dim, None, None)
            last, first = window(ndim, dim, length - WIDTH, length), window(ndim, dim, 0, WIDTH)
            routes.append((offset_along(axis, 1), source, last, target, whole))
            routes.append((offset_along(axis, -1), source, first, target + 1, whole))
        else:
            arrays += [(value, pl.ANY), (value, pltpu.VMEM)]
            extended = value.shape[:dim] + (length + 2 * WIDTH,) + value.shape[dim + 1 :]
            out_shapes.append(jax.ShapeDtypeStruct(extended, value.dtype))
            source, target = len(arrays) - 2, len(out_shapes) - 1
            last, first = window(ndim, dim, length - WIDTH, length), window(ndim, dim, 0, WIDTH)
            ahead = window(ndim, dim, length + WIDTH, length + 2 * WIDTH)
            routes.append((offset_along(axis, 1), source, last, target, first))
            routes.append((offset_along(axis, -1), source, first, target, ahead))
            moves.append((source + 1, window(ndim, dim, None, None), target,
                          window(ndim, dim, WIDTH, length + WIDTH)))
    near = tuple(move[2] for move in moves)
    received = exchange(arrays, routes, out_shapes, tag, zeta, moves=moves, near=near)
    padded, place = [], 0
    for value, axis, dim in items:
        if dim == value.ndim - 1:
            both = received[place].reshape((2, value.shape[0], WIDTH) + value.shape[1:dim])
            both = jnp.moveaxis(both, 2, dim + 1)
            before, after = both[0], both[1]
            place += 1
        elif dim == value.ndim - 2:
            before, after = received[place], received[place + 1]
            place += 2
        else:
            padded.append(received[place])
            place += 1
            continue
        padded.append(jnp.concatenate([before, value, after], axis=dim))
    if zeta is not None:
        padded.append(received[-1])
    return padded


def exchange_primitive(conserved, matrix, tag):
    primitive = jax.ShapeDtypeStruct((4,) + conserved.shape[1:], conserved.dtype)
    length_x, length_y = primitive.shape[1], primitive.shape[2]
    every = slice(None)
    routes = [
        ((1, 0, 0), 0, (every, slice(length_x - WIDTH, length_x)), 0, (every, slice(0, WIDTH))),
        ((-1, 0, 0), 0, (every, slice(0, WIDTH)), 0, (every, slice(length_x + WIDTH, length_x + 2 * WIDTH))),
        ((0, 1, 0), 0, (every, every, slice(length_y - WIDTH, length_y)), 1, every),
        ((0, -1, 0), 0, (every, every, slice(0, WIDTH)), 2, every),
    ]
    moves = [(0, every, 0, (every, slice(WIDTH, length_x + WIDTH)))]
    extended_x = (primitive.shape[0], length_x + 2 * WIDTH) + primitive.shape[2:]
    face_y = primitive.shape[:2] + (WIDTH,) + primitive.shape[3:]
    out_shapes = [jax.ShapeDtypeStruct(face, primitive.dtype) for face in (extended_x, face_y, face_y)]
    padded_x, before_y, after_y, swept, primitive, pressure = exchange(
        [], routes, out_shapes, tag, (primitive, matrix), conserved, moves=moves, near=(0,)
    )
    return (
        padded_x,
        jnp.concatenate([before_y, primitive, after_y], axis=2),
        swept,
        primitive,
        pressure,
    )


def exchange_plane(value, tag):
    length_x, length_y = value.shape[1], value.shape[2]
    faces_y = jnp.stack(
        [
            lax.slice_in_dim(value, length_y - WIDTH, length_y, axis=2),
            lax.slice_in_dim(value, 0, WIDTH, axis=2),
        ]
    )
    last_x, first_x = slice(length_x - WIDTH, length_x), slice(0, WIDTH)
    every = slice(None)
    routes = [
        ((1, 0, 0), 0, (every, last_x), 0, every),
        ((-1, 0, 0), 0, (every, first_x), 1, every),
        ((0, 1, 0), 1, 0, 2, every),
        ((0, -1, 0), 1, 1, 3, every),
        ((1, 1, 0), 1, (0, every, last_x), 4, every),
        ((-1, 1, 0), 1, (0, every, first_x), 5, every),
        ((1, -1, 0), 1, (1, every, last_x), 6, every),
        ((-1, -1, 0), 1, (1, every, first_x), 7, every),
    ]
    fields, depth = value.shape[0], value.shape[3]
    out_shapes = (
        [jax.ShapeDtypeStruct((fields, WIDTH, length_y, depth), value.dtype)] * 2
        + [jax.ShapeDtypeStruct((fields, length_x, WIDTH, depth), value.dtype)] * 2
        + [jax.ShapeDtypeStruct((fields, WIDTH, WIDTH, depth), value.dtype)] * 4
    )
    x_before, x_after, y_before, y_after, both_before, x_after_y_before, x_before_y_after, both_after = (
        exchange([(value, pl.ANY), (faces_y, pl.ANY)], routes, out_shapes, tag)
    )
    sections = [
        jnp.concatenate([both_before, x_before, x_before_y_after], axis=2),
        jnp.concatenate([y_before, value, y_after], axis=2),
        jnp.concatenate([x_after_y_before, x_after, both_after], axis=2),
    ]
    return jnp.concatenate(sections, axis=1)


def sweep_zeta(value, matrix, tag):
    return exchange([], [], [], tag, (value, matrix), precision=lax.Precision.HIGHEST)[-1]


def with_halo(value, sides, width):
    for axis, dim in sides:
        count, length = (lax.axis_size(axis), value.shape[dim])
        up = [(i, (i + 1) % count) for i in range(count)]
        down = [(j, i) for i, j in up]
        last = lax.slice_in_dim(value, length - width, length, axis=dim)
        initial = lax.slice_in_dim(value, 0, width, axis=dim)
        before = lax.ppermute(last, axis, up)
        after = lax.ppermute(initial, axis, down)
        value = jnp.concatenate([before, value, after], axis=dim)
    return value


def banded_solve(system, source):
    extent = system.shape[0]
    lower = np.zeros(extent)
    upper = np.zeros(extent)
    middle = np.array([float(system[index, index]) for index in range(extent)])
    for index in range(1, extent):
        lower[index] = system[index, index - 1]
        upper[index - 1] = system[index - 1, index]
    rights = np.array(source)
    for index in range(1, extent):
        factor = lower[index] / middle[index - 1]
        middle[index] = middle[index] - factor * upper[index - 1]
        rights[index] = rights[index] - factor * rights[index - 1]
    answer = np.zeros(rights.shape)
    answer[extent - 1] = rights[extent - 1] / middle[extent - 1]
    for index in range(extent - 2, -1, -1):
        answer[index] = (rights[index] - upper[index] * answer[index + 1]) / middle[index]
    return answer


def derivative_table(length):
    extent = length + 2 * WIDTH
    system = np.eye(extent)
    source = np.zeros((extent, extent))
    for position in range(2, extent - 2):
        system[position, position - 1] = 1.0 / 3.0
        system[position, position + 1] = 1.0 / 3.0
        source[position, position + 1] = 7.0 / 9.0
        source[position, position - 1] = -7.0 / 9.0
        source[position, position + 2] = 1.0 / 36.0
        source[position, position - 2] = -1.0 / 36.0
    source[1, 2] = 0.5
    source[1, 0] = -0.5
    source[extent - 2, extent - 1] = 0.5
    source[extent - 2, extent - 3] = -0.5
    source[0, 1] = 1.0
    source[0, 0] = -1.0
    source[extent - 1, extent - 1] = 1.0
    source[extent - 1, extent - 2] = -1.0
    return banded_solve(system, source)[WIDTH : WIDTH + length]


def filter_table(length):
    strength = 0.4
    coeffs = [
        (193.0 + 126.0 * strength) / 256.0,
        (105.0 + 302.0 * strength) / 256.0,
        15.0 * (2.0 * strength - 1.0) / 64.0,
        45.0 * (1.0 - 2.0 * strength) / 512.0,
        5.0 * (2.0 * strength - 1.0) / 256.0,
        (1.0 - 2.0 * strength) / 512.0,
    ]
    extent = length + 2 * WIDTH
    system = np.eye(extent)
    source = np.eye(extent)
    for position in range(5, extent - 5):
        system[position, position - 1] = strength
        system[position, position + 1] = strength
        source[position, position] = coeffs[0]
        for offset in range(1, 6):
            source[position, position + offset] = coeffs[offset] / 2.0
            source[position, position - offset] = coeffs[offset] / 2.0
    return banded_solve(system, source)[WIDTH : WIDTH + length]


def sweep_lines(padded, matrix, dim, precision=lax.Precision.HIGHEST):
    return jnp.einsum(line_forms[dim], matrix, padded, precision=precision)


def faces_xi(values):
    return with_halo(values, (("xi", 1),), WIDTH)


def faces_eta(values):
    return with_halo(values, (("eta", 2),), WIDTH)


def faces_zeta(values):
    return with_halo(values, (("zeta", 3),), WIDTH)


def basic_quantities(conserved_solution):
    density = conserved_solution[0]
    fluid_speed_vector = conserved_solution[1:4] / density
    thermodynamic_stress_scalar = 0.4 * (
        conserved_solution[4] - 0.5 * jnp.sum(conserved_solution[1:4] * fluid_speed_vector, axis=0)
    )
    return (fluid_speed_vector, thermodynamic_stress_scalar, thermodynamic_stress_scalar / density)


def fluxes(
    conserved_solution, fluid_speed_vector, thermodynamic_stress_scalar, slopes, metrics, jacobian
):
    physical = [
        [
            jacobian
            * (
                metrics[0, column] * slopes[0][member]
                + metrics[1, column] * slopes[1][member]
                + metrics[2, column] * slopes[2][member]
            )
            for column in range(3)
        ]
        for member in range(4)
    ]
    spread = physical[0][0] + physical[1][1] + physical[2][2]
    totals = []
    for column in range(3):
        stress = [
            viscosity * (physical[member][column] + physical[column][member]) for member in range(3)
        ]
        stress[column] = stress[column] - 2.0 / 3.0 * viscosity * spread
        subdomain_parts = [conserved_solution[1 + column]]
        for member in range(3):
            carried = conserved_solution[1 + member] * fluid_speed_vector[column] - stress[member]
            if member == column:
                carried = carried + thermodynamic_stress_scalar
            subdomain_parts.append(carried)
        worked = (
            fluid_speed_vector[0] * stress[0]
            + fluid_speed_vector[1] * stress[1]
            + fluid_speed_vector[2] * stress[2]
        )
        subdomain_parts.append(
            (conserved_solution[4] + thermodynamic_stress_scalar) * fluid_speed_vector[column]
            - worked
            - conduction * physical[3][column]
        )
        totals.append(jnp.stack(subdomain_parts))
    return [
        metrics[direction, 0] * totals[0]
        + metrics[direction, 1] * totals[1]
        + metrics[direction, 2] * totals[2]
        for direction in range(3)
    ]


def local(conserved_solution, metrics, jacobian):
    lengths = conserved_solution.shape[1:]
    derive = [jnp.asarray(derivative_table(length), dtype=jnp.float32) for length in lengths]
    smooth = [jnp.asarray(filter_table(length), dtype=jnp.float32) for length in lengths]
    padded = exchange_primitive(conserved_solution, derive[2], 0)
    slopes = [sweep_lines(padded[k], derive[k], k + 1, lax.Precision.HIGH) for k in range(2)]
    slopes.append(padded[2])
    fluid_speed_vector, thermodynamic_stress_scalar = padded[3][0:3], padded[4]
    contra = fluxes(
        conserved_solution,
        fluid_speed_vector,
        thermodynamic_stress_scalar,
        slopes,
        metrics,
        jacobian,
    )
    padded = exchange_faces([(contra[0], "xi", 1), (contra[1], "eta", 2)], 1, (contra[2], derive[2]))
    divergence = sweep_lines(padded[0], derive[0], 1, lax.Precision.HIGH)
    divergence = divergence + sweep_lines(padded[1], derive[1], 2, lax.Precision.HIGH)
    divergence = divergence + padded[2]
    sectioned = conserved_solution - step_duration * jacobian * divergence
    result = sweep_lines(exchange_plane(sectioned, 2), smooth[0], 1)
    result = sweep_lines(result, smooth[1], 2)
    result = sweep_zeta(result, smooth[2], 4)
    return result


def solution(mesh):
    in_specs = (
        P(None, "xi", "eta", "zeta"),
        P(None, None, "xi", "eta", "zeta"),
        P("xi", "eta", "zeta"),
    )
    out_specs = P(None, "xi", "eta", "zeta")
    return jax.shard_map(local, mesh=mesh, in_specs=in_specs, out_specs=out_specs, check_vma=False)
```

```python
import functools

import jax
import jax.numpy as jnp
import numpy as np
from jax import lax
from jax.experimental import pallas as pl
from jax.experimental.pallas import tpu as pltpu
from jax.sharding import PartitionSpec as P

WIDTH = 5


viscosity = 0.15
conduction = 0.15 * 1.4 / (0.4 * 0.72)
step_duration = 0.08
line_forms = ("", "al,flyz->fayz", "al,fxlz->fxaz", "al,fxyl->fxya")
MESH = pl.DeviceIdType.MESH
AXES = ("xi", "eta", "zeta")


def primitive_state(conserved):
    density = conserved[0]
    speed = conserved[1:4] / density
    pressure = 0.4 * (conserved[4] - 0.5 * jnp.sum(conserved[1:4] * speed, axis=0))
    return speed, pressure, pressure / density


def exchange_kernel(routes, sizes, count, zeta, prepare, precision, moves, *refs):
    sources = list(refs[:count])
    refs = refs[count:]
    if prepare:
        conserved_ref = sources.pop()
    if zeta:
        if not prepare:
            block_ref = refs[0]
            refs = refs[1:]
        middle_ref, lower_ref, upper_ref = refs[:3]
        refs = refs[3:]
    extra = (1 if zeta else 0) + (2 if prepare else 0)
    targets = refs[: len(refs) - 3 - (3 if zeta else 0) - extra]
    refs = refs[len(targets) :]
    if zeta:
        out_ref = refs[0]
        refs = refs[1:]
    if prepare:
        made, pressure_ref = refs[:2]
        refs = refs[2:]
        sources.append(made)
        if zeta:
            block_ref = made
    if zeta:
        turned, before, after = refs[:3]
        refs = refs[3:]
    send_sems, recv_sems, move_sems = refs
    here = [lax.axis_index(axis) for axis in AXES]

    def device(offset):
        return tuple(
            lax.rem(here[slot] + offset[slot] + sizes[slot], sizes[slot]) for slot in range(3)
        )

    offsets = [route[0] for route in routes] + ([(0, 0, 1), (0, 0, -1)] if zeta else [])
    partners = []
    for offset in offsets:
        for way in (offset, tuple(-step for step in offset)):
            if way not in partners:
                partners.append(way)
    barrier = pltpu.get_barrier_semaphore()
    for offset in partners:
        pl.semaphore_signal(barrier, inc=1, device_id=device(offset), device_id_type=MESH)
    if prepare:
        speed, pressure, temperature = primitive_state(conserved_ref[...])
        made[0:3] = speed
        made[3] = temperature
        pressure_ref[...] = pressure
    if zeta:
        fields, length_x, length_y, depth = block_ref.shape
        rows = fields * length_x * length_y
        turned[...] = block_ref[...].reshape(rows, depth).T
        total = jnp.dot(middle_ref[...], turned[...], precision=precision,
                        preferred_element_type=jnp.float32)
    local = []
    for index, (source, source_at, target, target_at) in enumerate(moves):
        local.append(
            pltpu.make_async_copy(
                sources[source].at[source_at], targets[target].at[target_at], move_sems.at[index]
            )
        )
        local[-1].start()
    pl.semaphore_wait(barrier, len(partners))
    copies = []
    for index, (offset, source, source_at, target, target_at) in enumerate(routes):
        copies.append(
            pltpu.make_async_remote_copy(
                src_ref=sources[source].at[source_at],
                dst_ref=targets[target].at[target_at],
                send_sem=send_sems.at[index],
                recv_sem=recv_sems.at[index],
                device_id=device(offset),
                device_id_type=MESH,
            )
        )
    if zeta:
        for index, (rows_at, landing, offset) in enumerate(
            ((pl.ds(depth - 8, 8), before, (0, 0, 1)), (pl.ds(0, 8), after, (0, 0, -1)))
        ):
            copies.append(
                pltpu.make_async_remote_copy(
                    src_ref=turned.at[rows_at],
                    dst_ref=landing,
                    send_sem=send_sems.at[len(routes) + index],
                    recv_sem=recv_sems.at[len(routes) + index],
                    device_id=device(offset),
                    device_id_type=MESH,
                )
            )
    for copy in copies:
        copy.start()
    for copy in copies + local:
        copy.wait()
    if zeta:
        total = total + jnp.dot(lower_ref[...], before[...], precision=precision,
                                preferred_element_type=jnp.float32)
        total = total + jnp.dot(upper_ref[...], after[...], precision=precision,
                                preferred_element_type=jnp.float32)
        out_ref[...] = total.T.reshape(fields, length_x, length_y, depth)


def exchange(arrays, routes, out_shapes, tag, zeta=None, prepare=None,
             precision=lax.Precision.HIGH, moves=()):
    sizes = tuple(lax.axis_size(axis) for axis in AXES)
    operands = [array for array, _ in arrays]
    in_specs = [pl.BlockSpec(memory_space=space) for _, space in arrays]
    out_specs = [pl.BlockSpec(memory_space=pl.ANY)] * len(out_shapes)
    out_shapes = list(out_shapes)
    scratch = []
    copies = len(routes)
    if prepare is not None:
        operands.append(prepare)
        in_specs.append(pl.BlockSpec(memory_space=pltpu.VMEM))
    if zeta is not None:
        value, matrix = zeta
        fields, length_x, length_y, depth = value.shape
        rows = fields * length_x * length_y
        padding = jnp.zeros((depth, 8 - WIDTH), matrix.dtype)
        if prepare is None:
            operands.append(value)
            in_specs.append(pl.BlockSpec(memory_space=pltpu.VMEM))
        operands += [
            matrix[:, WIDTH : WIDTH + depth],
            jnp.concatenate([padding, matrix[:, :WIDTH]], axis=1),
            jnp.concatenate([matrix[:, WIDTH + depth :], padding], axis=1),
        ]
        in_specs += [pl.BlockSpec(memory_space=pltpu.VMEM)] * 3
        out_shapes.append(jax.ShapeDtypeStruct(value.shape, value.dtype))
        out_specs.append(pl.BlockSpec(memory_space=pltpu.VMEM))
        scratch = [pltpu.VMEM((depth, rows), jnp.float32), pltpu.VMEM((8, rows), jnp.float32),
                   pltpu.VMEM((8, rows), jnp.float32)]
        copies += 2
    if prepare is not None:
        out_shapes += [
            jax.ShapeDtypeStruct(zeta[0].shape, jnp.float32),
            jax.ShapeDtypeStruct(prepare.shape[1:], jnp.float32),
        ]
        out_specs += [pl.BlockSpec(memory_space=pltpu.VMEM)] * 2
    return pl.pallas_call(
        functools.partial(
            exchange_kernel, tuple(routes), sizes, len(arrays) + (prepare is not None),
            zeta is not None, prepare is not None, precision, tuple(moves),
        ),
        out_shape=out_shapes,
        in_specs=in_specs,
        out_specs=out_specs,
        scratch_shapes=scratch + [
            pltpu.SemaphoreType.DMA((copies,)),
            pltpu.SemaphoreType.DMA((copies,)),
            pltpu.SemaphoreType.DMA((max(1, len(moves)),)),
        ],
        compiler_params=pltpu.CompilerParams(collective_id=tag, has_side_effects=True),
    )(*operands)


def offset_along(axis, step):
    return tuple(step if name == axis else 0 for name in AXES)


def window(ndim, dim, start, stop):
    return tuple(slice(start, stop) if axis == dim else slice(None) for axis in range(ndim))


def exchange_faces(items, tag, zeta=None):
    arrays, routes, out_shapes, moves = [], [], [], []
    for value, axis, dim in items:
        ndim, length = value.ndim, value.shape[dim]
        if dim == ndim - 1:
            both = jnp.stack(
                [
                    lax.slice_in_dim(value, length - WIDTH, length, axis=dim),
                    lax.slice_in_dim(value, 0, WIDTH, axis=dim),
                ]
            )
            both = jnp.moveaxis(both, dim + 1, 2).reshape(2, value.shape[0], WIDTH, -1)
            arrays.append((both, pl.ANY))
            out_shapes.append(jax.ShapeDtypeStruct(both.shape, both.dtype))
            source, target = len(arrays) - 1, len(out_shapes) - 1
            routes.append((offset_along(axis, 1), source, 0, target, 0))
            routes.append((offset_along(axis, -1), source, 1, target, 1))
        elif dim == ndim - 2:
            face = value.shape[:dim] + (WIDTH,) + value.shape[dim + 1 :]
            arrays.append((value, pltpu.VMEM))
            out_shapes += [jax.ShapeDtypeStruct(face, value.dtype)] * 2
            source, target = len(arrays) - 1, len(out_shapes) - 2
            whole = window(ndim, dim, None, None)
            last, first = window(ndim, dim, length - WIDTH, length), window(ndim, dim, 0, WIDTH)
            routes.append((offset_along(axis, 1), source, last, target, whole))
            routes.append((offset_along(axis, -1), source, first, target + 1, whole))
        else:
            arrays += [(value, pl.ANY), (value, pltpu.VMEM)]
            extended = value.shape[:dim] + (length + 2 * WIDTH,) + value.shape[dim + 1 :]
            out_shapes.append(jax.ShapeDtypeStruct(extended, value.dtype))
            source, target = len(arrays) - 2, len(out_shapes) - 1
            last, first = window(ndim, dim, length - WIDTH, length), window(ndim, dim, 0, WIDTH)
            ahead = window(ndim, dim, length + WIDTH, length + 2 * WIDTH)
            routes.append((offset_along(axis, 1), source, last, target, first))
            routes.append((offset_along(axis, -1), source, first, target, ahead))
            moves.append((source + 1, window(ndim, dim, None, None), target,
                          window(ndim, dim, WIDTH, length + WIDTH)))
    received = exchange(arrays, routes, out_shapes, tag, zeta, moves=moves)
    padded, place = [], 0
    for value, axis, dim in items:
        if dim == value.ndim - 1:
            both = received[place].reshape((2, value.shape[0], WIDTH) + value.shape[1:dim])
            both = jnp.moveaxis(both, 2, dim + 1)
            before, after = both[0], both[1]
            place += 1
        elif dim == value.ndim - 2:
            before, after = received[place], received[place + 1]
            place += 2
        else:
            padded.append(received[place])
            place += 1
            continue
        padded.append(jnp.concatenate([before, value, after], axis=dim))
    if zeta is not None:
        padded.append(received[-1])
    return padded


def exchange_primitive(conserved, matrix, tag):
    primitive = jax.ShapeDtypeStruct((4,) + conserved.shape[1:], conserved.dtype)
    length_x, length_y = primitive.shape[1], primitive.shape[2]
    every = slice(None)
    routes = [
        ((1, 0, 0), 0, (every, slice(length_x - WIDTH, length_x)), 0, (every, slice(0, WIDTH))),
        ((-1, 0, 0), 0, (every, slice(0, WIDTH)), 0, (every, slice(length_x + WIDTH, length_x + 2 * WIDTH))),
        ((0, 1, 0), 0, (every, every, slice(length_y - WIDTH, length_y)), 1, every),
        ((0, -1, 0), 0, (every, every, slice(0, WIDTH)), 2, every),
    ]
    moves = [(0, every, 0, (every, slice(WIDTH, length_x + WIDTH)))]
    extended_x = (primitive.shape[0], length_x + 2 * WIDTH) + primitive.shape[2:]
    face_y = primitive.shape[:2] + (WIDTH,) + primitive.shape[3:]
    out_shapes = [jax.ShapeDtypeStruct(face, primitive.dtype) for face in (extended_x, face_y, face_y)]
    padded_x, before_y, after_y, swept, primitive, pressure = exchange(
        [], routes, out_shapes, tag, (primitive, matrix), conserved, moves=moves
    )
    return (
        padded_x,
        jnp.concatenate([before_y, primitive, after_y], axis=2),
        swept,
        primitive,
        pressure,
    )


def exchange_plane(value, tag):
    length_x, length_y = value.shape[1], value.shape[2]
    faces_y = jnp.stack(
        [
            lax.slice_in_dim(value, length_y - WIDTH, length_y, axis=2),
            lax.slice_in_dim(value, 0, WIDTH, axis=2),
        ]
    )
    last_x, first_x = slice(length_x - WIDTH, length_x), slice(0, WIDTH)
    every = slice(None)
    routes = [
        ((1, 0, 0), 0, (every, last_x), 0, every),
        ((-1, 0, 0), 0, (every, first_x), 1, every),
        ((0, 1, 0), 1, 0, 2, every),
        ((0, -1, 0), 1, 1, 3, every),
        ((1, 1, 0), 1, (0, every, last_x), 4, every),
        ((-1, 1, 0), 1, (0, every, first_x), 5, every),
        ((1, -1, 0), 1, (1, every, last_x), 6, every),
        ((-1, -1, 0), 1, (1, every, first_x), 7, every),
    ]
    fields, depth = value.shape[0], value.shape[3]
    out_shapes = (
        [jax.ShapeDtypeStruct((fields, WIDTH, length_y, depth), value.dtype)] * 2
        + [jax.ShapeDtypeStruct((fields, length_x, WIDTH, depth), value.dtype)] * 2
        + [jax.ShapeDtypeStruct((fields, WIDTH, WIDTH, depth), value.dtype)] * 4
    )
    x_before, x_after, y_before, y_after, both_before, x_after_y_before, x_before_y_after, both_after = (
        exchange([(value, pl.ANY), (faces_y, pl.ANY)], routes, out_shapes, tag)
    )
    sections = [
        jnp.concatenate([both_before, x_before, x_before_y_after], axis=2),
        jnp.concatenate([y_before, value, y_after], axis=2),
        jnp.concatenate([x_after_y_before, x_after, both_after], axis=2),
    ]
    return jnp.concatenate(sections, axis=1)


def sweep_zeta(value, matrix, tag):
    return exchange([], [], [], tag, (value, matrix), precision=lax.Precision.HIGHEST)[-1]


def with_halo(value, sides, width):
    for axis, dim in sides:
        count, length = (lax.axis_size(axis), value.shape[dim])
        up = [(i, (i + 1) % count) for i in range(count)]
        down = [(j, i) for i, j in up]
        last = lax.slice_in_dim(value, length - width, length, axis=dim)
        initial = lax.slice_in_dim(value, 0, width, axis=dim)
        before = lax.ppermute(last, axis, up)
        after = lax.ppermute(initial, axis, down)
        value = jnp.concatenate([before, value, after], axis=dim)
    return value


def banded_solve(system, source):
    extent = system.shape[0]
    lower = np.zeros(extent)
    upper = np.zeros(extent)
    middle = np.array([float(system[index, index]) for index in range(extent)])
    for index in range(1, extent):
        lower[index] = system[index, index - 1]
        upper[index - 1] = system[index - 1, index]
    rights = np.array(source)
    for index in range(1, extent):
        factor = lower[index] / middle[index - 1]
        middle[index] = middle[index] - factor * upper[index - 1]
        rights[index] = rights[index] - factor * rights[index - 1]
    answer = np.zeros(rights.shape)
    answer[extent - 1] = rights[extent - 1] / middle[extent - 1]
    for index in range(extent - 2, -1, -1):
        answer[index] = (rights[index] - upper[index] * answer[index + 1]) / middle[index]
    return answer


def derivative_table(length):
    extent = length + 2 * WIDTH
    system = np.eye(extent)
    source = np.zeros((extent, extent))
    for position in range(2, extent - 2):
        system[position, position - 1] = 1.0 / 3.0
        system[position, position + 1] = 1.0 / 3.0
        source[position, position + 1] = 7.0 / 9.0
        source[position, position - 1] = -7.0 / 9.0
        source[position, position + 2] = 1.0 / 36.0
        source[position, position - 2] = -1.0 / 36.0
    source[1, 2] = 0.5
    source[1, 0] = -0.5
    source[extent - 2, extent - 1] = 0.5
    source[extent - 2, extent - 3] = -0.5
    source[0, 1] = 1.0
    source[0, 0] = -1.0
    source[extent - 1, extent - 1] = 1.0
    source[extent - 1, extent - 2] = -1.0
    return banded_solve(system, source)[WIDTH : WIDTH + length]


def filter_table(length):
    strength = 0.4
    coeffs = [
        (193.0 + 126.0 * strength) / 256.0,
        (105.0 + 302.0 * strength) / 256.0,
        15.0 * (2.0 * strength - 1.0) / 64.0,
        45.0 * (1.0 - 2.0 * strength) / 512.0,
        5.0 * (2.0 * strength - 1.0) / 256.0,
        (1.0 - 2.0 * strength) / 512.0,
    ]
    extent = length + 2 * WIDTH
    system = np.eye(extent)
    source = np.eye(extent)
    for position in range(5, extent - 5):
        system[position, position - 1] = strength
        system[position, position + 1] = strength
        source[position, position] = coeffs[0]
        for offset in range(1, 6):
            source[position, position + offset] = coeffs[offset] / 2.0
            source[position, position - offset] = coeffs[offset] / 2.0
    return banded_solve(system, source)[WIDTH : WIDTH + length]


def sweep_lines(padded, matrix, dim, precision=lax.Precision.HIGHEST):
    return jnp.einsum(line_forms[dim], matrix, padded, precision=precision)


def faces_xi(values):
    return with_halo(values, (("xi", 1),), WIDTH)


def faces_eta(values):
    return with_halo(values, (("eta", 2),), WIDTH)


def faces_zeta(values):
    return with_halo(values, (("zeta", 3),), WIDTH)


def basic_quantities(conserved_solution):
    density = conserved_solution[0]
    fluid_speed_vector = conserved_solution[1:4] / density
    thermodynamic_stress_scalar = 0.4 * (
        conserved_solution[4] - 0.5 * jnp.sum(conserved_solution[1:4] * fluid_speed_vector, axis=0)
    )
    return (fluid_speed_vector, thermodynamic_stress_scalar, thermodynamic_stress_scalar / density)


def fluxes(
    conserved_solution, fluid_speed_vector, thermodynamic_stress_scalar, slopes, metrics, jacobian
):
    physical = [
        [
            jacobian
            * (
                metrics[0, column] * slopes[0][member]
                + metrics[1, column] * slopes[1][member]
                + metrics[2, column] * slopes[2][member]
            )
            for column in range(3)
        ]
        for member in range(4)
    ]
    spread = physical[0][0] + physical[1][1] + physical[2][2]
    totals = []
    for column in range(3):
        stress = [
            viscosity * (physical[member][column] + physical[column][member]) for member in range(3)
        ]
        stress[column] = stress[column] - 2.0 / 3.0 * viscosity * spread
        subdomain_parts = [conserved_solution[1 + column]]
        for member in range(3):
            carried = conserved_solution[1 + member] * fluid_speed_vector[column] - stress[member]
            if member == column:
                carried = carried + thermodynamic_stress_scalar
            subdomain_parts.append(carried)
        worked = (
            fluid_speed_vector[0] * stress[0]
            + fluid_speed_vector[1] * stress[1]
            + fluid_speed_vector[2] * stress[2]
        )
        subdomain_parts.append(
            (conserved_solution[4] + thermodynamic_stress_scalar) * fluid_speed_vector[column]
            - worked
            - conduction * physical[3][column]
        )
        totals.append(jnp.stack(subdomain_parts))
    return [
        metrics[direction, 0] * totals[0]
        + metrics[direction, 1] * totals[1]
        + metrics[direction, 2] * totals[2]
        for direction in range(3)
    ]


def local(conserved_solution, metrics, jacobian):
    lengths = conserved_solution.shape[1:]
    derive = [jnp.asarray(derivative_table(length), dtype=jnp.float32) for length in lengths]
    smooth = [jnp.asarray(filter_table(length), dtype=jnp.float32) for length in lengths]
    padded = exchange_primitive(conserved_solution, derive[2], 0)
    slopes = [sweep_lines(padded[k], derive[k], k + 1, lax.Precision.HIGH) for k in range(2)]
    slopes.append(padded[2])
    fluid_speed_vector, thermodynamic_stress_scalar = padded[3][0:3], padded[4]
    contra = fluxes(
        conserved_solution,
        fluid_speed_vector,
        thermodynamic_stress_scalar,
        slopes,
        metrics,
        jacobian,
    )
    padded = exchange_faces([(contra[0], "xi", 1), (contra[1], "eta", 2)], 1, (contra[2], derive[2]))
    divergence = sweep_lines(padded[0], derive[0], 1, lax.Precision.HIGH)
    divergence = divergence + sweep_lines(padded[1], derive[1], 2, lax.Precision.HIGH)
    divergence = divergence + padded[2]
    sectioned = conserved_solution - step_duration * jacobian * divergence
    result = sweep_lines(exchange_plane(sectioned, 2), smooth[0], 1)
    result = sweep_lines(result, smooth[1], 2)
    result = sweep_zeta(result, smooth[2], 4)
    return result


def solution(mesh):
    in_specs = (
        P(None, "xi", "eta", "zeta"),
        P(None, None, "xi", "eta", "zeta"),
        P("xi", "eta", "zeta"),
    )
    out_specs = P(None, "xi", "eta", "zeta")
    return jax.shard_map(local, mesh=mesh, in_specs=in_specs, out_specs=out_specs, check_vma=False)
```

```python
import functools

import jax
import jax.numpy as jnp
import numpy as np
from jax import lax
from jax.experimental import pallas as pl
from jax.experimental.pallas import tpu as pltpu
from jax.sharding import PartitionSpec as P

WIDTH = 5


viscosity = 0.15
conduction = 0.15 * 1.4 / (0.4 * 0.72)
step_duration = 0.08
line_forms = ("", "al,flyz->fayz", "al,fxlz->fxaz", "al,fxyl->fxya")
MESH = pl.DeviceIdType.MESH
AXES = ("xi", "eta", "zeta")


def primitive_state(conserved):
    density = conserved[0]
    speed = conserved[1:4] / density
    pressure = 0.4 * (conserved[4] - 0.5 * jnp.sum(conserved[1:4] * speed, axis=0))
    return speed, pressure, pressure / density


def exchange_kernel(routes, sizes, count, zeta, prepare, precision, moves, *refs):
    sources = list(refs[:count])
    refs = refs[count:]
    if prepare:
        conserved_ref = sources.pop()
    if zeta:
        if not prepare:
            block_ref = refs[0]
            refs = refs[1:]
        middle_ref, lower_ref, upper_ref = refs[:3]
        refs = refs[3:]
    extra = (1 if zeta else 0) + (2 if prepare else 0)
    targets = refs[: len(refs) - 3 - (3 if zeta else 0) - extra]
    refs = refs[len(targets) :]
    if zeta:
        out_ref = refs[0]
        refs = refs[1:]
    if prepare:
        made, pressure_ref = refs[:2]
        refs = refs[2:]
        sources.append(made)
        if zeta:
            block_ref = made
    if zeta:
        turned, before, after = refs[:3]
        refs = refs[3:]
    send_sems, recv_sems, move_sems = refs
    here = [lax.axis_index(axis) for axis in AXES]

    def device(offset):
        return tuple(
            lax.rem(here[slot] + offset[slot] + sizes[slot], sizes[slot]) for slot in range(3)
        )

    offsets = [route[0] for route in routes] + ([(0, 0, 1), (0, 0, -1)] if zeta else [])
    partners = []
    for offset in offsets:
        for way in (offset, tuple(-step for step in offset)):
            if way not in partners:
                partners.append(way)
    barrier = pltpu.get_barrier_semaphore()
    for offset in partners:
        pl.semaphore_signal(barrier, inc=1, device_id=device(offset), device_id_type=MESH)
    if prepare:
        speed, pressure, temperature = primitive_state(conserved_ref[...])
        made[0:3] = speed
        made[3] = temperature
        pressure_ref[...] = pressure
    if zeta:
        fields, length_x, length_y, depth = block_ref.shape
        rows = fields * length_x * length_y
        turned[...] = block_ref[...].reshape(rows, depth).T
        total = jnp.dot(middle_ref[...], turned[...], precision=precision,
                        preferred_element_type=jnp.float32)
    local = []
    for index, (source, source_at, target, target_at) in enumerate(moves):
        local.append(
            pltpu.make_async_copy(
                sources[source].at[source_at], targets[target].at[target_at], move_sems.at[index]
            )
        )
        local[-1].start()
    pl.semaphore_wait(barrier, len(partners))
    copies = []
    for index, (offset, source, source_at, target, target_at) in enumerate(routes):
        copies.append(
            pltpu.make_async_remote_copy(
                src_ref=sources[source].at[source_at],
                dst_ref=targets[target].at[target_at],
                send_sem=send_sems.at[index],
                recv_sem=recv_sems.at[index],
                device_id=device(offset),
                device_id_type=MESH,
            )
        )
    if zeta:
        for index, (rows_at, landing, offset) in enumerate(
            ((pl.ds(depth - 8, 8), before, (0, 0, 1)), (pl.ds(0, 8), after, (0, 0, -1)))
        ):
            copies.append(
                pltpu.make_async_remote_copy(
                    src_ref=turned.at[rows_at],
                    dst_ref=landing,
                    send_sem=send_sems.at[len(routes) + index],
                    recv_sem=recv_sems.at[len(routes) + index],
                    device_id=device(offset),
                    device_id_type=MESH,
                )
            )
    for copy in copies:
        copy.start()
    for copy in copies + local:
        copy.wait()
    if zeta:
        total = total + jnp.dot(lower_ref[...], before[...], precision=precision,
                                preferred_element_type=jnp.float32)
        total = total + jnp.dot(upper_ref[...], after[...], precision=precision,
                                preferred_element_type=jnp.float32)
        out_ref[...] = total.T.reshape(fields, length_x, length_y, depth)


def exchange(arrays, routes, out_shapes, tag, zeta=None, prepare=None,
             precision=lax.Precision.HIGH, moves=()):
    sizes = tuple(lax.axis_size(axis) for axis in AXES)
    operands = [array for array, _ in arrays]
    in_specs = [pl.BlockSpec(memory_space=space) for _, space in arrays]
    out_specs = [pl.BlockSpec(memory_space=pl.ANY)] * len(out_shapes)
    out_shapes = list(out_shapes)
    scratch = []
    copies = len(routes)
    if prepare is not None:
        operands.append(prepare)
        in_specs.append(pl.BlockSpec(memory_space=pltpu.VMEM))
    if zeta is not None:
        value, matrix = zeta
        fields, length_x, length_y, depth = value.shape
        rows = fields * length_x * length_y
        padding = jnp.zeros((depth, 8 - WIDTH), matrix.dtype)
        if prepare is None:
            operands.append(value)
            in_specs.append(pl.BlockSpec(memory_space=pltpu.VMEM))
        operands += [
            matrix[:, WIDTH : WIDTH + depth],
            jnp.concatenate([padding, matrix[:, :WIDTH]], axis=1),
            jnp.concatenate([matrix[:, WIDTH + depth :], padding], axis=1),
        ]
        in_specs += [pl.BlockSpec(memory_space=pltpu.VMEM)] * 3
        out_shapes.append(jax.ShapeDtypeStruct(value.shape, value.dtype))
        out_specs.append(pl.BlockSpec(memory_space=pltpu.VMEM))
        scratch = [pltpu.VMEM((depth, rows), jnp.float32), pltpu.VMEM((8, rows), jnp.float32),
                   pltpu.VMEM((8, rows), jnp.float32)]
        copies += 2
    if prepare is not None:
        out_shapes += [
            jax.ShapeDtypeStruct(zeta[0].shape, jnp.float32),
            jax.ShapeDtypeStruct(prepare.shape[1:], jnp.float32),
        ]
        out_specs += [pl.BlockSpec(memory_space=pltpu.VMEM)] * 2
    return pl.pallas_call(
        functools.partial(
            exchange_kernel, tuple(routes), sizes, len(arrays) + (prepare is not None),
            zeta is not None, prepare is not None, precision, tuple(moves),
        ),
        out_shape=out_shapes,
        in_specs=in_specs,
        out_specs=out_specs,
        scratch_shapes=scratch + [
            pltpu.SemaphoreType.DMA((copies,)),
            pltpu.SemaphoreType.DMA((copies,)),
            pltpu.SemaphoreType.DMA((max(1, len(moves)),)),
        ],
        compiler_params=pltpu.CompilerParams(collective_id=tag, has_side_effects=True),
    )(*operands)


def offset_along(axis, step):
    return tuple(step if name == axis else 0 for name in AXES)


def window(ndim, dim, start, stop):
    return tuple(slice(start, stop) if axis == dim else slice(None) for axis in range(ndim))


def exchange_faces(items, tag, zeta=None):
    arrays, routes, out_shapes, moves = [], [], [], []
    for value, axis, dim in items:
        ndim, length = value.ndim, value.shape[dim]
        if dim == ndim - 1:
            both = jnp.stack(
                [
                    lax.slice_in_dim(value, length - WIDTH, length, axis=dim),
                    lax.slice_in_dim(value, 0, WIDTH, axis=dim),
                ]
            )
            both = jnp.moveaxis(both, dim + 1, 2).reshape(2, value.shape[0], WIDTH, -1)
            arrays.append((both, pl.ANY))
            out_shapes.append(jax.ShapeDtypeStruct(both.shape, both.dtype))
            source, target = len(arrays) - 1, len(out_shapes) - 1
            routes.append((offset_along(axis, 1), source, 0, target, 0))
            routes.append((offset_along(axis, -1), source, 1, target, 1))
        elif dim == ndim - 2:
            face = value.shape[:dim] + (WIDTH,) + value.shape[dim + 1 :]
            arrays.append((value, pltpu.VMEM))
            out_shapes += [jax.ShapeDtypeStruct(face, value.dtype)] * 2
            source, target = len(arrays) - 1, len(out_shapes) - 2
            whole = window(ndim, dim, None, None)
            last, first = window(ndim, dim, length - WIDTH, length), window(ndim, dim, 0, WIDTH)
            routes.append((offset_along(axis, 1), source, last, target, whole))
            routes.append((offset_along(axis, -1), source, first, target + 1, whole))
        else:
            arrays += [(value, pl.ANY), (value, pltpu.VMEM)]
            extended = value.shape[:dim] + (length + 2 * WIDTH,) + value.shape[dim + 1 :]
            out_shapes.append(jax.ShapeDtypeStruct(extended, value.dtype))
            source, target = len(arrays) - 2, len(out_shapes) - 1
            last, first = window(ndim, dim, length - WIDTH, length), window(ndim, dim, 0, WIDTH)
            ahead = window(ndim, dim, length + WIDTH, length + 2 * WIDTH)
            routes.append((offset_along(axis, 1), source, last, target, first))
            routes.append((offset_along(axis, -1), source, first, target, ahead))
            moves.append((source + 1, window(ndim, dim, None, None), target,
                          window(ndim, dim, WIDTH, length + WIDTH)))
    received = exchange(arrays, routes, out_shapes, tag, zeta, moves=moves)
    padded, place = [], 0
    for value, axis, dim in items:
        if dim == value.ndim - 1:
            both = received[place].reshape((2, value.shape[0], WIDTH) + value.shape[1:dim])
            both = jnp.moveaxis(both, 2, dim + 1)
            before, after = both[0], both[1]
            place += 1
        elif dim == value.ndim - 2:
            before, after = received[place], received[place + 1]
            place += 2
        else:
            padded.append(received[place])
            place += 1
            continue
        padded.append(jnp.concatenate([before, value, after], axis=dim))
    if zeta is not None:
        padded.append(received[-1])
    return padded


def exchange_primitive(conserved, matrix, tag):
    primitive = jax.ShapeDtypeStruct((4,) + conserved.shape[1:], conserved.dtype)
    length_x, length_y = primitive.shape[1], primitive.shape[2]
    every = slice(None)
    routes = [
        ((1, 0, 0), 0, (every, slice(length_x - WIDTH, length_x)), 0, (every, slice(0, WIDTH))),
        ((-1, 0, 0), 0, (every, slice(0, WIDTH)), 0, (every, slice(length_x + WIDTH, length_x + 2 * WIDTH))),
        ((0, 1, 0), 0, (every, every, slice(length_y - WIDTH, length_y)), 1, every),
        ((0, -1, 0), 0, (every, every, slice(0, WIDTH)), 2, every),
    ]
    moves = [(0, every, 0, (every, slice(WIDTH, length_x + WIDTH)))]
    extended_x = (primitive.shape[0], length_x + 2 * WIDTH) + primitive.shape[2:]
    face_y = primitive.shape[:2] + (WIDTH,) + primitive.shape[3:]
    out_shapes = [jax.ShapeDtypeStruct(face, primitive.dtype) for face in (extended_x, face_y, face_y)]
    padded_x, before_y, after_y, swept, primitive, pressure = exchange(
        [], routes, out_shapes, tag, (primitive, matrix), conserved, moves=moves
    )
    return (
        padded_x,
        jnp.concatenate([before_y, primitive, after_y], axis=2),
        swept,
        primitive,
        pressure,
    )


def exchange_plane(value, tag):
    length_x, length_y = value.shape[1], value.shape[2]
    faces_y = jnp.stack(
        [
            lax.slice_in_dim(value, length_y - WIDTH, length_y, axis=2),
            lax.slice_in_dim(value, 0, WIDTH, axis=2),
        ]
    )
    last_x, first_x = slice(length_x - WIDTH, length_x), slice(0, WIDTH)
    every = slice(None)
    routes = [
        ((1, 0, 0), 0, (every, last_x), 0, every),
        ((-1, 0, 0), 0, (every, first_x), 1, every),
        ((0, 1, 0), 1, 0, 2, every),
        ((0, -1, 0), 1, 1, 3, every),
        ((1, 1, 0), 1, (0, every, last_x), 4, every),
        ((-1, 1, 0), 1, (0, every, first_x), 5, every),
        ((1, -1, 0), 1, (1, every, last_x), 6, every),
        ((-1, -1, 0), 1, (1, every, first_x), 7, every),
    ]
    fields, depth = value.shape[0], value.shape[3]
    out_shapes = (
        [jax.ShapeDtypeStruct((fields, WIDTH, length_y, depth), value.dtype)] * 2
        + [jax.ShapeDtypeStruct((fields, length_x, WIDTH, depth), value.dtype)] * 2
        + [jax.ShapeDtypeStruct((fields, WIDTH, WIDTH, depth), value.dtype)] * 4
    )
    x_before, x_after, y_before, y_after, both_before, x_after_y_before, x_before_y_after, both_after = (
        exchange([(value, pl.ANY), (faces_y, pl.ANY)], routes, out_shapes, tag)
    )
    sections = [
        jnp.concatenate([both_before, x_before, x_before_y_after], axis=2),
        jnp.concatenate([y_before, value, y_after], axis=2),
        jnp.concatenate([x_after_y_before, x_after, both_after], axis=2),
    ]
    return jnp.concatenate(sections, axis=1)


def filter_kernel(sizes, value_ref, middle_ref, lower_ref, upper_ref, smooth_ref, *refs):
    faces = refs[:8]
    turned, before, after, stacked, send_sems, recv_sems = refs[8:]
    fields, length_x, length_y, depth = value_ref.shape
    rows = fields * length_x * length_y
    here = [lax.axis_index(axis) for axis in AXES]

    def device(offset):
        return tuple(
            lax.rem(here[slot] + offset[slot] + sizes[slot], sizes[slot]) for slot in range(3)
        )

    plane = [(1, 0, 0), (-1, 0, 0), (0, 1, 0), (0, -1, 0), (1, 1, 0), (-1, 1, 0), (1, -1, 0), (-1, -1, 0)]
    partners = plane + [(0, 0, 1), (0, 0, -1)]
    barrier = pltpu.get_barrier_semaphore()
    for offset in partners:
        pl.semaphore_signal(barrier, inc=1, device_id=device(offset), device_id_type=MESH)
    turned[...] = value_ref[...].reshape(rows, depth).T
    total = jnp.dot(middle_ref[...], turned[...], precision=lax.Precision.HIGHEST,
                    preferred_element_type=jnp.float32)
    pl.semaphore_wait(barrier, len(partners))
    along_z = [
        pltpu.make_async_remote_copy(
            src_ref=turned.at[pl.ds(depth - 8, 8)], dst_ref=before,
            send_sem=send_sems.at[8], recv_sem=recv_sems.at[8],
            device_id=device((0, 0, 1)), device_id_type=MESH,
        ),
        pltpu.make_async_remote_copy(
            src_ref=turned.at[pl.ds(0, 8)], dst_ref=after,
            send_sem=send_sems.at[9], recv_sem=recv_sems.at[9],
            device_id=device((0, 0, -1)), device_id_type=MESH,
        ),
    ]
    for copy in along_z:
        copy.start()
    for copy in along_z:
        copy.wait()
    total = total + jnp.dot(lower_ref[...], before[...], precision=lax.Precision.HIGHEST,
                            preferred_element_type=jnp.float32)
    total = total + jnp.dot(upper_ref[...], after[...], precision=lax.Precision.HIGHEST,
                            preferred_element_type=jnp.float32)
    smooth_ref[...] = total.T.reshape(fields, length_x, length_y, depth)
    stacked[0] = smooth_ref[:, :, length_y - WIDTH :, :]
    stacked[1] = smooth_ref[:, :, :WIDTH, :]
    last_x, first_x = pl.ds(length_x - WIDTH, WIDTH), pl.ds(0, WIDTH)
    every = slice(None)
    sources = [
        smooth_ref.at[every, last_x], smooth_ref.at[every, first_x],
        stacked.at[0], stacked.at[1],
        stacked.at[0, every, last_x], stacked.at[0, every, first_x],
        stacked.at[1, every, last_x], stacked.at[1, every, first_x],
    ]
    copies = []
    for index, offset in enumerate(plane):
        copies.append(
            pltpu.make_async_remote_copy(
                src_ref=sources[index], dst_ref=faces[index],
                send_sem=send_sems.at[index], recv_sem=recv_sems.at[index],
                device_id=device(offset), device_id_type=MESH,
            )
        )
        copies[-1].start()
    for copy in copies:
        copy.wait()


def filter_all(value, smooth, tag):
    sizes = tuple(lax.axis_size(axis) for axis in AXES)
    fields, length_x, length_y, depth = value.shape
    rows = fields * length_x * length_y
    matrix = smooth[2]
    padding = jnp.zeros((depth, 8 - WIDTH), matrix.dtype)
    x_face = jax.ShapeDtypeStruct((fields, WIDTH, length_y, depth), value.dtype)
    y_face = jax.ShapeDtypeStruct((fields, length_x, WIDTH, depth), value.dtype)
    edge = jax.ShapeDtypeStruct((fields, WIDTH, WIDTH, depth), value.dtype)
    outs = pl.pallas_call(
        functools.partial(filter_kernel, sizes),
        out_shape=[jax.ShapeDtypeStruct(value.shape, value.dtype)] + [x_face] * 2 + [y_face] * 2 + [edge] * 4,
        in_specs=[pl.BlockSpec(memory_space=pltpu.VMEM)] * 4,
        out_specs=[pl.BlockSpec(memory_space=pltpu.VMEM)] + [pl.BlockSpec(memory_space=pl.ANY)] * 8,
        scratch_shapes=[
            pltpu.VMEM((depth, rows), jnp.float32),
            pltpu.VMEM((8, rows), jnp.float32),
            pltpu.VMEM((8, rows), jnp.float32),
            pltpu.VMEM((2, fields, length_x, WIDTH, depth), jnp.float32),
            pltpu.SemaphoreType.DMA((10,)),
            pltpu.SemaphoreType.DMA((10,)),
        ],
        compiler_params=pltpu.CompilerParams(collective_id=tag, has_side_effects=True),
    )(
        value,
        matrix[:, WIDTH : WIDTH + depth],
        jnp.concatenate([padding, matrix[:, :WIDTH]], axis=1),
        jnp.concatenate([matrix[:, WIDTH + depth :], padding], axis=1),
    )
    smoothed, x_before, x_after, y_before, y_after, both_before, x_after_y_before, x_before_y_after, both_after = outs
    sections = [
        jnp.concatenate([both_before, x_before, x_before_y_after], axis=2),
        jnp.concatenate([y_before, smoothed, y_after], axis=2),
        jnp.concatenate([x_after_y_before, x_after, both_after], axis=2),
    ]
    result = sweep_lines(jnp.concatenate(sections, axis=1), smooth[0], 1)
    return sweep_lines(result, smooth[1], 2)


def sweep_zeta(value, matrix, tag):
    return exchange([], [], [], tag, (value, matrix), precision=lax.Precision.HIGHEST)[-1]


def with_halo(value, sides, width):
    for axis, dim in sides:
        count, length = (lax.axis_size(axis), value.shape[dim])
        up = [(i, (i + 1) % count) for i in range(count)]
        down = [(j, i) for i, j in up]
        last = lax.slice_in_dim(value, length - width, length, axis=dim)
        initial = lax.slice_in_dim(value, 0, width, axis=dim)
        before = lax.ppermute(last, axis, up)
        after = lax.ppermute(initial, axis, down)
        value = jnp.concatenate([before, value, after], axis=dim)
    return value


def banded_solve(system, source):
    extent = system.shape[0]
    lower = np.zeros(extent)
    upper = np.zeros(extent)
    middle = np.array([float(system[index, index]) for index in range(extent)])
    for index in range(1, extent):
        lower[index] = system[index, index - 1]
        upper[index - 1] = system[index - 1, index]
    rights = np.array(source)
    for index in range(1, extent):
        factor = lower[index] / middle[index - 1]
        middle[index] = middle[index] - factor * upper[index - 1]
        rights[index] = rights[index] - factor * rights[index - 1]
    answer = np.zeros(rights.shape)
    answer[extent - 1] = rights[extent - 1] / middle[extent - 1]
    for index in range(extent - 2, -1, -1):
        answer[index] = (rights[index] - upper[index] * answer[index + 1]) / middle[index]
    return answer


def derivative_table(length):
    extent = length + 2 * WIDTH
    system = np.eye(extent)
    source = np.zeros((extent, extent))
    for position in range(2, extent - 2):
        system[position, position - 1] = 1.0 / 3.0
        system[position, position + 1] = 1.0 / 3.0
        source[position, position + 1] = 7.0 / 9.0
        source[position, position - 1] = -7.0 / 9.0
        source[position, position + 2] = 1.0 / 36.0
        source[position, position - 2] = -1.0 / 36.0
    source[1, 2] = 0.5
    source[1, 0] = -0.5
    source[extent - 2, extent - 1] = 0.5
    source[extent - 2, extent - 3] = -0.5
    source[0, 1] = 1.0
    source[0, 0] = -1.0
    source[extent - 1, extent - 1] = 1.0
    source[extent - 1, extent - 2] = -1.0
    return banded_solve(system, source)[WIDTH : WIDTH + length]


def filter_table(length):
    strength = 0.4
    coeffs = [
        (193.0 + 126.0 * strength) / 256.0,
        (105.0 + 302.0 * strength) / 256.0,
        15.0 * (2.0 * strength - 1.0) / 64.0,
        45.0 * (1.0 - 2.0 * strength) / 512.0,
        5.0 * (2.0 * strength - 1.0) / 256.0,
        (1.0 - 2.0 * strength) / 512.0,
    ]
    extent = length + 2 * WIDTH
    system = np.eye(extent)
    source = np.eye(extent)
    for position in range(5, extent - 5):
        system[position, position - 1] = strength
        system[position, position + 1] = strength
        source[position, position] = coeffs[0]
        for offset in range(1, 6):
            source[position, position + offset] = coeffs[offset] / 2.0
            source[position, position - offset] = coeffs[offset] / 2.0
    return banded_solve(system, source)[WIDTH : WIDTH + length]


def sweep_lines(padded, matrix, dim, precision=lax.Precision.HIGHEST):
    return jnp.einsum(line_forms[dim], matrix, padded, precision=precision)


def faces_xi(values):
    return with_halo(values, (("xi", 1),), WIDTH)


def faces_eta(values):
    return with_halo(values, (("eta", 2),), WIDTH)


def faces_zeta(values):
    return with_halo(values, (("zeta", 3),), WIDTH)


def basic_quantities(conserved_solution):
    density = conserved_solution[0]
    fluid_speed_vector = conserved_solution[1:4] / density
    thermodynamic_stress_scalar = 0.4 * (
        conserved_solution[4] - 0.5 * jnp.sum(conserved_solution[1:4] * fluid_speed_vector, axis=0)
    )
    return (fluid_speed_vector, thermodynamic_stress_scalar, thermodynamic_stress_scalar / density)


def fluxes(
    conserved_solution, fluid_speed_vector, thermodynamic_stress_scalar, slopes, metrics, jacobian
):
    physical = [
        [
            jacobian
            * (
                metrics[0, column] * slopes[0][member]
                + metrics[1, column] * slopes[1][member]
                + metrics[2, column] * slopes[2][member]
            )
            for column in range(3)
        ]
        for member in range(4)
    ]
    spread = physical[0][0] + physical[1][1] + physical[2][2]
    totals = []
    for column in range(3):
        stress = [
            viscosity * (physical[member][column] + physical[column][member]) for member in range(3)
        ]
        stress[column] = stress[column] - 2.0 / 3.0 * viscosity * spread
        subdomain_parts = [conserved_solution[1 + column]]
        for member in range(3):
            carried = conserved_solution[1 + member] * fluid_speed_vector[column] - stress[member]
            if member == column:
                carried = carried + thermodynamic_stress_scalar
            subdomain_parts.append(carried)
        worked = (
            fluid_speed_vector[0] * stress[0]
            + fluid_speed_vector[1] * stress[1]
            + fluid_speed_vector[2] * stress[2]
        )
        subdomain_parts.append(
            (conserved_solution[4] + thermodynamic_stress_scalar) * fluid_speed_vector[column]
            - worked
            - conduction * physical[3][column]
        )
        totals.append(jnp.stack(subdomain_parts))
    return [
        metrics[direction, 0] * totals[0]
        + metrics[direction, 1] * totals[1]
        + metrics[direction, 2] * totals[2]
        for direction in range(3)
    ]


def local(conserved_solution, metrics, jacobian):
    lengths = conserved_solution.shape[1:]
    derive = [jnp.asarray(derivative_table(length), dtype=jnp.float32) for length in lengths]
    smooth = [jnp.asarray(filter_table(length), dtype=jnp.float32) for length in lengths]
    padded = exchange_primitive(conserved_solution, derive[2], 0)
    slopes = [sweep_lines(padded[k], derive[k], k + 1, lax.Precision.HIGH) for k in range(2)]
    slopes.append(padded[2])
    fluid_speed_vector, thermodynamic_stress_scalar = padded[3][0:3], padded[4]
    contra = fluxes(
        conserved_solution,
        fluid_speed_vector,
        thermodynamic_stress_scalar,
        slopes,
        metrics,
        jacobian,
    )
    padded = exchange_faces([(contra[0], "xi", 1), (contra[1], "eta", 2)], 1, (contra[2], derive[2]))
    divergence = sweep_lines(padded[0], derive[0], 1, lax.Precision.HIGH)
    divergence = divergence + sweep_lines(padded[1], derive[1], 2, lax.Precision.HIGH)
    divergence = divergence + padded[2]
    sectioned = conserved_solution - step_duration * jacobian * divergence
    return filter_all(sectioned, smooth, 2)


def solution(mesh):
    in_specs = (
        P(None, "xi", "eta", "zeta"),
        P(None, None, "xi", "eta", "zeta"),
        P("xi", "eta", "zeta"),
    )
    out_specs = P(None, "xi", "eta", "zeta")
    return jax.shard_map(local, mesh=mesh, in_specs=in_specs, out_specs=out_specs, check_vma=False)
```

```python
import functools

import jax
import jax.numpy as jnp
import numpy as np
from jax import lax
from jax.experimental import pallas as pl
from jax.experimental.pallas import tpu as pltpu
from jax.sharding import PartitionSpec as P

WIDTH = 5


viscosity = 0.15
conduction = 0.15 * 1.4 / (0.4 * 0.72)
step_duration = 0.08
line_forms = ("", "al,flyz->fayz", "al,fxlz->fxaz", "al,fxyl->fxya")
MESH = pl.DeviceIdType.MESH
AXES = ("xi", "eta", "zeta")


def primitive_state(conserved):
    density = conserved[0]
    speed = conserved[1:4] / density
    pressure = 0.4 * (conserved[4] - 0.5 * jnp.sum(conserved[1:4] * speed, axis=0))
    return speed, pressure, pressure / density


def exchange_kernel(routes, sizes, count, zeta, prepare, precision, moves, *refs):
    sources = list(refs[:count])
    refs = refs[count:]
    if prepare:
        conserved_ref = sources.pop()
    if zeta:
        if not prepare:
            block_ref = refs[0]
            refs = refs[1:]
        middle_ref, lower_ref, upper_ref = refs[:3]
        refs = refs[3:]
    extra = (1 if zeta else 0) + (2 if prepare else 0)
    targets = refs[: len(refs) - 3 - (3 if zeta else 0) - extra]
    refs = refs[len(targets) :]
    if zeta:
        out_ref = refs[0]
        refs = refs[1:]
    if prepare:
        made, pressure_ref = refs[:2]
        refs = refs[2:]
        sources.append(made)
        if zeta:
            block_ref = made
    if zeta:
        turned, before, after = refs[:3]
        refs = refs[3:]
    send_sems, recv_sems, move_sems = refs
    here = [lax.axis_index(axis) for axis in AXES]

    def device(offset):
        return tuple(
            lax.rem(here[slot] + offset[slot] + sizes[slot], sizes[slot]) for slot in range(3)
        )

    offsets = [route[0] for route in routes] + ([(0, 0, 1), (0, 0, -1)] if zeta else [])
    partners = []
    for offset in offsets:
        for way in (offset, tuple(-step for step in offset)):
            if way not in partners:
                partners.append(way)
    barrier = pltpu.get_barrier_semaphore()
    for offset in partners:
        pl.semaphore_signal(barrier, inc=1, device_id=device(offset), device_id_type=MESH)
    if prepare:
        speed, pressure, temperature = primitive_state(conserved_ref[...])
        made[0:3] = speed
        made[3] = temperature
        pressure_ref[...] = pressure
    if zeta:
        fields, length_x, length_y, depth = block_ref.shape
        rows = fields * length_x * length_y
        turned[...] = block_ref[...].reshape(rows, depth).T
        if not prepare:
            total = jnp.dot(middle_ref[...], turned[...], precision=precision,
                            preferred_element_type=jnp.float32)
    local = []
    for index, (source, source_at, target, target_at) in enumerate(moves):
        local.append(
            pltpu.make_async_copy(
                sources[source].at[source_at], targets[target].at[target_at], move_sems.at[index]
            )
        )
        local[-1].start()
    pl.semaphore_wait(barrier, len(partners))
    copies = []
    for index, (offset, source, source_at, target, target_at) in enumerate(routes):
        copies.append(
            pltpu.make_async_remote_copy(
                src_ref=sources[source].at[source_at],
                dst_ref=targets[target].at[target_at],
                send_sem=send_sems.at[index],
                recv_sem=recv_sems.at[index],
                device_id=device(offset),
                device_id_type=MESH,
            )
        )
    if zeta:
        for index, (rows_at, landing, offset) in enumerate(
            ((pl.ds(depth - 8, 8), before, (0, 0, 1)), (pl.ds(0, 8), after, (0, 0, -1)))
        ):
            copies.append(
                pltpu.make_async_remote_copy(
                    src_ref=turned.at[rows_at],
                    dst_ref=landing,
                    send_sem=send_sems.at[len(routes) + index],
                    recv_sem=recv_sems.at[len(routes) + index],
                    device_id=device(offset),
                    device_id_type=MESH,
                )
            )
    for copy in copies:
        copy.start()
    if zeta and prepare:
        total = jnp.dot(middle_ref[...], turned[...], precision=precision,
                        preferred_element_type=jnp.float32)
    for copy in copies + local:
        copy.wait()
    if zeta:
        total = total + jnp.dot(lower_ref[...], before[...], precision=precision,
                                preferred_element_type=jnp.float32)
        total = total + jnp.dot(upper_ref[...], after[...], precision=precision,
                                preferred_element_type=jnp.float32)
        out_ref[...] = total.T.reshape(fields, length_x, length_y, depth)


def exchange(arrays, routes, out_shapes, tag, zeta=None, prepare=None,
             precision=lax.Precision.HIGH, moves=()):
    sizes = tuple(lax.axis_size(axis) for axis in AXES)
    operands = [array for array, _ in arrays]
    in_specs = [pl.BlockSpec(memory_space=space) for _, space in arrays]
    out_specs = [pl.BlockSpec(memory_space=pl.ANY)] * len(out_shapes)
    out_shapes = list(out_shapes)
    scratch = []
    copies = len(routes)
    if prepare is not None:
        operands.append(prepare)
        in_specs.append(pl.BlockSpec(memory_space=pltpu.VMEM))
    if zeta is not None:
        value, matrix = zeta
        fields, length_x, length_y, depth = value.shape
        rows = fields * length_x * length_y
        padding = jnp.zeros((depth, 8 - WIDTH), matrix.dtype)
        if prepare is None:
            operands.append(value)
            in_specs.append(pl.BlockSpec(memory_space=pltpu.VMEM))
        operands += [
            matrix[:, WIDTH : WIDTH + depth],
            jnp.concatenate([padding, matrix[:, :WIDTH]], axis=1),
            jnp.concatenate([matrix[:, WIDTH + depth :], padding], axis=1),
        ]
        in_specs += [pl.BlockSpec(memory_space=pltpu.VMEM)] * 3
        out_shapes.append(jax.ShapeDtypeStruct(value.shape, value.dtype))
        out_specs.append(pl.BlockSpec(memory_space=pltpu.VMEM))
        scratch = [pltpu.VMEM((depth, rows), jnp.float32), pltpu.VMEM((8, rows), jnp.float32),
                   pltpu.VMEM((8, rows), jnp.float32)]
        copies += 2
    if prepare is not None:
        out_shapes += [
            jax.ShapeDtypeStruct(zeta[0].shape, jnp.float32),
            jax.ShapeDtypeStruct(prepare.shape[1:], jnp.float32),
        ]
        out_specs += [pl.BlockSpec(memory_space=pltpu.VMEM)] * 2
    return pl.pallas_call(
        functools.partial(
            exchange_kernel, tuple(routes), sizes, len(arrays) + (prepare is not None),
            zeta is not None, prepare is not None, precision, tuple(moves),
        ),
        out_shape=out_shapes,
        in_specs=in_specs,
        out_specs=out_specs,
        scratch_shapes=scratch + [
            pltpu.SemaphoreType.DMA((copies,)),
            pltpu.SemaphoreType.DMA((copies,)),
            pltpu.SemaphoreType.DMA((max(1, len(moves)),)),
        ],
        compiler_params=pltpu.CompilerParams(collective_id=tag, has_side_effects=True),
    )(*operands)


def offset_along(axis, step):
    return tuple(step if name == axis else 0 for name in AXES)


def window(ndim, dim, start, stop):
    return tuple(slice(start, stop) if axis == dim else slice(None) for axis in range(ndim))


def exchange_faces(items, tag, zeta=None):
    arrays, routes, out_shapes, moves = [], [], [], []
    for value, axis, dim in items:
        ndim, length = value.ndim, value.shape[dim]
        if dim == ndim - 1:
            both = jnp.stack(
                [
                    lax.slice_in_dim(value, length - WIDTH, length, axis=dim),
                    lax.slice_in_dim(value, 0, WIDTH, axis=dim),
                ]
            )
            both = jnp.moveaxis(both, dim + 1, 2).reshape(2, value.shape[0], WIDTH, -1)
            arrays.append((both, pl.ANY))
            out_shapes.append(jax.ShapeDtypeStruct(both.shape, both.dtype))
            source, target = len(arrays) - 1, len(out_shapes) - 1
            routes.append((offset_along(axis, 1), source, 0, target, 0))
            routes.append((offset_along(axis, -1), source, 1, target, 1))
        elif dim == ndim - 2:
            face = value.shape[:dim] + (WIDTH,) + value.shape[dim + 1 :]
            arrays.append((value, pltpu.VMEM))
            out_shapes += [jax.ShapeDtypeStruct(face, value.dtype)] * 2
            source, target = len(arrays) - 1, len(out_shapes) - 2
            whole = window(ndim, dim, None, None)
            last, first = window(ndim, dim, length - WIDTH, length), window(ndim, dim, 0, WIDTH)
            routes.append((offset_along(axis, 1), source, last, target, whole))
            routes.append((offset_along(axis, -1), source, first, target + 1, whole))
        else:
            arrays += [(value, pl.ANY), (value, pltpu.VMEM)]
            extended = value.shape[:dim] + (length + 2 * WIDTH,) + value.shape[dim + 1 :]
            out_shapes.append(jax.ShapeDtypeStruct(extended, value.dtype))
            source, target = len(arrays) - 2, len(out_shapes) - 1
            last, first = window(ndim, dim, length - WIDTH, length), window(ndim, dim, 0, WIDTH)
            ahead = window(ndim, dim, length + WIDTH, length + 2 * WIDTH)
            routes.append((offset_along(axis, 1), source, last, target, first))
            routes.append((offset_along(axis, -1), source, first, target, ahead))
            moves.append((source + 1, window(ndim, dim, None, None), target,
                          window(ndim, dim, WIDTH, length + WIDTH)))
    received = exchange(arrays, routes, out_shapes, tag, zeta, moves=moves)
    padded, place = [], 0
    for value, axis, dim in items:
        if dim == value.ndim - 1:
            both = received[place].reshape((2, value.shape[0], WIDTH) + value.shape[1:dim])
            both = jnp.moveaxis(both, 2, dim + 1)
            before, after = both[0], both[1]
            place += 1
        elif dim == value.ndim - 2:
            before, after = received[place], received[place + 1]
            place += 2
        else:
            padded.append(received[place])
            place += 1
            continue
        padded.append(jnp.concatenate([before, value, after], axis=dim))
    if zeta is not None:
        padded.append(received[-1])
    return padded


def exchange_primitive(conserved, matrix, tag):
    primitive = jax.ShapeDtypeStruct((4,) + conserved.shape[1:], conserved.dtype)
    length_x, length_y = primitive.shape[1], primitive.shape[2]
    every = slice(None)
    routes = [
        ((1, 0, 0), 0, (every, slice(length_x - WIDTH, length_x)), 0, (every, slice(0, WIDTH))),
        ((-1, 0, 0), 0, (every, slice(0, WIDTH)), 0, (every, slice(length_x + WIDTH, length_x + 2 * WIDTH))),
        ((0, 1, 0), 0, (every, every, slice(length_y - WIDTH, length_y)), 1, every),
        ((0, -1, 0), 0, (every, every, slice(0, WIDTH)), 2, every),
    ]
    moves = [(0, every, 0, (every, slice(WIDTH, length_x + WIDTH)))]
    extended_x = (primitive.shape[0], length_x + 2 * WIDTH) + primitive.shape[2:]
    face_y = primitive.shape[:2] + (WIDTH,) + primitive.shape[3:]
    out_shapes = [jax.ShapeDtypeStruct(face, primitive.dtype) for face in (extended_x, face_y, face_y)]
    padded_x, before_y, after_y, swept, primitive, pressure = exchange(
        [], routes, out_shapes, tag, (primitive, matrix), conserved, moves=moves
    )
    return (
        padded_x,
        jnp.concatenate([before_y, primitive, after_y], axis=2),
        swept,
        primitive,
        pressure,
    )


def exchange_plane(value, tag):
    length_x, length_y = value.shape[1], value.shape[2]
    faces_y = jnp.stack(
        [
            lax.slice_in_dim(value, length_y - WIDTH, length_y, axis=2),
            lax.slice_in_dim(value, 0, WIDTH, axis=2),
        ]
    )
    last_x, first_x = slice(length_x - WIDTH, length_x), slice(0, WIDTH)
    every = slice(None)
    routes = [
        ((1, 0, 0), 0, (every, last_x), 0, every),
        ((-1, 0, 0), 0, (every, first_x), 1, every),
        ((0, 1, 0), 1, 0, 2, every),
        ((0, -1, 0), 1, 1, 3, every),
        ((1, 1, 0), 1, (0, every, last_x), 4, every),
        ((-1, 1, 0), 1, (0, every, first_x), 5, every),
        ((1, -1, 0), 1, (1, every, last_x), 6, every),
        ((-1, -1, 0), 1, (1, every, first_x), 7, every),
    ]
    fields, depth = value.shape[0], value.shape[3]
    out_shapes = (
        [jax.ShapeDtypeStruct((fields, WIDTH, length_y, depth), value.dtype)] * 2
        + [jax.ShapeDtypeStruct((fields, length_x, WIDTH, depth), value.dtype)] * 2
        + [jax.ShapeDtypeStruct((fields, WIDTH, WIDTH, depth), value.dtype)] * 4
    )
    x_before, x_after, y_before, y_after, both_before, x_after_y_before, x_before_y_after, both_after = (
        exchange([(value, pl.ANY), (faces_y, pl.ANY)], routes, out_shapes, tag)
    )
    sections = [
        jnp.concatenate([both_before, x_before, x_before_y_after], axis=2),
        jnp.concatenate([y_before, value, y_after], axis=2),
        jnp.concatenate([x_after_y_before, x_after, both_after], axis=2),
    ]
    return jnp.concatenate(sections, axis=1)


def filter_kernel(sizes, value_ref, middle_ref, lower_ref, upper_ref, smooth_ref, *refs):
    faces = refs[:8]
    turned, before, after, stacked, send_sems, recv_sems = refs[8:]
    fields, length_x, length_y, depth = value_ref.shape
    rows = fields * length_x * length_y
    here = [lax.axis_index(axis) for axis in AXES]

    def device(offset):
        return tuple(
            lax.rem(here[slot] + offset[slot] + sizes[slot], sizes[slot]) for slot in range(3)
        )

    plane = [(1, 0, 0), (-1, 0, 0), (0, 1, 0), (0, -1, 0), (1, 1, 0), (-1, 1, 0), (1, -1, 0), (-1, -1, 0)]
    partners = plane + [(0, 0, 1), (0, 0, -1)]
    barrier = pltpu.get_barrier_semaphore()
    for offset in partners:
        pl.semaphore_signal(barrier, inc=1, device_id=device(offset), device_id_type=MESH)
    turned[...] = value_ref[...].reshape(rows, depth).T
    total = jnp.dot(middle_ref[...], turned[...], precision=lax.Precision.HIGHEST,
                    preferred_element_type=jnp.float32)
    pl.semaphore_wait(barrier, len(partners))
    along_z = [
        pltpu.make_async_remote_copy(
            src_ref=turned.at[pl.ds(depth - 8, 8)], dst_ref=before,
            send_sem=send_sems.at[8], recv_sem=recv_sems.at[8],
            device_id=device((0, 0, 1)), device_id_type=MESH,
        ),
        pltpu.make_async_remote_copy(
            src_ref=turned.at[pl.ds(0, 8)], dst_ref=after,
            send_sem=send_sems.at[9], recv_sem=recv_sems.at[9],
            device_id=device((0, 0, -1)), device_id_type=MESH,
        ),
    ]
    for copy in along_z:
        copy.start()
    for copy in along_z:
        copy.wait()
    total = total + jnp.dot(lower_ref[...], before[...], precision=lax.Precision.HIGHEST,
                            preferred_element_type=jnp.float32)
    total = total + jnp.dot(upper_ref[...], after[...], precision=lax.Precision.HIGHEST,
                            preferred_element_type=jnp.float32)
    smooth_ref[...] = total.T.reshape(fields, length_x, length_y, depth)
    last_x, first_x = pl.ds(length_x - WIDTH, WIDTH), pl.ds(0, WIDTH)
    every = slice(None)
    sources = [
        smooth_ref.at[every, last_x], smooth_ref.at[every, first_x],
        stacked.at[0], stacked.at[1],
        stacked.at[0, every, last_x], stacked.at[0, every, first_x],
        stacked.at[1, every, last_x], stacked.at[1, every, first_x],
    ]
    copies = []
    for index, offset in enumerate(plane):
        if index == 2:
            stacked[0] = smooth_ref[:, :, length_y - WIDTH :, :]
            stacked[1] = smooth_ref[:, :, :WIDTH, :]
        copies.append(
            pltpu.make_async_remote_copy(
                src_ref=sources[index], dst_ref=faces[index],
                send_sem=send_sems.at[index], recv_sem=recv_sems.at[index],
                device_id=device(offset), device_id_type=MESH,
            )
        )
        copies[-1].start()
    for copy in copies:
        copy.wait()


def filter_all(value, smooth, tag):
    sizes = tuple(lax.axis_size(axis) for axis in AXES)
    fields, length_x, length_y, depth = value.shape
    rows = fields * length_x * length_y
    matrix = smooth[2]
    padding = jnp.zeros((depth, 8 - WIDTH), matrix.dtype)
    x_face = jax.ShapeDtypeStruct((fields, WIDTH, length_y, depth), value.dtype)
    y_face = jax.ShapeDtypeStruct((fields, length_x, WIDTH, depth), value.dtype)
    edge = jax.ShapeDtypeStruct((fields, WIDTH, WIDTH, depth), value.dtype)
    outs = pl.pallas_call(
        functools.partial(filter_kernel, sizes),
        out_shape=[jax.ShapeDtypeStruct(value.shape, value.dtype)] + [x_face] * 2 + [y_face] * 2 + [edge] * 4,
        in_specs=[pl.BlockSpec(memory_space=pltpu.VMEM)] * 4,
        out_specs=[pl.BlockSpec(memory_space=pltpu.VMEM)] + [pl.BlockSpec(memory_space=pl.ANY)] * 8,
        scratch_shapes=[
            pltpu.VMEM((depth, rows), jnp.float32),
            pltpu.VMEM((8, rows), jnp.float32),
            pltpu.VMEM((8, rows), jnp.float32),
            pltpu.VMEM((2, fields, length_x, WIDTH, depth), jnp.float32),
            pltpu.SemaphoreType.DMA((10,)),
            pltpu.SemaphoreType.DMA((10,)),
        ],
        compiler_params=pltpu.CompilerParams(collective_id=tag, has_side_effects=True),
    )(
        value,
        matrix[:, WIDTH : WIDTH + depth],
        jnp.concatenate([padding, matrix[:, :WIDTH]], axis=1),
        jnp.concatenate([matrix[:, WIDTH + depth :], padding], axis=1),
    )
    smoothed, x_before, x_after, y_before, y_after, both_before, x_after_y_before, x_before_y_after, both_after = outs
    sections = [
        jnp.concatenate([both_before, x_before, x_before_y_after], axis=2),
        jnp.concatenate([y_before, smoothed, y_after], axis=2),
        jnp.concatenate([x_after_y_before, x_after, both_after], axis=2),
    ]
    result = sweep_lines(jnp.concatenate(sections, axis=1), smooth[0], 1)
    return sweep_lines(result, smooth[1], 2)


def sweep_zeta(value, matrix, tag):
    return exchange([], [], [], tag, (value, matrix), precision=lax.Precision.HIGHEST)[-1]


def with_halo(value, sides, width):
    for axis, dim in sides:
        count, length = (lax.axis_size(axis), value.shape[dim])
        up = [(i, (i + 1) % count) for i in range(count)]
        down = [(j, i) for i, j in up]
        last = lax.slice_in_dim(value, length - width, length, axis=dim)
        initial = lax.slice_in_dim(value, 0, width, axis=dim)
        before = lax.ppermute(last, axis, up)
        after = lax.ppermute(initial, axis, down)
        value = jnp.concatenate([before, value, after], axis=dim)
    return value


def banded_solve(system, source):
    extent = system.shape[0]
    lower = np.zeros(extent)
    upper = np.zeros(extent)
    middle = np.array([float(system[index, index]) for index in range(extent)])
    for index in range(1, extent):
        lower[index] = system[index, index - 1]
        upper[index - 1] = system[index - 1, index]
    rights = np.array(source)
    for index in range(1, extent):
        factor = lower[index] / middle[index - 1]
        middle[index] = middle[index] - factor * upper[index - 1]
        rights[index] = rights[index] - factor * rights[index - 1]
    answer = np.zeros(rights.shape)
    answer[extent - 1] = rights[extent - 1] / middle[extent - 1]
    for index in range(extent - 2, -1, -1):
        answer[index] = (rights[index] - upper[index] * answer[index + 1]) / middle[index]
    return answer


def derivative_table(length):
    extent = length + 2 * WIDTH
    system = np.eye(extent)
    source = np.zeros((extent, extent))
    for position in range(2, extent - 2):
        system[position, position - 1] = 1.0 / 3.0
        system[position, position + 1] = 1.0 / 3.0
        source[position, position + 1] = 7.0 / 9.0
        source[position, position - 1] = -7.0 / 9.0
        source[position, position + 2] = 1.0 / 36.0
        source[position, position - 2] = -1.0 / 36.0
    source[1, 2] = 0.5
    source[1, 0] = -0.5
    source[extent - 2, extent - 1] = 0.5
    source[extent - 2, extent - 3] = -0.5
    source[0, 1] = 1.0
    source[0, 0] = -1.0
    source[extent - 1, extent - 1] = 1.0
    source[extent - 1, extent - 2] = -1.0
    return banded_solve(system, source)[WIDTH : WIDTH + length]


def filter_table(length):
    strength = 0.4
    coeffs = [
        (193.0 + 126.0 * strength) / 256.0,
        (105.0 + 302.0 * strength) / 256.0,
        15.0 * (2.0 * strength - 1.0) / 64.0,
        45.0 * (1.0 - 2.0 * strength) / 512.0,
        5.0 * (2.0 * strength - 1.0) / 256.0,
        (1.0 - 2.0 * strength) / 512.0,
    ]
    extent = length + 2 * WIDTH
    system = np.eye(extent)
    source = np.eye(extent)
    for position in range(5, extent - 5):
        system[position, position - 1] = strength
        system[position, position + 1] = strength
        source[position, position] = coeffs[0]
        for offset in range(1, 6):
            source[position, position + offset] = coeffs[offset] / 2.0
            source[position, position - offset] = coeffs[offset] / 2.0
    return banded_solve(system, source)[WIDTH : WIDTH + length]


def sweep_lines(padded, matrix, dim, precision=lax.Precision.HIGHEST):
    return jnp.einsum(line_forms[dim], matrix, padded, precision=precision)


def faces_xi(values):
    return with_halo(values, (("xi", 1),), WIDTH)


def faces_eta(values):
    return with_halo(values, (("eta", 2),), WIDTH)


def faces_zeta(values):
    return with_halo(values, (("zeta", 3),), WIDTH)


def basic_quantities(conserved_solution):
    density = conserved_solution[0]
    fluid_speed_vector = conserved_solution[1:4] / density
    thermodynamic_stress_scalar = 0.4 * (
        conserved_solution[4] - 0.5 * jnp.sum(conserved_solution[1:4] * fluid_speed_vector, axis=0)
    )
    return (fluid_speed_vector, thermodynamic_stress_scalar, thermodynamic_stress_scalar / density)


def fluxes(
    conserved_solution, fluid_speed_vector, thermodynamic_stress_scalar, slopes, metrics, jacobian
):
    physical = [
        [
            jacobian
            * (
                metrics[0, column] * slopes[0][member]
                + metrics[1, column] * slopes[1][member]
                + metrics[2, column] * slopes[2][member]
            )
            for column in range(3)
        ]
        for member in range(4)
    ]
    spread = physical[0][0] + physical[1][1] + physical[2][2]
    totals = []
    for column in range(3):
        stress = [
            viscosity * (physical[member][column] + physical[column][member]) for member in range(3)
        ]
        stress[column] = stress[column] - 2.0 / 3.0 * viscosity * spread
        subdomain_parts = [conserved_solution[1 + column]]
        for member in range(3):
            carried = conserved_solution[1 + member] * fluid_speed_vector[column] - stress[member]
            if member == column:
                carried = carried + thermodynamic_stress_scalar
            subdomain_parts.append(carried)
        worked = (
            fluid_speed_vector[0] * stress[0]
            + fluid_speed_vector[1] * stress[1]
            + fluid_speed_vector[2] * stress[2]
        )
        subdomain_parts.append(
            (conserved_solution[4] + thermodynamic_stress_scalar) * fluid_speed_vector[column]
            - worked
            - conduction * physical[3][column]
        )
        totals.append(jnp.stack(subdomain_parts))
    return [
        metrics[direction, 0] * totals[0]
        + metrics[direction, 1] * totals[1]
        + metrics[direction, 2] * totals[2]
        for direction in range(3)
    ]


def local(conserved_solution, metrics, jacobian):
    lengths = conserved_solution.shape[1:]
    derive = [jnp.asarray(derivative_table(length), dtype=jnp.float32) for length in lengths]
    smooth = [jnp.asarray(filter_table(length), dtype=jnp.float32) for length in lengths]
    padded = exchange_primitive(conserved_solution, derive[2], 0)
    slopes = [sweep_lines(padded[k], derive[k], k + 1, lax.Precision.HIGH) for k in range(2)]
    slopes.append(padded[2])
    fluid_speed_vector, thermodynamic_stress_scalar = padded[3][0:3], padded[4]
    contra = fluxes(
        conserved_solution,
        fluid_speed_vector,
        thermodynamic_stress_scalar,
        slopes,
        metrics,
        jacobian,
    )
    padded = exchange_faces([(contra[0], "xi", 1), (contra[1], "eta", 2)], 1, (contra[2], derive[2]))
    divergence = sweep_lines(padded[0], derive[0], 1, lax.Precision.HIGH)
    divergence = divergence + sweep_lines(padded[1], derive[1], 2, lax.Precision.HIGH)
    divergence = divergence + padded[2]
    sectioned = conserved_solution - step_duration * jacobian * divergence
    return filter_all(sectioned, smooth, 2)


def solution(mesh):
    in_specs = (
        P(None, "xi", "eta", "zeta"),
        P(None, None, "xi", "eta", "zeta"),
        P("xi", "eta", "zeta"),
    )
    out_specs = P(None, "xi", "eta", "zeta")
    return jax.shard_map(local, mesh=mesh, in_specs=in_specs, out_specs=out_specs, check_vma=False)
```

```python
import functools

import jax
import jax.numpy as jnp
import numpy as np
from jax import lax
from jax.experimental import pallas as pl
from jax.experimental.pallas import tpu as pltpu
from jax.sharding import PartitionSpec as P

WIDTH = 5


viscosity = 0.15
conduction = 0.15 * 1.4 / (0.4 * 0.72)
step_duration = 0.08
line_forms = ("", "al,flyz->fayz", "al,fxlz->fxaz", "al,fxyl->fxya")
MESH = pl.DeviceIdType.MESH
AXES = ("xi", "eta", "zeta")


def primitive_state(conserved):
    density = conserved[0]
    speed = conserved[1:4] / density
    pressure = 0.4 * (conserved[4] - 0.5 * jnp.sum(conserved[1:4] * speed, axis=0))
    return speed, pressure, pressure / density


def exchange_kernel(routes, sizes, count, zeta, prepare, precision, moves, *refs):
    sources = list(refs[:count])
    refs = refs[count:]
    if prepare:
        conserved_ref = sources.pop()
    if zeta:
        if not prepare:
            block_ref = refs[0]
            refs = refs[1:]
        middle_ref, lower_ref, upper_ref = refs[:3]
        refs = refs[3:]
    extra = (1 if zeta else 0) + (2 if prepare else 0)
    targets = refs[: len(refs) - 3 - (3 if zeta else 0) - extra]
    refs = refs[len(targets) :]
    if zeta:
        out_ref = refs[0]
        refs = refs[1:]
    if prepare:
        made, pressure_ref = refs[:2]
        refs = refs[2:]
        sources.append(made)
        if zeta:
            block_ref = made
    if zeta:
        turned, before, after = refs[:3]
        refs = refs[3:]
    send_sems, recv_sems, move_sems = refs
    here = [lax.axis_index(axis) for axis in AXES]

    def device(offset):
        return tuple(
            lax.rem(here[slot] + offset[slot] + sizes[slot], sizes[slot]) for slot in range(3)
        )

    offsets = [route[0] for route in routes] + ([(0, 0, 1), (0, 0, -1)] if zeta else [])
    partners = []
    for offset in offsets:
        for way in (offset, tuple(-step for step in offset)):
            if way not in partners:
                partners.append(way)
    barrier = pltpu.get_barrier_semaphore()
    for offset in partners:
        pl.semaphore_signal(barrier, inc=1, device_id=device(offset), device_id_type=MESH)
    if prepare:
        speed, pressure, temperature = primitive_state(conserved_ref[...])
        made[0:3] = speed
        made[3] = temperature
        pressure_ref[...] = pressure
    if zeta:
        fields, length_x, length_y, depth = block_ref.shape
        rows = fields * length_x * length_y
        turned[...] = block_ref[...].reshape(rows, depth).T
        if not prepare:
            total = jnp.dot(middle_ref[...], turned[...], precision=precision,
                            preferred_element_type=jnp.float32)
    local = []
    for index, (source, source_at, target, target_at) in enumerate(moves):
        local.append(
            pltpu.make_async_copy(
                sources[source].at[source_at], targets[target].at[target_at], move_sems.at[index]
            )
        )
        local[-1].start()
    pl.semaphore_wait(barrier, len(partners))
    copies = []
    for index, (offset, source, source_at, target, target_at) in enumerate(routes):
        copies.append(
            pltpu.make_async_remote_copy(
                src_ref=sources[source].at[source_at],
                dst_ref=targets[target].at[target_at],
                send_sem=send_sems.at[index],
                recv_sem=recv_sems.at[index],
                device_id=device(offset),
                device_id_type=MESH,
            )
        )
    if zeta:
        for index, (rows_at, landing, offset) in enumerate(
            ((pl.ds(depth - 8, 8), before, (0, 0, 1)), (pl.ds(0, 8), after, (0, 0, -1)))
        ):
            copies.append(
                pltpu.make_async_remote_copy(
                    src_ref=turned.at[rows_at],
                    dst_ref=landing,
                    send_sem=send_sems.at[len(routes) + index],
                    recv_sem=recv_sems.at[len(routes) + index],
                    device_id=device(offset),
                    device_id_type=MESH,
                )
            )
    for copy in copies:
        copy.start()
    if zeta and prepare:
        total = jnp.dot(middle_ref[...], turned[...], precision=precision,
                        preferred_element_type=jnp.float32)
    for copy in copies + local:
        copy.wait()
    if zeta:
        total = total + jnp.dot(lower_ref[...], before[...], precision=precision,
                                preferred_element_type=jnp.float32)
        total = total + jnp.dot(upper_ref[...], after[...], precision=precision,
                                preferred_element_type=jnp.float32)
        out_ref[...] = total.T.reshape(fields, length_x, length_y, depth)


def exchange(arrays, routes, out_shapes, tag, zeta=None, prepare=None,
             precision=lax.Precision.HIGH, moves=()):
    sizes = tuple(lax.axis_size(axis) for axis in AXES)
    operands = [array for array, _ in arrays]
    in_specs = [pl.BlockSpec(memory_space=space) for _, space in arrays]
    out_specs = [pl.BlockSpec(memory_space=pl.ANY)] * len(out_shapes)
    out_shapes = list(out_shapes)
    scratch = []
    copies = len(routes)
    if prepare is not None:
        operands.append(prepare)
        in_specs.append(pl.BlockSpec(memory_space=pltpu.VMEM))
    if zeta is not None:
        value, matrix = zeta
        fields, length_x, length_y, depth = value.shape
        rows = fields * length_x * length_y
        padding = jnp.zeros((depth, 8 - WIDTH), matrix.dtype)
        if prepare is None:
            operands.append(value)
            in_specs.append(pl.BlockSpec(memory_space=pltpu.VMEM))
        operands += [
            matrix[:, WIDTH : WIDTH + depth],
            jnp.concatenate([padding, matrix[:, :WIDTH]], axis=1),
            jnp.concatenate([matrix[:, WIDTH + depth :], padding], axis=1),
        ]
        in_specs += [pl.BlockSpec(memory_space=pltpu.VMEM)] * 3
        out_shapes.append(jax.ShapeDtypeStruct(value.shape, value.dtype))
        out_specs.append(pl.BlockSpec(memory_space=pltpu.VMEM))
        scratch = [pltpu.VMEM((depth, rows), jnp.float32), pltpu.VMEM((8, rows), jnp.float32),
                   pltpu.VMEM((8, rows), jnp.float32)]
        copies += 2
    if prepare is not None:
        out_shapes += [
            jax.ShapeDtypeStruct(zeta[0].shape, jnp.float32),
            jax.ShapeDtypeStruct(prepare.shape[1:], jnp.float32),
        ]
        out_specs += [pl.BlockSpec(memory_space=pltpu.VMEM)] * 2
    return pl.pallas_call(
        functools.partial(
            exchange_kernel, tuple(routes), sizes, len(arrays) + (prepare is not None),
            zeta is not None, prepare is not None, precision, tuple(moves),
        ),
        out_shape=out_shapes,
        in_specs=in_specs,
        out_specs=out_specs,
        scratch_shapes=scratch + [
            pltpu.SemaphoreType.DMA((copies,)),
            pltpu.SemaphoreType.DMA((copies,)),
            pltpu.SemaphoreType.DMA((max(1, len(moves)),)),
        ],
        compiler_params=pltpu.CompilerParams(collective_id=tag, has_side_effects=True),
    )(*operands)


def offset_along(axis, step):
    return tuple(step if name == axis else 0 for name in AXES)


def window(ndim, dim, start, stop):
    return tuple(slice(start, stop) if axis == dim else slice(None) for axis in range(ndim))


def exchange_faces(items, tag, zeta=None):
    arrays, routes, out_shapes, moves = [], [], [], []
    for value, axis, dim in items:
        ndim, length = value.ndim, value.shape[dim]
        if dim == ndim - 1:
            both = jnp.stack(
                [
                    lax.slice_in_dim(value, length - WIDTH, length, axis=dim),
                    lax.slice_in_dim(value, 0, WIDTH, axis=dim),
                ]
            )
            both = jnp.moveaxis(both, dim + 1, 2).reshape(2, value.shape[0], WIDTH, -1)
            arrays.append((both, pl.ANY))
            out_shapes.append(jax.ShapeDtypeStruct(both.shape, both.dtype))
            source, target = len(arrays) - 1, len(out_shapes) - 1
            routes.append((offset_along(axis, 1), source, 0, target, 0))
            routes.append((offset_along(axis, -1), source, 1, target, 1))
        elif dim == ndim - 2:
            face = value.shape[:dim] + (WIDTH,) + value.shape[dim + 1 :]
            arrays.append((value, pltpu.VMEM))
            out_shapes += [jax.ShapeDtypeStruct(face, value.dtype)] * 2
            source, target = len(arrays) - 1, len(out_shapes) - 2
            whole = window(ndim, dim, None, None)
            last, first = window(ndim, dim, length - WIDTH, length), window(ndim, dim, 0, WIDTH)
            routes.append((offset_along(axis, 1), source, last, target, whole))
            routes.append((offset_along(axis, -1), source, first, target + 1, whole))
        else:
            arrays.append((value, pl.ANY))
            face = value.shape[:dim] + (WIDTH,) + value.shape[dim + 1 :]
            out_shapes += [jax.ShapeDtypeStruct(face, value.dtype)] * 2
            source, target = len(arrays) - 1, len(out_shapes) - 2
            whole = window(ndim, dim, None, None)
            last, first = window(ndim, dim, length - WIDTH, length), window(ndim, dim, 0, WIDTH)
            routes.append((offset_along(axis, 1), source, last, target, whole))
            routes.append((offset_along(axis, -1), source, first, target + 1, whole))
    received = exchange(arrays, routes, out_shapes, tag, zeta, moves=moves)
    padded, place = [], 0
    for value, axis, dim in items:
        if dim == value.ndim - 1:
            both = received[place].reshape((2, value.shape[0], WIDTH) + value.shape[1:dim])
            both = jnp.moveaxis(both, 2, dim + 1)
            before, after = both[0], both[1]
            place += 1
        else:
            before, after = received[place], received[place + 1]
            place += 2
        padded.append(jnp.concatenate([before, value, after], axis=dim))
    if zeta is not None:
        padded.append(received[-1])
    return padded


def exchange_primitive(conserved, matrix, tag):
    primitive = jax.ShapeDtypeStruct((4,) + conserved.shape[1:], conserved.dtype)
    length_x, length_y = primitive.shape[1], primitive.shape[2]
    every = slice(None)
    routes = [
        ((1, 0, 0), 0, (every, slice(length_x - WIDTH, length_x)), 0, (every, slice(0, WIDTH))),
        ((-1, 0, 0), 0, (every, slice(0, WIDTH)), 0, (every, slice(length_x + WIDTH, length_x + 2 * WIDTH))),
        ((0, 1, 0), 0, (every, every, slice(length_y - WIDTH, length_y)), 1, every),
        ((0, -1, 0), 0, (every, every, slice(0, WIDTH)), 2, every),
    ]
    moves = [(0, every, 0, (every, slice(WIDTH, length_x + WIDTH)))]
    extended_x = (primitive.shape[0], length_x + 2 * WIDTH) + primitive.shape[2:]
    face_y = primitive.shape[:2] + (WIDTH,) + primitive.shape[3:]
    out_shapes = [jax.ShapeDtypeStruct(face, primitive.dtype) for face in (extended_x, face_y, face_y)]
    padded_x, before_y, after_y, swept, primitive, pressure = exchange(
        [], routes, out_shapes, tag, (primitive, matrix), conserved, moves=moves
    )
    return (
        padded_x,
        jnp.concatenate([before_y, primitive, after_y], axis=2),
        swept,
        primitive,
        pressure,
    )


def exchange_plane(value, tag):
    length_x, length_y = value.shape[1], value.shape[2]
    faces_y = jnp.stack(
        [
            lax.slice_in_dim(value, length_y - WIDTH, length_y, axis=2),
            lax.slice_in_dim(value, 0, WIDTH, axis=2),
        ]
    )
    last_x, first_x = slice(length_x - WIDTH, length_x), slice(0, WIDTH)
    every = slice(None)
    routes = [
        ((1, 0, 0), 0, (every, last_x), 0, every),
        ((-1, 0, 0), 0, (every, first_x), 1, every),
        ((0, 1, 0), 1, 0, 2, every),
        ((0, -1, 0), 1, 1, 3, every),
        ((1, 1, 0), 1, (0, every, last_x), 4, every),
        ((-1, 1, 0), 1, (0, every, first_x), 5, every),
        ((1, -1, 0), 1, (1, every, last_x), 6, every),
        ((-1, -1, 0), 1, (1, every, first_x), 7, every),
    ]
    fields, depth = value.shape[0], value.shape[3]
    out_shapes = (
        [jax.ShapeDtypeStruct((fields, WIDTH, length_y, depth), value.dtype)] * 2
        + [jax.ShapeDtypeStruct((fields, length_x, WIDTH, depth), value.dtype)] * 2
        + [jax.ShapeDtypeStruct((fields, WIDTH, WIDTH, depth), value.dtype)] * 4
    )
    x_before, x_after, y_before, y_after, both_before, x_after_y_before, x_before_y_after, both_after = (
        exchange([(value, pl.ANY), (faces_y, pl.ANY)], routes, out_shapes, tag)
    )
    sections = [
        jnp.concatenate([both_before, x_before, x_before_y_after], axis=2),
        jnp.concatenate([y_before, value, y_after], axis=2),
        jnp.concatenate([x_after_y_before, x_after, both_after], axis=2),
    ]
    return jnp.concatenate(sections, axis=1)


def filter_kernel(sizes, value_ref, middle_ref, lower_ref, upper_ref, smooth_ref, *refs):
    faces = refs[:8]
    turned, before, after, stacked, send_sems, recv_sems = refs[8:]
    fields, length_x, length_y, depth = value_ref.shape
    rows = fields * length_x * length_y
    here = [lax.axis_index(axis) for axis in AXES]

    def device(offset):
        return tuple(
            lax.rem(here[slot] + offset[slot] + sizes[slot], sizes[slot]) for slot in range(3)
        )

    plane = [(1, 0, 0), (-1, 0, 0), (0, 1, 0), (0, -1, 0), (1, 1, 0), (-1, 1, 0), (1, -1, 0), (-1, -1, 0)]
    partners = plane + [(0, 0, 1), (0, 0, -1)]
    barrier = pltpu.get_barrier_semaphore()
    for offset in partners:
        pl.semaphore_signal(barrier, inc=1, device_id=device(offset), device_id_type=MESH)
    turned[...] = value_ref[...].reshape(rows, depth).T
    total = jnp.dot(middle_ref[...], turned[...], precision=lax.Precision.HIGHEST,
                    preferred_element_type=jnp.float32)
    pl.semaphore_wait(barrier, len(partners))
    along_z = [
        pltpu.make_async_remote_copy(
            src_ref=turned.at[pl.ds(depth - 8, 8)], dst_ref=before,
            send_sem=send_sems.at[8], recv_sem=recv_sems.at[8],
            device_id=device((0, 0, 1)), device_id_type=MESH,
        ),
        pltpu.make_async_remote_copy(
            src_ref=turned.at[pl.ds(0, 8)], dst_ref=after,
            send_sem=send_sems.at[9], recv_sem=recv_sems.at[9],
            device_id=device((0, 0, -1)), device_id_type=MESH,
        ),
    ]
    for copy in along_z:
        copy.start()
    for copy in along_z:
        copy.wait()
    total = total + jnp.dot(lower_ref[...], before[...], precision=lax.Precision.HIGHEST,
                            preferred_element_type=jnp.float32)
    total = total + jnp.dot(upper_ref[...], after[...], precision=lax.Precision.HIGHEST,
                            preferred_element_type=jnp.float32)
    smooth_ref[...] = total.T.reshape(fields, length_x, length_y, depth)
    last_x, first_x = pl.ds(length_x - WIDTH, WIDTH), pl.ds(0, WIDTH)
    every = slice(None)
    sources = [
        smooth_ref.at[every, last_x], smooth_ref.at[every, first_x],
        stacked.at[0], stacked.at[1],
        stacked.at[0, every, last_x], stacked.at[0, every, first_x],
        stacked.at[1, every, last_x], stacked.at[1, every, first_x],
    ]
    copies = []
    for index, offset in enumerate(plane):
        if index == 2:
            stacked[0] = smooth_ref[:, :, length_y - WIDTH :, :]
            stacked[1] = smooth_ref[:, :, :WIDTH, :]
        copies.append(
            pltpu.make_async_remote_copy(
                src_ref=sources[index], dst_ref=faces[index],
                send_sem=send_sems.at[index], recv_sem=recv_sems.at[index],
                device_id=device(offset), device_id_type=MESH,
            )
        )
        copies[-1].start()
    for copy in copies:
        copy.wait()


def filter_all(value, smooth, tag):
    sizes = tuple(lax.axis_size(axis) for axis in AXES)
    fields, length_x, length_y, depth = value.shape
    rows = fields * length_x * length_y
    matrix = smooth[2]
    padding = jnp.zeros((depth, 8 - WIDTH), matrix.dtype)
    x_face = jax.ShapeDtypeStruct((fields, WIDTH, length_y, depth), value.dtype)
    y_face = jax.ShapeDtypeStruct((fields, length_x, WIDTH, depth), value.dtype)
    edge = jax.ShapeDtypeStruct((fields, WIDTH, WIDTH, depth), value.dtype)
    outs = pl.pallas_call(
        functools.partial(filter_kernel, sizes),
        out_shape=[jax.ShapeDtypeStruct(value.shape, value.dtype)] + [x_face] * 2 + [y_face] * 2 + [edge] * 4,
        in_specs=[pl.BlockSpec(memory_space=pltpu.VMEM)] * 4,
        out_specs=[pl.BlockSpec(memory_space=pltpu.VMEM)] + [pl.BlockSpec(memory_space=pl.ANY)] * 8,
        scratch_shapes=[
            pltpu.VMEM((depth, rows), jnp.float32),
            pltpu.VMEM((8, rows), jnp.float32),
            pltpu.VMEM((8, rows), jnp.float32),
            pltpu.VMEM((2, fields, length_x, WIDTH, depth), jnp.float32),
            pltpu.SemaphoreType.DMA((10,)),
            pltpu.SemaphoreType.DMA((10,)),
        ],
        compiler_params=pltpu.CompilerParams(collective_id=tag, has_side_effects=True),
    )(
        value,
        matrix[:, WIDTH : WIDTH + depth],
        jnp.concatenate([padding, matrix[:, :WIDTH]], axis=1),
        jnp.concatenate([matrix[:, WIDTH + depth :], padding], axis=1),
    )
    smoothed, x_before, x_after, y_before, y_after, both_before, x_after_y_before, x_before_y_after, both_after = outs
    sections = [
        jnp.concatenate([both_before, x_before, x_before_y_after], axis=2),
        jnp.concatenate([y_before, smoothed, y_after], axis=2),
        jnp.concatenate([x_after_y_before, x_after, both_after], axis=2),
    ]
    result = sweep_lines(jnp.concatenate(sections, axis=1), smooth[0], 1)
    return sweep_lines(result, smooth[1], 2)


def sweep_zeta(value, matrix, tag):
    return exchange([], [], [], tag, (value, matrix), precision=lax.Precision.HIGHEST)[-1]


def with_halo(value, sides, width):
    for axis, dim in sides:
        count, length = (lax.axis_size(axis), value.shape[dim])
        up = [(i, (i + 1) % count) for i in range(count)]
        down = [(j, i) for i, j in up]
        last = lax.slice_in_dim(value, length - width, length, axis=dim)
        initial = lax.slice_in_dim(value, 0, width, axis=dim)
        before = lax.ppermute(last, axis, up)
        after = lax.ppermute(initial, axis, down)
        value = jnp.concatenate([before, value, after], axis=dim)
    return value


def banded_solve(system, source):
    extent = system.shape[0]
    lower = np.zeros(extent)
    upper = np.zeros(extent)
    middle = np.array([float(system[index, index]) for index in range(extent)])
    for index in range(1, extent):
        lower[index] = system[index, index - 1]
        upper[index - 1] = system[index - 1, index]
    rights = np.array(source)
    for index in range(1, extent):
        factor = lower[index] / middle[index - 1]
        middle[index] = middle[index] - factor * upper[index - 1]
        rights[index] = rights[index] - factor * rights[index - 1]
    answer = np.zeros(rights.shape)
    answer[extent - 1] = rights[extent - 1] / middle[extent - 1]
    for index in range(extent - 2, -1, -1):
        answer[index] = (rights[index] - upper[index] * answer[index + 1]) / middle[index]
    return answer


def derivative_table(length):
    extent = length + 2 * WIDTH
    system = np.eye(extent)
    source = np.zeros((extent, extent))
    for position in range(2, extent - 2):
        system[position, position - 1] = 1.0 / 3.0
        system[position, position + 1] = 1.0 / 3.0
        source[position, position + 1] = 7.0 / 9.0
        source[position, position - 1] = -7.0 / 9.0
        source[position, position + 2] = 1.0 / 36.0
        source[position, position - 2] = -1.0 / 36.0
    source[1, 2] = 0.5
    source[1, 0] = -0.5
    source[extent - 2, extent - 1] = 0.5
    source[extent - 2, extent - 3] = -0.5
    source[0, 1] = 1.0
    source[0, 0] = -1.0
    source[extent - 1, extent - 1] = 1.0
    source[extent - 1, extent - 2] = -1.0
    return banded_solve(system, source)[WIDTH : WIDTH + length]


def filter_table(length):
    strength = 0.4
    coeffs = [
        (193.0 + 126.0 * strength) / 256.0,
        (105.0 + 302.0 * strength) / 256.0,
        15.0 * (2.0 * strength - 1.0) / 64.0,
        45.0 * (1.0 - 2.0 * strength) / 512.0,
        5.0 * (2.0 * strength - 1.0) / 256.0,
        (1.0 - 2.0 * strength) / 512.0,
    ]
    extent = length + 2 * WIDTH
    system = np.eye(extent)
    source = np.eye(extent)
    for position in range(5, extent - 5):
        system[position, position - 1] = strength
        system[position, position + 1] = strength
        source[position, position] = coeffs[0]
        for offset in range(1, 6):
            source[position, position + offset] = coeffs[offset] / 2.0
            source[position, position - offset] = coeffs[offset] / 2.0
    return banded_solve(system, source)[WIDTH : WIDTH + length]


def sweep_lines(padded, matrix, dim, precision=lax.Precision.HIGHEST):
    return jnp.einsum(line_forms[dim], matrix, padded, precision=precision)


def faces_xi(values):
    return with_halo(values, (("xi", 1),), WIDTH)


def faces_eta(values):
    return with_halo(values, (("eta", 2),), WIDTH)


def faces_zeta(values):
    return with_halo(values, (("zeta", 3),), WIDTH)


def basic_quantities(conserved_solution):
    density = conserved_solution[0]
    fluid_speed_vector = conserved_solution[1:4] / density
    thermodynamic_stress_scalar = 0.4 * (
        conserved_solution[4] - 0.5 * jnp.sum(conserved_solution[1:4] * fluid_speed_vector, axis=0)
    )
    return (fluid_speed_vector, thermodynamic_stress_scalar, thermodynamic_stress_scalar / density)


def fluxes(
    conserved_solution, fluid_speed_vector, thermodynamic_stress_scalar, slopes, metrics, jacobian
):
    physical = [
        [
            jacobian
            * (
                metrics[0, column] * slopes[0][member]
                + metrics[1, column] * slopes[1][member]
                + metrics[2, column] * slopes[2][member]
            )
            for column in range(3)
        ]
        for member in range(4)
    ]
    spread = physical[0][0] + physical[1][1] + physical[2][2]
    totals = []
    for column in range(3):
        stress = [
            viscosity * (physical[member][column] + physical[column][member]) for member in range(3)
        ]
        stress[column] = stress[column] - 2.0 / 3.0 * viscosity * spread
        subdomain_parts = [conserved_solution[1 + column]]
        for member in range(3):
            carried = conserved_solution[1 + member] * fluid_speed_vector[column] - stress[member]
            if member == column:
                carried = carried + thermodynamic_stress_scalar
            subdomain_parts.append(carried)
        worked = (
            fluid_speed_vector[0] * stress[0]
            + fluid_speed_vector[1] * stress[1]
            + fluid_speed_vector[2] * stress[2]
        )
        subdomain_parts.append(
            (conserved_solution[4] + thermodynamic_stress_scalar) * fluid_speed_vector[column]
            - worked
            - conduction * physical[3][column]
        )
        totals.append(jnp.stack(subdomain_parts))
    return [
        metrics[direction, 0] * totals[0]
        + metrics[direction, 1] * totals[1]
        + metrics[direction, 2] * totals[2]
        for direction in range(3)
    ]


def local(conserved_solution, metrics, jacobian):
    lengths = conserved_solution.shape[1:]
    derive = [jnp.asarray(derivative_table(length), dtype=jnp.float32) for length in lengths]
    smooth = [jnp.asarray(filter_table(length), dtype=jnp.float32) for length in lengths]
    padded = exchange_primitive(conserved_solution, derive[2], 0)
    slopes = [sweep_lines(padded[k], derive[k], k + 1, lax.Precision.HIGH) for k in range(2)]
    slopes.append(padded[2])
    fluid_speed_vector, thermodynamic_stress_scalar = padded[3][0:3], padded[4]
    contra = fluxes(
        conserved_solution,
        fluid_speed_vector,
        thermodynamic_stress_scalar,
        slopes,
        metrics,
        jacobian,
    )
    padded = exchange_faces([(contra[0], "xi", 1), (contra[1], "eta", 2)], 1, (contra[2], derive[2]))
    divergence = sweep_lines(padded[0], derive[0], 1, lax.Precision.HIGH)
    divergence = divergence + sweep_lines(padded[1], derive[1], 2, lax.Precision.HIGH)
    divergence = divergence + padded[2]
    sectioned = conserved_solution - step_duration * jacobian * divergence
    return filter_all(sectioned, smooth, 2)


def solution(mesh):
    in_specs = (
        P(None, "xi", "eta", "zeta"),
        P(None, None, "xi", "eta", "zeta"),
        P("xi", "eta", "zeta"),
    )
    out_specs = P(None, "xi", "eta", "zeta")
    return jax.shard_map(local, mesh=mesh, in_specs=in_specs, out_specs=out_specs, check_vma=False)
```

```python
import functools

import jax
import jax.numpy as jnp
import numpy as np
from jax import lax
from jax.experimental import pallas as pl
from jax.experimental.pallas import tpu as pltpu
from jax.sharding import PartitionSpec as P

WIDTH = 5


viscosity = 0.15
conduction = 0.15 * 1.4 / (0.4 * 0.72)
step_duration = 0.08
line_forms = ("", "al,flyz->fayz", "al,fxlz->fxaz", "al,fxyl->fxya")
MESH = pl.DeviceIdType.MESH
AXES = ("xi", "eta", "zeta")


def primitive_state(conserved):
    density = conserved[0]
    speed = conserved[1:4] / density
    pressure = 0.4 * (conserved[4] - 0.5 * jnp.sum(conserved[1:4] * speed, axis=0))
    return speed, pressure, pressure / density


def exchange_kernel(routes, sizes, count, zeta, prepare, precision, moves, *refs):
    sources = list(refs[:count])
    refs = refs[count:]
    if prepare:
        conserved_ref = sources.pop()
    if zeta:
        if not prepare:
            block_ref = refs[0]
            refs = refs[1:]
        middle_ref, lower_ref, upper_ref = refs[:3]
        refs = refs[3:]
    extra = (1 if zeta else 0) + (2 if prepare else 0)
    targets = refs[: len(refs) - 3 - (3 if zeta else 0) - extra]
    refs = refs[len(targets) :]
    if zeta:
        out_ref = refs[0]
        refs = refs[1:]
    if prepare:
        made, pressure_ref = refs[:2]
        refs = refs[2:]
        sources.append(made)
        if zeta:
            block_ref = made
    if zeta:
        turned, before, after = refs[:3]
        refs = refs[3:]
    send_sems, recv_sems, move_sems = refs
    here = [lax.axis_index(axis) for axis in AXES]

    def device(offset):
        return tuple(
            lax.rem(here[slot] + offset[slot] + sizes[slot], sizes[slot]) for slot in range(3)
        )

    offsets = [route[0] for route in routes] + ([(0, 0, 1), (0, 0, -1)] if zeta else [])
    partners = []
    for offset in offsets:
        for way in (offset, tuple(-step for step in offset)):
            if way not in partners:
                partners.append(way)
    barrier = pltpu.get_barrier_semaphore()
    for offset in partners:
        pl.semaphore_signal(barrier, inc=1, device_id=device(offset), device_id_type=MESH)
    if prepare:
        speed, pressure, temperature = primitive_state(conserved_ref[...])
        made[0:3] = speed
        made[3] = temperature
        pressure_ref[...] = pressure
    if zeta:
        fields, length_x, length_y, depth = block_ref.shape
        rows = fields * length_x * length_y
        if not prepare:
            turned[...] = block_ref[...].reshape(rows, depth).T
            total = jnp.dot(middle_ref[...], turned[...], precision=precision,
                            preferred_element_type=jnp.float32)
    local = []
    for index, (source, source_at, target, target_at) in enumerate(moves):
        local.append(
            pltpu.make_async_copy(
                sources[source].at[source_at], targets[target].at[target_at], move_sems.at[index]
            )
        )
        local[-1].start()
    pl.semaphore_wait(barrier, len(partners))
    copies = []
    for index, (offset, source, source_at, target, target_at) in enumerate(routes):
        copies.append(
            pltpu.make_async_remote_copy(
                src_ref=sources[source].at[source_at],
                dst_ref=targets[target].at[target_at],
                send_sem=send_sems.at[index],
                recv_sem=recv_sems.at[index],
                device_id=device(offset),
                device_id_type=MESH,
            )
        )
        copies[-1].start()
    if zeta and prepare:
        turned[...] = block_ref[...].reshape(rows, depth).T
    if zeta:
        for index, (rows_at, landing, offset) in enumerate(
            ((pl.ds(depth - 8, 8), before, (0, 0, 1)), (pl.ds(0, 8), after, (0, 0, -1)))
        ):
            copies.append(
                pltpu.make_async_remote_copy(
                    src_ref=turned.at[rows_at],
                    dst_ref=landing,
                    send_sem=send_sems.at[len(routes) + index],
                    recv_sem=recv_sems.at[len(routes) + index],
                    device_id=device(offset),
                    device_id_type=MESH,
                )
            )
            copies[-1].start()
    if zeta and prepare:
        total = jnp.dot(middle_ref[...], turned[...], precision=precision,
                        preferred_element_type=jnp.float32)
    for copy in copies + local:
        copy.wait()
    if zeta:
        total = total + jnp.dot(lower_ref[...], before[...], precision=precision,
                                preferred_element_type=jnp.float32)
        total = total + jnp.dot(upper_ref[...], after[...], precision=precision,
                                preferred_element_type=jnp.float32)
        out_ref[...] = total.T.reshape(fields, length_x, length_y, depth)


def exchange(arrays, routes, out_shapes, tag, zeta=None, prepare=None,
             precision=lax.Precision.HIGH, moves=()):
    sizes = tuple(lax.axis_size(axis) for axis in AXES)
    operands = [array for array, _ in arrays]
    in_specs = [pl.BlockSpec(memory_space=space) for _, space in arrays]
    out_specs = [pl.BlockSpec(memory_space=pl.ANY)] * len(out_shapes)
    out_shapes = list(out_shapes)
    scratch = []
    copies = len(routes)
    if prepare is not None:
        operands.append(prepare)
        in_specs.append(pl.BlockSpec(memory_space=pltpu.VMEM))
    if zeta is not None:
        value, matrix = zeta
        fields, length_x, length_y, depth = value.shape
        rows = fields * length_x * length_y
        padding = jnp.zeros((depth, 8 - WIDTH), matrix.dtype)
        if prepare is None:
            operands.append(value)
            in_specs.append(pl.BlockSpec(memory_space=pltpu.VMEM))
        operands += [
            matrix[:, WIDTH : WIDTH + depth],
            jnp.concatenate([padding, matrix[:, :WIDTH]], axis=1),
            jnp.concatenate([matrix[:, WIDTH + depth :], padding], axis=1),
        ]
        in_specs += [pl.BlockSpec(memory_space=pltpu.VMEM)] * 3
        out_shapes.append(jax.ShapeDtypeStruct(value.shape, value.dtype))
        out_specs.append(pl.BlockSpec(memory_space=pltpu.VMEM))
        scratch = [pltpu.VMEM((depth, rows), jnp.float32), pltpu.VMEM((8, rows), jnp.float32),
                   pltpu.VMEM((8, rows), jnp.float32)]
        copies += 2
    if prepare is not None:
        out_shapes += [
            jax.ShapeDtypeStruct(zeta[0].shape, jnp.float32),
            jax.ShapeDtypeStruct(prepare.shape[1:], jnp.float32),
        ]
        out_specs += [pl.BlockSpec(memory_space=pltpu.VMEM)] * 2
    return pl.pallas_call(
        functools.partial(
            exchange_kernel, tuple(routes), sizes, len(arrays) + (prepare is not None),
            zeta is not None, prepare is not None, precision, tuple(moves),
        ),
        out_shape=out_shapes,
        in_specs=in_specs,
        out_specs=out_specs,
        scratch_shapes=scratch + [
            pltpu.SemaphoreType.DMA((copies,)),
            pltpu.SemaphoreType.DMA((copies,)),
            pltpu.SemaphoreType.DMA((max(1, len(moves)),)),
        ],
        compiler_params=pltpu.CompilerParams(collective_id=tag, has_side_effects=True),
    )(*operands)


def offset_along(axis, step):
    return tuple(step if name == axis else 0 for name in AXES)


def window(ndim, dim, start, stop):
    return tuple(slice(start, stop) if axis == dim else slice(None) for axis in range(ndim))


def exchange_faces(items, tag, zeta=None):
    arrays, routes, out_shapes, moves = [], [], [], []
    for value, axis, dim in items:
        ndim, length = value.ndim, value.shape[dim]
        if dim == ndim - 1:
            both = jnp.stack(
                [
                    lax.slice_in_dim(value, length - WIDTH, length, axis=dim),
                    lax.slice_in_dim(value, 0, WIDTH, axis=dim),
                ]
            )
            both = jnp.moveaxis(both, dim + 1, 2).reshape(2, value.shape[0], WIDTH, -1)
            arrays.append((both, pl.ANY))
            out_shapes.append(jax.ShapeDtypeStruct(both.shape, both.dtype))
            source, target = len(arrays) - 1, len(out_shapes) - 1
            routes.append((offset_along(axis, 1), source, 0, target, 0))
            routes.append((offset_along(axis, -1), source, 1, target, 1))
        elif dim == ndim - 2:
            face = value.shape[:dim] + (WIDTH,) + value.shape[dim + 1 :]
            arrays.append((value, pltpu.VMEM))
            out_shapes += [jax.ShapeDtypeStruct(face, value.dtype)] * 2
            source, target = len(arrays) - 1, len(out_shapes) - 2
            whole = window(ndim, dim, None, None)
            last, first = window(ndim, dim, length - WIDTH, length), window(ndim, dim, 0, WIDTH)
            routes.append((offset_along(axis, 1), source, last, target, whole))
            routes.append((offset_along(axis, -1), source, first, target + 1, whole))
        else:
            arrays += [(value, pl.ANY), (value, pltpu.VMEM)]
            extended = value.shape[:dim] + (length + 2 * WIDTH,) + value.shape[dim + 1 :]
            out_shapes.append(jax.ShapeDtypeStruct(extended, value.dtype))
            source, target = len(arrays) - 2, len(out_shapes) - 1
            last, first = window(ndim, dim, length - WIDTH, length), window(ndim, dim, 0, WIDTH)
            ahead = window(ndim, dim, length + WIDTH, length + 2 * WIDTH)
            routes.append((offset_along(axis, 1), source, last, target, first))
            routes.append((offset_along(axis, -1), source, first, target, ahead))
            moves.append((source + 1, window(ndim, dim, None, None), target,
                          window(ndim, dim, WIDTH, length + WIDTH)))
    received = exchange(arrays, routes, out_shapes, tag, zeta, moves=moves)
    padded, place = [], 0
    for value, axis, dim in items:
        if dim == value.ndim - 1:
            both = received[place].reshape((2, value.shape[0], WIDTH) + value.shape[1:dim])
            both = jnp.moveaxis(both, 2, dim + 1)
            before, after = both[0], both[1]
            place += 1
        elif dim == value.ndim - 2:
            before, after = received[place], received[place + 1]
            place += 2
        else:
            padded.append(received[place])
            place += 1
            continue
        padded.append(jnp.concatenate([before, value, after], axis=dim))
    if zeta is not None:
        padded.append(received[-1])
    return padded


def exchange_primitive(conserved, matrix, tag):
    primitive = jax.ShapeDtypeStruct((4,) + conserved.shape[1:], conserved.dtype)
    length_x, length_y = primitive.shape[1], primitive.shape[2]
    every = slice(None)
    routes = [
        ((1, 0, 0), 0, (every, slice(length_x - WIDTH, length_x)), 0, (every, slice(0, WIDTH))),
        ((-1, 0, 0), 0, (every, slice(0, WIDTH)), 0, (every, slice(length_x + WIDTH, length_x + 2 * WIDTH))),
        ((0, 1, 0), 0, (every, every, slice(length_y - WIDTH, length_y)), 1, every),
        ((0, -1, 0), 0, (every, every, slice(0, WIDTH)), 2, every),
    ]
    moves = [(0, every, 0, (every, slice(WIDTH, length_x + WIDTH)))]
    extended_x = (primitive.shape[0], length_x + 2 * WIDTH) + primitive.shape[2:]
    face_y = primitive.shape[:2] + (WIDTH,) + primitive.shape[3:]
    out_shapes = [jax.ShapeDtypeStruct(face, primitive.dtype) for face in (extended_x, face_y, face_y)]
    padded_x, before_y, after_y, swept, primitive, pressure = exchange(
        [], routes, out_shapes, tag, (primitive, matrix), conserved, moves=moves
    )
    return (
        padded_x,
        jnp.concatenate([before_y, primitive, after_y], axis=2),
        swept,
        primitive,
        pressure,
    )


def exchange_plane(value, tag):
    length_x, length_y = value.shape[1], value.shape[2]
    faces_y = jnp.stack(
        [
            lax.slice_in_dim(value, length_y - WIDTH, length_y, axis=2),
            lax.slice_in_dim(value, 0, WIDTH, axis=2),
        ]
    )
    last_x, first_x = slice(length_x - WIDTH, length_x), slice(0, WIDTH)
    every = slice(None)
    routes = [
        ((1, 0, 0), 0, (every, last_x), 0, every),
        ((-1, 0, 0), 0, (every, first_x), 1, every),
        ((0, 1, 0), 1, 0, 2, every),
        ((0, -1, 0), 1, 1, 3, every),
        ((1, 1, 0), 1, (0, every, last_x), 4, every),
        ((-1, 1, 0), 1, (0, every, first_x), 5, every),
        ((1, -1, 0), 1, (1, every, last_x), 6, every),
        ((-1, -1, 0), 1, (1, every, first_x), 7, every),
    ]
    fields, depth = value.shape[0], value.shape[3]
    out_shapes = (
        [jax.ShapeDtypeStruct((fields, WIDTH, length_y, depth), value.dtype)] * 2
        + [jax.ShapeDtypeStruct((fields, length_x, WIDTH, depth), value.dtype)] * 2
        + [jax.ShapeDtypeStruct((fields, WIDTH, WIDTH, depth), value.dtype)] * 4
    )
    x_before, x_after, y_before, y_after, both_before, x_after_y_before, x_before_y_after, both_after = (
        exchange([(value, pl.ANY), (faces_y, pl.ANY)], routes, out_shapes, tag)
    )
    sections = [
        jnp.concatenate([both_before, x_before, x_before_y_after], axis=2),
        jnp.concatenate([y_before, value, y_after], axis=2),
        jnp.concatenate([x_after_y_before, x_after, both_after], axis=2),
    ]
    return jnp.concatenate(sections, axis=1)


def filter_kernel(sizes, value_ref, middle_ref, lower_ref, upper_ref, smooth_ref, *refs):
    faces = refs[:8]
    turned, before, after, stacked, send_sems, recv_sems = refs[8:]
    fields, length_x, length_y, depth = value_ref.shape
    rows = fields * length_x * length_y
    here = [lax.axis_index(axis) for axis in AXES]

    def device(offset):
        return tuple(
            lax.rem(here[slot] + offset[slot] + sizes[slot], sizes[slot]) for slot in range(3)
        )

    plane = [(1, 0, 0), (-1, 0, 0), (0, 1, 0), (0, -1, 0), (1, 1, 0), (-1, 1, 0), (1, -1, 0), (-1, -1, 0)]
    partners = plane + [(0, 0, 1), (0, 0, -1)]
    barrier = pltpu.get_barrier_semaphore()
    for offset in partners:
        pl.semaphore_signal(barrier, inc=1, device_id=device(offset), device_id_type=MESH)
    turned[...] = value_ref[...].reshape(rows, depth).T
    total = jnp.dot(middle_ref[...], turned[...], precision=lax.Precision.HIGHEST,
                    preferred_element_type=jnp.float32)
    pl.semaphore_wait(barrier, len(partners))
    along_z = [
        pltpu.make_async_remote_copy(
            src_ref=turned.at[pl.ds(depth - 8, 8)], dst_ref=before,
            send_sem=send_sems.at[8], recv_sem=recv_sems.at[8],
            device_id=device((0, 0, 1)), device_id_type=MESH,
        ),
        pltpu.make_async_remote_copy(
            src_ref=turned.at[pl.ds(0, 8)], dst_ref=after,
            send_sem=send_sems.at[9], recv_sem=recv_sems.at[9],
            device_id=device((0, 0, -1)), device_id_type=MESH,
        ),
    ]
    for copy in along_z:
        copy.start()
    for copy in along_z:
        copy.wait()
    total = total + jnp.dot(lower_ref[...], before[...], precision=lax.Precision.HIGHEST,
                            preferred_element_type=jnp.float32)
    total = total + jnp.dot(upper_ref[...], after[...], precision=lax.Precision.HIGHEST,
                            preferred_element_type=jnp.float32)
    smooth_ref[...] = total.T.reshape(fields, length_x, length_y, depth)
    last_x, first_x = pl.ds(length_x - WIDTH, WIDTH), pl.ds(0, WIDTH)
    every = slice(None)
    sources = [
        smooth_ref.at[every, last_x], smooth_ref.at[every, first_x],
        stacked.at[0], stacked.at[1],
        stacked.at[0, every, last_x], stacked.at[0, every, first_x],
        stacked.at[1, every, last_x], stacked.at[1, every, first_x],
    ]
    copies = []
    for index, offset in enumerate(plane):
        if index == 2:
            stacked[0] = smooth_ref[:, :, length_y - WIDTH :, :]
            stacked[1] = smooth_ref[:, :, :WIDTH, :]
        copies.append(
            pltpu.make_async_remote_copy(
                src_ref=sources[index], dst_ref=faces[index],
                send_sem=send_sems.at[index], recv_sem=recv_sems.at[index],
                device_id=device(offset), device_id_type=MESH,
            )
        )
        copies[-1].start()
    for copy in copies:
        copy.wait()


def filter_all(value, smooth, tag):
    sizes = tuple(lax.axis_size(axis) for axis in AXES)
    fields, length_x, length_y, depth = value.shape
    rows = fields * length_x * length_y
    matrix = smooth[2]
    padding = jnp.zeros((depth, 8 - WIDTH), matrix.dtype)
    x_face = jax.ShapeDtypeStruct((fields, WIDTH, length_y, depth), value.dtype)
    y_face = jax.ShapeDtypeStruct((fields, length_x, WIDTH, depth), value.dtype)
    edge = jax.ShapeDtypeStruct((fields, WIDTH, WIDTH, depth), value.dtype)
    outs = pl.pallas_call(
        functools.partial(filter_kernel, sizes),
        out_shape=[jax.ShapeDtypeStruct(value.shape, value.dtype)] + [x_face] * 2 + [y_face] * 2 + [edge] * 4,
        in_specs=[pl.BlockSpec(memory_space=pltpu.VMEM)] * 4,
        out_specs=[pl.BlockSpec(memory_space=pltpu.VMEM)] + [pl.BlockSpec(memory_space=pl.ANY)] * 8,
        scratch_shapes=[
            pltpu.VMEM((depth, rows), jnp.float32),
            pltpu.VMEM((8, rows), jnp.float32),
            pltpu.VMEM((8, rows), jnp.float32),
            pltpu.VMEM((2, fields, length_x, WIDTH, depth), jnp.float32),
            pltpu.SemaphoreType.DMA((10,)),
            pltpu.SemaphoreType.DMA((10,)),
        ],
        compiler_params=pltpu.CompilerParams(collective_id=tag, has_side_effects=True),
    )(
        value,
        matrix[:, WIDTH : WIDTH + depth],
        jnp.concatenate([padding, matrix[:, :WIDTH]], axis=1),
        jnp.concatenate([matrix[:, WIDTH + depth :], padding], axis=1),
    )
    smoothed, x_before, x_after, y_before, y_after, both_before, x_after_y_before, x_before_y_after, both_after = outs
    sections = [
        jnp.concatenate([both_before, x_before, x_before_y_after], axis=2),
        jnp.concatenate([y_before, smoothed, y_after], axis=2),
        jnp.concatenate([x_after_y_before, x_after, both_after], axis=2),
    ]
    result = sweep_lines(jnp.concatenate(sections, axis=1), smooth[0], 1)
    return sweep_lines(result, smooth[1], 2)


def sweep_zeta(value, matrix, tag):
    return exchange([], [], [], tag, (value, matrix), precision=lax.Precision.HIGHEST)[-1]


def with_halo(value, sides, width):
    for axis, dim in sides:
        count, length = (lax.axis_size(axis), value.shape[dim])
        up = [(i, (i + 1) % count) for i in range(count)]
        down = [(j, i) for i, j in up]
        last = lax.slice_in_dim(value, length - width, length, axis=dim)
        initial = lax.slice_in_dim(value, 0, width, axis=dim)
        before = lax.ppermute(last, axis, up)
        after = lax.ppermute(initial, axis, down)
        value = jnp.concatenate([before, value, after], axis=dim)
    return value


def banded_solve(system, source):
    extent = system.shape[0]
    lower = np.zeros(extent)
    upper = np.zeros(extent)
    middle = np.array([float(system[index, index]) for index in range(extent)])
    for index in range(1, extent):
        lower[index] = system[index, index - 1]
        upper[index - 1] = system[index - 1, index]
    rights = np.array(source)
    for index in range(1, extent):
        factor = lower[index] / middle[index - 1]
        middle[index] = middle[index] - factor * upper[index - 1]
        rights[index] = rights[index] - factor * rights[index - 1]
    answer = np.zeros(rights.shape)
    answer[extent - 1] = rights[extent - 1] / middle[extent - 1]
    for index in range(extent - 2, -1, -1):
        answer[index] = (rights[index] - upper[index] * answer[index + 1]) / middle[index]
    return answer


def derivative_table(length):
    extent = length + 2 * WIDTH
    system = np.eye(extent)
    source = np.zeros((extent, extent))
    for position in range(2, extent - 2):
        system[position, position - 1] = 1.0 / 3.0
        system[position, position + 1] = 1.0 / 3.0
        source[position, position + 1] = 7.0 / 9.0
        source[position, position - 1] = -7.0 / 9.0
        source[position, position + 2] = 1.0 / 36.0
        source[position, position - 2] = -1.0 / 36.0
    source[1, 2] = 0.5
    source[1, 0] = -0.5
    source[extent - 2, extent - 1] = 0.5
    source[extent - 2, extent - 3] = -0.5
    source[0, 1] = 1.0
    source[0, 0] = -1.0
    source[extent - 1, extent - 1] = 1.0
    source[extent - 1, extent - 2] = -1.0
    return banded_solve(system, source)[WIDTH : WIDTH + length]


def filter_table(length):
    strength = 0.4
    coeffs = [
        (193.0 + 126.0 * strength) / 256.0,
        (105.0 + 302.0 * strength) / 256.0,
        15.0 * (2.0 * strength - 1.0) / 64.0,
        45.0 * (1.0 - 2.0 * strength) / 512.0,
        5.0 * (2.0 * strength - 1.0) / 256.0,
        (1.0 - 2.0 * strength) / 512.0,
    ]
    extent = length + 2 * WIDTH
    system = np.eye(extent)
    source = np.eye(extent)
    for position in range(5, extent - 5):
        system[position, position - 1] = strength
        system[position, position + 1] = strength
        source[position, position] = coeffs[0]
        for offset in range(1, 6):
            source[position, position + offset] = coeffs[offset] / 2.0
            source[position, position - offset] = coeffs[offset] / 2.0
    return banded_solve(system, source)[WIDTH : WIDTH + length]


def sweep_lines(padded, matrix, dim, precision=lax.Precision.HIGHEST):
    return jnp.einsum(line_forms[dim], matrix, padded, precision=precision)


def faces_xi(values):
    return with_halo(values, (("xi", 1),), WIDTH)


def faces_eta(values):
    return with_halo(values, (("eta", 2),), WIDTH)


def faces_zeta(values):
    return with_halo(values, (("zeta", 3),), WIDTH)


def basic_quantities(conserved_solution):
    density = conserved_solution[0]
    fluid_speed_vector = conserved_solution[1:4] / density
    thermodynamic_stress_scalar = 0.4 * (
        conserved_solution[4] - 0.5 * jnp.sum(conserved_solution[1:4] * fluid_speed_vector, axis=0)
    )
    return (fluid_speed_vector, thermodynamic_stress_scalar, thermodynamic_stress_scalar / density)


def fluxes(
    conserved_solution, fluid_speed_vector, thermodynamic_stress_scalar, slopes, metrics, jacobian
):
    physical = [
        [
            jacobian
            * (
                metrics[0, column] * slopes[0][member]
                + metrics[1, column] * slopes[1][member]
                + metrics[2, column] * slopes[2][member]
            )
            for column in range(3)
        ]
        for member in range(4)
    ]
    spread = physical[0][0] + physical[1][1] + physical[2][2]
    totals = []
    for column in range(3):
        stress = [
            viscosity * (physical[member][column] + physical[column][member]) for member in range(3)
        ]
        stress[column] = stress[column] - 2.0 / 3.0 * viscosity * spread
        subdomain_parts = [conserved_solution[1 + column]]
        for member in range(3):
            carried = conserved_solution[1 + member] * fluid_speed_vector[column] - stress[member]
            if member == column:
                carried = carried + thermodynamic_stress_scalar
            subdomain_parts.append(carried)
        worked = (
            fluid_speed_vector[0] * stress[0]
            + fluid_speed_vector[1] * stress[1]
            + fluid_speed_vector[2] * stress[2]
        )
        subdomain_parts.append(
            (conserved_solution[4] + thermodynamic_stress_scalar) * fluid_speed_vector[column]
            - worked
            - conduction * physical[3][column]
        )
        totals.append(jnp.stack(subdomain_parts))
    return [
        metrics[direction, 0] * totals[0]
        + metrics[direction, 1] * totals[1]
        + metrics[direction, 2] * totals[2]
        for direction in range(3)
    ]


def local(conserved_solution, metrics, jacobian):
    lengths = conserved_solution.shape[1:]
    derive = [jnp.asarray(derivative_table(length), dtype=jnp.float32) for length in lengths]
    smooth = [jnp.asarray(filter_table(length), dtype=jnp.float32) for length in lengths]
    padded = exchange_primitive(conserved_solution, derive[2], 0)
    slopes = [sweep_lines(padded[k], derive[k], k + 1, lax.Precision.HIGH) for k in range(2)]
    slopes.append(padded[2])
    fluid_speed_vector, thermodynamic_stress_scalar = padded[3][0:3], padded[4]
    contra = fluxes(
        conserved_solution,
        fluid_speed_vector,
        thermodynamic_stress_scalar,
        slopes,
        metrics,
        jacobian,
    )
    padded = exchange_faces([(contra[0], "xi", 1), (contra[1], "eta", 2)], 1, (contra[2], derive[2]))
    divergence = sweep_lines(padded[0], derive[0], 1, lax.Precision.HIGH)
    divergence = divergence + sweep_lines(padded[1], derive[1], 2, lax.Precision.HIGH)
    divergence = divergence + padded[2]
    sectioned = conserved_solution - step_duration * jacobian * divergence
    return filter_all(sectioned, smooth, 2)


def solution(mesh):
    in_specs = (
        P(None, "xi", "eta", "zeta"),
        P(None, None, "xi", "eta", "zeta"),
        P("xi", "eta", "zeta"),
    )
    out_specs = P(None, "xi", "eta", "zeta")
    return jax.shard_map(local, mesh=mesh, in_specs=in_specs, out_specs=out_specs, check_vma=False)
```

```python
import functools

import jax
import jax.numpy as jnp
import numpy as np
from jax import lax
from jax.experimental import pallas as pl
from jax.experimental.pallas import tpu as pltpu
from jax.sharding import PartitionSpec as P

WIDTH = 5


viscosity = 0.15
conduction = 0.15 * 1.4 / (0.4 * 0.72)
step_duration = 0.08
line_forms = ("", "al,flyz->fayz", "al,fxlz->fxaz", "al,fxyl->fxya")
MESH = pl.DeviceIdType.MESH
AXES = ("xi", "eta", "zeta")


def primitive_state(conserved):
    density = conserved[0]
    speed = conserved[1:4] / density
    pressure = 0.4 * (conserved[4] - 0.5 * jnp.sum(conserved[1:4] * speed, axis=0))
    return speed, pressure, pressure / density


def exchange_kernel(routes, sizes, count, zeta, prepare, precision, moves, *refs):
    sources = list(refs[:count])
    refs = refs[count:]
    if prepare:
        conserved_ref = sources.pop()
    if zeta:
        if not prepare:
            block_ref = refs[0]
            refs = refs[1:]
        middle_ref, lower_ref, upper_ref = refs[:3]
        refs = refs[3:]
    extra = (1 if zeta else 0) + (2 if prepare else 0)
    targets = refs[: len(refs) - 3 - (3 if zeta else 0) - extra]
    refs = refs[len(targets) :]
    if zeta:
        out_ref = refs[0]
        refs = refs[1:]
    if prepare:
        made, pressure_ref = refs[:2]
        refs = refs[2:]
        sources.append(made)
        if zeta:
            block_ref = made
    if zeta:
        turned, before, after = refs[:3]
        refs = refs[3:]
    send_sems, recv_sems, move_sems = refs
    here = [lax.axis_index(axis) for axis in AXES]

    def device(offset):
        return tuple(
            lax.rem(here[slot] + offset[slot] + sizes[slot], sizes[slot]) for slot in range(3)
        )

    offsets = [route[0] for route in routes] + ([(0, 0, 1), (0, 0, -1)] if zeta else [])
    partners = []
    for offset in offsets:
        for way in (offset, tuple(-step for step in offset)):
            if way not in partners:
                partners.append(way)
    barrier = pltpu.get_barrier_semaphore()
    for offset in partners:
        pl.semaphore_signal(barrier, inc=1, device_id=device(offset), device_id_type=MESH)
    if prepare:
        speed, pressure, temperature = primitive_state(conserved_ref[...])
        made[0:3] = speed
        made[3] = temperature
        pressure_ref[...] = pressure
    if zeta:
        fields, length_x, length_y, depth = block_ref.shape
        rows = fields * length_x * length_y
        turned[...] = block_ref[...].reshape(rows, depth).T
        if not prepare:
            total = jnp.dot(middle_ref[...], turned[...], precision=precision,
                            preferred_element_type=jnp.float32)
    local = []
    for index, (source, source_at, target, target_at) in enumerate(moves):
        local.append(
            pltpu.make_async_copy(
                sources[source].at[source_at], targets[target].at[target_at], move_sems.at[index]
            )
        )
        local[-1].start()
    pl.semaphore_wait(barrier, len(partners))
    copies = []
    for index, (offset, source, source_at, target, target_at) in enumerate(routes):
        copies.append(
            pltpu.make_async_remote_copy(
                src_ref=sources[source].at[source_at],
                dst_ref=targets[target].at[target_at],
                send_sem=send_sems.at[index],
                recv_sem=recv_sems.at[index],
                device_id=device(offset),
                device_id_type=MESH,
            )
        )
    if zeta:
        for index, (rows_at, landing, offset) in enumerate(
            ((pl.ds(depth - 8, 8), before, (0, 0, 1)), (pl.ds(0, 8), after, (0, 0, -1)))
        ):
            copies.append(
                pltpu.make_async_remote_copy(
                    src_ref=turned.at[rows_at],
                    dst_ref=landing,
                    send_sem=send_sems.at[len(routes) + index],
                    recv_sem=recv_sems.at[len(routes) + index],
                    device_id=device(offset),
                    device_id_type=MESH,
                )
            )
    for copy in copies:
        copy.start()
    if zeta and prepare:
        total = jnp.dot(middle_ref[...], turned[...], precision=precision,
                        preferred_element_type=jnp.float32)
    for copy in copies + local:
        copy.wait()
    if zeta:
        total = total + jnp.dot(lower_ref[...], before[...], precision=precision,
                                preferred_element_type=jnp.float32)
        total = total + jnp.dot(upper_ref[...], after[...], precision=precision,
                                preferred_element_type=jnp.float32)
        out_ref[...] = total.T.reshape(fields, length_x, length_y, depth)


def exchange(arrays, routes, out_shapes, tag, zeta=None, prepare=None,
             precision=lax.Precision.HIGH, moves=()):
    sizes = tuple(lax.axis_size(axis) for axis in AXES)
    operands = [array for array, _ in arrays]
    in_specs = [pl.BlockSpec(memory_space=space) for _, space in arrays]
    out_specs = [pl.BlockSpec(memory_space=pl.ANY)] * len(out_shapes)
    out_shapes = list(out_shapes)
    scratch = []
    copies = len(routes)
    if prepare is not None:
        operands.append(prepare)
        in_specs.append(pl.BlockSpec(memory_space=pltpu.VMEM))
    if zeta is not None:
        value, matrix = zeta
        fields, length_x, length_y, depth = value.shape
        rows = fields * length_x * length_y
        padding = jnp.zeros((depth, 8 - WIDTH), matrix.dtype)
        if prepare is None:
            operands.append(value)
            in_specs.append(pl.BlockSpec(memory_space=pltpu.VMEM))
        operands += [
            matrix[:, WIDTH : WIDTH + depth],
            jnp.concatenate([padding, matrix[:, :WIDTH]], axis=1),
            jnp.concatenate([matrix[:, WIDTH + depth :], padding], axis=1),
        ]
        in_specs += [pl.BlockSpec(memory_space=pltpu.VMEM)] * 3
        out_shapes.append(jax.ShapeDtypeStruct(value.shape, value.dtype))
        out_specs.append(pl.BlockSpec(memory_space=pltpu.VMEM))
        scratch = [pltpu.VMEM((depth, rows), jnp.float32), pltpu.VMEM((8, rows), jnp.float32),
                   pltpu.VMEM((8, rows), jnp.float32)]
        copies += 2
    if prepare is not None:
        out_shapes += [
            jax.ShapeDtypeStruct(zeta[0].shape, jnp.float32),
            jax.ShapeDtypeStruct(prepare.shape[1:], jnp.float32),
        ]
        out_specs += [pl.BlockSpec(memory_space=pltpu.VMEM)] * 2
    return pl.pallas_call(
        functools.partial(
            exchange_kernel, tuple(routes), sizes, len(arrays) + (prepare is not None),
            zeta is not None, prepare is not None, precision, tuple(moves),
        ),
        out_shape=out_shapes,
        in_specs=in_specs,
        out_specs=out_specs,
        scratch_shapes=scratch + [
            pltpu.SemaphoreType.DMA((copies,)),
            pltpu.SemaphoreType.DMA((copies,)),
            pltpu.SemaphoreType.DMA((max(1, len(moves)),)),
        ],
        compiler_params=pltpu.CompilerParams(collective_id=tag, has_side_effects=True),
    )(*operands)


def offset_along(axis, step):
    return tuple(step if name == axis else 0 for name in AXES)


def window(ndim, dim, start, stop):
    return tuple(slice(start, stop) if axis == dim else slice(None) for axis in range(ndim))


def exchange_faces(items, tag, zeta=None):
    arrays, routes, out_shapes, moves = [], [], [], []
    for value, axis, dim in items:
        ndim, length = value.ndim, value.shape[dim]
        if dim == ndim - 1:
            both = jnp.stack(
                [
                    lax.slice_in_dim(value, length - WIDTH, length, axis=dim),
                    lax.slice_in_dim(value, 0, WIDTH, axis=dim),
                ]
            )
            both = jnp.moveaxis(both, dim + 1, 2).reshape(2, value.shape[0], WIDTH, -1)
            arrays.append((both, pl.ANY))
            out_shapes.append(jax.ShapeDtypeStruct(both.shape, both.dtype))
            source, target = len(arrays) - 1, len(out_shapes) - 1
            routes.append((offset_along(axis, 1), source, 0, target, 0))
            routes.append((offset_along(axis, -1), source, 1, target, 1))
        elif dim == ndim - 2:
            face = value.shape[:dim] + (WIDTH,) + value.shape[dim + 1 :]
            arrays.append((value, pltpu.VMEM))
            out_shapes += [jax.ShapeDtypeStruct(face, value.dtype)] * 2
            source, target = len(arrays) - 1, len(out_shapes) - 2
            whole = window(ndim, dim, None, None)
            last, first = window(ndim, dim, length - WIDTH, length), window(ndim, dim, 0, WIDTH)
            routes.append((offset_along(axis, 1), source, last, target, whole))
            routes.append((offset_along(axis, -1), source, first, target + 1, whole))
        else:
            arrays += [(value, pl.ANY), (value, pltpu.VMEM)]
            extended = value.shape[:dim] + (length + 2 * WIDTH,) + value.shape[dim + 1 :]
            out_shapes.append(jax.ShapeDtypeStruct(extended, value.dtype))
            source, target = len(arrays) - 2, len(out_shapes) - 1
            last, first = window(ndim, dim, length - WIDTH, length), window(ndim, dim, 0, WIDTH)
            ahead = window(ndim, dim, length + WIDTH, length + 2 * WIDTH)
            routes.append((offset_along(axis, 1), source, last, target, first))
            routes.append((offset_along(axis, -1), source, first, target, ahead))
            moves.append((source + 1, window(ndim, dim, None, None), target,
                          window(ndim, dim, WIDTH, length + WIDTH)))
    received = exchange(arrays, routes, out_shapes, tag, zeta, moves=moves)
    padded, place = [], 0
    for value, axis, dim in items:
        if dim == value.ndim - 1:
            both = received[place].reshape((2, value.shape[0], WIDTH) + value.shape[1:dim])
            both = jnp.moveaxis(both, 2, dim + 1)
            before, after = both[0], both[1]
            place += 1
        elif dim == value.ndim - 2:
            before, after = received[place], received[place + 1]
            place += 2
        else:
            padded.append(received[place])
            place += 1
            continue
        padded.append(jnp.concatenate([before, value, after], axis=dim))
    if zeta is not None:
        padded.append(received[-1])
    return padded


def exchange_primitive(conserved, matrix, tag):
    primitive = jax.ShapeDtypeStruct((4,) + conserved.shape[1:], conserved.dtype)
    length_x, length_y = primitive.shape[1], primitive.shape[2]
    every = slice(None)
    routes = [
        ((1, 0, 0), 0, (every, slice(length_x - WIDTH, length_x)), 0, (every, slice(0, WIDTH))),
        ((-1, 0, 0), 0, (every, slice(0, WIDTH)), 0, (every, slice(length_x + WIDTH, length_x + 2 * WIDTH))),
        ((0, 1, 0), 0, (every, every, slice(length_y - WIDTH, length_y)), 1, every),
        ((0, -1, 0), 0, (every, every, slice(0, WIDTH)), 2, every),
    ]
    moves = [(0, every, 0, (every, slice(WIDTH, length_x + WIDTH)))]
    extended_x = (primitive.shape[0], length_x + 2 * WIDTH) + primitive.shape[2:]
    face_y = primitive.shape[:2] + (WIDTH,) + primitive.shape[3:]
    out_shapes = [jax.ShapeDtypeStruct(face, primitive.dtype) for face in (extended_x, face_y, face_y)]
    padded_x, before_y, after_y, swept, primitive, pressure = exchange(
        [], routes, out_shapes, tag, (primitive, matrix), conserved, moves=moves
    )
    return (
        padded_x,
        jnp.concatenate([before_y, primitive, after_y], axis=2),
        swept,
        primitive,
        pressure,
    )


def exchange_plane(value, tag):
    length_x, length_y = value.shape[1], value.shape[2]
    faces_y = jnp.stack(
        [
            lax.slice_in_dim(value, length_y - WIDTH, length_y, axis=2),
            lax.slice_in_dim(value, 0, WIDTH, axis=2),
        ]
    )
    last_x, first_x = slice(length_x - WIDTH, length_x), slice(0, WIDTH)
    every = slice(None)
    routes = [
        ((1, 0, 0), 0, (every, last_x), 0, every),
        ((-1, 0, 0), 0, (every, first_x), 1, every),
        ((0, 1, 0), 1, 0, 2, every),
        ((0, -1, 0), 1, 1, 3, every),
        ((1, 1, 0), 1, (0, every, last_x), 4, every),
        ((-1, 1, 0), 1, (0, every, first_x), 5, every),
        ((1, -1, 0), 1, (1, every, last_x), 6, every),
        ((-1, -1, 0), 1, (1, every, first_x), 7, every),
    ]
    fields, depth = value.shape[0], value.shape[3]
    out_shapes = (
        [jax.ShapeDtypeStruct((fields, WIDTH, length_y, depth), value.dtype)] * 2
        + [jax.ShapeDtypeStruct((fields, length_x, WIDTH, depth), value.dtype)] * 2
        + [jax.ShapeDtypeStruct((fields, WIDTH, WIDTH, depth), value.dtype)] * 4
    )
    x_before, x_after, y_before, y_after, both_before, x_after_y_before, x_before_y_after, both_after = (
        exchange([(value, pl.ANY), (faces_y, pl.ANY)], routes, out_shapes, tag)
    )
    sections = [
        jnp.concatenate([both_before, x_before, x_before_y_after], axis=2),
        jnp.concatenate([y_before, value, y_after], axis=2),
        jnp.concatenate([x_after_y_before, x_after, both_after], axis=2),
    ]
    return jnp.concatenate(sections, axis=1)


def filter_kernel(sizes, value_ref, middle_ref, lower_ref, upper_ref, smooth_ref, *refs):
    faces = refs[:8]
    turned, before, after, stacked, send_sems, recv_sems = refs[8:]
    fields, length_x, length_y, depth = value_ref.shape
    rows = fields * length_x * length_y
    here = [lax.axis_index(axis) for axis in AXES]

    def device(offset):
        return tuple(
            lax.rem(here[slot] + offset[slot] + sizes[slot], sizes[slot]) for slot in range(3)
        )

    plane = [(1, 0, 0), (-1, 0, 0), (0, 1, 0), (0, -1, 0), (1, 1, 0), (-1, 1, 0), (1, -1, 0), (-1, -1, 0)]
    partners = plane + [(0, 0, 1), (0, 0, -1)]
    barrier = pltpu.get_barrier_semaphore()
    for offset in partners:
        pl.semaphore_signal(barrier, inc=1, device_id=device(offset), device_id_type=MESH)
    turned[...] = value_ref[...].reshape(rows, depth).T
    total = jnp.dot(middle_ref[...], turned[...], precision=lax.Precision.HIGHEST,
                    preferred_element_type=jnp.float32)
    pl.semaphore_wait(barrier, len(partners))
    along_z = [
        pltpu.make_async_remote_copy(
            src_ref=turned.at[pl.ds(depth - 8, 8)], dst_ref=before,
            send_sem=send_sems.at[8], recv_sem=recv_sems.at[8],
            device_id=device((0, 0, 1)), device_id_type=MESH,
        ),
        pltpu.make_async_remote_copy(
            src_ref=turned.at[pl.ds(0, 8)], dst_ref=after,
            send_sem=send_sems.at[9], recv_sem=recv_sems.at[9],
            device_id=device((0, 0, -1)), device_id_type=MESH,
        ),
    ]
    for copy in along_z:
        copy.start()
    for copy in along_z:
        copy.wait()
    total = total + jnp.dot(lower_ref[...], before[...], precision=lax.Precision.HIGHEST,
                            preferred_element_type=jnp.float32)
    total = total + jnp.dot(upper_ref[...], after[...], precision=lax.Precision.HIGHEST,
                            preferred_element_type=jnp.float32)
    smooth_ref[...] = total.T.reshape(fields, length_x, length_y, depth)
    last_x, first_x = pl.ds(length_x - WIDTH, WIDTH), pl.ds(0, WIDTH)
    every = slice(None)
    sources = [
        smooth_ref.at[every, last_x], smooth_ref.at[every, first_x],
        stacked.at[0], stacked.at[1],
        stacked.at[0, every, last_x], stacked.at[0, every, first_x],
        stacked.at[1, every, last_x], stacked.at[1, every, first_x],
    ]
    copies = []
    for index, offset in enumerate(plane):
        if index == 2:
            stacked[0] = smooth_ref[:, :, length_y - WIDTH :, :]
            stacked[1] = smooth_ref[:, :, :WIDTH, :]
        copies.append(
            pltpu.make_async_remote_copy(
                src_ref=sources[index], dst_ref=faces[index],
                send_sem=send_sems.at[index], recv_sem=recv_sems.at[index],
                device_id=device(offset), device_id_type=MESH,
            )
        )
        copies[-1].start()
    for copy in copies:
        copy.wait()


def filter_all(value, smooth, tag):
    sizes = tuple(lax.axis_size(axis) for axis in AXES)
    fields, length_x, length_y, depth = value.shape
    rows = fields * length_x * length_y
    matrix = smooth[2]
    padding = jnp.zeros((depth, 8 - WIDTH), matrix.dtype)
    x_face = jax.ShapeDtypeStruct((fields, WIDTH, length_y, depth), value.dtype)
    y_face = jax.ShapeDtypeStruct((fields, length_x, WIDTH, depth), value.dtype)
    edge = jax.ShapeDtypeStruct((fields, WIDTH, WIDTH, depth), value.dtype)
    outs = pl.pallas_call(
        functools.partial(filter_kernel, sizes),
        out_shape=[jax.ShapeDtypeStruct(value.shape, value.dtype)] + [x_face] * 2 + [y_face] * 2 + [edge] * 4,
        in_specs=[pl.BlockSpec(memory_space=pltpu.VMEM)] * 4,
        out_specs=[pl.BlockSpec(memory_space=pltpu.VMEM)] + [pl.BlockSpec(memory_space=pl.ANY)] * 8,
        scratch_shapes=[
            pltpu.VMEM((depth, rows), jnp.float32),
            pltpu.VMEM((8, rows), jnp.float32),
            pltpu.VMEM((8, rows), jnp.float32),
            pltpu.VMEM((2, fields, length_x, WIDTH, depth), jnp.float32),
            pltpu.SemaphoreType.DMA((10,)),
            pltpu.SemaphoreType.DMA((10,)),
        ],
        compiler_params=pltpu.CompilerParams(collective_id=tag, has_side_effects=True),
    )(
        value,
        matrix[:, WIDTH : WIDTH + depth],
        jnp.concatenate([padding, matrix[:, :WIDTH]], axis=1),
        jnp.concatenate([matrix[:, WIDTH + depth :], padding], axis=1),
    )
    smoothed, x_before, x_after, y_before, y_after, both_before, x_after_y_before, x_before_y_after, both_after = outs
    sections = [
        jnp.concatenate([both_before, x_before, x_before_y_after], axis=2),
        jnp.concatenate([y_before, smoothed, y_after], axis=2),
        jnp.concatenate([x_after_y_before, x_after, both_after], axis=2),
    ]
    bounds = (0, WIDTH, WIDTH + length_x, length_x + 2 * WIDTH)
    result = sum(
        sweep_lines(section, smooth[0][:, bounds[index] : bounds[index + 1]], 1)
        for index, section in enumerate(sections)
    )
    return sweep_lines(result, smooth[1], 2)


def sweep_zeta(value, matrix, tag):
    return exchange([], [], [], tag, (value, matrix), precision=lax.Precision.HIGHEST)[-1]


def with_halo(value, sides, width):
    for axis, dim in sides:
        count, length = (lax.axis_size(axis), value.shape[dim])
        up = [(i, (i + 1) % count) for i in range(count)]
        down = [(j, i) for i, j in up]
        last = lax.slice_in_dim(value, length - width, length, axis=dim)
        initial = lax.slice_in_dim(value, 0, width, axis=dim)
        before = lax.ppermute(last, axis, up)
        after = lax.ppermute(initial, axis, down)
        value = jnp.concatenate([before, value, after], axis=dim)
    return value


def banded_solve(system, source):
    extent = system.shape[0]
    lower = np.zeros(extent)
    upper = np.zeros(extent)
    middle = np.array([float(system[index, index]) for index in range(extent)])
    for index in range(1, extent):
        lower[index] = system[index, index - 1]
        upper[index - 1] = system[index - 1, index]
    rights = np.array(source)
    for index in range(1, extent):
        factor = lower[index] / middle[index - 1]
        middle[index] = middle[index] - factor * upper[index - 1]
        rights[index] = rights[index] - factor * rights[index - 1]
    answer = np.zeros(rights.shape)
    answer[extent - 1] = rights[extent - 1] / middle[extent - 1]
    for index in range(extent - 2, -1, -1):
        answer[index] = (rights[index] - upper[index] * answer[index + 1]) / middle[index]
    return answer


def derivative_table(length):
    extent = length + 2 * WIDTH
    system = np.eye(extent)
    source = np.zeros((extent, extent))
    for position in range(2, extent - 2):
        system[position, position - 1] = 1.0 / 3.0
        system[position, position + 1] = 1.0 / 3.0
        source[position, position + 1] = 7.0 / 9.0
        source[position, position - 1] = -7.0 / 9.0
        source[position, position + 2] = 1.0 / 36.0
        source[position, position - 2] = -1.0 / 36.0
    source[1, 2] = 0.5
    source[1, 0] = -0.5
    source[extent - 2, extent - 1] = 0.5
    source[extent - 2, extent - 3] = -0.5
    source[0, 1] = 1.0
    source[0, 0] = -1.0
    source[extent - 1, extent - 1] = 1.0
    source[extent - 1, extent - 2] = -1.0
    return banded_solve(system, source)[WIDTH : WIDTH + length]


def filter_table(length):
    strength = 0.4
    coeffs = [
        (193.0 + 126.0 * strength) / 256.0,
        (105.0 + 302.0 * strength) / 256.0,
        15.0 * (2.0 * strength - 1.0) / 64.0,
        45.0 * (1.0 - 2.0 * strength) / 512.0,
        5.0 * (2.0 * strength - 1.0) / 256.0,
        (1.0 - 2.0 * strength) / 512.0,
    ]
    extent = length + 2 * WIDTH
    system = np.eye(extent)
    source = np.eye(extent)
    for position in range(5, extent - 5):
        system[position, position - 1] = strength
        system[position, position + 1] = strength
        source[position, position] = coeffs[0]
        for offset in range(1, 6):
            source[position, position + offset] = coeffs[offset] / 2.0
            source[position, position - offset] = coeffs[offset] / 2.0
    return banded_solve(system, source)[WIDTH : WIDTH + length]


def sweep_lines(padded, matrix, dim, precision=lax.Precision.HIGHEST):
    return jnp.einsum(line_forms[dim], matrix, padded, precision=precision)


def faces_xi(values):
    return with_halo(values, (("xi", 1),), WIDTH)


def faces_eta(values):
    return with_halo(values, (("eta", 2),), WIDTH)


def faces_zeta(values):
    return with_halo(values, (("zeta", 3),), WIDTH)


def basic_quantities(conserved_solution):
    density = conserved_solution[0]
    fluid_speed_vector = conserved_solution[1:4] / density
    thermodynamic_stress_scalar = 0.4 * (
        conserved_solution[4] - 0.5 * jnp.sum(conserved_solution[1:4] * fluid_speed_vector, axis=0)
    )
    return (fluid_speed_vector, thermodynamic_stress_scalar, thermodynamic_stress_scalar / density)


def fluxes(
    conserved_solution, fluid_speed_vector, thermodynamic_stress_scalar, slopes, metrics, jacobian
):
    physical = [
        [
            jacobian
            * (
                metrics[0, column] * slopes[0][member]
                + metrics[1, column] * slopes[1][member]
                + metrics[2, column] * slopes[2][member]
            )
            for column in range(3)
        ]
        for member in range(4)
    ]
    spread = physical[0][0] + physical[1][1] + physical[2][2]
    totals = []
    for column in range(3):
        stress = [
            viscosity * (physical[member][column] + physical[column][member]) for member in range(3)
        ]
        stress[column] = stress[column] - 2.0 / 3.0 * viscosity * spread
        subdomain_parts = [conserved_solution[1 + column]]
        for member in range(3):
            carried = conserved_solution[1 + member] * fluid_speed_vector[column] - stress[member]
            if member == column:
                carried = carried + thermodynamic_stress_scalar
            subdomain_parts.append(carried)
        worked = (
            fluid_speed_vector[0] * stress[0]
            + fluid_speed_vector[1] * stress[1]
            + fluid_speed_vector[2] * stress[2]
        )
        subdomain_parts.append(
            (conserved_solution[4] + thermodynamic_stress_scalar) * fluid_speed_vector[column]
            - worked
            - conduction * physical[3][column]
        )
        totals.append(jnp.stack(subdomain_parts))
    return [
        metrics[direction, 0] * totals[0]
        + metrics[direction, 1] * totals[1]
        + metrics[direction, 2] * totals[2]
        for direction in range(3)
    ]


def local(conserved_solution, metrics, jacobian):
    lengths = conserved_solution.shape[1:]
    derive = [jnp.asarray(derivative_table(length), dtype=jnp.float32) for length in lengths]
    smooth = [jnp.asarray(filter_table(length), dtype=jnp.float32) for length in lengths]
    padded = exchange_primitive(conserved_solution, derive[2], 0)
    slopes = [sweep_lines(padded[k], derive[k], k + 1, lax.Precision.HIGH) for k in range(2)]
    slopes.append(padded[2])
    fluid_speed_vector, thermodynamic_stress_scalar = padded[3][0:3], padded[4]
    contra = fluxes(
        conserved_solution,
        fluid_speed_vector,
        thermodynamic_stress_scalar,
        slopes,
        metrics,
        jacobian,
    )
    padded = exchange_faces([(contra[0], "xi", 1), (contra[1], "eta", 2)], 1, (contra[2], derive[2]))
    divergence = sweep_lines(padded[0], derive[0], 1, lax.Precision.HIGH)
    divergence = divergence + sweep_lines(padded[1], derive[1], 2, lax.Precision.HIGH)
    divergence = divergence + padded[2]
    sectioned = conserved_solution - step_duration * jacobian * divergence
    return filter_all(sectioned, smooth, 2)


def solution(mesh):
    in_specs = (
        P(None, "xi", "eta", "zeta"),
        P(None, None, "xi", "eta", "zeta"),
        P("xi", "eta", "zeta"),
    )
    out_specs = P(None, "xi", "eta", "zeta")
    return jax.shard_map(local, mesh=mesh, in_specs=in_specs, out_specs=out_specs, check_vma=False)
```

```python
import functools

import jax
import jax.numpy as jnp
import numpy as np
from jax import lax
from jax.experimental import pallas as pl
from jax.experimental.pallas import tpu as pltpu
from jax.sharding import PartitionSpec as P

WIDTH = 5


viscosity = 0.15
conduction = 0.15 * 1.4 / (0.4 * 0.72)
step_duration = 0.08
line_forms = ("", "al,flyz->fayz", "al,fxlz->fxaz", "al,fxyl->fxya")
MESH = pl.DeviceIdType.MESH
AXES = ("xi", "eta", "zeta")


def primitive_state(conserved):
    density = conserved[0]
    speed = conserved[1:4] / density
    pressure = 0.4 * (conserved[4] - 0.5 * jnp.sum(conserved[1:4] * speed, axis=0))
    return speed, pressure, pressure / density


def exchange_kernel(routes, sizes, count, zeta, prepare, precision, moves, *refs):
    sources = list(refs[:count])
    refs = refs[count:]
    if prepare:
        conserved_ref = sources.pop()
    if zeta:
        if not prepare:
            block_ref = refs[0]
            refs = refs[1:]
        middle_ref, lower_ref, upper_ref = refs[:3]
        refs = refs[3:]
    extra = (1 if zeta else 0) + (2 if prepare else 0)
    targets = refs[: len(refs) - 3 - (3 if zeta else 0) - extra]
    refs = refs[len(targets) :]
    if zeta:
        out_ref = refs[0]
        refs = refs[1:]
    if prepare:
        made, pressure_ref = refs[:2]
        refs = refs[2:]
        sources.append(made)
        if zeta:
            block_ref = made
    if zeta:
        turned, before, after = refs[:3]
        refs = refs[3:]
    send_sems, recv_sems, move_sems = refs
    here = [lax.axis_index(axis) for axis in AXES]

    def device(offset):
        return tuple(
            lax.rem(here[slot] + offset[slot] + sizes[slot], sizes[slot]) for slot in range(3)
        )

    offsets = [route[0] for route in routes] + ([(0, 0, 1), (0, 0, -1)] if zeta else [])
    partners = []
    for offset in offsets:
        for way in (offset, tuple(-step for step in offset)):
            if way not in partners:
                partners.append(way)
    barrier = pltpu.get_barrier_semaphore()
    for offset in partners:
        pl.semaphore_signal(barrier, inc=1, device_id=device(offset), device_id_type=MESH)
    if prepare:
        speed, pressure, temperature = primitive_state(conserved_ref[...])
        made[0:3] = speed
        made[3] = temperature
        pressure_ref[...] = pressure
    if zeta:
        fields, length_x, length_y, depth = block_ref.shape
        rows = fields * length_x * length_y
        turned[...] = block_ref[...].reshape(rows, depth).T
        if not prepare:
            total = jnp.dot(middle_ref[...], turned[...], precision=precision,
                            preferred_element_type=jnp.float32)
    local = []
    for index, (source, source_at, target, target_at) in enumerate(moves):
        local.append(
            pltpu.make_async_copy(
                sources[source].at[source_at], targets[target].at[target_at], move_sems.at[index]
            )
        )
        local[-1].start()
    pl.semaphore_wait(barrier, len(partners))
    copies = []
    for index, (offset, source, source_at, target, target_at) in enumerate(routes):
        copies.append(
            pltpu.make_async_remote_copy(
                src_ref=sources[source].at[source_at],
                dst_ref=targets[target].at[target_at],
                send_sem=send_sems.at[index],
                recv_sem=recv_sems.at[index],
                device_id=device(offset),
                device_id_type=MESH,
            )
        )
    if zeta:
        for index, (rows_at, landing, offset) in enumerate(
            ((pl.ds(depth - 8, 8), before, (0, 0, 1)), (pl.ds(0, 8), after, (0, 0, -1)))
        ):
            copies.append(
                pltpu.make_async_remote_copy(
                    src_ref=turned.at[rows_at],
                    dst_ref=landing,
                    send_sem=send_sems.at[len(routes) + index],
                    recv_sem=recv_sems.at[len(routes) + index],
                    device_id=device(offset),
                    device_id_type=MESH,
                )
            )
    for copy in copies:
        copy.start()
    if zeta and prepare:
        total = jnp.dot(middle_ref[...], turned[...], precision=precision,
                        preferred_element_type=jnp.float32)
    for copy in copies + local:
        copy.wait()
    if zeta:
        total = total + jnp.dot(lower_ref[...], before[...], precision=precision,
                                preferred_element_type=jnp.float32)
        total = total + jnp.dot(upper_ref[...], after[...], precision=precision,
                                preferred_element_type=jnp.float32)
        out_ref[...] = total.T.reshape(fields, length_x, length_y, depth)


def exchange(arrays, routes, out_shapes, tag, zeta=None, prepare=None,
             precision=lax.Precision.HIGH, moves=()):
    sizes = tuple(lax.axis_size(axis) for axis in AXES)
    operands = [array for array, _ in arrays]
    in_specs = [pl.BlockSpec(memory_space=space) for _, space in arrays]
    out_specs = [pl.BlockSpec(memory_space=pl.ANY)] * len(out_shapes)
    out_shapes = list(out_shapes)
    scratch = []
    copies = len(routes)
    if prepare is not None:
        operands.append(prepare)
        in_specs.append(pl.BlockSpec(memory_space=pltpu.VMEM))
    if zeta is not None:
        value, matrix = zeta
        fields, length_x, length_y, depth = value.shape
        rows = fields * length_x * length_y
        padding = jnp.zeros((depth, 8 - WIDTH), matrix.dtype)
        if prepare is None:
            operands.append(value)
            in_specs.append(pl.BlockSpec(memory_space=pltpu.VMEM))
        operands += [
            matrix[:, WIDTH : WIDTH + depth],
            jnp.concatenate([padding, matrix[:, :WIDTH]], axis=1),
            jnp.concatenate([matrix[:, WIDTH + depth :], padding], axis=1),
        ]
        in_specs += [pl.BlockSpec(memory_space=pltpu.VMEM)] * 3
        out_shapes.append(jax.ShapeDtypeStruct(value.shape, value.dtype))
        out_specs.append(pl.BlockSpec(memory_space=pltpu.VMEM))
        scratch = [pltpu.VMEM((depth, rows), jnp.float32), pltpu.VMEM((8, rows), jnp.float32),
                   pltpu.VMEM((8, rows), jnp.float32)]
        copies += 2
    if prepare is not None:
        out_shapes += [
            jax.ShapeDtypeStruct(zeta[0].shape, jnp.float32),
            jax.ShapeDtypeStruct(prepare.shape[1:], jnp.float32),
        ]
        out_specs += [pl.BlockSpec(memory_space=pltpu.VMEM)] * 2
    return pl.pallas_call(
        functools.partial(
            exchange_kernel, tuple(routes), sizes, len(arrays) + (prepare is not None),
            zeta is not None, prepare is not None, precision, tuple(moves),
        ),
        out_shape=out_shapes,
        in_specs=in_specs,
        out_specs=out_specs,
        scratch_shapes=scratch + [
            pltpu.SemaphoreType.DMA((copies,)),
            pltpu.SemaphoreType.DMA((copies,)),
            pltpu.SemaphoreType.DMA((max(1, len(moves)),)),
        ],
        compiler_params=pltpu.CompilerParams(collective_id=tag, has_side_effects=True),
    )(*operands)


def offset_along(axis, step):
    return tuple(step if name == axis else 0 for name in AXES)


def window(ndim, dim, start, stop):
    return tuple(slice(start, stop) if axis == dim else slice(None) for axis in range(ndim))


def exchange_faces(items, tag, zeta=None):
    arrays, routes, out_shapes, moves = [], [], [], []
    for value, axis, dim in items:
        ndim, length = value.ndim, value.shape[dim]
        if dim == ndim - 1:
            both = jnp.stack(
                [
                    lax.slice_in_dim(value, length - WIDTH, length, axis=dim),
                    lax.slice_in_dim(value, 0, WIDTH, axis=dim),
                ]
            )
            both = jnp.moveaxis(both, dim + 1, 2).reshape(2, value.shape[0], WIDTH, -1)
            arrays.append((both, pl.ANY))
            out_shapes.append(jax.ShapeDtypeStruct(both.shape, both.dtype))
            source, target = len(arrays) - 1, len(out_shapes) - 1
            routes.append((offset_along(axis, 1), source, 0, target, 0))
            routes.append((offset_along(axis, -1), source, 1, target, 1))
        elif dim == ndim - 2:
            face = value.shape[:dim] + (WIDTH,) + value.shape[dim + 1 :]
            arrays.append((value, pltpu.VMEM))
            out_shapes += [jax.ShapeDtypeStruct(face, value.dtype)] * 2
            source, target = len(arrays) - 1, len(out_shapes) - 2
            whole = window(ndim, dim, None, None)
            last, first = window(ndim, dim, length - WIDTH, length), window(ndim, dim, 0, WIDTH)
            routes.append((offset_along(axis, 1), source, last, target, whole))
            routes.append((offset_along(axis, -1), source, first, target + 1, whole))
        else:
            arrays += [(value, pl.ANY), (value, pltpu.VMEM)]
            extended = value.shape[:dim] + (length + 2 * WIDTH,) + value.shape[dim + 1 :]
            out_shapes.append(jax.ShapeDtypeStruct(extended, value.dtype))
            source, target = len(arrays) - 2, len(out_shapes) - 1
            last, first = window(ndim, dim, length - WIDTH, length), window(ndim, dim, 0, WIDTH)
            ahead = window(ndim, dim, length + WIDTH, length + 2 * WIDTH)
            routes.append((offset_along(axis, 1), source, last, target, first))
            routes.append((offset_along(axis, -1), source, first, target, ahead))
            moves.append((source + 1, window(ndim, dim, None, None), target,
                          window(ndim, dim, WIDTH, length + WIDTH)))
    received = exchange(arrays, routes, out_shapes, tag, zeta, moves=moves)
    padded, place = [], 0
    for value, axis, dim in items:
        if dim == value.ndim - 1:
            both = received[place].reshape((2, value.shape[0], WIDTH) + value.shape[1:dim])
            both = jnp.moveaxis(both, 2, dim + 1)
            before, after = both[0], both[1]
            place += 1
        elif dim == value.ndim - 2:
            before, after = received[place], received[place + 1]
            place += 2
        else:
            padded.append(received[place])
            place += 1
            continue
        padded.append(jnp.concatenate([before, value, after], axis=dim))
    if zeta is not None:
        padded.append(received[-1])
    return padded


def exchange_primitive(conserved, matrix, tag):
    primitive = jax.ShapeDtypeStruct((4,) + conserved.shape[1:], conserved.dtype)
    length_x, length_y = primitive.shape[1], primitive.shape[2]
    every = slice(None)
    routes = [
        ((1, 0, 0), 0, (every, slice(length_x - WIDTH, length_x)), 0, (every, slice(0, WIDTH))),
        ((-1, 0, 0), 0, (every, slice(0, WIDTH)), 0, (every, slice(length_x + WIDTH, length_x + 2 * WIDTH))),
        ((0, 1, 0), 0, (every, every, slice(length_y - WIDTH, length_y)), 1, every),
        ((0, -1, 0), 0, (every, every, slice(0, WIDTH)), 2, every),
    ]
    moves = [(0, every, 0, (every, slice(WIDTH, length_x + WIDTH)))]
    extended_x = (primitive.shape[0], length_x + 2 * WIDTH) + primitive.shape[2:]
    face_y = primitive.shape[:2] + (WIDTH,) + primitive.shape[3:]
    out_shapes = [jax.ShapeDtypeStruct(face, primitive.dtype) for face in (extended_x, face_y, face_y)]
    padded_x, before_y, after_y, swept, primitive, pressure = exchange(
        [], routes, out_shapes, tag, (primitive, matrix), conserved, moves=moves
    )
    return (
        padded_x,
        jnp.concatenate([before_y, primitive, after_y], axis=2),
        swept,
        primitive,
        pressure,
    )


def exchange_plane(value, tag):
    length_x, length_y = value.shape[1], value.shape[2]
    faces_y = jnp.stack(
        [
            lax.slice_in_dim(value, length_y - WIDTH, length_y, axis=2),
            lax.slice_in_dim(value, 0, WIDTH, axis=2),
        ]
    )
    last_x, first_x = slice(length_x - WIDTH, length_x), slice(0, WIDTH)
    every = slice(None)
    routes = [
        ((1, 0, 0), 0, (every, last_x), 0, every),
        ((-1, 0, 0), 0, (every, first_x), 1, every),
        ((0, 1, 0), 1, 0, 2, every),
        ((0, -1, 0), 1, 1, 3, every),
        ((1, 1, 0), 1, (0, every, last_x), 4, every),
        ((-1, 1, 0), 1, (0, every, first_x), 5, every),
        ((1, -1, 0), 1, (1, every, last_x), 6, every),
        ((-1, -1, 0), 1, (1, every, first_x), 7, every),
    ]
    fields, depth = value.shape[0], value.shape[3]
    out_shapes = (
        [jax.ShapeDtypeStruct((fields, WIDTH, length_y, depth), value.dtype)] * 2
        + [jax.ShapeDtypeStruct((fields, length_x, WIDTH, depth), value.dtype)] * 2
        + [jax.ShapeDtypeStruct((fields, WIDTH, WIDTH, depth), value.dtype)] * 4
    )
    x_before, x_after, y_before, y_after, both_before, x_after_y_before, x_before_y_after, both_after = (
        exchange([(value, pl.ANY), (faces_y, pl.ANY)], routes, out_shapes, tag)
    )
    sections = [
        jnp.concatenate([both_before, x_before, x_before_y_after], axis=2),
        jnp.concatenate([y_before, value, y_after], axis=2),
        jnp.concatenate([x_after_y_before, x_after, both_after], axis=2),
    ]
    return jnp.concatenate(sections, axis=1)


def filter_kernel(sizes, value_ref, middle_ref, lower_ref, upper_ref, smooth_ref, *refs):
    faces = refs[:8]
    turned, before, after, stacked, send_sems, recv_sems = refs[8:]
    fields, length_x, length_y, depth = value_ref.shape
    rows = fields * length_x * length_y
    here = [lax.axis_index(axis) for axis in AXES]

    def device(offset):
        return tuple(
            lax.rem(here[slot] + offset[slot] + sizes[slot], sizes[slot]) for slot in range(3)
        )

    plane = [(1, 0, 0), (-1, 0, 0), (0, 1, 0), (0, -1, 0), (1, 1, 0), (-1, 1, 0), (1, -1, 0), (-1, -1, 0)]
    partners = plane + [(0, 0, 1), (0, 0, -1)]
    barrier = pltpu.get_barrier_semaphore()
    for offset in partners:
        pl.semaphore_signal(barrier, inc=1, device_id=device(offset), device_id_type=MESH)
    turned[...] = value_ref[...].reshape(rows, depth).T
    total = jnp.dot(middle_ref[...], turned[...], precision=lax.Precision.HIGHEST,
                    preferred_element_type=jnp.float32)
    pl.semaphore_wait(barrier, len(partners))
    along_z = [
        pltpu.make_async_remote_copy(
            src_ref=turned.at[pl.ds(depth - 8, 8)], dst_ref=before,
            send_sem=send_sems.at[8], recv_sem=recv_sems.at[8],
            device_id=device((0, 0, 1)), device_id_type=MESH,
        ),
        pltpu.make_async_remote_copy(
            src_ref=turned.at[pl.ds(0, 8)], dst_ref=after,
            send_sem=send_sems.at[9], recv_sem=recv_sems.at[9],
            device_id=device((0, 0, -1)), device_id_type=MESH,
        ),
    ]
    for copy in along_z:
        copy.start()
    for copy in along_z:
        copy.wait()
    total = total + jnp.dot(lower_ref[...], before[...], precision=lax.Precision.HIGHEST,
                            preferred_element_type=jnp.float32)
    total = total + jnp.dot(upper_ref[...], after[...], precision=lax.Precision.HIGHEST,
                            preferred_element_type=jnp.float32)
    smooth_ref[...] = total.T.reshape(fields, length_x, length_y, depth)
    last_x, first_x = pl.ds(length_x - WIDTH, WIDTH), pl.ds(0, WIDTH)
    every = slice(None)
    sources = [
        smooth_ref.at[every, last_x], smooth_ref.at[every, first_x],
        stacked.at[0], stacked.at[1],
        stacked.at[0, every, last_x], stacked.at[0, every, first_x],
        stacked.at[1, every, last_x], stacked.at[1, every, first_x],
    ]
    copies = []
    for index, offset in enumerate(plane):
        if index == 2:
            stacked[0] = smooth_ref[:, :, length_y - WIDTH :, :]
            stacked[1] = smooth_ref[:, :, :WIDTH, :]
        copies.append(
            pltpu.make_async_remote_copy(
                src_ref=sources[index], dst_ref=faces[index],
                send_sem=send_sems.at[index], recv_sem=recv_sems.at[index],
                device_id=device(offset), device_id_type=MESH,
            )
        )
        copies[-1].start()
    for copy in copies:
        copy.wait()


def filter_all(value, smooth, tag):
    sizes = tuple(lax.axis_size(axis) for axis in AXES)
    fields, length_x, length_y, depth = value.shape
    rows = fields * length_x * length_y
    matrix = smooth[2]
    padding = jnp.zeros((depth, 8 - WIDTH), matrix.dtype)
    x_face = jax.ShapeDtypeStruct((fields, WIDTH, length_y, depth), value.dtype)
    y_face = jax.ShapeDtypeStruct((fields, length_x, WIDTH, depth), value.dtype)
    edge = jax.ShapeDtypeStruct((fields, WIDTH, WIDTH, depth), value.dtype)
    outs = pl.pallas_call(
        functools.partial(filter_kernel, sizes),
        out_shape=[jax.ShapeDtypeStruct(value.shape, value.dtype)] + [x_face] * 2 + [y_face] * 2 + [edge] * 4,
        in_specs=[pl.BlockSpec(memory_space=pltpu.VMEM)] * 4,
        out_specs=[pl.BlockSpec(memory_space=pltpu.VMEM)] * 9,
        scratch_shapes=[
            pltpu.VMEM((depth, rows), jnp.float32),
            pltpu.VMEM((8, rows), jnp.float32),
            pltpu.VMEM((8, rows), jnp.float32),
            pltpu.VMEM((2, fields, length_x, WIDTH, depth), jnp.float32),
            pltpu.SemaphoreType.DMA((10,)),
            pltpu.SemaphoreType.DMA((10,)),
        ],
        compiler_params=pltpu.CompilerParams(collective_id=tag, has_side_effects=True),
    )(
        value,
        matrix[:, WIDTH : WIDTH + depth],
        jnp.concatenate([padding, matrix[:, :WIDTH]], axis=1),
        jnp.concatenate([matrix[:, WIDTH + depth :], padding], axis=1),
    )
    smoothed, x_before, x_after, y_before, y_after, both_before, x_after_y_before, x_before_y_after, both_after = outs
    sections = [
        jnp.concatenate([both_before, x_before, x_before_y_after], axis=2),
        jnp.concatenate([y_before, smoothed, y_after], axis=2),
        jnp.concatenate([x_after_y_before, x_after, both_after], axis=2),
    ]
    result = sweep_lines(jnp.concatenate(sections, axis=1), smooth[0], 1)
    return sweep_lines(result, smooth[1], 2)


def sweep_zeta(value, matrix, tag):
    return exchange([], [], [], tag, (value, matrix), precision=lax.Precision.HIGHEST)[-1]


def with_halo(value, sides, width):
    for axis, dim in sides:
        count, length = (lax.axis_size(axis), value.shape[dim])
        up = [(i, (i + 1) % count) for i in range(count)]
        down = [(j, i) for i, j in up]
        last = lax.slice_in_dim(value, length - width, length, axis=dim)
        initial = lax.slice_in_dim(value, 0, width, axis=dim)
        before = lax.ppermute(last, axis, up)
        after = lax.ppermute(initial, axis, down)
        value = jnp.concatenate([before, value, after], axis=dim)
    return value


def banded_solve(system, source):
    extent = system.shape[0]
    lower = np.zeros(extent)
    upper = np.zeros(extent)
    middle = np.array([float(system[index, index]) for index in range(extent)])
    for index in range(1, extent):
        lower[index] = system[index, index - 1]
        upper[index - 1] = system[index - 1, index]
    rights = np.array(source)
    for index in range(1, extent):
        factor = lower[index] / middle[index - 1]
        middle[index] = middle[index] - factor * upper[index - 1]
        rights[index] = rights[index] - factor * rights[index - 1]
    answer = np.zeros(rights.shape)
    answer[extent - 1] = rights[extent - 1] / middle[extent - 1]
    for index in range(extent - 2, -1, -1):
        answer[index] = (rights[index] - upper[index] * answer[index + 1]) / middle[index]
    return answer


def derivative_table(length):
    extent = length + 2 * WIDTH
    system = np.eye(extent)
    source = np.zeros((extent, extent))
    for position in range(2, extent - 2):
        system[position, position - 1] = 1.0 / 3.0
        system[position, position + 1] = 1.0 / 3.0
        source[position, position + 1] = 7.0 / 9.0
        source[position, position - 1] = -7.0 / 9.0
        source[position, position + 2] = 1.0 / 36.0
        source[position, position - 2] = -1.0 / 36.0
    source[1, 2] = 0.5
    source[1, 0] = -0.5
    source[extent - 2, extent - 1] = 0.5
    source[extent - 2, extent - 3] = -0.5
    source[0, 1] = 1.0
    source[0, 0] = -1.0
    source[extent - 1, extent - 1] = 1.0
    source[extent - 1, extent - 2] = -1.0
    return banded_solve(system, source)[WIDTH : WIDTH + length]


def filter_table(length):
    strength = 0.4
    coeffs = [
        (193.0 + 126.0 * strength) / 256.0,
        (105.0 + 302.0 * strength) / 256.0,
        15.0 * (2.0 * strength - 1.0) / 64.0,
        45.0 * (1.0 - 2.0 * strength) / 512.0,
        5.0 * (2.0 * strength - 1.0) / 256.0,
        (1.0 - 2.0 * strength) / 512.0,
    ]
    extent = length + 2 * WIDTH
    system = np.eye(extent)
    source = np.eye(extent)
    for position in range(5, extent - 5):
        system[position, position - 1] = strength
        system[position, position + 1] = strength
        source[position, position] = coeffs[0]
        for offset in range(1, 6):
            source[position, position + offset] = coeffs[offset] / 2.0
            source[position, position - offset] = coeffs[offset] / 2.0
    return banded_solve(system, source)[WIDTH : WIDTH + length]


def sweep_lines(padded, matrix, dim, precision=lax.Precision.HIGHEST):
    return jnp.einsum(line_forms[dim], matrix, padded, precision=precision)


def faces_xi(values):
    return with_halo(values, (("xi", 1),), WIDTH)


def faces_eta(values):
    return with_halo(values, (("eta", 2),), WIDTH)


def faces_zeta(values):
    return with_halo(values, (("zeta", 3),), WIDTH)


def basic_quantities(conserved_solution):
    density = conserved_solution[0]
    fluid_speed_vector = conserved_solution[1:4] / density
    thermodynamic_stress_scalar = 0.4 * (
        conserved_solution[4] - 0.5 * jnp.sum(conserved_solution[1:4] * fluid_speed_vector, axis=0)
    )
    return (fluid_speed_vector, thermodynamic_stress_scalar, thermodynamic_stress_scalar / density)


def fluxes(
    conserved_solution, fluid_speed_vector, thermodynamic_stress_scalar, slopes, metrics, jacobian
):
    physical = [
        [
            jacobian
            * (
                metrics[0, column] * slopes[0][member]
                + metrics[1, column] * slopes[1][member]
                + metrics[2, column] * slopes[2][member]
            )
            for column in range(3)
        ]
        for member in range(4)
    ]
    spread = physical[0][0] + physical[1][1] + physical[2][2]
    totals = []
    for column in range(3):
        stress = [
            viscosity * (physical[member][column] + physical[column][member]) for member in range(3)
        ]
        stress[column] = stress[column] - 2.0 / 3.0 * viscosity * spread
        subdomain_parts = [conserved_solution[1 + column]]
        for member in range(3):
            carried = conserved_solution[1 + member] * fluid_speed_vector[column] - stress[member]
            if member == column:
                carried = carried + thermodynamic_stress_scalar
            subdomain_parts.append(carried)
        worked = (
            fluid_speed_vector[0] * stress[0]
            + fluid_speed_vector[1] * stress[1]
            + fluid_speed_vector[2] * stress[2]
        )
        subdomain_parts.append(
            (conserved_solution[4] + thermodynamic_stress_scalar) * fluid_speed_vector[column]
            - worked
            - conduction * physical[3][column]
        )
        totals.append(jnp.stack(subdomain_parts))
    return [
        metrics[direction, 0] * totals[0]
        + metrics[direction, 1] * totals[1]
        + metrics[direction, 2] * totals[2]
        for direction in range(3)
    ]


def local(conserved_solution, metrics, jacobian):
    lengths = conserved_solution.shape[1:]
    derive = [jnp.asarray(derivative_table(length), dtype=jnp.float32) for length in lengths]
    smooth = [jnp.asarray(filter_table(length), dtype=jnp.float32) for length in lengths]
    padded = exchange_primitive(conserved_solution, derive[2], 0)
    slopes = [sweep_lines(padded[k], derive[k], k + 1, lax.Precision.HIGH) for k in range(2)]
    slopes.append(padded[2])
    fluid_speed_vector, thermodynamic_stress_scalar = padded[3][0:3], padded[4]
    contra = fluxes(
        conserved_solution,
        fluid_speed_vector,
        thermodynamic_stress_scalar,
        slopes,
        metrics,
        jacobian,
    )
    padded = exchange_faces([(contra[0], "xi", 1), (contra[1], "eta", 2)], 1, (contra[2], derive[2]))
    divergence = sweep_lines(padded[0], derive[0], 1, lax.Precision.HIGH)
    divergence = divergence + sweep_lines(padded[1], derive[1], 2, lax.Precision.HIGH)
    divergence = divergence + padded[2]
    sectioned = conserved_solution - step_duration * jacobian * divergence
    return filter_all(sectioned, smooth, 2)


def solution(mesh):
    in_specs = (
        P(None, "xi", "eta", "zeta"),
        P(None, None, "xi", "eta", "zeta"),
        P("xi", "eta", "zeta"),
    )
    out_specs = P(None, "xi", "eta", "zeta")
    return jax.shard_map(local, mesh=mesh, in_specs=in_specs, out_specs=out_specs, check_vma=False)
```

```python
import functools

import jax
import jax.numpy as jnp
import numpy as np
from jax import lax
from jax.experimental import pallas as pl
from jax.experimental.pallas import tpu as pltpu
from jax.sharding import PartitionSpec as P

WIDTH = 5


viscosity = 0.15
conduction = 0.15 * 1.4 / (0.4 * 0.72)
step_duration = 0.08
line_forms = ("", "al,flyz->fayz", "al,fxlz->fxaz", "al,fxyl->fxya")
MESH = pl.DeviceIdType.MESH
AXES = ("xi", "eta", "zeta")


def primitive_state(conserved):
    density = conserved[0]
    speed = conserved[1:4] / density
    pressure = 0.4 * (conserved[4] - 0.5 * jnp.sum(conserved[1:4] * speed, axis=0))
    return speed, pressure, pressure / density


def exchange_kernel(routes, sizes, count, zeta, prepare, precision, moves, *refs):
    sources = list(refs[:count])
    refs = refs[count:]
    if prepare:
        conserved_ref = sources.pop()
    if zeta:
        if not prepare:
            block_ref = refs[0]
            refs = refs[1:]
        middle_ref, lower_ref, upper_ref = refs[:3]
        refs = refs[3:]
    extra = (1 if zeta else 0) + (2 if prepare else 0)
    targets = refs[: len(refs) - 3 - (3 if zeta else 0) - extra]
    refs = refs[len(targets) :]
    if zeta:
        out_ref = refs[0]
        refs = refs[1:]
    if prepare:
        made, pressure_ref = refs[:2]
        refs = refs[2:]
        sources.append(made)
        if zeta:
            block_ref = made
    if zeta:
        turned, before, after = refs[:3]
        refs = refs[3:]
    send_sems, recv_sems, move_sems = refs
    here = [lax.axis_index(axis) for axis in AXES]

    def device(offset):
        return tuple(
            lax.rem(here[slot] + offset[slot] + sizes[slot], sizes[slot]) for slot in range(3)
        )

    offsets = [route[0] for route in routes] + ([(0, 0, 1), (0, 0, -1)] if zeta else [])
    partners = []
    for offset in offsets:
        for way in (offset, tuple(-step for step in offset)):
            if way not in partners:
                partners.append(way)
    barrier = pltpu.get_barrier_semaphore()
    for offset in partners:
        pl.semaphore_signal(barrier, inc=1, device_id=device(offset), device_id_type=MESH)
    if prepare:
        speed, pressure, temperature = primitive_state(conserved_ref[...])
        made[0:3] = speed
        made[3] = temperature
        pressure_ref[...] = pressure
    if zeta:
        fields, length_x, length_y, depth = block_ref.shape
        rows = fields * length_x * length_y
        turned[...] = block_ref[...].reshape(rows, depth).T
        if not prepare:
            total = jnp.dot(middle_ref[...], turned[...], precision=precision,
                            preferred_element_type=jnp.float32)
    local = []
    for index, (source, source_at, target, target_at) in enumerate(moves):
        local.append(
            pltpu.make_async_copy(
                sources[source].at[source_at], targets[target].at[target_at], move_sems.at[index]
            )
        )
        local[-1].start()
    pl.semaphore_wait(barrier, len(partners))
    copies = []
    for index, (offset, source, source_at, target, target_at) in enumerate(routes):
        copies.append(
            pltpu.make_async_remote_copy(
                src_ref=sources[source].at[source_at],
                dst_ref=targets[target].at[target_at],
                send_sem=send_sems.at[index],
                recv_sem=recv_sems.at[index],
                device_id=device(offset),
                device_id_type=MESH,
            )
        )
    if zeta:
        for index, (rows_at, landing, offset) in enumerate(
            ((pl.ds(depth - 8, 8), before, (0, 0, 1)), (pl.ds(0, 8), after, (0, 0, -1)))
        ):
            copies.append(
                pltpu.make_async_remote_copy(
                    src_ref=turned.at[rows_at],
                    dst_ref=landing,
                    send_sem=send_sems.at[len(routes) + index],
                    recv_sem=recv_sems.at[len(routes) + index],
                    device_id=device(offset),
                    device_id_type=MESH,
                )
            )
    for copy in copies:
        copy.start()
    if zeta and prepare:
        total = jnp.dot(middle_ref[...], turned[...], precision=precision,
                        preferred_element_type=jnp.float32)
    for copy in copies + local:
        copy.wait()
    if zeta:
        total = total + jnp.dot(lower_ref[...], before[...], precision=precision,
                                preferred_element_type=jnp.float32)
        total = total + jnp.dot(upper_ref[...], after[...], precision=precision,
                                preferred_element_type=jnp.float32)
        out_ref[...] = total.T.reshape(fields, length_x, length_y, depth)


def exchange(arrays, routes, out_shapes, tag, zeta=None, prepare=None,
             precision=lax.Precision.HIGH, moves=()):
    sizes = tuple(lax.axis_size(axis) for axis in AXES)
    operands = [array for array, _ in arrays]
    in_specs = [pl.BlockSpec(memory_space=space) for _, space in arrays]
    out_specs = [pl.BlockSpec(memory_space=pl.ANY)] * len(out_shapes)
    out_shapes = list(out_shapes)
    scratch = []
    copies = len(routes)
    if prepare is not None:
        operands.append(prepare)
        in_specs.append(pl.BlockSpec(memory_space=pltpu.VMEM))
    if zeta is not None:
        value, matrix = zeta
        fields, length_x, length_y, depth = value.shape
        rows = fields * length_x * length_y
        padding = jnp.zeros((depth, 8 - WIDTH), matrix.dtype)
        if prepare is None:
            operands.append(value)
            in_specs.append(pl.BlockSpec(memory_space=pltpu.VMEM))
        operands += [
            matrix[:, WIDTH : WIDTH + depth],
            jnp.concatenate([padding, matrix[:, :WIDTH]], axis=1),
            jnp.concatenate([matrix[:, WIDTH + depth :], padding], axis=1),
        ]
        in_specs += [pl.BlockSpec(memory_space=pltpu.VMEM)] * 3
        out_shapes.append(jax.ShapeDtypeStruct(value.shape, value.dtype))
        out_specs.append(pl.BlockSpec(memory_space=pltpu.VMEM))
        scratch = [pltpu.VMEM((depth, rows), jnp.float32), pltpu.VMEM((8, rows), jnp.float32),
                   pltpu.VMEM((8, rows), jnp.float32)]
        copies += 2
    if prepare is not None:
        out_shapes += [
            jax.ShapeDtypeStruct(zeta[0].shape, jnp.float32),
            jax.ShapeDtypeStruct(prepare.shape[1:], jnp.float32),
        ]
        out_specs += [pl.BlockSpec(memory_space=pltpu.VMEM)] * 2
    return pl.pallas_call(
        functools.partial(
            exchange_kernel, tuple(routes), sizes, len(arrays) + (prepare is not None),
            zeta is not None, prepare is not None, precision, tuple(moves),
        ),
        out_shape=out_shapes,
        in_specs=in_specs,
        out_specs=out_specs,
        scratch_shapes=scratch + [
            pltpu.SemaphoreType.DMA((copies,)),
            pltpu.SemaphoreType.DMA((copies,)),
            pltpu.SemaphoreType.DMA((max(1, len(moves)),)),
        ],
        compiler_params=pltpu.CompilerParams(collective_id=tag, has_side_effects=True),
    )(*operands)


def offset_along(axis, step):
    return tuple(step if name == axis else 0 for name in AXES)


def window(ndim, dim, start, stop):
    return tuple(slice(start, stop) if axis == dim else slice(None) for axis in range(ndim))


def exchange_faces(items, tag, zeta=None):
    arrays, routes, out_shapes, moves = [], [], [], []
    for value, axis, dim in items:
        ndim, length = value.ndim, value.shape[dim]
        if dim == ndim - 1:
            both = jnp.stack(
                [
                    lax.slice_in_dim(value, length - WIDTH, length, axis=dim),
                    lax.slice_in_dim(value, 0, WIDTH, axis=dim),
                ]
            )
            both = jnp.moveaxis(both, dim + 1, 2).reshape(2, value.shape[0], WIDTH, -1)
            arrays.append((both, pl.ANY))
            out_shapes.append(jax.ShapeDtypeStruct(both.shape, both.dtype))
            source, target = len(arrays) - 1, len(out_shapes) - 1
            routes.append((offset_along(axis, 1), source, 0, target, 0))
            routes.append((offset_along(axis, -1), source, 1, target, 1))
        elif dim == ndim - 2:
            face = value.shape[:dim] + (WIDTH,) + value.shape[dim + 1 :]
            arrays.append((value, pltpu.VMEM))
            out_shapes += [jax.ShapeDtypeStruct(face, value.dtype)] * 2
            source, target = len(arrays) - 1, len(out_shapes) - 2
            whole = window(ndim, dim, None, None)
            last, first = window(ndim, dim, length - WIDTH, length), window(ndim, dim, 0, WIDTH)
            routes.append((offset_along(axis, 1), source, last, target, whole))
            routes.append((offset_along(axis, -1), source, first, target + 1, whole))
        else:
            arrays += [(value, pl.ANY), (value, pltpu.VMEM)]
            extended = value.shape[:dim] + (length + 2 * WIDTH,) + value.shape[dim + 1 :]
            out_shapes.append(jax.ShapeDtypeStruct(extended, value.dtype))
            source, target = len(arrays) - 2, len(out_shapes) - 1
            last, first = window(ndim, dim, length - WIDTH, length), window(ndim, dim, 0, WIDTH)
            ahead = window(ndim, dim, length + WIDTH, length + 2 * WIDTH)
            routes.append((offset_along(axis, 1), source, last, target, first))
            routes.append((offset_along(axis, -1), source, first, target, ahead))
            moves.append((source + 1, window(ndim, dim, None, None), target,
                          window(ndim, dim, WIDTH, length + WIDTH)))
    received = exchange(arrays, routes, out_shapes, tag, zeta, moves=moves)
    padded, place = [], 0
    for value, axis, dim in items:
        if dim == value.ndim - 1:
            both = received[place].reshape((2, value.shape[0], WIDTH) + value.shape[1:dim])
            both = jnp.moveaxis(both, 2, dim + 1)
            before, after = both[0], both[1]
            place += 1
        elif dim == value.ndim - 2:
            before, after = received[place], received[place + 1]
            place += 2
        else:
            padded.append(received[place])
            place += 1
            continue
        padded.append(jnp.concatenate([before, value, after], axis=dim))
    if zeta is not None:
        padded.append(received[-1])
    return padded


def exchange_primitive(conserved, matrix, tag):
    primitive = jax.ShapeDtypeStruct((4,) + conserved.shape[1:], conserved.dtype)
    length_x, length_y = primitive.shape[1], primitive.shape[2]
    every = slice(None)
    routes = [
        ((1, 0, 0), 0, (every, slice(length_x - WIDTH, length_x)), 0, (every, slice(0, WIDTH))),
        ((-1, 0, 0), 0, (every, slice(0, WIDTH)), 0, (every, slice(length_x + WIDTH, length_x + 2 * WIDTH))),
        ((0, 1, 0), 0, (every, every, slice(length_y - WIDTH, length_y)), 1, every),
        ((0, -1, 0), 0, (every, every, slice(0, WIDTH)), 2, every),
    ]
    moves = [(0, every, 0, (every, slice(WIDTH, length_x + WIDTH)))]
    extended_x = (primitive.shape[0], length_x + 2 * WIDTH) + primitive.shape[2:]
    face_y = primitive.shape[:2] + (WIDTH,) + primitive.shape[3:]
    out_shapes = [jax.ShapeDtypeStruct(face, primitive.dtype) for face in (extended_x, face_y, face_y)]
    padded_x, before_y, after_y, swept, primitive, pressure = exchange(
        [], routes, out_shapes, tag, (primitive, matrix), conserved, moves=moves
    )
    return (
        padded_x,
        jnp.concatenate([before_y, primitive, after_y], axis=2),
        swept,
        primitive,
        pressure,
    )


def exchange_plane(value, tag):
    length_x, length_y = value.shape[1], value.shape[2]
    faces_y = jnp.stack(
        [
            lax.slice_in_dim(value, length_y - WIDTH, length_y, axis=2),
            lax.slice_in_dim(value, 0, WIDTH, axis=2),
        ]
    )
    last_x, first_x = slice(length_x - WIDTH, length_x), slice(0, WIDTH)
    every = slice(None)
    routes = [
        ((1, 0, 0), 0, (every, last_x), 0, every),
        ((-1, 0, 0), 0, (every, first_x), 1, every),
        ((0, 1, 0), 1, 0, 2, every),
        ((0, -1, 0), 1, 1, 3, every),
        ((1, 1, 0), 1, (0, every, last_x), 4, every),
        ((-1, 1, 0), 1, (0, every, first_x), 5, every),
        ((1, -1, 0), 1, (1, every, last_x), 6, every),
        ((-1, -1, 0), 1, (1, every, first_x), 7, every),
    ]
    fields, depth = value.shape[0], value.shape[3]
    out_shapes = (
        [jax.ShapeDtypeStruct((fields, WIDTH, length_y, depth), value.dtype)] * 2
        + [jax.ShapeDtypeStruct((fields, length_x, WIDTH, depth), value.dtype)] * 2
        + [jax.ShapeDtypeStruct((fields, WIDTH, WIDTH, depth), value.dtype)] * 4
    )
    x_before, x_after, y_before, y_after, both_before, x_after_y_before, x_before_y_after, both_after = (
        exchange([(value, pl.ANY), (faces_y, pl.ANY)], routes, out_shapes, tag)
    )
    sections = [
        jnp.concatenate([both_before, x_before, x_before_y_after], axis=2),
        jnp.concatenate([y_before, value, y_after], axis=2),
        jnp.concatenate([x_after_y_before, x_after, both_after], axis=2),
    ]
    return jnp.concatenate(sections, axis=1)


def filter_kernel(sizes, value_ref, middle_ref, lower_ref, upper_ref, smooth_ref, *refs):
    faces = refs[:8]
    turned, before, after, stacked, send_sems, recv_sems = refs[8:]
    fields, length_x, length_y, depth = value_ref.shape
    rows = fields * length_x * length_y
    here = [lax.axis_index(axis) for axis in AXES]

    def device(offset):
        return tuple(
            lax.rem(here[slot] + offset[slot] + sizes[slot], sizes[slot]) for slot in range(3)
        )

    plane = [(1, 0, 0), (-1, 0, 0), (0, 1, 0), (0, -1, 0), (1, 1, 0), (-1, 1, 0), (1, -1, 0), (-1, -1, 0)]
    partners = plane + [(0, 0, 1), (0, 0, -1)]
    barrier = pltpu.get_barrier_semaphore()
    for offset in partners:
        pl.semaphore_signal(barrier, inc=1, device_id=device(offset), device_id_type=MESH)
    turned[...] = value_ref[...].reshape(rows, depth).T
    total = jnp.dot(middle_ref[...], turned[...], precision=lax.Precision.HIGHEST,
                    preferred_element_type=jnp.float32)
    pl.semaphore_wait(barrier, len(partners))
    along_z = [
        pltpu.make_async_remote_copy(
            src_ref=turned.at[pl.ds(depth - 8, 8)], dst_ref=before,
            send_sem=send_sems.at[8], recv_sem=recv_sems.at[8],
            device_id=device((0, 0, 1)), device_id_type=MESH,
        ),
        pltpu.make_async_remote_copy(
            src_ref=turned.at[pl.ds(0, 8)], dst_ref=after,
            send_sem=send_sems.at[9], recv_sem=recv_sems.at[9],
            device_id=device((0, 0, -1)), device_id_type=MESH,
        ),
    ]
    for copy in along_z:
        copy.start()
    for copy in along_z:
        copy.wait()
    total = total + jnp.dot(lower_ref[...], before[...], precision=lax.Precision.HIGHEST,
                            preferred_element_type=jnp.float32)
    total = total + jnp.dot(upper_ref[...], after[...], precision=lax.Precision.HIGHEST,
                            preferred_element_type=jnp.float32)
    smooth_ref[...] = total.T.reshape(fields, length_x, length_y, depth)
    last_x, first_x = pl.ds(length_x - WIDTH, WIDTH), pl.ds(0, WIDTH)
    every = slice(None)
    sources = [
        smooth_ref.at[every, last_x], smooth_ref.at[every, first_x],
        stacked.at[0], stacked.at[1],
        stacked.at[0, every, last_x], stacked.at[0, every, first_x],
        stacked.at[1, every, last_x], stacked.at[1, every, first_x],
    ]
    copies = []
    for index, offset in enumerate(plane):
        if index == 2:
            stacked[0] = smooth_ref[:, :, length_y - WIDTH :, :]
            stacked[1] = smooth_ref[:, :, :WIDTH, :]
        copies.append(
            pltpu.make_async_remote_copy(
                src_ref=sources[index], dst_ref=faces[index],
                send_sem=send_sems.at[index], recv_sem=recv_sems.at[index],
                device_id=device(offset), device_id_type=MESH,
            )
        )
        copies[-1].start()
    for copy in copies:
        copy.wait()


def filter_all(value, smooth, tag):
    sizes = tuple(lax.axis_size(axis) for axis in AXES)
    fields, length_x, length_y, depth = value.shape
    rows = fields * length_x * length_y
    matrix = smooth[2]
    padding = jnp.zeros((depth, 8 - WIDTH), matrix.dtype)
    x_face = jax.ShapeDtypeStruct((fields, WIDTH, length_y, depth), value.dtype)
    y_face = jax.ShapeDtypeStruct((fields, length_x, WIDTH, depth), value.dtype)
    edge = jax.ShapeDtypeStruct((fields, WIDTH, WIDTH, depth), value.dtype)
    outs = pl.pallas_call(
        functools.partial(filter_kernel, sizes),
        out_shape=[jax.ShapeDtypeStruct(value.shape, value.dtype)] + [x_face] * 2 + [y_face] * 2 + [edge] * 4,
        in_specs=[pl.BlockSpec(memory_space=pltpu.VMEM)] * 4,
        out_specs=[pl.BlockSpec(memory_space=pltpu.VMEM)] + [pl.BlockSpec(memory_space=pl.ANY)] * 8,
        scratch_shapes=[
            pltpu.VMEM((depth, rows), jnp.float32),
            pltpu.VMEM((8, rows), jnp.float32),
            pltpu.VMEM((8, rows), jnp.float32),
            pltpu.VMEM((2, fields, length_x, WIDTH, depth), jnp.float32),
            pltpu.SemaphoreType.DMA((10,)),
            pltpu.SemaphoreType.DMA((10,)),
        ],
        compiler_params=pltpu.CompilerParams(collective_id=tag, has_side_effects=True),
    )(
        value,
        matrix[:, WIDTH : WIDTH + depth],
        jnp.concatenate([padding, matrix[:, :WIDTH]], axis=1),
        jnp.concatenate([matrix[:, WIDTH + depth :], padding], axis=1),
    )
    smoothed, x_before, x_after, y_before, y_after, both_before, x_after_y_before, x_before_y_after, both_after = outs
    sections = [
        jnp.concatenate([both_before, x_before, x_before_y_after], axis=2),
        jnp.concatenate([y_before, smoothed, y_after], axis=2),
        jnp.concatenate([x_after_y_before, x_after, both_after], axis=2),
    ]
    result = sweep_lines(jnp.concatenate(sections, axis=1), smooth[1], 2)
    return sweep_lines(result, smooth[0], 1)


def sweep_zeta(value, matrix, tag):
    return exchange([], [], [], tag, (value, matrix), precision=lax.Precision.HIGHEST)[-1]


def with_halo(value, sides, width):
    for axis, dim in sides:
        count, length = (lax.axis_size(axis), value.shape[dim])
        up = [(i, (i + 1) % count) for i in range(count)]
        down = [(j, i) for i, j in up]
        last = lax.slice_in_dim(value, length - width, length, axis=dim)
        initial = lax.slice_in_dim(value, 0, width, axis=dim)
        before = lax.ppermute(last, axis, up)
        after = lax.ppermute(initial, axis, down)
        value = jnp.concatenate([before, value, after], axis=dim)
    return value


def banded_solve(system, source):
    extent = system.shape[0]
    lower = np.zeros(extent)
    upper = np.zeros(extent)
    middle = np.array([float(system[index, index]) for index in range(extent)])
    for index in range(1, extent):
        lower[index] = system[index, index - 1]
        upper[index - 1] = system[index - 1, index]
    rights = np.array(source)
    for index in range(1, extent):
        factor = lower[index] / middle[index - 1]
        middle[index] = middle[index] - factor * upper[index - 1]
        rights[index] = rights[index] - factor * rights[index - 1]
    answer = np.zeros(rights.shape)
    answer[extent - 1] = rights[extent - 1] / middle[extent - 1]
    for index in range(extent - 2, -1, -1):
        answer[index] = (rights[index] - upper[index] * answer[index + 1]) / middle[index]
    return answer


def derivative_table(length):
    extent = length + 2 * WIDTH
    system = np.eye(extent)
    source = np.zeros((extent, extent))
    for position in range(2, extent - 2):
        system[position, position - 1] = 1.0 / 3.0
        system[position, position + 1] = 1.0 / 3.0
        source[position, position + 1] = 7.0 / 9.0
        source[position, position - 1] = -7.0 / 9.0
        source[position, position + 2] = 1.0 / 36.0
        source[position, position - 2] = -1.0 / 36.0
    source[1, 2] = 0.5
    source[1, 0] = -0.5
    source[extent - 2, extent - 1] = 0.5
    source[extent - 2, extent - 3] = -0.5
    source[0, 1] = 1.0
    source[0, 0] = -1.0
    source[extent - 1, extent - 1] = 1.0
    source[extent - 1, extent - 2] = -1.0
    return banded_solve(system, source)[WIDTH : WIDTH + length]


def filter_table(length):
    strength = 0.4
    coeffs = [
        (193.0 + 126.0 * strength) / 256.0,
        (105.0 + 302.0 * strength) / 256.0,
        15.0 * (2.0 * strength - 1.0) / 64.0,
        45.0 * (1.0 - 2.0 * strength) / 512.0,
        5.0 * (2.0 * strength - 1.0) / 256.0,
        (1.0 - 2.0 * strength) / 512.0,
    ]
    extent = length + 2 * WIDTH
    system = np.eye(extent)
    source = np.eye(extent)
    for position in range(5, extent - 5):
        system[position, position - 1] = strength
        system[position, position + 1] = strength
        source[position, position] = coeffs[0]
        for offset in range(1, 6):
            source[position, position + offset] = coeffs[offset] / 2.0
            source[position, position - offset] = coeffs[offset] / 2.0
    return banded_solve(system, source)[WIDTH : WIDTH + length]


def sweep_lines(padded, matrix, dim, precision=lax.Precision.HIGHEST):
    return jnp.einsum(line_forms[dim], matrix, padded, precision=precision)


def faces_xi(values):
    return with_halo(values, (("xi", 1),), WIDTH)


def faces_eta(values):
    return with_halo(values, (("eta", 2),), WIDTH)


def faces_zeta(values):
    return with_halo(values, (("zeta", 3),), WIDTH)


def basic_quantities(conserved_solution):
    density = conserved_solution[0]
    fluid_speed_vector = conserved_solution[1:4] / density
    thermodynamic_stress_scalar = 0.4 * (
        conserved_solution[4] - 0.5 * jnp.sum(conserved_solution[1:4] * fluid_speed_vector, axis=0)
    )
    return (fluid_speed_vector, thermodynamic_stress_scalar, thermodynamic_stress_scalar / density)


def fluxes(
    conserved_solution, fluid_speed_vector, thermodynamic_stress_scalar, slopes, metrics, jacobian
):
    physical = [
        [
            jacobian
            * (
                metrics[0, column] * slopes[0][member]
                + metrics[1, column] * slopes[1][member]
                + metrics[2, column] * slopes[2][member]
            )
            for column in range(3)
        ]
        for member in range(4)
    ]
    spread = physical[0][0] + physical[1][1] + physical[2][2]
    totals = []
    for column in range(3):
        stress = [
            viscosity * (physical[member][column] + physical[column][member]) for member in range(3)
        ]
        stress[column] = stress[column] - 2.0 / 3.0 * viscosity * spread
        subdomain_parts = [conserved_solution[1 + column]]
        for member in range(3):
            carried = conserved_solution[1 + member] * fluid_speed_vector[column] - stress[member]
            if member == column:
                carried = carried + thermodynamic_stress_scalar
            subdomain_parts.append(carried)
        worked = (
            fluid_speed_vector[0] * stress[0]
            + fluid_speed_vector[1] * stress[1]
            + fluid_speed_vector[2] * stress[2]
        )
        subdomain_parts.append(
            (conserved_solution[4] + thermodynamic_stress_scalar) * fluid_speed_vector[column]
            - worked
            - conduction * physical[3][column]
        )
        totals.append(jnp.stack(subdomain_parts))
    return [
        metrics[direction, 0] * totals[0]
        + metrics[direction, 1] * totals[1]
        + metrics[direction, 2] * totals[2]
        for direction in range(3)
    ]


def local(conserved_solution, metrics, jacobian):
    lengths = conserved_solution.shape[1:]
    derive = [jnp.asarray(derivative_table(length), dtype=jnp.float32) for length in lengths]
    smooth = [jnp.asarray(filter_table(length), dtype=jnp.float32) for length in lengths]
    padded = exchange_primitive(conserved_solution, derive[2], 0)
    slopes = [sweep_lines(padded[k], derive[k], k + 1, lax.Precision.HIGH) for k in range(2)]
    slopes.append(padded[2])
    fluid_speed_vector, thermodynamic_stress_scalar = padded[3][0:3], padded[4]
    contra = fluxes(
        conserved_solution,
        fluid_speed_vector,
        thermodynamic_stress_scalar,
        slopes,
        metrics,
        jacobian,
    )
    padded = exchange_faces([(contra[0], "xi", 1), (contra[1], "eta", 2)], 1, (contra[2], derive[2]))
    divergence = sweep_lines(padded[0], derive[0], 1, lax.Precision.HIGH)
    divergence = divergence + sweep_lines(padded[1], derive[1], 2, lax.Precision.HIGH)
    divergence = divergence + padded[2]
    sectioned = conserved_solution - step_duration * jacobian * divergence
    return filter_all(sectioned, smooth, 2)


def solution(mesh):
    in_specs = (
        P(None, "xi", "eta", "zeta"),
        P(None, None, "xi", "eta", "zeta"),
        P("xi", "eta", "zeta"),
    )
    out_specs = P(None, "xi", "eta", "zeta")
    return jax.shard_map(local, mesh=mesh, in_specs=in_specs, out_specs=out_specs, check_vma=False)
```

```python
import functools

import jax
import jax.numpy as jnp
import numpy as np
from jax import lax
from jax.experimental import pallas as pl
from jax.experimental.pallas import tpu as pltpu
from jax.sharding import PartitionSpec as P

WIDTH = 5


viscosity = 0.15
conduction = 0.15 * 1.4 / (0.4 * 0.72)
step_duration = 0.08
line_forms = ("", "al,flyz->fayz", "al,fxlz->fxaz", "al,fxyl->fxya")
MESH = pl.DeviceIdType.MESH
AXES = ("xi", "eta", "zeta")


def primitive_state(conserved):
    density = conserved[0]
    speed = conserved[1:4] / density
    pressure = 0.4 * (conserved[4] - 0.5 * jnp.sum(conserved[1:4] * speed, axis=0))
    return speed, pressure, pressure / density


def exchange_kernel(routes, sizes, count, zeta, prepare, precision, moves, *refs):
    sources = list(refs[:count])
    refs = refs[count:]
    if prepare:
        conserved_ref = sources.pop()
    if zeta:
        if not prepare:
            block_ref = refs[0]
            refs = refs[1:]
        middle_ref, lower_ref, upper_ref = refs[:3]
        refs = refs[3:]
    extra = (1 if zeta else 0) + (2 if prepare else 0)
    targets = refs[: len(refs) - 3 - (3 if zeta else 0) - extra]
    refs = refs[len(targets) :]
    if zeta:
        out_ref = refs[0]
        refs = refs[1:]
    if prepare:
        made, pressure_ref = refs[:2]
        refs = refs[2:]
        sources.append(made)
        if zeta:
            block_ref = made
    if zeta:
        turned, before, after = refs[:3]
        refs = refs[3:]
    send_sems, recv_sems, move_sems = refs
    here = [lax.axis_index(axis) for axis in AXES]

    def device(offset):
        return tuple(
            lax.rem(here[slot] + offset[slot] + sizes[slot], sizes[slot]) for slot in range(3)
        )

    offsets = [route[0] for route in routes] + ([(0, 0, 1), (0, 0, -1)] if zeta else [])
    partners = []
    for offset in offsets:
        for way in (offset, tuple(-step for step in offset)):
            if way not in partners:
                partners.append(way)
    barrier = pltpu.get_barrier_semaphore()
    for offset in partners:
        pl.semaphore_signal(barrier, inc=1, device_id=device(offset), device_id_type=MESH)
    if prepare:
        speed, pressure, temperature = primitive_state(conserved_ref[...])
        made[0:3] = speed
        made[3] = temperature
        pressure_ref[...] = pressure
    if zeta:
        fields, length_x, length_y, depth = block_ref.shape
        rows = fields * length_x * length_y
        turned[...] = block_ref[...].reshape(rows, depth).T
        if not prepare:
            total = jnp.dot(middle_ref[...], turned[...], precision=precision,
                            preferred_element_type=jnp.float32)
    local = []
    for index, (source, source_at, target, target_at) in enumerate(moves):
        local.append(
            pltpu.make_async_copy(
                sources[source].at[source_at], targets[target].at[target_at], move_sems.at[index]
            )
        )
        local[-1].start()
    pl.semaphore_wait(barrier, len(partners))
    copies = []
    for index, (offset, source, source_at, target, target_at) in enumerate(routes):
        copies.append(
            pltpu.make_async_remote_copy(
                src_ref=sources[source].at[source_at],
                dst_ref=targets[target].at[target_at],
                send_sem=send_sems.at[index],
                recv_sem=recv_sems.at[index],
                device_id=device(offset),
                device_id_type=MESH,
            )
        )
    if zeta:
        for index, (rows_at, landing, offset) in enumerate(
            ((pl.ds(depth - 8, 8), before, (0, 0, 1)), (pl.ds(0, 8), after, (0, 0, -1)))
        ):
            copies.append(
                pltpu.make_async_remote_copy(
                    src_ref=turned.at[rows_at],
                    dst_ref=landing,
                    send_sem=send_sems.at[len(routes) + index],
                    recv_sem=recv_sems.at[len(routes) + index],
                    device_id=device(offset),
                    device_id_type=MESH,
                )
            )
    for copy in copies:
        copy.start()
    if zeta and prepare:
        total = jnp.dot(middle_ref[...], turned[...], precision=precision,
                        preferred_element_type=jnp.float32)
    for copy in copies + local:
        copy.wait()
    if zeta:
        total = total + jnp.dot(lower_ref[...], before[...], precision=precision,
                                preferred_element_type=jnp.float32)
        total = total + jnp.dot(upper_ref[...], after[...], precision=precision,
                                preferred_element_type=jnp.float32)
        out_ref[...] = total.T.reshape(fields, length_x, length_y, depth)


def exchange(arrays, routes, out_shapes, tag, zeta=None, prepare=None,
             precision=lax.Precision.HIGH, moves=()):
    sizes = tuple(lax.axis_size(axis) for axis in AXES)
    operands = [array for array, _ in arrays]
    in_specs = [pl.BlockSpec(memory_space=space) for _, space in arrays]
    out_specs = [pl.BlockSpec(memory_space=pl.ANY)] * len(out_shapes)
    out_shapes = list(out_shapes)
    scratch = []
    copies = len(routes)
    if prepare is not None:
        operands.append(prepare)
        in_specs.append(pl.BlockSpec(memory_space=pltpu.VMEM))
    if zeta is not None:
        value, matrix = zeta
        fields, length_x, length_y, depth = value.shape
        rows = fields * length_x * length_y
        padding = jnp.zeros((depth, 8 - WIDTH), matrix.dtype)
        if prepare is None:
            operands.append(value)
            in_specs.append(pl.BlockSpec(memory_space=pltpu.VMEM))
        operands += [
            matrix[:, WIDTH : WIDTH + depth],
            jnp.concatenate([padding, matrix[:, :WIDTH]], axis=1),
            jnp.concatenate([matrix[:, WIDTH + depth :], padding], axis=1),
        ]
        in_specs += [pl.BlockSpec(memory_space=pltpu.VMEM)] * 3
        out_shapes.append(jax.ShapeDtypeStruct(value.shape, value.dtype))
        out_specs.append(pl.BlockSpec(memory_space=pltpu.VMEM))
        scratch = [pltpu.VMEM((depth, rows), jnp.float32), pltpu.VMEM((8, rows), jnp.float32),
                   pltpu.VMEM((8, rows), jnp.float32)]
        copies += 2
    if prepare is not None:
        out_shapes += [
            jax.ShapeDtypeStruct(zeta[0].shape, jnp.float32),
            jax.ShapeDtypeStruct(prepare.shape[1:], jnp.float32),
        ]
        out_specs += [pl.BlockSpec(memory_space=pltpu.VMEM)] * 2
    return pl.pallas_call(
        functools.partial(
            exchange_kernel, tuple(routes), sizes, len(arrays) + (prepare is not None),
            zeta is not None, prepare is not None, precision, tuple(moves),
        ),
        out_shape=out_shapes,
        in_specs=in_specs,
        out_specs=out_specs,
        scratch_shapes=scratch + [
            pltpu.SemaphoreType.DMA((copies,)),
            pltpu.SemaphoreType.DMA((copies,)),
            pltpu.SemaphoreType.DMA((max(1, len(moves)),)),
        ],
        compiler_params=pltpu.CompilerParams(collective_id=tag, has_side_effects=True),
    )(*operands)


def offset_along(axis, step):
    return tuple(step if name == axis else 0 for name in AXES)


def window(ndim, dim, start, stop):
    return tuple(slice(start, stop) if axis == dim else slice(None) for axis in range(ndim))


def exchange_faces(items, tag, zeta=None):
    arrays, routes, out_shapes, moves = [], [], [], []
    for value, axis, dim in items:
        ndim, length = value.ndim, value.shape[dim]
        if dim == ndim - 1:
            both = jnp.stack(
                [
                    lax.slice_in_dim(value, length - WIDTH, length, axis=dim),
                    lax.slice_in_dim(value, 0, WIDTH, axis=dim),
                ]
            )
            both = jnp.moveaxis(both, dim + 1, 2).reshape(2, value.shape[0], WIDTH, -1)
            arrays.append((both, pl.ANY))
            out_shapes.append(jax.ShapeDtypeStruct(both.shape, both.dtype))
            source, target = len(arrays) - 1, len(out_shapes) - 1
            routes.append((offset_along(axis, 1), source, 0, target, 0))
            routes.append((offset_along(axis, -1), source, 1, target, 1))
        elif dim == ndim - 2:
            face = value.shape[:dim] + (WIDTH,) + value.shape[dim + 1 :]
            arrays.append((value, pltpu.VMEM))
            out_shapes += [jax.ShapeDtypeStruct(face, value.dtype)] * 2
            source, target = len(arrays) - 1, len(out_shapes) - 2
            whole = window(ndim, dim, None, None)
            last, first = window(ndim, dim, length - WIDTH, length), window(ndim, dim, 0, WIDTH)
            routes.append((offset_along(axis, 1), source, last, target, whole))
            routes.append((offset_along(axis, -1), source, first, target + 1, whole))
        else:
            arrays += [(value, pl.ANY), (value, pltpu.VMEM)]
            extended = value.shape[:dim] + (length + 2 * WIDTH,) + value.shape[dim + 1 :]
            out_shapes.append(jax.ShapeDtypeStruct(extended, value.dtype))
            source, target = len(arrays) - 2, len(out_shapes) - 1
            last, first = window(ndim, dim, length - WIDTH, length), window(ndim, dim, 0, WIDTH)
            ahead = window(ndim, dim, length + WIDTH, length + 2 * WIDTH)
            routes.append((offset_along(axis, 1), source, last, target, first))
            routes.append((offset_along(axis, -1), source, first, target, ahead))
            moves.append((source + 1, window(ndim, dim, None, None), target,
                          window(ndim, dim, WIDTH, length + WIDTH)))
    received = exchange(arrays, routes, out_shapes, tag, zeta, moves=moves)
    padded, place = [], 0
    for value, axis, dim in items:
        if dim == value.ndim - 1:
            both = received[place].reshape((2, value.shape[0], WIDTH) + value.shape[1:dim])
            both = jnp.moveaxis(both, 2, dim + 1)
            before, after = both[0], both[1]
            place += 1
        elif dim == value.ndim - 2:
            before, after = received[place], received[place + 1]
            place += 2
        else:
            padded.append(received[place])
            place += 1
            continue
        padded.append(jnp.concatenate([before, value, after], axis=dim))
    if zeta is not None:
        padded.append(received[-1])
    return padded


def exchange_primitive(conserved, matrix, tag):
    primitive = jax.ShapeDtypeStruct((4,) + conserved.shape[1:], conserved.dtype)
    length_x, length_y = primitive.shape[1], primitive.shape[2]
    every = slice(None)
    routes = [
        ((1, 0, 0), 0, (every, slice(length_x - WIDTH, length_x)), 0, (every, slice(0, WIDTH))),
        ((-1, 0, 0), 0, (every, slice(0, WIDTH)), 0, (every, slice(length_x + WIDTH, length_x + 2 * WIDTH))),
        ((0, 1, 0), 0, (every, every, slice(length_y - WIDTH, length_y)), 1, every),
        ((0, -1, 0), 0, (every, every, slice(0, WIDTH)), 2, every),
    ]
    moves = [(0, every, 0, (every, slice(WIDTH, length_x + WIDTH)))]
    extended_x = (primitive.shape[0], length_x + 2 * WIDTH) + primitive.shape[2:]
    face_y = primitive.shape[:2] + (WIDTH,) + primitive.shape[3:]
    out_shapes = [jax.ShapeDtypeStruct(face, primitive.dtype) for face in (extended_x, face_y, face_y)]
    padded_x, before_y, after_y, swept, primitive, pressure = exchange(
        [], routes, out_shapes, tag, (primitive, matrix), conserved, moves=moves
    )
    return (
        padded_x,
        jnp.concatenate([before_y, primitive, after_y], axis=2),
        swept,
        primitive,
        pressure,
    )


def exchange_plane(value, tag):
    length_x, length_y = value.shape[1], value.shape[2]
    faces_y = jnp.stack(
        [
            lax.slice_in_dim(value, length_y - WIDTH, length_y, axis=2),
            lax.slice_in_dim(value, 0, WIDTH, axis=2),
        ]
    )
    last_x, first_x = slice(length_x - WIDTH, length_x), slice(0, WIDTH)
    every = slice(None)
    routes = [
        ((1, 0, 0), 0, (every, last_x), 0, every),
        ((-1, 0, 0), 0, (every, first_x), 1, every),
        ((0, 1, 0), 1, 0, 2, every),
        ((0, -1, 0), 1, 1, 3, every),
        ((1, 1, 0), 1, (0, every, last_x), 4, every),
        ((-1, 1, 0), 1, (0, every, first_x), 5, every),
        ((1, -1, 0), 1, (1, every, last_x), 6, every),
        ((-1, -1, 0), 1, (1, every, first_x), 7, every),
    ]
    fields, depth = value.shape[0], value.shape[3]
    out_shapes = (
        [jax.ShapeDtypeStruct((fields, WIDTH, length_y, depth), value.dtype)] * 2
        + [jax.ShapeDtypeStruct((fields, length_x, WIDTH, depth), value.dtype)] * 2
        + [jax.ShapeDtypeStruct((fields, WIDTH, WIDTH, depth), value.dtype)] * 4
    )
    x_before, x_after, y_before, y_after, both_before, x_after_y_before, x_before_y_after, both_after = (
        exchange([(value, pl.ANY), (faces_y, pl.ANY)], routes, out_shapes, tag)
    )
    sections = [
        jnp.concatenate([both_before, x_before, x_before_y_after], axis=2),
        jnp.concatenate([y_before, value, y_after], axis=2),
        jnp.concatenate([x_after_y_before, x_after, both_after], axis=2),
    ]
    return jnp.concatenate(sections, axis=1)


def filter_kernel(sizes, value_ref, middle_ref, lower_ref, upper_ref, smooth_ref, *refs):
    faces = refs[:8]
    turned, before, after, stacked, send_sems, recv_sems = refs[8:]
    fields, length_x, length_y, depth = value_ref.shape
    rows = fields * length_x * length_y
    here = [lax.axis_index(axis) for axis in AXES]

    def device(offset):
        return tuple(
            lax.rem(here[slot] + offset[slot] + sizes[slot], sizes[slot]) for slot in range(3)
        )

    plane = [(1, 0, 0), (-1, 0, 0), (0, 1, 0), (0, -1, 0), (1, 1, 0), (-1, 1, 0), (1, -1, 0), (-1, -1, 0)]
    partners = plane + [(0, 0, 1), (0, 0, -1)]
    barrier = pltpu.get_barrier_semaphore()
    for offset in partners:
        pl.semaphore_signal(barrier, inc=1, device_id=device(offset), device_id_type=MESH)
    turned[...] = value_ref[...].reshape(rows, depth).T
    total = jnp.dot(middle_ref[...], turned[...], precision=lax.Precision.HIGHEST,
                    preferred_element_type=jnp.float32)
    pl.semaphore_wait(barrier, len(partners))
    along_z = [
        pltpu.make_async_remote_copy(
            src_ref=turned.at[pl.ds(depth - 8, 8)], dst_ref=before,
            send_sem=send_sems.at[8], recv_sem=recv_sems.at[8],
            device_id=device((0, 0, 1)), device_id_type=MESH,
        ),
        pltpu.make_async_remote_copy(
            src_ref=turned.at[pl.ds(0, 8)], dst_ref=after,
            send_sem=send_sems.at[9], recv_sem=recv_sems.at[9],
            device_id=device((0, 0, -1)), device_id_type=MESH,
        ),
    ]
    for copy in along_z:
        copy.start()
    for copy in along_z:
        copy.wait()
    total = total + jnp.dot(lower_ref[...], before[...], precision=lax.Precision.HIGHEST,
                            preferred_element_type=jnp.float32)
    total = total + jnp.dot(upper_ref[...], after[...], precision=lax.Precision.HIGHEST,
                            preferred_element_type=jnp.float32)
    smooth_ref[...] = total.T.reshape(fields, length_x, length_y, depth)
    last_x, first_x = pl.ds(length_x - WIDTH, WIDTH), pl.ds(0, WIDTH)
    every = slice(None)
    sources = [
        smooth_ref.at[every, last_x], smooth_ref.at[every, first_x],
        stacked.at[0], stacked.at[1],
        stacked.at[0, every, last_x], stacked.at[0, every, first_x],
        stacked.at[1, every, last_x], stacked.at[1, every, first_x],
    ]
    copies = []
    for index, offset in enumerate(plane):
        if index == 2:
            stacked[0] = smooth_ref[:, :, length_y - WIDTH :, :]
            stacked[1] = smooth_ref[:, :, :WIDTH, :]
        copies.append(
            pltpu.make_async_remote_copy(
                src_ref=sources[index], dst_ref=faces[index],
                send_sem=send_sems.at[index], recv_sem=recv_sems.at[index],
                device_id=device(offset), device_id_type=MESH,
            )
        )
        copies[-1].start()
    for copy in copies:
        copy.wait()


def filter_all(value, smooth, tag):
    sizes = tuple(lax.axis_size(axis) for axis in AXES)
    fields, length_x, length_y, depth = value.shape
    rows = fields * length_x * length_y
    matrix = smooth[2]
    padding = jnp.zeros((depth, 8 - WIDTH), matrix.dtype)
    x_face = jax.ShapeDtypeStruct((fields, WIDTH, length_y, depth), value.dtype)
    y_face = jax.ShapeDtypeStruct((fields, length_x, WIDTH, depth), value.dtype)
    edge = jax.ShapeDtypeStruct((fields, WIDTH, WIDTH, depth), value.dtype)
    outs = pl.pallas_call(
        functools.partial(filter_kernel, sizes),
        out_shape=[jax.ShapeDtypeStruct(value.shape, value.dtype)] + [x_face] * 2 + [y_face] * 2 + [edge] * 4,
        in_specs=[pl.BlockSpec(memory_space=pltpu.VMEM)] * 4,
        out_specs=[pl.BlockSpec(memory_space=pltpu.VMEM)] + [pl.BlockSpec(memory_space=pl.ANY)] * 8,
        scratch_shapes=[
            pltpu.VMEM((depth, rows), jnp.float32),
            pltpu.VMEM((8, rows), jnp.float32),
            pltpu.VMEM((8, rows), jnp.float32),
            pltpu.VMEM((2, fields, length_x, WIDTH, depth), jnp.float32),
            pltpu.SemaphoreType.DMA((10,)),
            pltpu.SemaphoreType.DMA((10,)),
        ],
        compiler_params=pltpu.CompilerParams(collective_id=tag, has_side_effects=True),
    )(
        value,
        matrix[:, WIDTH : WIDTH + depth],
        jnp.concatenate([padding, matrix[:, :WIDTH]], axis=1),
        jnp.concatenate([matrix[:, WIDTH + depth :], padding], axis=1),
    )
    smoothed, x_before, x_after, y_before, y_after, both_before, x_after_y_before, x_before_y_after, both_after = outs
    sections = [
        jnp.concatenate([both_before, y_before, x_after_y_before], axis=1),
        jnp.concatenate([x_before, smoothed, x_after], axis=1),
        jnp.concatenate([x_before_y_after, y_after, both_after], axis=1),
    ]
    result = sweep_lines(jnp.concatenate(sections, axis=2), smooth[1], 2)
    return sweep_lines(result, smooth[0], 1)


def sweep_zeta(value, matrix, tag):
    return exchange([], [], [], tag, (value, matrix), precision=lax.Precision.HIGHEST)[-1]


def with_halo(value, sides, width):
    for axis, dim in sides:
        count, length = (lax.axis_size(axis), value.shape[dim])
        up = [(i, (i + 1) % count) for i in range(count)]
        down = [(j, i) for i, j in up]
        last = lax.slice_in_dim(value, length - width, length, axis=dim)
        initial = lax.slice_in_dim(value, 0, width, axis=dim)
        before = lax.ppermute(last, axis, up)
        after = lax.ppermute(initial, axis, down)
        value = jnp.concatenate([before, value, after], axis=dim)
    return value


def banded_solve(system, source):
    extent = system.shape[0]
    lower = np.zeros(extent)
    upper = np.zeros(extent)
    middle = np.array([float(system[index, index]) for index in range(extent)])
    for index in range(1, extent):
        lower[index] = system[index, index - 1]
        upper[index - 1] = system[index - 1, index]
    rights = np.array(source)
    for index in range(1, extent):
        factor = lower[index] / middle[index - 1]
        middle[index] = middle[index] - factor * upper[index - 1]
        rights[index] = rights[index] - factor * rights[index - 1]
    answer = np.zeros(rights.shape)
    answer[extent - 1] = rights[extent - 1] / middle[extent - 1]
    for index in range(extent - 2, -1, -1):
        answer[index] = (rights[index] - upper[index] * answer[index + 1]) / middle[index]
    return answer


def derivative_table(length):
    extent = length + 2 * WIDTH
    system = np.eye(extent)
    source = np.zeros((extent, extent))
    for position in range(2, extent - 2):
        system[position, position - 1] = 1.0 / 3.0
        system[position, position + 1] = 1.0 / 3.0
        source[position, position + 1] = 7.0 / 9.0
        source[position, position - 1] = -7.0 / 9.0
        source[position, position + 2] = 1.0 / 36.0
        source[position, position - 2] = -1.0 / 36.0
    source[1, 2] = 0.5
    source[1, 0] = -0.5
    source[extent - 2, extent - 1] = 0.5
    source[extent - 2, extent - 3] = -0.5
    source[0, 1] = 1.0
    source[0, 0] = -1.0
    source[extent - 1, extent - 1] = 1.0
    source[extent - 1, extent - 2] = -1.0
    return banded_solve(system, source)[WIDTH : WIDTH + length]


def filter_table(length):
    strength = 0.4
    coeffs = [
        (193.0 + 126.0 * strength) / 256.0,
        (105.0 + 302.0 * strength) / 256.0,
        15.0 * (2.0 * strength - 1.0) / 64.0,
        45.0 * (1.0 - 2.0 * strength) / 512.0,
        5.0 * (2.0 * strength - 1.0) / 256.0,
        (1.0 - 2.0 * strength) / 512.0,
    ]
    extent = length + 2 * WIDTH
    system = np.eye(extent)
    source = np.eye(extent)
    for position in range(5, extent - 5):
        system[position, position - 1] = strength
        system[position, position + 1] = strength
        source[position, position] = coeffs[0]
        for offset in range(1, 6):
            source[position, position + offset] = coeffs[offset] / 2.0
            source[position, position - offset] = coeffs[offset] / 2.0
    return banded_solve(system, source)[WIDTH : WIDTH + length]


def sweep_lines(padded, matrix, dim, precision=lax.Precision.HIGHEST):
    return jnp.einsum(line_forms[dim], matrix, padded, precision=precision)


def faces_xi(values):
    return with_halo(values, (("xi", 1),), WIDTH)


def faces_eta(values):
    return with_halo(values, (("eta", 2),), WIDTH)


def faces_zeta(values):
    return with_halo(values, (("zeta", 3),), WIDTH)


def basic_quantities(conserved_solution):
    density = conserved_solution[0]
    fluid_speed_vector = conserved_solution[1:4] / density
    thermodynamic_stress_scalar = 0.4 * (
        conserved_solution[4] - 0.5 * jnp.sum(conserved_solution[1:4] * fluid_speed_vector, axis=0)
    )
    return (fluid_speed_vector, thermodynamic_stress_scalar, thermodynamic_stress_scalar / density)


def fluxes(
    conserved_solution, fluid_speed_vector, thermodynamic_stress_scalar, slopes, metrics, jacobian
):
    physical = [
        [
            jacobian
            * (
                metrics[0, column] * slopes[0][member]
                + metrics[1, column] * slopes[1][member]
                + metrics[2, column] * slopes[2][member]
            )
            for column in range(3)
        ]
        for member in range(4)
    ]
    spread = physical[0][0] + physical[1][1] + physical[2][2]
    totals = []
    for column in range(3):
        stress = [
            viscosity * (physical[member][column] + physical[column][member]) for member in range(3)
        ]
        stress[column] = stress[column] - 2.0 / 3.0 * viscosity * spread
        subdomain_parts = [conserved_solution[1 + column]]
        for member in range(3):
            carried = conserved_solution[1 + member] * fluid_speed_vector[column] - stress[member]
            if member == column:
                carried = carried + thermodynamic_stress_scalar
            subdomain_parts.append(carried)
        worked = (
            fluid_speed_vector[0] * stress[0]
            + fluid_speed_vector[1] * stress[1]
            + fluid_speed_vector[2] * stress[2]
        )
        subdomain_parts.append(
            (conserved_solution[4] + thermodynamic_stress_scalar) * fluid_speed_vector[column]
            - worked
            - conduction * physical[3][column]
        )
        totals.append(jnp.stack(subdomain_parts))
    return [
        metrics[direction, 0] * totals[0]
        + metrics[direction, 1] * totals[1]
        + metrics[direction, 2] * totals[2]
        for direction in range(3)
    ]


def local(conserved_solution, metrics, jacobian):
    lengths = conserved_solution.shape[1:]
    derive = [jnp.asarray(derivative_table(length), dtype=jnp.float32) for length in lengths]
    smooth = [jnp.asarray(filter_table(length), dtype=jnp.float32) for length in lengths]
    padded = exchange_primitive(conserved_solution, derive[2], 0)
    slopes = [sweep_lines(padded[k], derive[k], k + 1, lax.Precision.HIGH) for k in range(2)]
    slopes.append(padded[2])
    fluid_speed_vector, thermodynamic_stress_scalar = padded[3][0:3], padded[4]
    contra = fluxes(
        conserved_solution,
        fluid_speed_vector,
        thermodynamic_stress_scalar,
        slopes,
        metrics,
        jacobian,
    )
    padded = exchange_faces([(contra[0], "xi", 1), (contra[1], "eta", 2)], 1, (contra[2], derive[2]))
    divergence = sweep_lines(padded[0], derive[0], 1, lax.Precision.HIGH)
    divergence = divergence + sweep_lines(padded[1], derive[1], 2, lax.Precision.HIGH)
    divergence = divergence + padded[2]
    sectioned = conserved_solution - step_duration * jacobian * divergence
    return filter_all(sectioned, smooth, 2)


def solution(mesh):
    in_specs = (
        P(None, "xi", "eta", "zeta"),
        P(None, None, "xi", "eta", "zeta"),
        P("xi", "eta", "zeta"),
    )
    out_specs = P(None, "xi", "eta", "zeta")
    return jax.shard_map(local, mesh=mesh, in_specs=in_specs, out_specs=out_specs, check_vma=False)
```
